32 devices in a mesh: grp: 2 (over y), seq: 4 (over z), head: 2 (over x), sub: 2 (over core).
Axes of the slice: x: 2, y: 2, z: 4, core: 2. Of those that a mesh axis runs over, the one named last changes fastest.
Arguments:
- token_ids: int32 [1024], P(('grp', 'seq')), parts along dimension 0, may hold values from 0 to 4, as said below
- basemap: int32 [5], replicated, may hold values from 0 to 4, as said below
- xz_table: bfloat16 [5, 2, 2048], P(None, None, 'head'), may hold values from -6 to 6
- bc_table: bfloat16 [5, 2, 128], replicated, may hold values from -6 to 6
- dt_table: float32 [5, 32], P(None, 'head')
- conv_x: bfloat16 [4, 2048], P(None, 'head'), may hold values from -3 to 3
- conv_bc: bfloat16 [4, 2, 128], replicated, may hold values from -3 to 3
- a_log: float32 [32], P('head'), may hold values from -0.7 to 0.7
- skip_gain: float32 [32], P('head'), may hold values from 0.5 to 1.5
- out_weight: bfloat16 [2048, 1024], P('head'), may hold values from -0.125 to 0.125
- cotangent: bfloat16 [1024, 1024], P(('grp', 'seq'), ('head', 'sub')), parts along dimension 0, may hold values from -0.3125 to 0.3125
Outputs:
- layer_out: bfloat16 [1024, 1024], P(('grp', 'seq'), ('head', 'sub')), parts along dimension 0
- d_out_weight: float32 [4096, 1024], P(('grp', 'head')), parts along dimension 0
- d_xz_table: float32 [10, 2, 2048], P('grp', None, 'head'), parts along dimension 0
- d_bc_table: float32 [10, 2, 128], P('grp'), parts along dimension 0
- d_dt_table: float32 [10, 32], P('grp', 'head'), parts along dimension 0
The draws below stay inside these ranges and needn't reach their ends.
There are 2 independent parts, one for each index of `grp`. The reference program is written for one: setup_inputs(seed, part) draws one part's arguments, and reference() takes and returns one part's arrays. A program takes and returns all parts, laid end to end along the dimension named above; an argument that names none is the same for every part. Nothing has to cross between parts.
Inputs may be any that keep to these rules, and one draw needn't show every extreme that they name: `token_ids`: exactly 3 positions hold 4; every other position holds 0 to 3. `basemap`: entry 4 is 4; entries 0 to 3 are a permutation of 0 to 3.
All inputs are finite; a program needn't handle non-finite values.
Results may differ from the reference program's by a relative error of at most 0.0049.
Values may be sent and summed in bfloat16 or wider, within the bound.
No kernel may reach another device: no remote copies, remote signals or barrier semaphores. Data moves between devices by JAX's collectives and lax.ppermute only.
A program may use at most 128 MiB of HBM per device.

```python
import jax
import jax.numpy as jnp
from jax import lax

D = 1024
HEADS = 32
HEAD_SIZE = 64
STATE = 128
CONV = 4
ALPHABET_LETTERS = 5
BLOCK = 128
NBURST = 3
LENGTH = 512
INNER = 2048


def draw_token_ids(key, part):
    base_ids = jax.random.randint(jax.random.fold_in(key, 1), (LENGTH,), 0, ALPHABET_LETTERS - 1, dtype=jnp.int32)
    shuffled = jax.random.permutation(jax.random.fold_in(key, 2), LENGTH)
    marked = jnp.zeros((LENGTH,), jnp.int32).at[shuffled[:NBURST]].set(1)
    return jnp.where(marked == 1, ALPHABET_LETTERS - 1, base_ids).astype(jnp.int32)


def draw_basemap(key, part):
    permuted = jax.random.permutation(jax.random.fold_in(key, 3), ALPHABET_LETTERS - 1).astype(jnp.int32)
    return jnp.concatenate([permuted, jnp.full((1,), ALPHABET_LETTERS - 1, jnp.int32)])


def decay_rates(key):
    return jax.random.uniform(jax.random.fold_in(key, 202), (HEADS,), jnp.float32, -0.7, 0.7)


def draw_a_log(key, part):
    return decay_rates(key)


def draw_dt_table(key, part):
    log_rates = decay_rates(key)
    fast_share = 0.5
    slow_low = 2.0
    slow_span = 32.0
    quick_spike_flags = jax.random.uniform(jax.random.fold_in(key, 303), (HEADS,), jnp.float32) < fast_share
    uniform_draw_values = jax.random.uniform(jax.random.fold_in(key, 404), (ALPHABET_LETTERS, HEADS), jnp.float32)
    level_draw = jax.random.uniform(jax.random.fold_in(key, 505), (HEADS,), jnp.float32)
    head_level = slow_low * jnp.exp(level_draw * jnp.log(slow_span))
    symbol_factor = jnp.exp((uniform_draw_values - 0.5) * jnp.log(3.0))
    slow_rates = head_level[None, :] * symbol_factor / LENGTH
    fast_rates = jnp.exp(jnp.log(1.0 / 50.0) + uniform_draw_values * jnp.log(50.0 / 30.0))
    surviving_share = 0.55 + 0.25 * uniform_draw_values
    drawn_spike = -jnp.log(surviving_share)
    quick_spike = 0.5 + uniform_draw_values
    drawn_shrink_rates = jnp.where(quick_spike_flags[None, :], fast_rates, slow_rates)
    spike_shrink_rates = jnp.where(quick_spike_flags[None, :], quick_spike, drawn_spike)
    line_index = jnp.arange(ALPHABET_LETTERS)[:, None]
    shrink_rate_table = jnp.where(line_index == ALPHABET_LETTERS - 1, spike_shrink_rates, drawn_shrink_rates)
    step_table = shrink_rate_table / jnp.exp(log_rates)[None, :]
    return jnp.log(jnp.expm1(step_table)).astype(jnp.float32)


def shard_levels(rng, shape, shards, low, high):
    gain, own = 1.0, jax.random.fold_in(rng, 6)
    for dim, blocks in shards:
        draws = jnp.exp(jax.random.uniform(jax.random.fold_in(own, dim), (blocks,), jnp.float32, low / len(shards), high / len(shards)))
        gain = gain * jnp.repeat(draws, shape[dim] // blocks).reshape([-1 if axis == dim else 1 for axis in range(len(shape))])
    return gain


def gaussian(rng, extent, width, bound, split=(), kind=jnp.bfloat16):
    drawn = width * jax.random.normal(rng, extent, jnp.float32)
    if split:
        drawn = drawn * shard_levels(rng, extent, split, -0.22, 0.18)
    return jnp.clip(drawn, -bound, bound).astype(kind)


def setup_inputs(seed: int = 0, part: int = 0) -> dict:
    arg_keys = jax.random.split(jax.random.key(seed), 12)
    own_keys = jax.random.split(jax.random.fold_in(arg_keys[11], part), 12)
    return {
        "token_ids": draw_token_ids(jax.random.fold_in(jax.random.fold_in(arg_keys[11], part), 71), part),
        "basemap": draw_basemap(jax.random.fold_in(arg_keys[11], 71), part),
        "xz_table": gaussian(arg_keys[2], (ALPHABET_LETTERS, 2, INNER), 1.0, 6.0, ((2, 2),)),
        "bc_table": gaussian(arg_keys[3], (ALPHABET_LETTERS, 2, STATE), 1.0, 6.0),
        "dt_table": draw_dt_table(jax.random.fold_in(arg_keys[11], 71), part),
        "conv_x": gaussian(arg_keys[5], (CONV, INNER), CONV ** -0.5, 3.0, ((1, 2),)),
        "conv_bc": gaussian(arg_keys[6], (CONV, 2, STATE), CONV ** -0.5, 3.0),
        "a_log": draw_a_log(jax.random.fold_in(arg_keys[11], 71), part),
        "skip_gain": jnp.clip(0.5 + 1.0 * jax.random.uniform(arg_keys[8], (HEADS,), jnp.float32) ** shard_levels(arg_keys[8], (HEADS,), ((0, 2),), -0.2, 0.2), 0.5, 1.5),
        "out_weight": gaussian(arg_keys[9], (INNER, D), INNER ** -0.5, 0.125, ((0, 2),)),
        "cotangent": gaussian(own_keys[10], (LENGTH, D), 0.02, 0.3125, ((0, 4), (1, 4))),
    }


PRECISE = lax.Precision.HIGHEST

def block_step(carry_state, pieces):
    scaled_x, logdec, b_mat, c_mat = pieces
    block_len = scaled_x.shape[0]
    running = jnp.cumsum(logdec, axis=0)
    by_head = running.T
    causal_mask = (jnp.arange(block_len)[:, None] >= jnp.arange(block_len)[None, :])[None, :, :]
    gap_matrix = by_head[:, :, None] - by_head[:, None, :]
    decay_mat = jnp.where(causal_mask, jnp.exp(jnp.where(causal_mask, gap_matrix, 0.0)), 0.0)
    scores = jnp.einsum('tn,sn->ts', c_mat, b_mat, precision=PRECISE)
    within = jnp.einsum('hts,shp->thp', scores[None, :, :] * decay_mat, scaled_x, precision=PRECISE)
    carried = jnp.exp(running)[:, :, None] * jnp.einsum('tn,hpn->thp', c_mat, carry_state, precision=PRECISE)
    to_end = jnp.exp(running[-1][None, :] - running)
    gained = jnp.einsum('shp,sn->hpn', to_end[:, :, None] * scaled_x, b_mat, precision=PRECISE)
    return (jnp.exp(running[-1])[:, None, None] * carry_state + gained, within + carried)

def state_pass(inputs, start_state, block_len):
    scaled_x, logdec, b_mat, c_mat = inputs
    block_count = scaled_x.shape[0] // block_len
    pieces = (scaled_x.reshape((block_count, block_len) + scaled_x.shape[1:]), logdec.reshape(block_count, block_len, -1), b_mat.reshape(block_count, block_len, -1), c_mat.reshape(block_count, block_len, -1))
    end_state, outputs = lax.scan(jax.checkpoint(block_step), start_state, pieces)
    return (outputs.reshape(scaled_x.shape), end_state)

def causal_conv(pre_values, weight):
    conv_width = weight.shape[0]
    length_now = pre_values.shape[0]
    padded = jnp.concatenate([jnp.zeros((conv_width - 1, pre_values.shape[1]), jnp.float32), pre_values], axis=0)
    summed = jnp.zeros_like(pre_values)
    for offset in range(conv_width):
        first_row = conv_width - 1 - offset
        summed = summed + weight[offset][None, :] * padded[first_row:first_row + length_now]
    return summed

def mixer(symbols, tables, frozen):
    xz_tab, bc_tab, dt_tab = tables
    conv_inner, conv_shared, log_rates, skip_vals = frozen
    length_now = symbols.shape[0]
    pre_x = xz_tab[symbols, 0]
    gate_act = jax.nn.silu(xz_tab[symbols, 1])
    pre_bc = bc_tab[symbols].reshape(length_now, 2 * STATE)
    dt_step = jax.nn.softplus(dt_tab[symbols])
    logdec = -jnp.exp(log_rates)[None, :] * dt_step
    flat_bc = conv_shared.reshape(CONV, 2 * STATE)
    zero_state = jnp.zeros((HEADS, HEAD_SIZE, STATE), jnp.float32)

    def one_way(px_vals, pbc_vals, step_vals, decay_vals):
        x_conv = jax.nn.silu(causal_conv(px_vals, conv_inner)).reshape(length_now, HEADS, HEAD_SIZE)
        bc_conv = jax.nn.silu(causal_conv(pbc_vals, flat_bc))
        outputs, unused_end = state_pass((x_conv * step_vals[:, :, None], decay_vals, bc_conv[:, :STATE], bc_conv[:, STATE:]), zero_state, BLOCK)
        return outputs + skip_vals[None, :, None] * x_conv
    forward_out = one_way(pre_x, pre_bc, dt_step, logdec)
    backward_out = jnp.flip(one_way(jnp.flip(pre_x, 0), jnp.flip(pre_bc, 0), jnp.flip(dt_step, 0), jnp.flip(logdec, 0)), 0)
    return (forward_out + backward_out).reshape(length_now, HEADS * HEAD_SIZE) * gate_act

def reference(token_ids, basemap, xz_table, bc_table, dt_table, conv_x, conv_bc, a_log, skip_gain, out_weight, cotangent):
    frozen = (conv_x.astype(jnp.float32), conv_bc.astype(jnp.float32), a_log, skip_gain)
    mirror_ids = basemap[jnp.flip(token_ids, 0)].astype(jnp.int32)

    def strands(tables):
        first_strand = mixer(token_ids, tables, frozen)
        second_strand = jnp.flip(mixer(mirror_ids, tables, frozen), 0)
        return (first_strand, second_strand)
    tables = (xz_table.astype(jnp.float32), bc_table.astype(jnp.float32), dt_table)
    (first_strand, second_strand), pullback = jax.vjp(strands, tables)
    rounded_first = first_strand.astype(jnp.bfloat16)
    rounded_second = second_strand.astype(jnp.bfloat16)
    layer_out = (jnp.dot(rounded_first, out_weight, preferred_element_type=jnp.float32) + jnp.dot(rounded_second, out_weight, preferred_element_type=jnp.float32)).astype(jnp.bfloat16)
    d_gated = jnp.einsum('tc,kc->tk', cotangent, out_weight, preferred_element_type=jnp.float32).astype(jnp.bfloat16)
    d_gated_wide = lax.optimization_barrier(d_gated).astype(jnp.float32)
    d_out_weight = jnp.einsum('tk,tc->kc', rounded_first, cotangent, preferred_element_type=jnp.float32) + jnp.einsum('tk,tc->kc', rounded_second, cotangent, preferred_element_type=jnp.float32)
    grads = pullback((d_gated_wide, d_gated_wide))[0]
    return (layer_out, d_out_weight, grads[0], grads[1], grads[2])
```

```python
import functools

import jax
import jax.numpy as jnp
from jax import lax
from jax.experimental import pallas as pl
from jax.experimental.pallas import tpu as pltpu
from jax.sharding import PartitionSpec as P

BLOCK = 128
LANES = 128
SYM = 8
F32 = jnp.float32
BF16 = jnp.bfloat16
NN = (((1,), (0,)), ((), ()))
NT = (((1,), (1,)), ((), ()))
TN = (((0,), (0,)), ((), ()))
X_ROW, Z_ROW, DT_ROW, MISC_ROW, TAB_ROWS = 0, 8, 16, 24, 32
VMEM_LIMIT = 56 * 1024 * 1024
XF, XB, ZZ, BCF, BCB, WIDE = 0, 128, 256, 384, 640, 896


def mm(a, b, dims):
    return lax.dot_general(a, b, dims, preferred_element_type=F32)


def halves(a):
    top = a.astype(BF16)
    return top, (a - top.astype(F32)).astype(BF16)


def thirds(a):
    top = a.astype(BF16).astype(F32)
    rest = a - top
    mid = rest.astype(BF16).astype(F32)
    return top, mid, rest - mid


def mm_fine(a, b, dims, terms):
    ah, al = halves(a)
    bh, bl = halves(b)
    (ca,), (cb,) = dims[0]
    left, right = [ah], [bh]
    if terms >= 2:
        left.append(al)
        right.append(bh)
    if terms >= 3:
        left.append(ah)
        right.append(bl)
    return mm(jnp.concatenate(left, ca), jnp.concatenate(right, cb), dims)


def permuted(table, scalars, count):
    row = lax.broadcasted_iota(jnp.int32, table[:SYM].shape, 0)
    out = jnp.zeros_like(table[:SYM])
    for k in range(count):
        picked = jnp.zeros_like(table[0:1])
        for m in range(count):
            picked = jnp.where(scalars[2 + k] == m, table[m : m + 1], picked)
        out = jnp.where(row == k, picked, out)
    return out


def sigmoid(v):
    return 1.0 / (1.0 + jnp.exp(-v))


def prepare(scalars, tok_refs, tabs_ref, bcp_ref, r, conv, vocab):
    ns = len(tok_refs)
    length = ns * BLOCK
    mine = scalars[1]
    for k in range(ns):
        at = jnp.where(mine >= k, mine - k, mine - k + ns)
        sym = lax.broadcasted_iota(jnp.int32, (SYM, BLOCK), 0)
        tok = jnp.broadcast_to(tok_refs[k][...], (SYM, BLOCK))
        r.oh[:, pl.ds(pl.multiple_of(at * BLOCK, BLOCK), BLOCK)] = (sym == tok).astype(F32)
    oh = r.oh[...]
    lane = lax.broadcasted_iota(jnp.int32, (SYM, length), 1)
    up = (
        lax.broadcasted_iota(jnp.int32, (BLOCK, BLOCK), 0)
        <= lax.broadcasted_iota(jnp.int32, (BLOCK, BLOCK), 1)
    ).astype(BF16)
    r.rows[...] = jnp.zeros_like(r.rows)
    for d in range(1 - conv, conv):
        shifted = oh if d == 0 else pltpu.roll(oh, (length - d) % length, 1)
        inside = jnp.logical_and(lane + d >= 0, lane + d < length)
        r.rows[SYM * (d + conv - 1) : SYM * (d + conv), :] = jnp.where(inside, shifted, 0.0)
    r.rows[64:128, :] = r.rows[0:64, :]
    oh_b = oh.astype(BF16)
    for b in range(ns):
        cols = slice(b * BLOCK, (b + 1) * BLOCK)
        inc = mm(oh_b[:, cols], up, NN)
        exc = inc - oh[:, cols]
        r.inc[:, cols] = inc
        r.exc[:, cols] = exc
        for k in range(3):
            r.rows[128 + SYM * k : 128 + SYM * (k + 1), cols] = inc
            r.rows[160 + SYM * k : 160 + SYM * (k + 1), cols] = exc
            r.rows[192 + SYM * k : 192 + SYM * (k + 1), cols] = oh[:, cols]
    r.wf[...] = jnp.zeros_like(r.wf)
    r.w2[...] = jnp.zeros_like(r.w2)
    for st in range(2):
        fetch = (lambda t: t) if st == 0 else (lambda t: permuted(t, scalars, vocab))
        xt = fetch(tabs_ref[X_ROW : X_ROW + SYM, :])
        zt = fetch(tabs_ref[Z_ROW : Z_ROW + SYM, :])
        dtt = fetch(tabs_ref[DT_ROW : DT_ROW + SYM, :])
        bct = fetch(bcp_ref[0:SYM, :])
        base = st * WIDE
        mid = SYM * (conv - 1)
        r.wf[mid : mid + SYM, base + ZZ : base + ZZ + LANES] = zt
        for k in range(conv):
            cx = tabs_ref[MISC_ROW + k : MISC_ROW + k + 1, :]
            cbc = bcp_ref[SYM + k : SYM + k + 1, :]
            lo, hi = mid - SYM * k, mid + SYM * k
            r.wf[lo : lo + SYM, base + XF : base + XF + LANES] = xt * cx
            r.wf[hi : hi + SYM, base + XB : base + XB + LANES] = xt * cx
            r.wf[lo : lo + SYM, base + BCF : base + BCF + 256] = bct * cbc
            r.wf[hi : hi + SYM, base + BCB : base + BCB + 256] = bct * cbc
        dt = jnp.maximum(dtt, 0.0) + jnp.log1p(jnp.exp(-jnp.abs(dtt)))
        ld = -jnp.exp(tabs_ref[MISC_ROW + 4 : MISC_ROW + 5, :]) * dt
        ld0 = jnp.broadcast_to(ld[:, 0:1], ld.shape)
        ld1 = jnp.broadcast_to(ld[:, 64:65], ld.shape)
        for i, t in enumerate((ld, ld0, ld1)):
            for k, piece in enumerate(thirds(t)):
                c = st * 384 + i * 128
                r.w2[SYM * k : SYM * (k + 1), c : c + 128] = piece
                r.w2[32 + SYM * k : 32 + SYM * (k + 1), 768 + c : 768 + c + 128] = piece
        for k, piece in enumerate(thirds(dt)):
            c = 1536 + st * 128
            r.w2[64 + SYM * k : 64 + SYM * (k + 1), c : c + 128] = piece
    wh, wl = halves(r.wf[...])
    turned = jnp.transpose(r.rows[...]).astype(BF16)
    r.pre[...] = mm(turned[:, 0:128], jnp.concatenate([wh, wl], 0), NN)
    w2 = r.w2[...].astype(BF16)
    r.pd[...] = mm(turned[:, 128:256], w2, NN)
    for st in range(2):
        for part, row0 in ((0, 0), (1, 32)):
            c = part * 768 + st * 384
            flat = mm(
                w2[row0 : row0 + 32, c : c + 128],
                r.rows[128 + row0 : 160 + row0, :].astype(BF16),
                TN,
            )
            for h in range(2):
                i = part * 4 + st * 2 + h
                r.prow[i : i + 1, :] = flat[64 * h : 64 * h + 1, :]


class Unit:
    def __init__(self, r, tabs_ref, st, b, nb):
        self.rows = rows = slice(b * BLOCK, (b + 1) * BLOCK)
        base = st * WIDE
        self.skip = tabs_ref[MISC_ROW + 5 : MISC_ROW + 6, :]
        self.dt = r.pd[rows, 1536 + st * 128 : 1536 + st * 128 + 128]
        self.p = r.pd[rows, st * 384 : st * 384 + 128]
        self.q = r.pd[rows, 768 + st * 384 : 768 + st * 384 + 128]
        self.total = self.p[BLOCK - 1 : BLOCK, :]
        self.r, self.st, self.b, self.base = r, st, b, base
        lane = lax.broadcasted_iota(jnp.int32, (BLOCK, LANES), 1)
        self.head0 = lane < 64
        row = lax.broadcasted_iota(jnp.int32, (BLOCK, BLOCK), 0)
        self.low = row >= lane
        self.upp = row <= lane

    def pre(self, col, width):
        return self.r.pre[self.rows, self.base + col : self.base + col + width]

    def act(self, col, width):
        v = self.pre(col, width)
        return v * sigmoid(v)

    def by_head(self, v):
        zero = jnp.zeros_like(v)
        return jnp.where(self.head0, v, zero), jnp.where(self.head0, zero, v)

    def decay(self, h):
        r, st = self.r, self.st
        c = st * 384 + 128 * (h + 1)
        pc = r.pd[self.rows, c : c + 128]
        qc = r.pd[self.rows, 768 + c : 768 + c + 128]
        pr = r.prow[st * 2 + h : st * 2 + h + 1, self.rows]
        qr = r.prow[4 + st * 2 + h : 4 + st * 2 + h + 1, self.rows]
        return jnp.exp(jnp.where(self.low, pc - pr, qr - qc))


def state_pass_fwd(r, tabs_ref, nb, units):
    for st in range(2):
        for b in range(nb):
            u = units[st][b]
            xf, xb = u.act(XF, 128), u.act(XB, 128)
            bcf, bcb = u.act(BCF, 256), u.act(BCB, 256)
            r.x[u.rows, st * 256 : st * 256 + 128] = xf
            r.x[u.rows, st * 256 + 128 : st * 256 + 256] = xb
            r.bc[u.rows, st * 512 : st * 512 + 256] = bcf
            r.bc[u.rows, st * 512 + 256 : st * 512 + 512] = bcb
            wf = jnp.exp(u.total - u.p) * (u.dt * xf)
            wb = jnp.exp(u.q) * (u.dt * xb)
            if b < nb - 1:
                r.s[st * 2, b + 1] = mm_fine(bcf[:, 0:128], wf, TN, 2)
            if b > 0:
                r.s[st * 2 + 1, b - 1] = mm_fine(bcb[:, 0:128], wb, TN, 2)
        for b in range(2, nb):
            r.s[st * 2, b] += jnp.exp(units[st][b - 1].total) * r.s[st * 2, b - 1]
        for b in range(nb - 3, -1, -1):
            r.s[st * 2 + 1, b] += jnp.exp(units[st][b + 1].total) * r.s[st * 2 + 1, b + 1]


class Names:
    pass


def named(refs, names):
    r = Names()
    for name, ref in zip(names, refs):
        setattr(r, name, ref)
    return r


PREP_NAMES = ("oh", "inc", "exc", "rows", "wf", "w2", "pre", "pd", "prow", "x", "bc", "s")


def prep_scratch(length):
    nb = length // BLOCK
    v = pltpu.VMEM
    return [
        v((SYM, length), F32),
        v((SYM, length), F32),
        v((SYM, length), F32),
        v((256, length), F32),
        v((64, 2 * WIDE), F32),
        v((128, 1792), F32),
        v((length, 2 * WIDE), F32),
        v((length, 1792), F32),
        v((SYM, length), F32),
        v((length, 512), F32),
        v((length, 1024), F32),
        v((4, nb, LANES, LANES), F32),
    ]


def forward_kernel(scalars, *refs, ns, conv, vocab):
    tok_refs, (tabs_ref, bcp_ref, out_ref) = refs[:ns], refs[ns : ns + 3]
    r = named(refs[ns + 3 :], PREP_NAMES)
    prepare(scalars, tok_refs, tabs_ref, bcp_ref, r, conv, vocab)
    units = [[Unit(r, tabs_ref, st, b, ns) for b in range(ns)] for st in range(2)]
    state_pass_fwd(r, tabs_ref, ns, units)
    for b in range(ns):
        gated = []
        for st in range(2):
            u = units[st][b]
            xf = r.x[u.rows, st * 256 : st * 256 + 128]
            xb = r.x[u.rows, st * 256 + 128 : st * 256 + 256]
            left, right = [], []
            d0, d1 = u.decay(0), u.decay(1)
            y = u.skip * (xf + xb)
            for way, x, mask in ((0, xf, u.low), (1, xb, u.upp)):
                c = st * 512 + way * 256
                bm, cm = r.bc[u.rows, c : c + 128], r.bc[u.rows, c + 128 : c + 256]
                g = jnp.where(mask, mm_fine(cm, bm, NT, 3), 0.0)
                left += [(g * d0).astype(BF16), (g * d1).astype(BF16)]
                right += list(u.by_head((u.dt * x).astype(BF16)))
                if (way == 0 and b > 0) or (way == 1 and b < ns - 1):
                    enter = jnp.exp(u.p) if way == 0 else jnp.exp(u.total - u.q)
                    y = y + enter * mm_fine(cm, r.s[st * 2 + way, b], NN, 2)
            y = y + mm(jnp.concatenate(left, 1), jnp.concatenate(right, 0), NN)
            gated.append(y * u.act(ZZ, 128))
        out_ref[units[0][b].rows, :] = (gated[0] + gated[1]).astype(BF16)


def backward_kernel(scalars, *refs, ns, conv, vocab):
    tok_refs, (tabs_ref, bcp_ref) = refs[:ns], refs[ns : ns + 2]
    dg_refs, out_ref = refs[ns + 2 : 2 * ns + 2], refs[2 * ns + 2]
    r = named(refs[2 * ns + 3 :], PREP_NAMES + ("ds", "dg", "dpre"))
    prepare(scalars, tok_refs, tabs_ref, bcp_ref, r, conv, vocab)
    mine = scalars[1]
    for k in range(ns):
        at = jnp.where(mine >= k, mine - k, mine - k + ns)
        r.dg[pl.ds(pl.multiple_of(at * BLOCK, BLOCK), BLOCK), :] = dg_refs[k][...].astype(F32)
    units = [[Unit(r, tabs_ref, st, b, ns) for b in range(ns)] for st in range(2)]
    state_pass_fwd(r, tabs_ref, ns, units)
    for st in range(2):
        for b in range(ns):
            u = units[st][b]
            dy = r.dg[u.rows, :] * u.act(ZZ, 128)
            cf = r.bc[u.rows, st * 512 + 128 : st * 512 + 256]
            cb = r.bc[u.rows, st * 512 + 384 : st * 512 + 512]
            if b > 0:
                r.ds[st * 2, b - 1] = mm_fine(cf, jnp.exp(u.p) * dy, TN, 2)
            if b < ns - 1:
                r.ds[st * 2 + 1, b + 1] = mm_fine(cb, jnp.exp(u.total - u.q) * dy, TN, 2)
        for b in range(ns - 3, -1, -1):
            r.ds[st * 2, b] += jnp.exp(units[st][b + 1].total) * r.ds[st * 2, b + 1]
        for b in range(2, ns):
            r.ds[st * 2 + 1, b] += jnp.exp(units[st][b - 1].total) * r.ds[st * 2 + 1, b - 1]
    d_steps, d_decays = [], []
    for st in range(2):
        d_step = jnp.zeros((SYM, LANES), F32)
        d_decay = jnp.zeros((SYM, LANES), F32)
        for b in range(ns):
            u = units[st][b]
            base = st * WIDE
            x = [r.x[u.rows, st * 256 + w * 128 : st * 256 + w * 128 + 128] for w in range(2)]
            dgv = r.dg[u.rows, :]
            pz = u.pre(ZZ, 128)
            sz = sigmoid(pz)
            dy = dgv * (pz * sz)
            dyr = dy.astype(BF16)
            dyw = dyr.astype(F32)
            dy0, dy1 = u.by_head(dyr)
            decays = (u.decay(0), u.decay(1))
            inputs = [u.dt * v for v in x]
            ur = [v.astype(BF16) for v in inputs]
            uw = [v.astype(F32) for v in ur]
            uh = [u.by_head(v) for v in ur]
            d_pair = mm(dyr, jnp.concatenate([uh[0][0], uh[0][1], uh[1][0], uh[1][1]], 0), NT)
            masks = (u.low, u.upp)
            ends = (jnp.exp(u.total - u.p), jnp.exp(u.q))
            enters = (jnp.exp(u.p), jnp.exp(u.total - u.q))
            weights, bms, cms = [], [], []
            for w in range(2):
                c = st * 512 + w * 256
                bm, cm = r.bc[u.rows, c : c + 128], r.bc[u.rows, c + 128 : c + 256]
                g = jnp.where(masks[w], mm_fine(cm, bm, NT, 3), 0.0)
                weights.append([(g * decays[0]).astype(BF16), (g * decays[1]).astype(BF16)])
                bms.append(bm)
                cms.append(cm)
            du_both = mm(
                jnp.concatenate(
                    [
                        jnp.concatenate([weights[0][0], weights[1][0]], 1),
                        jnp.concatenate([weights[0][1], weights[1][1]], 1),
                    ],
                    0,
                ),
                jnp.concatenate([dy0, dy1], 0),
                TN,
            )
            y = u.skip * (x[0] + x[1])
            mixes, step_part, flat = [], 0.0, 0.0
            for w in range(2):
                inner = mm(
                    jnp.concatenate(weights[w], 1), jnp.concatenate([uh[w][0], uh[w][1]], 0), NN
                )
                du_in = du_both[w * BLOCK : (w + 1) * BLOCK]
                has_enter = (w == 0 and b > 0) or (w == 1 and b < ns - 1)
                has_leave = (w == 0 and b < ns - 1) or (w == 1 and b > 0)
                y = y + inner
                row = dyw * inner - uw[w] * du_in
                du = du_in
                d_g = jnp.where(
                    masks[w],
                    d_pair[:, w * 256 : w * 256 + 128] * decays[0]
                    + d_pair[:, w * 256 + 128 : w * 256 + 256] * decays[1],
                    0.0,
                ).astype(BF16)
                d_c = mm(d_g, bms[w].astype(BF16), NN)
                d_b = mm(d_g, cms[w].astype(BF16), TN)
                enter_part = gain_part = None
                if has_enter:
                    state = r.s[st * 2 + w, b]
                    carried = enters[w] * mm_fine(cms[w], state, NN, 2)
                    y = y + carried
                    enter_part = dy * carried
                    d_c = d_c + mm((enters[w] * dy).astype(BF16), state.astype(BF16), NT)
                if has_leave:
                    d_state = r.ds[st * 2 + w, b]
                    d_gain = mm_fine(bms[w], d_state, NN, 2)
                    du = du + ends[w] * d_gain
                    gain = ends[w] * inputs[w]
                    gain_part = gain * d_gain
                    d_b = d_b + mm(gain.astype(BF16), d_state.astype(BF16), NT)
                if has_enter and has_leave:
                    flat = flat + jnp.exp(u.total) * jnp.sum(state * d_state, 0, keepdims=True)
                if w == 1:
                    row = -row
                if enter_part is not None:
                    row = row + enter_part if w == 0 else row - enter_part
                if gain_part is not None:
                    row = row - gain_part if w == 0 else row + gain_part
                if w == 0 and gain_part is not None:
                    flat = flat + jnp.sum(gain_part, 0, keepdims=True)
                if w == 1 and enter_part is not None:
                    flat = flat + jnp.sum(enter_part, 0, keepdims=True)
                mixes.append(row)
                step_part = step_part + du * x[w]
                dx = du * u.dt + dy * u.skip
                px = u.pre((XF, XB)[w], 128)
                sx = sigmoid(px)
                col = base + (XF, XB)[w]
                r.dpre[u.rows, col : col + 128] = (dx * (sx * (1.0 + px * (1.0 - sx)))).astype(BF16)
                col = (BCF, BCB)[w]
                for i, grad in enumerate((d_b, d_c)):
                    pb = u.pre(col + 128 * i, 128)
                    sb = sigmoid(pb)
                    at = base + col + 128 * i
                    r.dpre[u.rows, at : at + 128] = (
                        grad * (sb * (1.0 + pb * (1.0 - sb)))
                    ).astype(BF16)
            d_z = dgv * y * (sz * (1.0 + pz * (1.0 - sz)))
            r.dpre[u.rows, base + ZZ : base + ZZ + 128] = d_z.astype(BF16)
            inc = r.inc[:, u.rows]
            exc = r.exc[:, u.rows]
            inc_b, exc_b, oh_b = inc.astype(BF16), exc.astype(BF16), r.oh[:, u.rows].astype(BF16)
            right = list(halves(mixes[0])) + list(halves(mixes[1]))
            d_decay = d_decay + mm(
                jnp.concatenate([inc_b, inc_b, exc_b, exc_b], 1), jnp.concatenate(right, 0), NN
            )
            d_decay = d_decay + inc[:, BLOCK - 1 : BLOCK] * flat
            d_step = d_step + mm(
                jnp.concatenate([oh_b, oh_b], 1), jnp.concatenate(halves(step_part), 0), NN
            )
        d_steps.append(d_step)
        d_decays.append(d_decay)
    d_tab = mm(r.rows[0:64, :].astype(BF16), r.dpre[...], NN)
    mid = SYM * (conv - 1)
    result = None
    for st in range(2):
        base = st * WIDE
        d_x = jnp.zeros((SYM, 128), F32)
        d_bc = jnp.zeros((SYM, 256), F32)
        for k in range(conv):
            cx = tabs_ref[MISC_ROW + k : MISC_ROW + k + 1, :]
            cbc = bcp_ref[SYM + k : SYM + k + 1, :]
            lo, hi = mid - SYM * k, mid + SYM * k
            d_x = d_x + cx * (
                d_tab[lo : lo + SYM, base + XF : base + XF + 128]
                + d_tab[hi : hi + SYM, base + XB : base + XB + 128]
            )
            d_bc = d_bc + cbc * (
                d_tab[lo : lo + SYM, base + BCF : base + BCF + 256]
                + d_tab[hi : hi + SYM, base + BCB : base + BCB + 256]
            )
        d_zt = d_tab[mid : mid + SYM, base + ZZ : base + ZZ + 128]
        dtt = tabs_ref[DT_ROW : DT_ROW + SYM, :]
        if st == 1:
            dtt = permuted(dtt, scalars, vocab)
        rate = -jnp.exp(tabs_ref[MISC_ROW + 4 : MISC_ROW + 5, :])
        d_dt = (d_steps[st] + rate * d_decays[st]) * sigmoid(dtt)
        wide = jnp.concatenate([d_x, d_zt, d_dt, d_bc], 1)
        if st == 0:
            result = wide
        else:
            row = lax.broadcasted_iota(jnp.int32, wide.shape, 0)
            for k in range(vocab):
                result = result + jnp.where(row == scalars[2 + k], wide[k : k + 1], 0.0)
    out_ref[...] = result


def call_forward(scalars, toks, tabs, bcp, conv, vocab):
    ns = len(toks)
    length = ns * BLOCK
    whole = lambda shape: pl.BlockSpec(shape, lambda i, s: (0,) * len(shape))
    return pl.pallas_call(
        functools.partial(forward_kernel, ns=ns, conv=conv, vocab=vocab),
        out_shape=jax.ShapeDtypeStruct((length, LANES), BF16),
        grid_spec=pltpu.PrefetchScalarGridSpec(
            num_scalar_prefetch=1,
            grid=(1,),
            in_specs=[whole((1, BLOCK))] * ns
            + [pl.BlockSpec((TAB_ROWS, LANES), lambda i, s: (0, s[0])), whole(bcp.shape)],
            out_specs=whole((length, LANES)),
            scratch_shapes=prep_scratch(length),
        ),
        compiler_params=pltpu.CompilerParams(vmem_limit_bytes=VMEM_LIMIT),
        name="mix_forward",
    )(scalars, *toks, tabs, bcp)


def call_backward(scalars, toks, tabs, bcp, d_gated, conv, vocab):
    ns = len(toks)
    length = ns * BLOCK
    whole = lambda shape: pl.BlockSpec(shape, lambda i, s: (0,) * len(shape))
    extra = [
        pltpu.VMEM((4, ns, LANES, LANES), F32),
        pltpu.VMEM((length, LANES), F32),
        pltpu.VMEM((length, 2 * WIDE), BF16),
    ]
    return pl.pallas_call(
        functools.partial(backward_kernel, ns=ns, conv=conv, vocab=vocab),
        out_shape=jax.ShapeDtypeStruct((SYM, 640), F32),
        grid_spec=pltpu.PrefetchScalarGridSpec(
            num_scalar_prefetch=1,
            grid=(1,),
            in_specs=[whole((1, BLOCK))] * ns
            + [pl.BlockSpec((TAB_ROWS, LANES), lambda i, s: (0, s[0])), whole(bcp.shape)]
            + [whole((BLOCK, LANES))] * ns,
            out_specs=whole((SYM, 640)),
            scratch_shapes=prep_scratch(length) + extra,
        ),
        compiler_params=pltpu.CompilerParams(vmem_limit_bytes=VMEM_LIMIT),
        name="mix_backward",
    )(scalars, *toks, tabs, bcp, *d_gated)


def weight_kernel(scalars, g_ref, cot_ref, out_ref, *, ns):
    mine = scalars[0]
    total = None
    for k in range(ns):
        at = jnp.where(mine >= k, mine - k, mine - k + ns)
        rows = g_ref[0, pl.ds(pl.multiple_of(at * BLOCK, BLOCK), BLOCK), :]
        part = mm(rows, cot_ref[k], TN)
        total = part if total is None else total + part
    out_ref[...] = total


def call_weight(scalars, gs, cots):
    slices, length, _ = gs.shape
    ns, _, columns = cots.shape
    return pl.pallas_call(
        functools.partial(weight_kernel, ns=ns),
        out_shape=jax.ShapeDtypeStruct((slices * LANES, columns), F32),
        grid_spec=pltpu.PrefetchScalarGridSpec(
            num_scalar_prefetch=1,
            grid=(slices,),
            in_specs=[
                pl.BlockSpec((1, length, LANES), lambda i, s: (i, 0, 0)),
                pl.BlockSpec((ns, BLOCK, columns), lambda i, s: (0, 0, 0)),
            ],
            out_specs=pl.BlockSpec((LANES, columns), lambda i, s: (s[1 + i], 0)),
        ),
        compiler_params=pltpu.CompilerParams(vmem_limit_bytes=VMEM_LIMIT),
        name="weight_grad",
    )(scalars, gs, cots)


def around(x, axis):
    n = lax.axis_size(axis)
    return [x] + [
        lax.ppermute(x, axis, [(i, (i + k) % n) for i in range(n)]) for k in range(1, n)
    ]


def by_channel(
    token_ids, basemap, xz_table, bc_table, dt_table, conv_x, conv_bc, a_log, skip_gain, out_weight, cotangent
):
    ns, nc, nh = lax.axis_size("seq"), lax.axis_size("sub"), lax.axis_size("head")
    s, c, h = lax.axis_index("seq"), lax.axis_index("sub"), lax.axis_index("head")
    vocab, _, inner = xz_table.shape
    conv = conv_x.shape[0]
    heads = dt_table.shape[1]
    width = out_weight.shape[1]
    j = c * ns + s
    toks = around(token_ids.reshape(1, BLOCK), "seq")
    cot_rows = lax.all_gather(cotangent, ("head", "sub"), axis=1, tiled=True)
    scalars = jnp.concatenate([jnp.stack([j, s]).astype(jnp.int32), basemap])
    pad = lambda a, n: jnp.pad(a, ((0, n - a.shape[0]), (0, 0)))
    spread = lambda a: jnp.repeat(a, inner // heads, axis=1)
    tabs = jnp.concatenate(
        [
            pad(xz_table[:, 0].astype(F32), SYM),
            pad(xz_table[:, 1].astype(F32), SYM),
            pad(spread(dt_table), SYM),
            conv_x.astype(F32),
            pad(spread(jnp.stack([a_log, skip_gain])), SYM - conv),
        ],
        0,
    )
    bcp = jnp.concatenate(
        [
            pad(bc_table.reshape(vocab, -1).astype(F32), SYM),
            pad(conv_bc.reshape(conv, -1).astype(F32), SYM),
        ],
        0,
    )
    weight_rows = lax.dynamic_slice_in_dim(out_weight, c * (ns * LANES), ns * LANES, 0)
    d_mine = lax.dot_general(cot_rows, weight_rows, NT, preferred_element_type=F32).astype(BF16)
    at = lambda k: lax.dynamic_slice_in_dim(d_mine, ((s + k) % ns) * LANES, LANES, 1)
    d_gated = [at(0)] + [
        lax.ppermute(at(k), "seq", [(i, (i + k) % ns) for i in range(ns)]) for k in range(1, ns)
    ]
    cots = around(cot_rows, "seq")
    gated = call_forward(scalars, toks, tabs, bcp, conv, vocab)
    grads = call_backward(scalars, toks, tabs, bcp, d_gated, conv, vocab)
    gs = jnp.stack(around(gated, "seq"), 0)
    other = lax.ppermute(gs, "sub", [(i, (i + 1) % nc) for i in range(nc)])
    gs = jnp.concatenate([gs, other], 0)
    order = (s - jnp.arange(ns, dtype=jnp.int32)) % ns
    place = jnp.concatenate([c * ns + order, (1 - c) * ns + order]).astype(jnp.int32)
    d_out_weight = call_weight(
        jnp.concatenate([s[None].astype(jnp.int32), place]), gs, jnp.stack(cots, 0)
    )
    mine = lax.dynamic_slice_in_dim(gs, s * BLOCK, BLOCK, 1)
    wg = out_weight.reshape(nc * ns, LANES, width)[place]
    part = width // (nh * nc)
    parts = []
    for k in range(nh):
        first = (((h + k) % nh) * nc + c) * part
        cols = lax.dynamic_slice_in_dim(wg, first, part, 2)
        parts.append(jnp.einsum("jtk,jkc->tc", mine, cols, preferred_element_type=F32))
    total = parts[0]
    for k in range(1, nh):
        total = total + lax.ppermute(parts[k], "head", [(i, (i + k) % nh) for i in range(nh)])
    layer_out = total.astype(BF16)
    own, shared = grads[:, : 3 * LANES], grads[:, 3 * LANES :]
    shared = lax.psum(shared, ("seq", "head", "sub"))
    owns = lax.all_gather(own, ("sub", "seq"))
    full = jnp.moveaxis(owns[:, :vocab], 0, 1).reshape(vocab, nc * ns, 3, LANES)
    full = jnp.moveaxis(full, 2, 1).reshape(vocab, 3, inner)
    d_xz = full[:, :2]
    d_dt = full[:, 2].reshape(vocab, heads, inner // heads).sum(-1)
    d_bc = shared[:vocab].reshape(bc_table.shape)
    return (layer_out, d_out_weight, d_xz, d_bc, d_dt)


PRECISE = lax.Precision.HIGHEST


def carried_in(part, axis, combine, identity):
    place = lax.axis_index(axis)
    gathered = jax.tree.map(lambda a: lax.all_gather(a, axis), part)
    state = jax.tree.map(lambda a, e: jnp.zeros_like(a) + jnp.asarray(e, a.dtype), part, identity)

    def one(hop, state):
        return combine(
            state, jax.tree.map(lambda a: lax.dynamic_index_in_dim(a, hop, 0, False), gathered)
        )

    return lax.fori_loop(0, place, one, state)


def carried_in_2(array, axis, combine, identity):
    length, mine = (lax.axis_size(axis), lax.axis_index(axis))
    everything = jax.tree.map(
        lambda part, kind: lax.all_gather(part.astype(kind), axis),
        array,
        jax.tree.map(lambda a: jnp.bfloat16 if a.dtype == jnp.float32 else a.dtype, array),
    )
    start = jax.tree.map(
        lambda part, zero: jnp.broadcast_to(jnp.asarray(zero, part.dtype), part.shape),
        array,
        identity,
    )

    def hop(k, before):
        at = length - 1 - k
        reached = at > mine
        new = combine(
            before, jax.tree.map(lambda part, own: part[at].astype(own.dtype), everything, array)
        )
        return jax.tree.map(lambda a, b: jnp.where(reached, a, b), new, before)

    return lax.fori_loop(0, length, hop, start)


def with_halo(block, sides, width):
    for axis, dim in sides:
        count = lax.axis_size(axis)
        forward = [(i, i + 1) for i in range(count - 1)]
        backward = [(target, source) for source, target in forward]
        low = lax.ppermute(
            lax.slice_in_dim(block, block.shape[dim] - width, None, axis=dim), axis, forward
        )
        high = lax.ppermute(lax.slice_in_dim(block, 0, width, axis=dim), axis, backward)
        block = jnp.concatenate([low, block, high], axis=dim)
    return block


def block_step(carry_state, pieces):
    scaled_x, logdec, b_mat, c_mat = pieces
    block_len = scaled_x.shape[0]
    running = jnp.cumsum(logdec, axis=0)
    by_head = running.T
    causal_mask = (jnp.arange(block_len)[:, None] >= jnp.arange(block_len)[None, :])[None, :, :]
    gap_matrix = by_head[:, :, None] - by_head[:, None, :]
    decay_mat = jnp.where(causal_mask, jnp.exp(jnp.where(causal_mask, gap_matrix, 0.0)), 0.0)
    scores = jnp.einsum("tn,sn->ts", c_mat, b_mat, precision=PRECISE)
    within = jnp.einsum("hts,shp->thp", scores[None, :, :] * decay_mat, scaled_x, precision=PRECISE)
    carried = jnp.exp(running)[:, :, None] * jnp.einsum(
        "tn,hpn->thp", c_mat, carry_state, precision=PRECISE
    )
    to_end = jnp.exp(running[-1][None, :] - running)
    gained = jnp.einsum("shp,sn->hpn", to_end[:, :, None] * scaled_x, b_mat, precision=PRECISE)
    return (jnp.exp(running[-1])[:, None, None] * carry_state + gained, within + carried)


def state_pass(inputs, start_state, block_len):
    scaled_x, logdec, b_mat, c_mat = inputs
    block_count = scaled_x.shape[0] // block_len
    pieces = (
        scaled_x.reshape((block_count, block_len) + scaled_x.shape[1:]),
        logdec.reshape(block_count, block_len, -1),
        b_mat.reshape(block_count, block_len, -1),
        c_mat.reshape(block_count, block_len, -1),
    )
    end_state, outputs = lax.scan(jax.checkpoint(block_step), start_state, pieces)
    return (outputs.reshape(scaled_x.shape), end_state)


def final_state(inputs):
    scaled_x, logdec, b_mat, c_mat = inputs
    running = jnp.cumsum(logdec, axis=0)
    to_end = jnp.exp(running[-1][None, :] - running)
    gained = jnp.einsum("shp,sn->hpn", to_end[:, :, None] * scaled_x, b_mat, precision=PRECISE)
    return (jnp.exp(running[-1]), gained)


def lookup(symbols, table):
    vocab_size = table.shape[0]
    onehot = (symbols[:, None] == jnp.arange(vocab_size, dtype=jnp.int32)[None, :]).astype(
        jnp.float32
    )
    return jnp.dot(onehot, table, precision=PRECISE)


def conv_rows(extended, weight, row_count, forward):
    conv_width = weight.shape[0]
    rim_width = conv_width - 1
    summed = jnp.zeros((row_count, extended.shape[1]), jnp.float32)
    for offset in range(conv_width):
        if forward:
            first_row = rim_width - offset
        else:
            first_row = rim_width + offset
        summed = summed + weight[offset][None, :] * extended[first_row : first_row + row_count]
    return summed


def open_inputs(ext_sym, inside_mask, tables, frozen):
    xz_tab, bc_tab, dt_tab = tables
    conv_inner, conv_shared, log_rates, skip_vals = frozen
    rim_width = conv_inner.shape[0] - 1
    row_count = ext_sym.shape[0] - 2 * rim_width
    vocab_size = xz_tab.shape[0]
    inner_dim = xz_tab.shape[2]
    head_count = dt_tab.shape[1]
    state_dim = bc_tab.shape[2]
    looked = lookup(ext_sym, xz_tab.reshape(vocab_size, 2 * inner_dim)) * inside_mask[:, None]
    pre_x = looked[:, :inner_dim]
    gate_act = jax.nn.silu(looked[rim_width : rim_width + row_count, inner_dim:])
    pre_bc = lookup(ext_sym, bc_tab.reshape(vocab_size, 2 * state_dim)) * inside_mask[:, None]
    dt_step = jax.nn.softplus(lookup(ext_sym[rim_width : rim_width + row_count], dt_tab))
    logdec = -jnp.exp(log_rates)[None, :] * dt_step
    flat_bc = conv_shared.reshape(conv_inner.shape[0], 2 * state_dim)

    def one_way(forward):
        x_conv = jax.nn.silu(conv_rows(pre_x, conv_inner, row_count, forward)).reshape(
            row_count, head_count, -1
        )
        bc_conv = jax.nn.silu(conv_rows(pre_bc, flat_bc, row_count, forward))
        return (x_conv, bc_conv[:, :state_dim], bc_conv[:, state_dim:])

    x_fwd, b_fwd, c_fwd = one_way(True)
    x_back, b_back, c_back = one_way(False)
    ahead_in = (x_fwd * dt_step[:, :, None], logdec, b_fwd, c_fwd)
    behind_in = (
        jnp.flip(x_back * dt_step[:, :, None], 0),
        jnp.flip(logdec, 0),
        jnp.flip(b_back, 0),
        jnp.flip(c_back, 0),
    )
    skip_term = skip_vals[None, :, None] * (x_fwd + x_back)
    return (ahead_in, behind_in, skip_term, gate_act)


def combine(earlier, later):
    decay_early, state_early = earlier
    decay_late, state_late = later
    return (decay_early * decay_late, decay_late[:, None, None] * state_early + state_late)


def carries(ahead_pair, behind_pair):
    ahead_out = carried_in(
        (ahead_pair[0], ahead_pair[1]),
        "seq",
        combine,
        (jnp.ones_like(ahead_pair[0]), jnp.zeros_like(ahead_pair[1])),
    )
    behind_out = carried_in_2(
        (behind_pair[0], behind_pair[1]),
        "seq",
        combine,
        (jnp.ones_like(behind_pair[0]), jnp.zeros_like(behind_pair[1])),
    )
    return (ahead_out[1], behind_out[1])


def decay_weights(adjoint, start_state):
    return jnp.sum(adjoint * start_state, axis=(1, 2))


def shards(
    token_ids,
    basemap,
    xz_table,
    bc_table,
    dt_table,
    conv_x,
    conv_bc,
    a_log,
    skip_gain,
    out_weight,
    cotangent,
):
    row_count = token_ids.shape[0]
    rim_width = conv_x.shape[0] - 1
    ext_ids = with_halo(token_ids, (("seq", 0),), rim_width)
    first_row = lax.axis_index("seq") * row_count - rim_width
    where_global = first_row + jnp.arange(row_count + 2 * rim_width, dtype=jnp.int32)
    inside_mask = jnp.logical_and(
        where_global >= 0, where_global < row_count * lax.axis_size("seq")
    ).astype(jnp.float32)
    vocab_size = basemap.shape[0]
    matches = ext_ids[:, None] == jnp.arange(vocab_size, dtype=jnp.int32)[None, :]
    mapped = jnp.sum(jnp.where(matches, basemap[None, :], 0), axis=1)
    ext_sym = jnp.where(lax.axis_index("sub") == 1, mapped, ext_ids)
    tables = (xz_table.astype(jnp.float32), bc_table.astype(jnp.float32), dt_table)
    frozen = (conv_x.astype(jnp.float32), conv_bc.astype(jnp.float32), a_log, skip_gain)

    def summary(tabs_in):
        ahead_in, behind_in, skip_term, gate_act = open_inputs(
            ext_sym, inside_mask, tabs_in, frozen
        )
        decay_fwd, end_fwd = final_state(ahead_in)
        decay_back, end_back = final_state(behind_in)
        return (decay_fwd, end_fwd, decay_back, end_back)

    (decay_fwd, end_fwd, decay_back, end_back), pull_summary = jax.vjp(summary, tables)
    start_fwd, start_back = carries((decay_fwd, end_fwd), (decay_back, end_back))

    def finished(tabs_in, begin_fwd, begin_back):
        ahead_in, behind_in, skip_term, gate_act = open_inputs(
            ext_sym, inside_mask, tabs_in, frozen
        )
        out_fwd, unused_fwd = state_pass(ahead_in, begin_fwd, BLOCK)
        out_back, unused_back = state_pass(behind_in, begin_back, BLOCK)
        return (out_fwd + jnp.flip(out_back, 0) + skip_term).reshape(row_count, -1) * gate_act

    gated, pull_finished = jax.vjp(finished, tables, start_fwd, start_back)
    gated_bf = gated.astype(jnp.bfloat16)
    products = jnp.dot(gated_bf, out_weight, preferred_element_type=jnp.float32)
    layer_out = lax.psum_scatter(products, ("head", "sub"), scatter_dimension=1, tiled=True).astype(
        jnp.bfloat16
    )
    full_cot = lax.all_gather(cotangent, ("head", "sub"), axis=1, tiled=True)
    d_gated = jnp.einsum(
        "tc,kc->tk", full_cot, out_weight, preferred_element_type=jnp.float32
    ).astype(jnp.bfloat16)
    weight_part = jnp.einsum("tk,tc->kc", gated_bf, full_cot, preferred_element_type=jnp.float32)
    d_gated_wide = lax.optimization_barrier(d_gated).astype(jnp.float32)
    grads_first, direct_fwd, direct_back = pull_finished(d_gated_wide)
    adjoint_back, adjoint_fwd = carries((decay_back, direct_back), (decay_fwd, direct_fwd))
    grads_second = pull_summary(
        (
            decay_weights(adjoint_fwd, start_fwd),
            adjoint_fwd,
            decay_weights(adjoint_back, start_back),
            adjoint_back,
        )
    )[0]
    d_tables = jax.tree.map(lambda former, latter: former + latter, grads_first, grads_second)
    d_xz, d_bc, d_dt = d_tables
    d_bc = lax.psum(d_bc, ("seq", "head", "sub"))
    d_out_weight, d_xz, d_dt = lax.psum((weight_part, d_xz, d_dt), ("seq", "sub"))
    return (layer_out, d_out_weight, d_xz, d_bc, d_dt)


def solution(mesh):
    in_specs = (
        P(("grp", "seq")),
        P(),
        P(None, None, "head"),
        P(),
        P(None, "head"),
        P(None, "head"),
        P(),
        P("head"),
        P("head"),
        P("head", None),
        P(("grp", "seq"), ("head", "sub")),
    )
    out_specs = (
        P(("grp", "seq"), ("head", "sub")),
        P(("grp", "head"), None),
        P("grp", None, "head"),
        P("grp", None, None),
        P("grp", "head"),
    )
    def run(*args):
        ns, nc = mesh.shape["seq"], mesh.shape["sub"]
        rows, inner, heads = args[0].shape[0], args[2].shape[2], args[4].shape[1]
        by_lanes = (
            rows == BLOCK
            and nc == 2
            and ns > 1
            and inner == ns * nc * LANES
            and inner == heads * (LANES // 2)
            and args[3].shape[2] == LANES
            and args[5].shape[0] == 4
            and args[9].shape[1] == args[10].shape[1] * nc * mesh.shape["head"]
        )
        return (by_channel if by_lanes else shards)(*args)

    return jax.shard_map(run, mesh=mesh, in_specs=in_specs, out_specs=out_specs, check_vma=False)
```

```python
import functools

import jax
import jax.numpy as jnp
from jax import lax
from jax.experimental import pallas as pl
from jax.experimental.pallas import tpu as pltpu
from jax.sharding import PartitionSpec as P

BLOCK = 128
LANES = 128
SYM = 8
F32 = jnp.float32
BF16 = jnp.bfloat16
NN = (((1,), (0,)), ((), ()))
NT = (((1,), (1,)), ((), ()))
TN = (((0,), (0,)), ((), ()))
X_ROW, Z_ROW, DT_ROW, MISC_ROW, TAB_ROWS = 0, 8, 16, 24, 32
RAW = 8
VMEM_LIMIT = 56 * 1024 * 1024
XF, XB, ZZ, BCF, BCB, WIDE = 0, 128, 256, 384, 640, 896


def mm(a, b, dims):
    return lax.dot_general(a, b, dims, preferred_element_type=F32)


def halves(a):
    top = a.astype(BF16)
    return top, (a - top.astype(F32)).astype(BF16)


def thirds(a):
    top = a.astype(BF16).astype(F32)
    rest = a - top
    mid = rest.astype(BF16).astype(F32)
    return top, mid, rest - mid


def mm_fine(a, b, dims, terms):
    ah, al = halves(a)
    bh, bl = halves(b)
    (ca,), (cb,) = dims[0]
    left, right = [ah], [bh]
    if terms >= 2:
        left.append(al)
        right.append(bh)
    if terms >= 3:
        left.append(ah)
        right.append(bl)
    return mm(jnp.concatenate(left, ca), jnp.concatenate(right, cb), dims)


def permuted(table, scalars, count):
    row = lax.broadcasted_iota(jnp.int32, table[:SYM].shape, 0)
    out = jnp.zeros_like(table[:SYM])
    for k in range(count):
        picked = jnp.zeros_like(table[0:1])
        for m in range(count):
            picked = jnp.where(scalars[k] == m, table[m : m + 1], picked)
        out = jnp.where(row == k, picked, out)
    return out


def sigmoid(v):
    return 1.0 / (1.0 + jnp.exp(-v))


def gather_tables(scalars, raw, tabs_ref, bcp_ref, conv, vocab):
    xz_ref, bc_ref, conv_ref, conv_bc_ref, dt_ref, a_log_ref, skip_ref = raw[1:]
    j = scalars[0]
    lanes = pl.ds(pl.multiple_of(j * LANES, LANES), LANES)
    head0 = lax.broadcasted_iota(jnp.int32, (1, LANES), 1) < 64
    pair = lambda a, b: jnp.where(head0, a, b)
    tabs_ref[...] = jnp.zeros_like(tabs_ref)
    bcp_ref[...] = jnp.zeros_like(bcp_ref)
    for k in range(vocab):
        tabs_ref[X_ROW + k : X_ROW + k + 1, :] = xz_ref[k, 0:1, lanes].astype(F32)
        tabs_ref[Z_ROW + k : Z_ROW + k + 1, :] = xz_ref[k, 1:2, lanes].astype(F32)
        tabs_ref[DT_ROW + k : DT_ROW + k + 1, :] = pair(dt_ref[k, 2 * j], dt_ref[k, 2 * j + 1])
        for i in range(2):
            bcp_ref[k : k + 1, i * 128 : i * 128 + 128] = bc_ref[k, i : i + 1, :].astype(F32)
    for k in range(conv):
        tabs_ref[MISC_ROW + k : MISC_ROW + k + 1, :] = conv_ref[k : k + 1, lanes].astype(F32)
        for i in range(2):
            bcp_ref[SYM + k : SYM + k + 1, i * 128 : i * 128 + 128] = conv_bc_ref[
                k, i : i + 1, :
            ].astype(F32)
    at = MISC_ROW + 4
    tabs_ref[at : at + 1, :] = pair(a_log_ref[2 * j], a_log_ref[2 * j + 1])
    tabs_ref[at + 1 : at + 2, :] = pair(skip_ref[2 * j], skip_ref[2 * j + 1])


def prepare(scalars, tok_refs, raw, tabs_ref, bcp_ref, r, conv, vocab):
    gather_tables(scalars, raw, tabs_ref, bcp_ref, conv, vocab)
    ns = len(tok_refs)
    length = ns * BLOCK
    mine = scalars[1]
    for k in range(ns):
        at = jnp.where(mine >= k, mine - k, mine - k + ns)
        sym = lax.broadcasted_iota(jnp.int32, (SYM, BLOCK), 0)
        tok = jnp.broadcast_to(tok_refs[k][...], (SYM, BLOCK))
        r.oh[:, pl.ds(pl.multiple_of(at * BLOCK, BLOCK), BLOCK)] = (sym == tok).astype(F32)
    oh = r.oh[...]
    lane = lax.broadcasted_iota(jnp.int32, (SYM, length), 1)
    up = (
        lax.broadcasted_iota(jnp.int32, (BLOCK, BLOCK), 0)
        <= lax.broadcasted_iota(jnp.int32, (BLOCK, BLOCK), 1)
    ).astype(BF16)
    r.rows[...] = jnp.zeros_like(r.rows)
    for d in range(1 - conv, conv):
        shifted = oh if d == 0 else pltpu.roll(oh, (length - d) % length, 1)
        inside = jnp.logical_and(lane + d >= 0, lane + d < length)
        r.rows[SYM * (d + conv - 1) : SYM * (d + conv), :] = jnp.where(inside, shifted, 0.0)
    r.rows[64:128, :] = r.rows[0:64, :]
    oh_b = oh.astype(BF16)
    for b in range(ns):
        cols = slice(b * BLOCK, (b + 1) * BLOCK)
        inc = mm(oh_b[:, cols], up, NN)
        exc = inc - oh[:, cols]
        r.inc[:, cols] = inc
        r.exc[:, cols] = exc
        for k in range(3):
            r.rows[128 + SYM * k : 128 + SYM * (k + 1), cols] = inc
            r.rows[160 + SYM * k : 160 + SYM * (k + 1), cols] = exc
            r.rows[192 + SYM * k : 192 + SYM * (k + 1), cols] = oh[:, cols]
    r.wf[...] = jnp.zeros_like(r.wf)
    r.w2[...] = jnp.zeros_like(r.w2)
    for st in range(2):
        fetch = (lambda t: t) if st == 0 else (lambda t: permuted(t, raw[0], vocab))
        xt = fetch(tabs_ref[X_ROW : X_ROW + SYM, :])
        zt = fetch(tabs_ref[Z_ROW : Z_ROW + SYM, :])
        dtt = fetch(tabs_ref[DT_ROW : DT_ROW + SYM, :])
        bct = fetch(bcp_ref[0:SYM, :])
        base = st * WIDE
        mid = SYM * (conv - 1)
        r.wf[mid : mid + SYM, base + ZZ : base + ZZ + LANES] = zt
        for k in range(conv):
            cx = tabs_ref[MISC_ROW + k : MISC_ROW + k + 1, :]
            cbc = bcp_ref[SYM + k : SYM + k + 1, :]
            lo, hi = mid - SYM * k, mid + SYM * k
            r.wf[lo : lo + SYM, base + XF : base + XF + LANES] = xt * cx
            r.wf[hi : hi + SYM, base + XB : base + XB + LANES] = xt * cx
            r.wf[lo : lo + SYM, base + BCF : base + BCF + 256] = bct * cbc
            r.wf[hi : hi + SYM, base + BCB : base + BCB + 256] = bct * cbc
        dt = jnp.maximum(dtt, 0.0) + jnp.log1p(jnp.exp(-jnp.abs(dtt)))
        ld = -jnp.exp(tabs_ref[MISC_ROW + 4 : MISC_ROW + 5, :]) * dt
        ld0 = jnp.broadcast_to(ld[:, 0:1], ld.shape)
        ld1 = jnp.broadcast_to(ld[:, 64:65], ld.shape)
        for i, t in enumerate((ld, ld0, ld1)):
            for k, piece in enumerate(thirds(t)):
                c = st * 384 + i * 128
                r.w2[SYM * k : SYM * (k + 1), c : c + 128] = piece
                r.w2[32 + SYM * k : 32 + SYM * (k + 1), 768 + c : 768 + c + 128] = piece
        for k, piece in enumerate(thirds(dt)):
            c = 1536 + st * 128
            r.w2[64 + SYM * k : 64 + SYM * (k + 1), c : c + 128] = piece
    wh, wl = halves(r.wf[...])
    turned = jnp.transpose(r.rows[...]).astype(BF16)
    r.pre[...] = mm(turned[:, 0:128], jnp.concatenate([wh, wl], 0), NN)
    w2 = r.w2[...].astype(BF16)
    r.pd[...] = mm(turned[:, 128:256], w2, NN)
    for st in range(2):
        for part, row0 in ((0, 0), (1, 32)):
            c = part * 768 + st * 384
            flat = mm(
                w2[row0 : row0 + 32, c : c + 128],
                r.rows[128 + row0 : 160 + row0, :].astype(BF16),
                TN,
            )
            for h in range(2):
                i = part * 4 + st * 2 + h
                r.prow[i : i + 1, :] = flat[64 * h : 64 * h + 1, :]


class Unit:
    def __init__(self, r, tabs_ref, st, b, nb):
        self.rows = rows = slice(b * BLOCK, (b + 1) * BLOCK)
        base = st * WIDE
        self.skip = tabs_ref[MISC_ROW + 5 : MISC_ROW + 6, :]
        self.dt = r.pd[rows, 1536 + st * 128 : 1536 + st * 128 + 128]
        self.p = r.pd[rows, st * 384 : st * 384 + 128]
        self.q = r.pd[rows, 768 + st * 384 : 768 + st * 384 + 128]
        self.total = self.p[BLOCK - 1 : BLOCK, :]
        self.r, self.st, self.b, self.base = r, st, b, base
        lane = lax.broadcasted_iota(jnp.int32, (BLOCK, LANES), 1)
        self.head0 = lane < 64
        row = lax.broadcasted_iota(jnp.int32, (BLOCK, BLOCK), 0)
        self.low = row >= lane
        self.upp = row <= lane

    def pre(self, col, width):
        return self.r.pre[self.rows, self.base + col : self.base + col + width]

    def act(self, col, width):
        v = self.pre(col, width)
        return v * sigmoid(v)

    def by_head(self, v):
        zero = jnp.zeros_like(v)
        return jnp.where(self.head0, v, zero), jnp.where(self.head0, zero, v)

    def decay(self, h):
        r, st = self.r, self.st
        c = st * 384 + 128 * (h + 1)
        pc = r.pd[self.rows, c : c + 128]
        qc = r.pd[self.rows, 768 + c : 768 + c + 128]
        pr = r.prow[st * 2 + h : st * 2 + h + 1, self.rows]
        qr = r.prow[4 + st * 2 + h : 4 + st * 2 + h + 1, self.rows]
        return jnp.exp(jnp.where(self.low, pc - pr, qr - qc))


def state_pass_fwd(r, tabs_ref, nb, units):
    for st in range(2):
        for b in range(nb):
            u = units[st][b]
            xf, xb = u.act(XF, 128), u.act(XB, 128)
            bcf, bcb = u.act(BCF, 256), u.act(BCB, 256)
            r.x[u.rows, st * 256 : st * 256 + 128] = xf
            r.x[u.rows, st * 256 + 128 : st * 256 + 256] = xb
            r.bc[u.rows, st * 512 : st * 512 + 256] = bcf
            r.bc[u.rows, st * 512 + 256 : st * 512 + 512] = bcb
            wf = jnp.exp(u.total - u.p) * (u.dt * xf)
            wb = jnp.exp(u.q) * (u.dt * xb)
            if b < nb - 1:
                r.s[st * 2, b + 1] = mm_fine(bcf[:, 0:128], wf, TN, 2)
            if b > 0:
                r.s[st * 2 + 1, b - 1] = mm_fine(bcb[:, 0:128], wb, TN, 2)
        for b in range(2, nb):
            r.s[st * 2, b] += jnp.exp(units[st][b - 1].total) * r.s[st * 2, b - 1]
        for b in range(nb - 3, -1, -1):
            r.s[st * 2 + 1, b] += jnp.exp(units[st][b + 1].total) * r.s[st * 2 + 1, b + 1]


class Names:
    pass


def named(refs, names):
    r = Names()
    for name, ref in zip(names, refs):
        setattr(r, name, ref)
    return r


PREP_NAMES = ("oh", "inc", "exc", "rows", "wf", "w2", "pre", "pd", "prow", "x", "bc", "s", "tabs", "bcp")


def prep_scratch(length):
    nb = length // BLOCK
    v = pltpu.VMEM
    return [
        v((SYM, length), F32),
        v((SYM, length), F32),
        v((SYM, length), F32),
        v((256, length), F32),
        v((64, 2 * WIDE), F32),
        v((128, 1792), F32),
        v((length, 2 * WIDE), F32),
        v((length, 1792), F32),
        v((SYM, length), F32),
        v((length, 512), F32),
        v((length, 1024), F32),
        v((4, nb, LANES, LANES), F32),
        v((TAB_ROWS, LANES), F32),
        v((2 * SYM, 256), F32),
    ]


def forward_kernel(scalars, *refs, ns, conv, vocab):
    tok_refs, raw, out_ref = refs[:ns], refs[ns : ns + RAW], refs[ns + RAW]
    r = named(refs[ns + RAW + 1 :], PREP_NAMES)
    tabs_ref, bcp_ref = r.tabs, r.bcp
    prepare(scalars, tok_refs, raw, tabs_ref, bcp_ref, r, conv, vocab)
    units = [[Unit(r, tabs_ref, st, b, ns) for b in range(ns)] for st in range(2)]
    state_pass_fwd(r, tabs_ref, ns, units)
    for b in range(ns):
        gated = []
        for st in range(2):
            u = units[st][b]
            xf = r.x[u.rows, st * 256 : st * 256 + 128]
            xb = r.x[u.rows, st * 256 + 128 : st * 256 + 256]
            left, right = [], []
            d0, d1 = u.decay(0), u.decay(1)
            y = u.skip * (xf + xb)
            for way, x, mask in ((0, xf, u.low), (1, xb, u.upp)):
                c = st * 512 + way * 256
                bm, cm = r.bc[u.rows, c : c + 128], r.bc[u.rows, c + 128 : c + 256]
                g = jnp.where(mask, mm_fine(cm, bm, NT, 3), 0.0)
                left += [(g * d0).astype(BF16), (g * d1).astype(BF16)]
                right += list(u.by_head((u.dt * x).astype(BF16)))
                if (way == 0 and b > 0) or (way == 1 and b < ns - 1):
                    enter = jnp.exp(u.p) if way == 0 else jnp.exp(u.total - u.q)
                    y = y + enter * mm_fine(cm, r.s[st * 2 + way, b], NN, 2)
            y = y + mm(jnp.concatenate(left, 1), jnp.concatenate(right, 0), NN)
            gated.append(y * u.act(ZZ, 128))
        out_ref[:, units[0][b].rows] = jnp.transpose(gated[0] + gated[1]).astype(BF16)


def backward_kernel(scalars, *refs, ns, conv, vocab):
    tok_refs, raw = refs[:ns], refs[ns : ns + RAW]
    dg_refs, out_ref = refs[ns + RAW : 2 * ns + RAW], refs[2 * ns + RAW]
    r = named(refs[2 * ns + RAW + 1 :], PREP_NAMES + ("ds", "dg", "dpre"))
    tabs_ref, bcp_ref = r.tabs, r.bcp
    prepare(scalars, tok_refs, raw, tabs_ref, bcp_ref, r, conv, vocab)
    mine = scalars[1]
    for k in range(ns):
        at = jnp.where(mine >= k, mine - k, mine - k + ns)
        r.dg[pl.ds(pl.multiple_of(at * BLOCK, BLOCK), BLOCK), :] = dg_refs[k][...].astype(F32)
    units = [[Unit(r, tabs_ref, st, b, ns) for b in range(ns)] for st in range(2)]
    state_pass_fwd(r, tabs_ref, ns, units)
    for st in range(2):
        for b in range(ns):
            u = units[st][b]
            dy = r.dg[u.rows, :] * u.act(ZZ, 128)
            cf = r.bc[u.rows, st * 512 + 128 : st * 512 + 256]
            cb = r.bc[u.rows, st * 512 + 384 : st * 512 + 512]
            if b > 0:
                r.ds[st * 2, b - 1] = mm_fine(cf, jnp.exp(u.p) * dy, TN, 2)
            if b < ns - 1:
                r.ds[st * 2 + 1, b + 1] = mm_fine(cb, jnp.exp(u.total - u.q) * dy, TN, 2)
        for b in range(ns - 3, -1, -1):
            r.ds[st * 2, b] += jnp.exp(units[st][b + 1].total) * r.ds[st * 2, b + 1]
        for b in range(2, ns):
            r.ds[st * 2 + 1, b] += jnp.exp(units[st][b - 1].total) * r.ds[st * 2 + 1, b - 1]
    d_steps, d_decays = [], []
    for st in range(2):
        d_step = jnp.zeros((SYM, LANES), F32)
        d_decay = jnp.zeros((SYM, LANES), F32)
        for b in range(ns):
            u = units[st][b]
            base = st * WIDE
            x = [r.x[u.rows, st * 256 + w * 128 : st * 256 + w * 128 + 128] for w in range(2)]
            dgv = r.dg[u.rows, :]
            pz = u.pre(ZZ, 128)
            sz = sigmoid(pz)
            dy = dgv * (pz * sz)
            dyr = dy.astype(BF16)
            dyw = dyr.astype(F32)
            dy0, dy1 = u.by_head(dyr)
            decays = (u.decay(0), u.decay(1))
            inputs = [u.dt * v for v in x]
            ur = [v.astype(BF16) for v in inputs]
            uw = [v.astype(F32) for v in ur]
            uh = [u.by_head(v) for v in ur]
            d_pair = mm(dyr, jnp.concatenate([uh[0][0], uh[0][1], uh[1][0], uh[1][1]], 0), NT)
            masks = (u.low, u.upp)
            ends = (jnp.exp(u.total - u.p), jnp.exp(u.q))
            enters = (jnp.exp(u.p), jnp.exp(u.total - u.q))
            weights, bms, cms = [], [], []
            for w in range(2):
                c = st * 512 + w * 256
                bm, cm = r.bc[u.rows, c : c + 128], r.bc[u.rows, c + 128 : c + 256]
                g = jnp.where(masks[w], mm_fine(cm, bm, NT, 3), 0.0)
                weights.append([(g * decays[0]).astype(BF16), (g * decays[1]).astype(BF16)])
                bms.append(bm)
                cms.append(cm)
            du_both = mm(
                jnp.concatenate(
                    [
                        jnp.concatenate([weights[0][0], weights[1][0]], 1),
                        jnp.concatenate([weights[0][1], weights[1][1]], 1),
                    ],
                    0,
                ),
                jnp.concatenate([dy0, dy1], 0),
                TN,
            )
            y = u.skip * (x[0] + x[1])
            mixes, step_part, flat = [], 0.0, 0.0
            for w in range(2):
                inner = mm(
                    jnp.concatenate(weights[w], 1), jnp.concatenate([uh[w][0], uh[w][1]], 0), NN
                )
                du_in = du_both[w * BLOCK : (w + 1) * BLOCK]
                has_enter = (w == 0 and b > 0) or (w == 1 and b < ns - 1)
                has_leave = (w == 0 and b < ns - 1) or (w == 1 and b > 0)
                y = y + inner
                row = dyw * inner - uw[w] * du_in
                du = du_in
                d_g = jnp.where(
                    masks[w],
                    d_pair[:, w * 256 : w * 256 + 128] * decays[0]
                    + d_pair[:, w * 256 + 128 : w * 256 + 256] * decays[1],
                    0.0,
                ).astype(BF16)
                d_c = mm(d_g, bms[w].astype(BF16), NN)
                d_b = mm(d_g, cms[w].astype(BF16), TN)
                enter_part = gain_part = None
                if has_enter:
                    state = r.s[st * 2 + w, b]
                    carried = enters[w] * mm_fine(cms[w], state, NN, 2)
                    y = y + carried
                    enter_part = dy * carried
                    d_c = d_c + mm((enters[w] * dy).astype(BF16), state.astype(BF16), NT)
                if has_leave:
                    d_state = r.ds[st * 2 + w, b]
                    d_gain = mm_fine(bms[w], d_state, NN, 2)
                    du = du + ends[w] * d_gain
                    gain = ends[w] * inputs[w]
                    gain_part = gain * d_gain
                    d_b = d_b + mm(gain.astype(BF16), d_state.astype(BF16), NT)
                if has_enter and has_leave:
                    flat = flat + jnp.exp(u.total) * jnp.sum(state * d_state, 0, keepdims=True)
                if w == 1:
                    row = -row
                if enter_part is not None:
                    row = row + enter_part if w == 0 else row - enter_part
                if gain_part is not None:
                    row = row - gain_part if w == 0 else row + gain_part
                if w == 0 and gain_part is not None:
                    flat = flat + jnp.sum(gain_part, 0, keepdims=True)
                if w == 1 and enter_part is not None:
                    flat = flat + jnp.sum(enter_part, 0, keepdims=True)
                mixes.append(row)
                step_part = step_part + du * x[w]
                dx = du * u.dt + dy * u.skip
                px = u.pre((XF, XB)[w], 128)
                sx = sigmoid(px)
                col = base + (XF, XB)[w]
                r.dpre[u.rows, col : col + 128] = (dx * (sx * (1.0 + px * (1.0 - sx)))).astype(BF16)
                col = (BCF, BCB)[w]
                for i, grad in enumerate((d_b, d_c)):
                    pb = u.pre(col + 128 * i, 128)
                    sb = sigmoid(pb)
                    at = base + col + 128 * i
                    r.dpre[u.rows, at : at + 128] = (
                        grad * (sb * (1.0 + pb * (1.0 - sb)))
                    ).astype(BF16)
            d_z = dgv * y * (sz * (1.0 + pz * (1.0 - sz)))
            r.dpre[u.rows, base + ZZ : base + ZZ + 128] = d_z.astype(BF16)
            inc = r.inc[:, u.rows]
            exc = r.exc[:, u.rows]
            inc_b, exc_b, oh_b = inc.astype(BF16), exc.astype(BF16), r.oh[:, u.rows].astype(BF16)
            right = list(halves(mixes[0])) + list(halves(mixes[1]))
            d_decay = d_decay + mm(
                jnp.concatenate([inc_b, inc_b, exc_b, exc_b], 1), jnp.concatenate(right, 0), NN
            )
            d_decay = d_decay + inc[:, BLOCK - 1 : BLOCK] * flat
            d_step = d_step + mm(
                jnp.concatenate([oh_b, oh_b], 1), jnp.concatenate(halves(step_part), 0), NN
            )
        d_steps.append(d_step)
        d_decays.append(d_decay)
    d_tab = mm(r.rows[0:64, :].astype(BF16), r.dpre[...], NN)
    mid = SYM * (conv - 1)
    result = None
    for st in range(2):
        base = st * WIDE
        d_x = jnp.zeros((SYM, 128), F32)
        d_bc = jnp.zeros((SYM, 256), F32)
        for k in range(conv):
            cx = tabs_ref[MISC_ROW + k : MISC_ROW + k + 1, :]
            cbc = bcp_ref[SYM + k : SYM + k + 1, :]
            lo, hi = mid - SYM * k, mid + SYM * k
            d_x = d_x + cx * (
                d_tab[lo : lo + SYM, base + XF : base + XF + 128]
                + d_tab[hi : hi + SYM, base + XB : base + XB + 128]
            )
            d_bc = d_bc + cbc * (
                d_tab[lo : lo + SYM, base + BCF : base + BCF + 256]
                + d_tab[hi : hi + SYM, base + BCB : base + BCB + 256]
            )
        d_zt = d_tab[mid : mid + SYM, base + ZZ : base + ZZ + 128]
        dtt = tabs_ref[DT_ROW : DT_ROW + SYM, :]
        if st == 1:
            dtt = permuted(dtt, raw[0], vocab)
        rate = -jnp.exp(tabs_ref[MISC_ROW + 4 : MISC_ROW + 5, :])
        d_dt = (d_steps[st] + rate * d_decays[st]) * sigmoid(dtt)
        wide = jnp.concatenate([d_x, d_zt, d_dt, d_bc], 1)
        if st == 0:
            result = wide
        else:
            row = lax.broadcasted_iota(jnp.int32, wide.shape, 0)
            for k in range(vocab):
                result = result + jnp.where(row == raw[0][k], wide[k : k + 1], 0.0)
    out_ref[...] = result


def whole(shape):
    return pl.BlockSpec(shape, lambda i, s: (0,) * len(shape))


SMEM = pl.BlockSpec(memory_space=pltpu.SMEM)


def raw_specs(raw):
    return [SMEM] + [whole(a.shape) for a in raw[1:5]] + [SMEM] * 3


PARAMS = pltpu.CompilerParams(vmem_limit_bytes=VMEM_LIMIT)


def call_forward(scalars, toks, raw):
    ns = len(toks)
    length = ns * BLOCK
    return pl.pallas_call(
        functools.partial(forward_kernel, ns=ns, conv=raw[3].shape[0], vocab=raw[1].shape[0]),
        out_shape=jax.ShapeDtypeStruct((LANES, length), BF16),
        grid_spec=pltpu.PrefetchScalarGridSpec(
            num_scalar_prefetch=1,
            grid=(1,),
            in_specs=[whole((1, BLOCK))] * ns + raw_specs(raw),
            out_specs=whole((LANES, length)),
            scratch_shapes=prep_scratch(length),
        ),
        compiler_params=PARAMS,
        name="mix_forward",
    )(scalars, *toks, *raw)


def call_backward(scalars, toks, raw, d_gated):
    ns = len(toks)
    length = ns * BLOCK
    extra = [
        pltpu.VMEM((4, ns, LANES, LANES), F32),
        pltpu.VMEM((length, LANES), F32),
        pltpu.VMEM((length, 2 * WIDE), BF16),
    ]
    return pl.pallas_call(
        functools.partial(backward_kernel, ns=ns, conv=raw[3].shape[0], vocab=raw[1].shape[0]),
        out_shape=jax.ShapeDtypeStruct((SYM, 640), F32),
        grid_spec=pltpu.PrefetchScalarGridSpec(
            num_scalar_prefetch=1,
            grid=(1,),
            in_specs=[whole((1, BLOCK))] * ns + raw_specs(raw) + [whole((BLOCK, LANES))] * ns,
            out_specs=whole((SYM, 640)),
            scratch_shapes=prep_scratch(length) + extra,
        ),
        compiler_params=PARAMS,
        name="mix_backward",
    )(scalars, *toks, *raw, *d_gated)


QUARTERS = 3


def d_gated_kernel(scalars, *refs, nq, ns):
    cots, weights, outs = refs[:nq], refs[nq : 2 * nq], refs[2 * nq :]
    cot = jnp.concatenate([a[...] for a in cots], 1)
    mine = scalars[1]
    for k in range(ns):
        to = jnp.where(mine + k >= ns, mine + k - ns, mine + k)
        rows = pl.ds(pl.multiple_of(to * LANES, LANES), LANES)
        weight = jnp.concatenate([w[rows, :] for w in weights], 1)
        outs[k][...] = mm(cot, weight, NT).astype(BF16)


def call_d_gated(scalars, cots, out_weight, ns):
    nq = len(cots)
    rows, cols = cots[0].shape
    weight_spec = lambda k: pl.BlockSpec((ns * LANES, cols), lambda i, s: (s[2], s[QUARTERS + k]))
    return pl.pallas_call(
        functools.partial(d_gated_kernel, nq=nq, ns=ns),
        out_shape=[jax.ShapeDtypeStruct((rows, LANES), BF16)] * ns,
        grid_spec=pltpu.PrefetchScalarGridSpec(
            num_scalar_prefetch=1,
            grid=(1,),
            in_specs=[whole((rows, cols))] * nq + [weight_spec(k) for k in range(nq)],
            out_specs=[whole((rows, LANES))] * ns,
        ),
        compiler_params=PARAMS,
        name="d_gated",
    )(scalars, *cots, *([out_weight] * nq))


def out_kernel(scalars, own_ref, other_ref, weight_ref, *refs, ns, nh, nc, cols):
    outs, acc = refs[:nh], refs[nh]
    i = pl.program_id(0)
    here = pl.ds(pl.multiple_of(scalars[1] * BLOCK, BLOCK), BLOCK)

    @pl.when(i == 0)
    def _():
        acc[...] = jnp.zeros_like(acc)

    def add(ref):
        weight = []
        for k in range(nh):
            at = scalars[QUARTERS + k * nc] * cols
            weight.append(weight_ref[:, pl.ds(pl.multiple_of(at, LANES), cols)])
        acc[...] += mm(ref[0, :, here], jnp.concatenate(weight, 1), TN)

    @pl.when(i < ns)
    def _():
        add(own_ref)

    @pl.when(i >= ns)
    def _():
        add(other_ref)

    @pl.when(i == pl.num_programs(0) - 1)
    def _():
        for k in range(nh):
            outs[k][...] = acc[:, k * cols : (k + 1) * cols]


def slice_specs(ns, length):
    return [
        pl.BlockSpec((1, LANES, length), lambda i, s: (jnp.minimum(i, ns - 1), 0, 0)),
        pl.BlockSpec((1, LANES, length), lambda i, s: (jnp.maximum(i - ns, 0), 0, 0)),
    ]


def call_out(scalars, own, other, out_weight, nh, nc):
    ns, _, length = own.shape
    width = out_weight.shape[1]
    cols = width // (nh * nc)
    places = QUARTERS + nh * nc
    return pl.pallas_call(
        functools.partial(out_kernel, ns=ns, nh=nh, nc=nc, cols=cols),
        out_shape=[jax.ShapeDtypeStruct((BLOCK, cols), F32)] * nh,
        grid_spec=pltpu.PrefetchScalarGridSpec(
            num_scalar_prefetch=1,
            grid=(ns * nc,),
            in_specs=slice_specs(ns, length)
            + [pl.BlockSpec((LANES, width), lambda i, s: (s[places + i], 0))],
            out_specs=[whole((BLOCK, cols))] * nh,
            scratch_shapes=[pltpu.VMEM((BLOCK, nh * cols), F32)],
        ),
        compiler_params=PARAMS,
        name="layer_out",
    )(scalars, own, other, out_weight)


def weight_kernel(scalars, own_ref, other_ref, cot_own, cot_other, out_ref, *, ns, nh, nc, cols):
    i = pl.program_id(0)
    mine = scalars[1]

    def fill(ref):
        chunks = []
        for k in range(ns):
            at = jnp.where(mine >= k, mine - k, mine - k + ns)
            chunks.append(ref[0, :, pl.ds(pl.multiple_of(at * BLOCK, BLOCK), BLOCK)])
        left = jnp.concatenate(chunks, 1)
        for k in range(nh):
            for m, cot in ((0, cot_own), (1, cot_other)):
                right = cot[k * ns : (k + 1) * ns].reshape(ns * BLOCK, cols)
                at = scalars[QUARTERS + k * nc + m] * cols
                out_ref[:, pl.ds(pl.multiple_of(at, LANES), cols)] = mm(left, right, NN)

    @pl.when(i < ns)
    def _():
        fill(own_ref)

    @pl.when(i >= ns)
    def _():
        fill(other_ref)


def call_weight(scalars, own, other, cot_own, cot_other, width, nh, nc):
    ns, _, length = own.shape
    cols = cot_own.shape[2]
    places = QUARTERS + nh * nc
    return pl.pallas_call(
        functools.partial(weight_kernel, ns=ns, nh=nh, nc=nc, cols=cols),
        out_shape=jax.ShapeDtypeStruct((ns * nc * LANES, width), F32),
        grid_spec=pltpu.PrefetchScalarGridSpec(
            num_scalar_prefetch=1,
            grid=(ns * nc,),
            in_specs=slice_specs(ns, length) + [whole(cot_own.shape)] * 2,
            out_specs=pl.BlockSpec((LANES, width), lambda i, s: (s[places + i], 0)),
        ),
        compiler_params=PARAMS,
        name="weight_grad",
    )(scalars, own, other, cot_own, cot_other)


def final_kernel(scalars, *refs, ns, nq, vocab, places):
    firsts, packed, shared = refs[:ns], refs[ns], refs[ns + 1 : ns + nq]
    xz_ref, bc_ref, dt_ref = refs[ns + nq :]
    d_bc = packed[:, ns * 384 : ns * 384 + 256]
    for a in list(firsts) + list(shared):
        d_bc = d_bc + a[:, a.shape[1] - 256 :]
    for i in range(2):
        for k in range(vocab):
            bc_ref[k, i : i + 1, :] = d_bc[k : k + 1, i * 128 : i * 128 + 128]
    lane = lax.broadcasted_iota(jnp.int32, (SYM, dt_ref.shape[1]), 1)
    d_dt = jnp.zeros((SYM, dt_ref.shape[1]), F32)
    for n in range(2 * ns):
        j = scalars[places + n]
        if n < ns:
            piece = firsts[n][:, 0:384]
        else:
            piece = packed[:, (n - ns) * 384 : (n - ns + 1) * 384]
        for i in range(2):
            for k in range(vocab):
                xz_ref[k, i : i + 1, pl.ds(pl.multiple_of(j * LANES, LANES), LANES)] = piece[
                    k : k + 1, i * 128 : i * 128 + 128
                ]
            total = jnp.sum(piece[:, 256 + 64 * i : 320 + 64 * i], 1, keepdims=True)
            d_dt = jnp.where(lane == 2 * j + i, total, d_dt)
    dt_ref[...] = d_dt[:vocab]


def call_final(scalars, firsts, packed, shared, raw, places):
    ns = len(firsts)
    shapes = [raw[1].shape, raw[2].shape, raw[5].shape]
    arrays = list(firsts) + [packed] + list(shared)
    return pl.pallas_call(
        functools.partial(
            final_kernel, ns=ns, nq=len(shared) + 1, vocab=raw[1].shape[0], places=places
        ),
        out_shape=[jax.ShapeDtypeStruct(a, F32) for a in shapes],
        grid_spec=pltpu.PrefetchScalarGridSpec(
            num_scalar_prefetch=1,
            grid=(1,),
            in_specs=[whole(a.shape) for a in arrays],
            out_specs=[whole(a) for a in shapes],
        ),
        compiler_params=PARAMS,
        name="place_grads",
    )(scalars, *arrays)


def around(x, axis):
    n = lax.axis_size(axis)
    return [x] + [
        lax.ppermute(x, axis, [(i, (i + k) % n) for i in range(n)]) for k in range(1, n)
    ]


def across(x, hops, nh, nc):
    pairs = [
        (a * nc + b, (a + hops[0]) % nh * nc + (b + hops[1]) % nc)
        for a in range(nh)
        for b in range(nc)
    ]
    return lax.ppermute(x, ("head", "sub"), pairs)


def by_channel(
    token_ids, basemap, xz_table, bc_table, dt_table, conv_x, conv_bc, a_log, skip_gain, out_weight, cotangent
):
    ns, nc, nh = lax.axis_size("seq"), lax.axis_size("sub"), lax.axis_size("head")
    s, c, h = lax.axis_index("seq"), lax.axis_index("sub"), lax.axis_index("head")
    width = out_weight.shape[1]
    raw = (basemap, xz_table, bc_table, conv_x, conv_bc, dt_table, a_log, skip_gain)
    hops = [(a, b) for a in range(nh) for b in range(nc)]
    toks = around(token_ids.reshape(1, BLOCK), "seq")
    near = [across(cotangent, hop, nh, nc) if any(hop) else cotangent for hop in hops]
    slot = jnp.arange(nh * nc, dtype=jnp.int32)
    quarters = (h - slot // nc) % nh * nc + (c - slot % nc) % nc
    slot = jnp.arange(ns * nc, dtype=jnp.int32)
    places = (c - slot // ns) % nc * ns + (s - slot % ns) % ns
    scalars = jnp.concatenate([jnp.stack([c * ns + s, s, c]), quarters, places]).astype(jnp.int32)
    d_parts = call_d_gated(scalars, near, out_weight, ns)
    d_gated = [d_parts[0]] + [
        lax.ppermute(d_parts[k], "seq", [(i, (i + k) % ns) for i in range(ns)])
        for k in range(1, ns)
    ]
    cots = jnp.stack(around(cotangent, "seq"), 0)
    gated = call_forward(scalars, toks, raw)
    cots = jnp.concatenate(
        [cots] + [across(cots, (k, 0), nh, nc) for k in range(1, nh)], 0
    )
    own = jnp.stack(around(gated, "seq"), 0)
    grads = call_backward(scalars, toks, raw, d_gated)
    cots_other = across(cots, (0, 1), nh, nc)
    other = across(own, (0, 1), nh, nc)
    firsts = around(grads, "seq")
    shared = sum(a[:, 384:] for a in firsts)
    packed = across(jnp.concatenate([a[:, :384] for a in firsts] + [shared], 1), (0, 1), nh, nc)
    far = [across(shared, hop, nh, nc) for hop in hops if hop[0]]
    parts = call_out(scalars, own, other, out_weight, nh, nc)
    total = parts[0]
    for k in range(1, nh):
        total = total + across(parts[k], (nh - k, 0), nh, nc)
    layer_out = total.astype(BF16)
    d_out_weight = call_weight(scalars, own, other, cots, cots_other, width, nh, nc)
    d_xz, d_bc, d_dt = call_final(scalars, firsts, packed, far, raw, QUARTERS + nh * nc)
    return (layer_out, d_out_weight, d_xz, d_bc, d_dt)


PRECISE = lax.Precision.HIGHEST


def carried_in(part, axis, combine, identity):
    place = lax.axis_index(axis)
    gathered = jax.tree.map(lambda a: lax.all_gather(a, axis), part)
    state = jax.tree.map(lambda a, e: jnp.zeros_like(a) + jnp.asarray(e, a.dtype), part, identity)

    def one(hop, state):
        return combine(
            state, jax.tree.map(lambda a: lax.dynamic_index_in_dim(a, hop, 0, False), gathered)
        )

    return lax.fori_loop(0, place, one, state)


def carried_in_2(array, axis, combine, identity):
    length, mine = (lax.axis_size(axis), lax.axis_index(axis))
    everything = jax.tree.map(
        lambda part, kind: lax.all_gather(part.astype(kind), axis),
        array,
        jax.tree.map(lambda a: jnp.bfloat16 if a.dtype == jnp.float32 else a.dtype, array),
    )
    start = jax.tree.map(
        lambda part, zero: jnp.broadcast_to(jnp.asarray(zero, part.dtype), part.shape),
        array,
        identity,
    )

    def hop(k, before):
        at = length - 1 - k
        reached = at > mine
        new = combine(
            before, jax.tree.map(lambda part, own: part[at].astype(own.dtype), everything, array)
        )
        return jax.tree.map(lambda a, b: jnp.where(reached, a, b), new, before)

    return lax.fori_loop(0, length, hop, start)


def with_halo(block, sides, width):
    for axis, dim in sides:
        count = lax.axis_size(axis)
        forward = [(i, i + 1) for i in range(count - 1)]
        backward = [(target, source) for source, target in forward]
        low = lax.ppermute(
            lax.slice_in_dim(block, block.shape[dim] - width, None, axis=dim), axis, forward
        )
        high = lax.ppermute(lax.slice_in_dim(block, 0, width, axis=dim), axis, backward)
        block = jnp.concatenate([low, block, high], axis=dim)
    return block


def block_step(carry_state, pieces):
    scaled_x, logdec, b_mat, c_mat = pieces
    block_len = scaled_x.shape[0]
    running = jnp.cumsum(logdec, axis=0)
    by_head = running.T
    causal_mask = (jnp.arange(block_len)[:, None] >= jnp.arange(block_len)[None, :])[None, :, :]
    gap_matrix = by_head[:, :, None] - by_head[:, None, :]
    decay_mat = jnp.where(causal_mask, jnp.exp(jnp.where(causal_mask, gap_matrix, 0.0)), 0.0)
    scores = jnp.einsum("tn,sn->ts", c_mat, b_mat, precision=PRECISE)
    within = jnp.einsum("hts,shp->thp", scores[None, :, :] * decay_mat, scaled_x, precision=PRECISE)
    carried = jnp.exp(running)[:, :, None] * jnp.einsum(
        "tn,hpn->thp", c_mat, carry_state, precision=PRECISE
    )
    to_end = jnp.exp(running[-1][None, :] - running)
    gained = jnp.einsum("shp,sn->hpn", to_end[:, :, None] * scaled_x, b_mat, precision=PRECISE)
    return (jnp.exp(running[-1])[:, None, None] * carry_state + gained, within + carried)


def state_pass(inputs, start_state, block_len):
    scaled_x, logdec, b_mat, c_mat = inputs
    block_count = scaled_x.shape[0] // block_len
    pieces = (
        scaled_x.reshape((block_count, block_len) + scaled_x.shape[1:]),
        logdec.reshape(block_count, block_len, -1),
        b_mat.reshape(block_count, block_len, -1),
        c_mat.reshape(block_count, block_len, -1),
    )
    end_state, outputs = lax.scan(jax.checkpoint(block_step), start_state, pieces)
    return (outputs.reshape(scaled_x.shape), end_state)


def final_state(inputs):
    scaled_x, logdec, b_mat, c_mat = inputs
    running = jnp.cumsum(logdec, axis=0)
    to_end = jnp.exp(running[-1][None, :] - running)
    gained = jnp.einsum("shp,sn->hpn", to_end[:, :, None] * scaled_x, b_mat, precision=PRECISE)
    return (jnp.exp(running[-1]), gained)


def lookup(symbols, table):
    vocab_size = table.shape[0]
    onehot = (symbols[:, None] == jnp.arange(vocab_size, dtype=jnp.int32)[None, :]).astype(
        jnp.float32
    )
    return jnp.dot(onehot, table, precision=PRECISE)


def conv_rows(extended, weight, row_count, forward):
    conv_width = weight.shape[0]
    rim_width = conv_width - 1
    summed = jnp.zeros((row_count, extended.shape[1]), jnp.float32)
    for offset in range(conv_width):
        if forward:
            first_row = rim_width - offset
        else:
            first_row = rim_width + offset
        summed = summed + weight[offset][None, :] * extended[first_row : first_row + row_count]
    return summed


def open_inputs(ext_sym, inside_mask, tables, frozen):
    xz_tab, bc_tab, dt_tab = tables
    conv_inner, conv_shared, log_rates, skip_vals = frozen
    rim_width = conv_inner.shape[0] - 1
    row_count = ext_sym.shape[0] - 2 * rim_width
    vocab_size = xz_tab.shape[0]
    inner_dim = xz_tab.shape[2]
    head_count = dt_tab.shape[1]
    state_dim = bc_tab.shape[2]
    looked = lookup(ext_sym, xz_tab.reshape(vocab_size, 2 * inner_dim)) * inside_mask[:, None]
    pre_x = looked[:, :inner_dim]
    gate_act = jax.nn.silu(looked[rim_width : rim_width + row_count, inner_dim:])
    pre_bc = lookup(ext_sym, bc_tab.reshape(vocab_size, 2 * state_dim)) * inside_mask[:, None]
    dt_step = jax.nn.softplus(lookup(ext_sym[rim_width : rim_width + row_count], dt_tab))
    logdec = -jnp.exp(log_rates)[None, :] * dt_step
    flat_bc = conv_shared.reshape(conv_inner.shape[0], 2 * state_dim)

    def one_way(forward):
        x_conv = jax.nn.silu(conv_rows(pre_x, conv_inner, row_count, forward)).reshape(
            row_count, head_count, -1
        )
        bc_conv = jax.nn.silu(conv_rows(pre_bc, flat_bc, row_count, forward))
        return (x_conv, bc_conv[:, :state_dim], bc_conv[:, state_dim:])

    x_fwd, b_fwd, c_fwd = one_way(True)
    x_back, b_back, c_back = one_way(False)
    ahead_in = (x_fwd * dt_step[:, :, None], logdec, b_fwd, c_fwd)
    behind_in = (
        jnp.flip(x_back * dt_step[:, :, None], 0),
        jnp.flip(logdec, 0),
        jnp.flip(b_back, 0),
        jnp.flip(c_back, 0),
    )
    skip_term = skip_vals[None, :, None] * (x_fwd + x_back)
    return (ahead_in, behind_in, skip_term, gate_act)


def combine(earlier, later):
    decay_early, state_early = earlier
    decay_late, state_late = later
    return (decay_early * decay_late, decay_late[:, None, None] * state_early + state_late)


def carries(ahead_pair, behind_pair):
    ahead_out = carried_in(
        (ahead_pair[0], ahead_pair[1]),
        "seq",
        combine,
        (jnp.ones_like(ahead_pair[0]), jnp.zeros_like(ahead_pair[1])),
    )
    behind_out = carried_in_2(
        (behind_pair[0], behind_pair[1]),
        "seq",
        combine,
        (jnp.ones_like(behind_pair[0]), jnp.zeros_like(behind_pair[1])),
    )
    return (ahead_out[1], behind_out[1])


def decay_weights(adjoint, start_state):
    return jnp.sum(adjoint * start_state, axis=(1, 2))


def shards(
    token_ids,
    basemap,
    xz_table,
    bc_table,
    dt_table,
    conv_x,
    conv_bc,
    a_log,
    skip_gain,
    out_weight,
    cotangent,
):
    row_count = token_ids.shape[0]
    rim_width = conv_x.shape[0] - 1
    ext_ids = with_halo(token_ids, (("seq", 0),), rim_width)
    first_row = lax.axis_index("seq") * row_count - rim_width
    where_global = first_row + jnp.arange(row_count + 2 * rim_width, dtype=jnp.int32)
    inside_mask = jnp.logical_and(
        where_global >= 0, where_global < row_count * lax.axis_size("seq")
    ).astype(jnp.float32)
    vocab_size = basemap.shape[0]
    matches = ext_ids[:, None] == jnp.arange(vocab_size, dtype=jnp.int32)[None, :]
    mapped = jnp.sum(jnp.where(matches, basemap[None, :], 0), axis=1)
    ext_sym = jnp.where(lax.axis_index("sub") == 1, mapped, ext_ids)
    tables = (xz_table.astype(jnp.float32), bc_table.astype(jnp.float32), dt_table)
    frozen = (conv_x.astype(jnp.float32), conv_bc.astype(jnp.float32), a_log, skip_gain)

    def summary(tabs_in):
        ahead_in, behind_in, skip_term, gate_act = open_inputs(
            ext_sym, inside_mask, tabs_in, frozen
        )
        decay_fwd, end_fwd = final_state(ahead_in)
        decay_back, end_back = final_state(behind_in)
        return (decay_fwd, end_fwd, decay_back, end_back)

    (decay_fwd, end_fwd, decay_back, end_back), pull_summary = jax.vjp(summary, tables)
    start_fwd, start_back = carries((decay_fwd, end_fwd), (decay_back, end_back))

    def finished(tabs_in, begin_fwd, begin_back):
        ahead_in, behind_in, skip_term, gate_act = open_inputs(
            ext_sym, inside_mask, tabs_in, frozen
        )
        out_fwd, unused_fwd = state_pass(ahead_in, begin_fwd, BLOCK)
        out_back, unused_back = state_pass(behind_in, begin_back, BLOCK)
        return (out_fwd + jnp.flip(out_back, 0) + skip_term).reshape(row_count, -1) * gate_act

    gated, pull_finished = jax.vjp(finished, tables, start_fwd, start_back)
    gated_bf = gated.astype(jnp.bfloat16)
    products = jnp.dot(gated_bf, out_weight, preferred_element_type=jnp.float32)
    layer_out = lax.psum_scatter(products, ("head", "sub"), scatter_dimension=1, tiled=True).astype(
        jnp.bfloat16
    )
    full_cot = lax.all_gather(cotangent, ("head", "sub"), axis=1, tiled=True)
    d_gated = jnp.einsum(
        "tc,kc->tk", full_cot, out_weight, preferred_element_type=jnp.float32
    ).astype(jnp.bfloat16)
    weight_part = jnp.einsum("tk,tc->kc", gated_bf, full_cot, preferred_element_type=jnp.float32)
    d_gated_wide = lax.optimization_barrier(d_gated).astype(jnp.float32)
    grads_first, direct_fwd, direct_back = pull_finished(d_gated_wide)
    adjoint_back, adjoint_fwd = carries((decay_back, direct_back), (decay_fwd, direct_fwd))
    grads_second = pull_summary(
        (
            decay_weights(adjoint_fwd, start_fwd),
            adjoint_fwd,
            decay_weights(adjoint_back, start_back),
            adjoint_back,
        )
    )[0]
    d_tables = jax.tree.map(lambda former, latter: former + latter, grads_first, grads_second)
    d_xz, d_bc, d_dt = d_tables
    d_bc = lax.psum(d_bc, ("seq", "head", "sub"))
    d_out_weight, d_xz, d_dt = lax.psum((weight_part, d_xz, d_dt), ("seq", "sub"))
    return (layer_out, d_out_weight, d_xz, d_bc, d_dt)


def solution(mesh):
    in_specs = (
        P(("grp", "seq")),
        P(),
        P(None, None, "head"),
        P(),
        P(None, "head"),
        P(None, "head"),
        P(),
        P("head"),
        P("head"),
        P("head", None),
        P(("grp", "seq"), ("head", "sub")),
    )
    out_specs = (
        P(("grp", "seq"), ("head", "sub")),
        P(("grp", "head"), None),
        P("grp", None, "head"),
        P("grp", None, None),
        P("grp", "head"),
    )
    def run(*args):
        ns, nc = mesh.shape["seq"], mesh.shape["sub"]
        rows, inner, heads = args[0].shape[0], args[2].shape[2], args[4].shape[1]
        by_lanes = (
            rows == BLOCK
            and nc == 2
            and ns > 1
            and inner == ns * nc * LANES
            and inner == heads * (LANES // 2)
            and args[3].shape[2] == LANES
            and args[5].shape[0] == 4
            and args[9].shape[1] == args[10].shape[1] * nc * mesh.shape["head"]
        )
        return (by_channel if by_lanes else shards)(*args)

    return jax.shard_map(run, mesh=mesh, in_specs=in_specs, out_specs=out_specs, check_vma=False)
```

```python
import functools

import jax
import jax.numpy as jnp
from jax import lax
from jax.experimental import pallas as pl
from jax.experimental.pallas import tpu as pltpu
from jax.sharding import PartitionSpec as P

BLOCK = 128
LANES = 128
SYM = 8
F32 = jnp.float32
BF16 = jnp.bfloat16
NN = (((1,), (0,)), ((), ()))
NT = (((1,), (1,)), ((), ()))
TN = (((0,), (0,)), ((), ()))
X_ROW, Z_ROW, DT_ROW, MISC_ROW, TAB_ROWS = 0, 8, 16, 24, 32
RAW = 8
VMEM_LIMIT = 56 * 1024 * 1024
XF, XB, ZZ, BCF, BCB, WIDE = 0, 128, 256, 384, 640, 896


def mm(a, b, dims):
    return lax.dot_general(a, b, dims, preferred_element_type=F32)


def halves(a):
    top = a.astype(BF16)
    return top, (a - top.astype(F32)).astype(BF16)


def thirds(a):
    top = a.astype(BF16).astype(F32)
    rest = a - top
    mid = rest.astype(BF16).astype(F32)
    return top, mid, rest - mid


def mm_fine(a, b, dims, terms):
    ah, al = halves(a)
    bh, bl = halves(b)
    (ca,), (cb,) = dims[0]
    left, right = [ah], [bh]
    if terms >= 2:
        left.append(al)
        right.append(bh)
    if terms >= 3:
        left.append(ah)
        right.append(bl)
    return mm(jnp.concatenate(left, ca), jnp.concatenate(right, cb), dims)


def permuted(table, scalars, count):
    row = lax.broadcasted_iota(jnp.int32, table[:SYM].shape, 0)
    out = jnp.zeros_like(table[:SYM])
    for k in range(count):
        picked = jnp.zeros_like(table[0:1])
        for m in range(count):
            picked = jnp.where(scalars[k] == m, table[m : m + 1], picked)
        out = jnp.where(row == k, picked, out)
    return out


def sigmoid(v):
    return 1.0 / (1.0 + jnp.exp(-v))


def gather_tables(scalars, raw, tabs_ref, bcp_ref, conv, vocab):
    xz_ref, bc_ref, conv_ref, conv_bc_ref, dt_ref, a_log_ref, skip_ref = raw[1:]
    j = scalars[0]
    lanes = pl.ds(pl.multiple_of(j * LANES, LANES), LANES)
    head0 = lax.broadcasted_iota(jnp.int32, (1, LANES), 1) < 64
    pair = lambda a, b: jnp.where(head0, a, b)
    tabs_ref[...] = jnp.zeros_like(tabs_ref)
    bcp_ref[...] = jnp.zeros_like(bcp_ref)
    for k in range(vocab):
        tabs_ref[X_ROW + k : X_ROW + k + 1, :] = xz_ref[k, 0:1, lanes].astype(F32)
        tabs_ref[Z_ROW + k : Z_ROW + k + 1, :] = xz_ref[k, 1:2, lanes].astype(F32)
        tabs_ref[DT_ROW + k : DT_ROW + k + 1, :] = pair(dt_ref[k, 2 * j], dt_ref[k, 2 * j + 1])
        for i in range(2):
            bcp_ref[k : k + 1, i * 128 : i * 128 + 128] = bc_ref[k, i : i + 1, :].astype(F32)
    for k in range(conv):
        tabs_ref[MISC_ROW + k : MISC_ROW + k + 1, :] = conv_ref[k : k + 1, lanes].astype(F32)
        for i in range(2):
            bcp_ref[SYM + k : SYM + k + 1, i * 128 : i * 128 + 128] = conv_bc_ref[
                k, i : i + 1, :
            ].astype(F32)
    at = MISC_ROW + 4
    tabs_ref[at : at + 1, :] = pair(a_log_ref[2 * j], a_log_ref[2 * j + 1])
    tabs_ref[at + 1 : at + 2, :] = pair(skip_ref[2 * j], skip_ref[2 * j + 1])


def prepare(scalars, tok_refs, raw, tabs_ref, bcp_ref, r, conv, vocab):
    gather_tables(scalars, raw, tabs_ref, bcp_ref, conv, vocab)
    ns = len(tok_refs)
    length = ns * BLOCK
    mine = scalars[1]
    for k in range(ns):
        at = jnp.where(mine >= k, mine - k, mine - k + ns)
        sym = lax.broadcasted_iota(jnp.int32, (SYM, BLOCK), 0).astype(F32)
        tok = jnp.broadcast_to(tok_refs[k][0:1, 0:BLOCK].astype(F32), (SYM, BLOCK))
        r.oh[:, pl.ds(pl.multiple_of(at * BLOCK, BLOCK), BLOCK)] = (sym == tok).astype(F32)
    oh = r.oh[...]
    lane = lax.broadcasted_iota(jnp.int32, (SYM, length), 1)
    up = (
        lax.broadcasted_iota(jnp.int32, (BLOCK, BLOCK), 0)
        <= lax.broadcasted_iota(jnp.int32, (BLOCK, BLOCK), 1)
    ).astype(BF16)
    r.rows[...] = jnp.zeros_like(r.rows)
    for d in range(1 - conv, conv):
        shifted = oh if d == 0 else pltpu.roll(oh, (length - d) % length, 1)
        inside = jnp.logical_and(lane + d >= 0, lane + d < length)
        r.rows[SYM * (d + conv - 1) : SYM * (d + conv), :] = jnp.where(inside, shifted, 0.0)
    r.rows[64:128, :] = r.rows[0:64, :]
    oh_b = oh.astype(BF16)
    for b in range(ns):
        cols = slice(b * BLOCK, (b + 1) * BLOCK)
        inc = mm(oh_b[:, cols], up, NN)
        exc = inc - oh[:, cols]
        r.inc[:, cols] = inc
        r.exc[:, cols] = exc
        for k in range(3):
            r.rows[128 + SYM * k : 128 + SYM * (k + 1), cols] = inc
            r.rows[160 + SYM * k : 160 + SYM * (k + 1), cols] = exc
            r.rows[192 + SYM * k : 192 + SYM * (k + 1), cols] = oh[:, cols]
    r.wf[...] = jnp.zeros_like(r.wf)
    r.w2[...] = jnp.zeros_like(r.w2)
    for st in range(2):
        fetch = (lambda t: t) if st == 0 else (lambda t: permuted(t, raw[0], vocab))
        xt = fetch(tabs_ref[X_ROW : X_ROW + SYM, :])
        zt = fetch(tabs_ref[Z_ROW : Z_ROW + SYM, :])
        dtt = fetch(tabs_ref[DT_ROW : DT_ROW + SYM, :])
        bct = fetch(bcp_ref[0:SYM, :])
        base = st * WIDE
        mid = SYM * (conv - 1)
        r.wf[mid : mid + SYM, base + ZZ : base + ZZ + LANES] = zt
        for k in range(conv):
            cx = tabs_ref[MISC_ROW + k : MISC_ROW + k + 1, :]
            cbc = bcp_ref[SYM + k : SYM + k + 1, :]
            lo, hi = mid - SYM * k, mid + SYM * k
            r.wf[lo : lo + SYM, base + XF : base + XF + LANES] = xt * cx
            r.wf[hi : hi + SYM, base + XB : base + XB + LANES] = xt * cx
            r.wf[lo : lo + SYM, base + BCF : base + BCF + 256] = bct * cbc
            r.wf[hi : hi + SYM, base + BCB : base + BCB + 256] = bct * cbc
        dt = jnp.maximum(dtt, 0.0) + jnp.log1p(jnp.exp(-jnp.abs(dtt)))
        ld = -jnp.exp(tabs_ref[MISC_ROW + 4 : MISC_ROW + 5, :]) * dt
        ld0 = jnp.broadcast_to(ld[:, 0:1], ld.shape)
        ld1 = jnp.broadcast_to(ld[:, 64:65], ld.shape)
        for i, t in enumerate((ld, ld0, ld1)):
            for k, piece in enumerate(thirds(t)):
                c = st * 384 + i * 128
                r.w2[SYM * k : SYM * (k + 1), c : c + 128] = piece
                r.w2[32 + SYM * k : 32 + SYM * (k + 1), 768 + c : 768 + c + 128] = piece
        for k, piece in enumerate(thirds(dt)):
            c = 1536 + st * 128
            r.w2[64 + SYM * k : 64 + SYM * (k + 1), c : c + 128] = piece
    wh, wl = halves(r.wf[...])
    turned = jnp.transpose(r.rows[...]).astype(BF16)
    r.pre[...] = mm(turned[:, 0:128], jnp.concatenate([wh, wl], 0), NN)
    w2 = r.w2[...].astype(BF16)
    r.pd[...] = mm(turned[:, 128:256], w2, NN)
    for st in range(2):
        for part, row0 in ((0, 0), (1, 32)):
            c = part * 768 + st * 384
            flat = mm(
                w2[row0 : row0 + 32, c : c + 128],
                r.rows[128 + row0 : 160 + row0, :].astype(BF16),
                TN,
            )
            for h in range(2):
                i = part * 4 + st * 2 + h
                r.prow[i : i + 1, :] = flat[64 * h : 64 * h + 1, :]


class Unit:
    def __init__(self, r, tabs_ref, st, b, nb):
        self.rows = rows = slice(b * BLOCK, (b + 1) * BLOCK)
        base = st * WIDE
        self.skip = tabs_ref[MISC_ROW + 5 : MISC_ROW + 6, :]
        self.dt = r.pd[rows, 1536 + st * 128 : 1536 + st * 128 + 128]
        self.p = r.pd[rows, st * 384 : st * 384 + 128]
        self.q = r.pd[rows, 768 + st * 384 : 768 + st * 384 + 128]
        self.total = self.p[BLOCK - 1 : BLOCK, :]
        self.r, self.st, self.b, self.base = r, st, b, base
        lane = lax.broadcasted_iota(jnp.int32, (BLOCK, LANES), 1)
        self.head0 = lane < 64
        row = lax.broadcasted_iota(jnp.int32, (BLOCK, BLOCK), 0)
        self.low = row >= lane
        self.upp = row <= lane

    def pre(self, col, width):
        return self.r.pre[self.rows, self.base + col : self.base + col + width]

    def act(self, col, width):
        v = self.pre(col, width)
        return v * sigmoid(v)

    def by_head(self, v):
        zero = jnp.zeros_like(v)
        return jnp.where(self.head0, v, zero), jnp.where(self.head0, zero, v)

    def decay(self, h):
        r, st = self.r, self.st
        c = st * 384 + 128 * (h + 1)
        pc = r.pd[self.rows, c : c + 128]
        qc = r.pd[self.rows, 768 + c : 768 + c + 128]
        pr = r.prow[st * 2 + h : st * 2 + h + 1, self.rows]
        qr = r.prow[4 + st * 2 + h : 4 + st * 2 + h + 1, self.rows]
        return jnp.exp(jnp.where(self.low, pc - pr, qr - qc))


def state_pass_fwd(r, tabs_ref, nb, units):
    for st in range(2):
        for b in range(nb):
            u = units[st][b]
            xf, xb = u.act(XF, 128), u.act(XB, 128)
            bcf, bcb = u.act(BCF, 256), u.act(BCB, 256)
            r.x[u.rows, st * 256 : st * 256 + 128] = xf
            r.x[u.rows, st * 256 + 128 : st * 256 + 256] = xb
            r.bc[u.rows, st * 512 : st * 512 + 256] = bcf
            r.bc[u.rows, st * 512 + 256 : st * 512 + 512] = bcb
            wf = jnp.exp(u.total - u.p) * (u.dt * xf)
            wb = jnp.exp(u.q) * (u.dt * xb)
            if b < nb - 1:
                r.s[st * 2, b + 1] = mm_fine(bcf[:, 0:128], wf, TN, 2)
            if b > 0:
                r.s[st * 2 + 1, b - 1] = mm_fine(bcb[:, 0:128], wb, TN, 2)
        for b in range(2, nb):
            r.s[st * 2, b] += jnp.exp(units[st][b - 1].total) * r.s[st * 2, b - 1]
        for b in range(nb - 3, -1, -1):
            r.s[st * 2 + 1, b] += jnp.exp(units[st][b + 1].total) * r.s[st * 2 + 1, b + 1]


class Names:
    pass


def named(refs, names):
    r = Names()
    for name, ref in zip(names, refs):
        setattr(r, name, ref)
    return r


PREP_NAMES = ("oh", "inc", "exc", "rows", "wf", "w2", "pre", "pd", "prow", "x", "bc", "s", "tabs", "bcp")


def prep_scratch(length):
    nb = length // BLOCK
    v = pltpu.VMEM
    return [
        v((SYM, length), F32),
        v((SYM, length), F32),
        v((SYM, length), F32),
        v((256, length), F32),
        v((64, 2 * WIDE), F32),
        v((128, 1792), F32),
        v((length, 2 * WIDE), F32),
        v((length, 1792), F32),
        v((SYM, length), F32),
        v((length, 512), F32),
        v((length, 1024), F32),
        v((4, nb, LANES, LANES), F32),
        v((TAB_ROWS, LANES), F32),
        v((2 * SYM, 256), F32),
    ]


def forward_kernel(scalars, *refs, ns, conv, vocab):
    tok_refs, raw, out_ref = refs[:ns], refs[ns : ns + RAW], refs[ns + RAW]
    r = named(refs[ns + RAW + 1 :], PREP_NAMES)
    tabs_ref, bcp_ref = r.tabs, r.bcp
    prepare(scalars, tok_refs, raw, tabs_ref, bcp_ref, r, conv, vocab)
    units = [[Unit(r, tabs_ref, st, b, ns) for b in range(ns)] for st in range(2)]
    state_pass_fwd(r, tabs_ref, ns, units)
    for b in range(ns):
        gated = []
        for st in range(2):
            u = units[st][b]
            xf = r.x[u.rows, st * 256 : st * 256 + 128]
            xb = r.x[u.rows, st * 256 + 128 : st * 256 + 256]
            left, right = [], []
            d0, d1 = u.decay(0), u.decay(1)
            y = u.skip * (xf + xb)
            for way, x, mask in ((0, xf, u.low), (1, xb, u.upp)):
                c = st * 512 + way * 256
                bm, cm = r.bc[u.rows, c : c + 128], r.bc[u.rows, c + 128 : c + 256]
                g = jnp.where(mask, mm_fine(cm, bm, NT, 3), 0.0)
                left += [(g * d0).astype(BF16), (g * d1).astype(BF16)]
                right += list(u.by_head((u.dt * x).astype(BF16)))
                if (way == 0 and b > 0) or (way == 1 and b < ns - 1):
                    enter = jnp.exp(u.p) if way == 0 else jnp.exp(u.total - u.q)
                    y = y + enter * mm_fine(cm, r.s[st * 2 + way, b], NN, 2)
            y = y + mm(jnp.concatenate(left, 1), jnp.concatenate(right, 0), NN)
            gated.append(y * u.act(ZZ, 128))
        out_ref[:, units[0][b].rows] = jnp.transpose(gated[0] + gated[1]).astype(BF16)


def backward_kernel(scalars, *refs, ns, nq, conv, vocab):
    tok_refs, raw = refs[:ns], refs[ns : ns + RAW]
    cot_refs, weight_ref, out_ref = (
        refs[ns + RAW : ns + RAW + nq],
        refs[ns + RAW + nq],
        refs[ns + RAW + nq + 1],
    )
    r = named(refs[ns + RAW + nq + 2 :], PREP_NAMES + ("ds", "dg", "dpre"))
    tabs_ref, bcp_ref = r.tabs, r.bcp
    prepare(scalars, tok_refs, raw, tabs_ref, bcp_ref, r, conv, vocab)
    cols = cot_refs[0].shape[2]
    cot = jnp.concatenate([a[...].reshape(ns * BLOCK, cols) for a in cot_refs], 1)
    weight = []
    for k in range(nq):
        at = pl.multiple_of(scalars[QUARTERS + k] * cols, LANES)
        weight.append(weight_ref[:, pl.ds(at, cols)])
    d_gated = mm(cot, jnp.concatenate(weight, 1), NT).astype(BF16).astype(F32)
    mine = scalars[1]
    for k in range(ns):
        at = jnp.where(mine >= k, mine - k, mine - k + ns)
        r.dg[pl.ds(pl.multiple_of(at * BLOCK, BLOCK), BLOCK), :] = d_gated[
            k * BLOCK : (k + 1) * BLOCK
        ]
    units = [[Unit(r, tabs_ref, st, b, ns) for b in range(ns)] for st in range(2)]
    state_pass_fwd(r, tabs_ref, ns, units)
    for st in range(2):
        for b in range(ns):
            u = units[st][b]
            dy = r.dg[u.rows, :] * u.act(ZZ, 128)
            cf = r.bc[u.rows, st * 512 + 128 : st * 512 + 256]
            cb = r.bc[u.rows, st * 512 + 384 : st * 512 + 512]
            if b > 0:
                r.ds[st * 2, b - 1] = mm_fine(cf, jnp.exp(u.p) * dy, TN, 2)
            if b < ns - 1:
                r.ds[st * 2 + 1, b + 1] = mm_fine(cb, jnp.exp(u.total - u.q) * dy, TN, 2)
        for b in range(ns - 3, -1, -1):
            r.ds[st * 2, b] += jnp.exp(units[st][b + 1].total) * r.ds[st * 2, b + 1]
        for b in range(2, ns):
            r.ds[st * 2 + 1, b] += jnp.exp(units[st][b - 1].total) * r.ds[st * 2 + 1, b - 1]
    d_steps, d_decays = [], []
    for st in range(2):
        d_step = jnp.zeros((SYM, LANES), F32)
        d_decay = jnp.zeros((SYM, LANES), F32)
        for b in range(ns):
            u = units[st][b]
            base = st * WIDE
            x = [r.x[u.rows, st * 256 + w * 128 : st * 256 + w * 128 + 128] for w in range(2)]
            dgv = r.dg[u.rows, :]
            pz = u.pre(ZZ, 128)
            sz = sigmoid(pz)
            dy = dgv * (pz * sz)
            dyr = dy.astype(BF16)
            dyw = dyr.astype(F32)
            dy0, dy1 = u.by_head(dyr)
            decays = (u.decay(0), u.decay(1))
            inputs = [u.dt * v for v in x]
            ur = [v.astype(BF16) for v in inputs]
            uw = [v.astype(F32) for v in ur]
            uh = [u.by_head(v) for v in ur]
            d_pair = mm(dyr, jnp.concatenate([uh[0][0], uh[0][1], uh[1][0], uh[1][1]], 0), NT)
            masks = (u.low, u.upp)
            ends = (jnp.exp(u.total - u.p), jnp.exp(u.q))
            enters = (jnp.exp(u.p), jnp.exp(u.total - u.q))
            weights, bms, cms = [], [], []
            for w in range(2):
                c = st * 512 + w * 256
                bm, cm = r.bc[u.rows, c : c + 128], r.bc[u.rows, c + 128 : c + 256]
                g = jnp.where(masks[w], mm_fine(cm, bm, NT, 3), 0.0)
                weights.append([(g * decays[0]).astype(BF16), (g * decays[1]).astype(BF16)])
                bms.append(bm)
                cms.append(cm)
            du_both = mm(
                jnp.concatenate(
                    [
                        jnp.concatenate([weights[0][0], weights[1][0]], 1),
                        jnp.concatenate([weights[0][1], weights[1][1]], 1),
                    ],
                    0,
                ),
                jnp.concatenate([dy0, dy1], 0),
                TN,
            )
            y = u.skip * (x[0] + x[1])
            mixes, step_part, flat = [], 0.0, 0.0
            for w in range(2):
                inner = mm(
                    jnp.concatenate(weights[w], 1), jnp.concatenate([uh[w][0], uh[w][1]], 0), NN
                )
                du_in = du_both[w * BLOCK : (w + 1) * BLOCK]
                has_enter = (w == 0 and b > 0) or (w == 1 and b < ns - 1)
                has_leave = (w == 0 and b < ns - 1) or (w == 1 and b > 0)
                y = y + inner
                row = dyw * inner - uw[w] * du_in
                du = du_in
                d_g = jnp.where(
                    masks[w],
                    d_pair[:, w * 256 : w * 256 + 128] * decays[0]
                    + d_pair[:, w * 256 + 128 : w * 256 + 256] * decays[1],
                    0.0,
                ).astype(BF16)
                d_c = mm(d_g, bms[w].astype(BF16), NN)
                d_b = mm(d_g, cms[w].astype(BF16), TN)
                enter_part = gain_part = None
                if has_enter:
                    state = r.s[st * 2 + w, b]
                    carried = enters[w] * mm_fine(cms[w], state, NN, 2)
                    y = y + carried
                    enter_part = dy * carried
                    d_c = d_c + mm((enters[w] * dy).astype(BF16), state.astype(BF16), NT)
                if has_leave:
                    d_state = r.ds[st * 2 + w, b]
                    d_gain = mm_fine(bms[w], d_state, NN, 2)
                    du = du + ends[w] * d_gain
                    gain = ends[w] * inputs[w]
                    gain_part = gain * d_gain
                    d_b = d_b + mm(gain.astype(BF16), d_state.astype(BF16), NT)
                if has_enter and has_leave:
                    flat = flat + jnp.exp(u.total) * jnp.sum(state * d_state, 0, keepdims=True)
                if w == 1:
                    row = -row
                if enter_part is not None:
                    row = row + enter_part if w == 0 else row - enter_part
                if gain_part is not None:
                    row = row - gain_part if w == 0 else row + gain_part
                if w == 0 and gain_part is not None:
                    flat = flat + jnp.sum(gain_part, 0, keepdims=True)
                if w == 1 and enter_part is not None:
                    flat = flat + jnp.sum(enter_part, 0, keepdims=True)
                mixes.append(row)
                step_part = step_part + du * x[w]
                dx = du * u.dt + dy * u.skip
                px = u.pre((XF, XB)[w], 128)
                sx = sigmoid(px)
                col = base + (XF, XB)[w]
                r.dpre[u.rows, col : col + 128] = (dx * (sx * (1.0 + px * (1.0 - sx)))).astype(BF16)
                col = (BCF, BCB)[w]
                for i, grad in enumerate((d_b, d_c)):
                    pb = u.pre(col + 128 * i, 128)
                    sb = sigmoid(pb)
                    at = base + col + 128 * i
                    r.dpre[u.rows, at : at + 128] = (
                        grad * (sb * (1.0 + pb * (1.0 - sb)))
                    ).astype(BF16)
            d_z = dgv * y * (sz * (1.0 + pz * (1.0 - sz)))
            r.dpre[u.rows, base + ZZ : base + ZZ + 128] = d_z.astype(BF16)
            inc = r.inc[:, u.rows]
            exc = r.exc[:, u.rows]
            inc_b, exc_b, oh_b = inc.astype(BF16), exc.astype(BF16), r.oh[:, u.rows].astype(BF16)
            right = list(halves(mixes[0])) + list(halves(mixes[1]))
            d_decay = d_decay + mm(
                jnp.concatenate([inc_b, inc_b, exc_b, exc_b], 1), jnp.concatenate(right, 0), NN
            )
            d_decay = d_decay + inc[:, BLOCK - 1 : BLOCK] * flat
            d_step = d_step + mm(
                jnp.concatenate([oh_b, oh_b], 1), jnp.concatenate(halves(step_part), 0), NN
            )
        d_steps.append(d_step)
        d_decays.append(d_decay)
    d_tab = mm(r.rows[0:64, :].astype(BF16), r.dpre[...], NN)
    mid = SYM * (conv - 1)
    result = None
    for st in range(2):
        base = st * WIDE
        d_x = jnp.zeros((SYM, 128), F32)
        d_bc = jnp.zeros((SYM, 256), F32)
        for k in range(conv):
            cx = tabs_ref[MISC_ROW + k : MISC_ROW + k + 1, :]
            cbc = bcp_ref[SYM + k : SYM + k + 1, :]
            lo, hi = mid - SYM * k, mid + SYM * k
            d_x = d_x + cx * (
                d_tab[lo : lo + SYM, base + XF : base + XF + 128]
                + d_tab[hi : hi + SYM, base + XB : base + XB + 128]
            )
            d_bc = d_bc + cbc * (
                d_tab[lo : lo + SYM, base + BCF : base + BCF + 256]
                + d_tab[hi : hi + SYM, base + BCB : base + BCB + 256]
            )
        d_zt = d_tab[mid : mid + SYM, base + ZZ : base + ZZ + 128]
        dtt = tabs_ref[DT_ROW : DT_ROW + SYM, :]
        if st == 1:
            dtt = permuted(dtt, raw[0], vocab)
        rate = -jnp.exp(tabs_ref[MISC_ROW + 4 : MISC_ROW + 5, :])
        d_dt = (d_steps[st] + rate * d_decays[st]) * sigmoid(dtt)
        wide = jnp.concatenate([d_x, d_zt, d_dt, d_bc], 1)
        if st == 0:
            result = wide
        else:
            row = lax.broadcasted_iota(jnp.int32, wide.shape, 0)
            for k in range(vocab):
                result = result + jnp.where(row == raw[0][k], wide[k : k + 1], 0.0)
    out_ref[...] = result


def whole(shape):
    return pl.BlockSpec(shape, lambda i, s: (0,) * len(shape))


SMEM = pl.BlockSpec(memory_space=pltpu.SMEM)


def raw_specs(raw):
    return [SMEM] + [whole(a.shape) for a in raw[1:5]] + [SMEM] * 3


PARAMS = pltpu.CompilerParams(vmem_limit_bytes=VMEM_LIMIT)


def token_specs(ns, pay):
    last = pay.shape[0] // 16 - 1
    return [pl.BlockSpec((16, pay.shape[1]), lambda i, s: (last, 0))] * ns


def call_forward(scalars, pays, raw):
    ns = len(pays)
    length = ns * BLOCK
    return pl.pallas_call(
        functools.partial(forward_kernel, ns=ns, conv=raw[3].shape[0], vocab=raw[1].shape[0]),
        out_shape=jax.ShapeDtypeStruct((LANES, length), BF16),
        grid_spec=pltpu.PrefetchScalarGridSpec(
            num_scalar_prefetch=1,
            grid=(1,),
            in_specs=token_specs(ns, pays[0]) + raw_specs(raw),
            out_specs=whole((LANES, length)),
            scratch_shapes=prep_scratch(length),
        ),
        compiler_params=PARAMS,
        cost_estimate=pl.CostEstimate(
            flops=6 * 10**9, transcendentals=0, bytes_accessed=8 * LANES * length
        ),
        name="mix_forward",
    )(scalars, *pays, *raw)


def call_backward(scalars, pays, raw, cots, out_weight):
    ns = len(pays)
    length = ns * BLOCK
    extra = [
        pltpu.VMEM((4, ns, LANES, LANES), F32),
        pltpu.VMEM((length, LANES), F32),
        pltpu.VMEM((length, 2 * WIDE), BF16),
    ]
    return pl.pallas_call(
        functools.partial(
            backward_kernel, ns=ns, nq=len(cots), conv=raw[3].shape[0], vocab=raw[1].shape[0]
        ),
        out_shape=jax.ShapeDtypeStruct((SYM, 640), F32),
        grid_spec=pltpu.PrefetchScalarGridSpec(
            num_scalar_prefetch=1,
            grid=(1,),
            in_specs=token_specs(ns, pays[0])
            + raw_specs(raw)
            + [whole(a.shape) for a in cots]
            + [pl.BlockSpec((LANES, out_weight.shape[1]), lambda i, s: (s[0], 0))],
            out_specs=whole((SYM, 640)),
            scratch_shapes=prep_scratch(length) + extra,
        ),
        compiler_params=PARAMS,
        cost_estimate=pl.CostEstimate(
            flops=10**10, transcendentals=0, bytes_accessed=8 * LANES * length
        ),
        name="mix_backward",
    )(scalars, *pays, *raw, *cots, out_weight)


QUARTERS = 3


def out_kernel(scalars, *refs, ns, nh, nc):
    slices, weights, outs = refs[: ns * nc], refs[ns * nc : ns * nc + nh], refs[ns * nc + nh :]
    here = pl.ds(pl.multiple_of(scalars[1] * BLOCK, BLOCK), BLOCK)
    places = QUARTERS + nh * nc
    rows = [pl.ds(pl.multiple_of(scalars[places + i] * LANES, LANES), LANES) for i in range(ns * nc)]
    left = jnp.concatenate([a[:, here] for a in slices], 0)
    for k in range(nh):
        outs[k][...] = mm(left, jnp.concatenate([weights[k][at, :] for at in rows], 0), TN)


def call_out(scalars, slices, out_weight, ns, nh, nc):
    rows, width = out_weight.shape
    cols = width // (nh * nc)
    weight_spec = lambda k: pl.BlockSpec((rows, cols), lambda i, s: (0, s[QUARTERS + k * nc]))
    return pl.pallas_call(
        functools.partial(out_kernel, ns=ns, nh=nh, nc=nc),
        out_shape=[jax.ShapeDtypeStruct((BLOCK, cols), F32)] * nh,
        grid_spec=pltpu.PrefetchScalarGridSpec(
            num_scalar_prefetch=1,
            grid=(1,),
            in_specs=[whole(a.shape) for a in slices] + [weight_spec(k) for k in range(nh)],
            out_specs=[whole((BLOCK, cols))] * nh,
        ),
        compiler_params=PARAMS,
        name="layer_out",
    )(scalars, *slices, *([out_weight] * nh))


def weight_kernel(scalars, *refs, ns, nh, nc):
    slices, cots = refs[: ns * nc], refs[ns * nc : ns * nc + nh * nc]
    out_ref, mark_ref, left = refs[ns * nc + nh * nc :]
    i = pl.program_id(0)
    mine = scalars[1]
    places = QUARTERS + nh * nc
    cols = cots[0].shape[2]

    @pl.when(i == 0)
    def _():
        mark_ref[...] = jnp.zeros_like(mark_ref)
        for n in range(ns * nc):
            for k in range(ns):
                at = jnp.where(mine >= k, mine - k, mine - k + ns)
                left[n * LANES : (n + 1) * LANES, k * BLOCK : (k + 1) * BLOCK] = slices[n][
                    :, pl.ds(pl.multiple_of(at * BLOCK, BLOCK), BLOCK)
                ]

    for q in range(nh * nc):

        @pl.when(i == q)
        def _():
            total = mm(left[...], cots[q][...].reshape(ns * BLOCK, cols), NN)
            for n in range(ns * nc):
                at = pl.multiple_of(scalars[places + n] * LANES, LANES)
                out_ref[pl.ds(at, LANES), :] = total[n * LANES : (n + 1) * LANES]


def call_weight(scalars, slices, cots, width, ns, nh, nc):
    length = slices[0].shape[1]
    rows = ns * nc * LANES
    return pl.pallas_call(
        functools.partial(weight_kernel, ns=ns, nh=nh, nc=nc),
        out_shape=[
            jax.ShapeDtypeStruct((rows, width), F32),
            jax.ShapeDtypeStruct((SYM, LANES), F32),
        ],
        grid_spec=pltpu.PrefetchScalarGridSpec(
            num_scalar_prefetch=1,
            grid=(nh * nc,),
            in_specs=[whole(a.shape) for a in slices] + [whole(a.shape) for a in cots],
            out_specs=[
                pl.BlockSpec((rows, width // (nh * nc)), lambda i, s: (0, s[QUARTERS + i])),
                whole((SYM, LANES)),
            ],
            scratch_shapes=[pltpu.VMEM((rows, length), BF16)],
        ),
        compiler_params=PARAMS,
        cost_estimate=pl.CostEstimate(
            flops=2 * rows * width * length, transcendentals=0, bytes_accessed=6 * rows * width
        ),
        name="weight_grad",
    )(scalars, *slices, *cots)


def final_kernel(scalars, *refs, ns, nq, nh, vocab, places):
    firsts, packed, shared = refs[:ns], refs[ns], refs[ns + 1 : ns + nq]
    parts = refs[ns + nq : ns + nq + nh]
    out_ref, xz_ref, bc_ref, dt_ref = refs[ns + nq + nh + 1 :]
    total = parts[0][...]
    for a in parts[1:]:
        total = total + a[...]
    out_ref[...] = total.astype(BF16)
    d_bc = packed[:, ns * 384 : ns * 384 + 256]
    for a in list(firsts) + list(shared):
        d_bc = d_bc + a[:, a.shape[1] - 256 :]
    for i in range(2):
        for k in range(vocab):
            bc_ref[k, i : i + 1, :] = d_bc[k : k + 1, i * 128 : i * 128 + 128]
    lane = lax.broadcasted_iota(jnp.int32, (SYM, dt_ref.shape[1]), 1)
    d_dt = jnp.zeros((SYM, dt_ref.shape[1]), F32)
    for n in range(2 * ns):
        j = scalars[places + n]
        if n < ns:
            piece = firsts[n][:, 0:384]
        else:
            piece = packed[:, (n - ns) * 384 : (n - ns + 1) * 384]
        for i in range(2):
            for k in range(vocab):
                xz_ref[k, i : i + 1, pl.ds(pl.multiple_of(j * LANES, LANES), LANES)] = piece[
                    k : k + 1, i * 128 : i * 128 + 128
                ]
            row = jnp.sum(piece[:, 256 + 64 * i : 320 + 64 * i], 1, keepdims=True)
            d_dt = jnp.where(lane == 2 * j + i, row, d_dt)
    dt_ref[...] = d_dt[:vocab]


def call_final(scalars, firsts, packed, shared, parts, mark, raw, places):
    ns = len(firsts)
    shapes = [raw[1].shape, raw[2].shape, raw[5].shape]
    arrays = list(firsts) + [packed] + list(shared) + list(parts)
    return pl.pallas_call(
        functools.partial(
            final_kernel,
            ns=ns,
            nq=len(shared) + 1,
            nh=len(parts),
            vocab=raw[1].shape[0],
            places=places,
        ),
        out_shape=[jax.ShapeDtypeStruct(parts[0].shape, BF16)]
        + [jax.ShapeDtypeStruct(a, F32) for a in shapes],
        grid_spec=pltpu.PrefetchScalarGridSpec(
            num_scalar_prefetch=1,
            grid=(1,),
            in_specs=[whole(a.shape) for a in arrays] + [pl.BlockSpec(memory_space=pl.ANY)],
            out_specs=[whole(parts[0].shape)] + [whole(a) for a in shapes],
        ),
        compiler_params=PARAMS,
        name="place_grads",
    )(scalars, *arrays, mark)


def around(x, axis):
    n = lax.axis_size(axis)
    return [x] + [
        lax.ppermute(x, axis, [(i, (i + k) % n) for i in range(n)]) for k in range(1, n)
    ]


def across(x, hops, nh, nc):
    pairs = [
        (a * nc + b, (a + hops[0]) % nh * nc + (b + hops[1]) % nc)
        for a in range(nh)
        for b in range(nc)
    ]
    return lax.ppermute(x, ("head", "sub"), pairs)


def by_channel(
    token_ids, basemap, xz_table, bc_table, dt_table, conv_x, conv_bc, a_log, skip_gain, out_weight, cotangent
):
    ns, nc, nh = lax.axis_size("seq"), lax.axis_size("sub"), lax.axis_size("head")
    s, c, h = lax.axis_index("seq"), lax.axis_index("sub"), lax.axis_index("head")
    width = out_weight.shape[1]
    cols = width // (nh * nc)
    raw = (basemap, xz_table, bc_table, conv_x, conv_bc, dt_table, a_log, skip_gain)
    symbols = jnp.pad(token_ids.astype(BF16).reshape(1, BLOCK), ((0, 15), (0, cols - BLOCK)))
    pays = around(jnp.concatenate([cotangent, symbols], 0), "seq")
    slot = jnp.arange(nh * nc, dtype=jnp.int32)
    quarters = (h - slot // nc) % nh * nc + (c - slot % nc) % nc
    slot = jnp.arange(ns * nc, dtype=jnp.int32)
    places = (c - slot // ns) % nc * ns + (s - slot % ns) % ns
    scalars = jnp.concatenate([jnp.stack([c * ns + s, s, c]), quarters, places]).astype(jnp.int32)
    stacked = jnp.stack([a[:BLOCK] for a in pays], 0)
    heads = [stacked] + [across(stacked, (k, 0), nh, nc) for k in range(1, nh)]
    side = across(stacked, (0, 1), nh, nc)
    gated = call_forward(scalars, pays, raw)
    heads, gated = lax.optimization_barrier((heads, gated))
    cots = [heads[0], side]
    for a in heads[1:]:
        cots += [a, across(a, (0, 1), nh, nc)]
    slices = around(gated, "seq")
    grads = call_backward(scalars, pays, raw, cots, out_weight)
    slices, grads = lax.optimization_barrier((slices, grads))
    slices = slices + [across(a, (0, 1), nh, nc) for a in slices]
    firsts = around(grads, "seq")
    shared = sum(a[:, 384:] for a in firsts)
    packed = across(jnp.concatenate([a[:, :384] for a in firsts] + [shared], 1), (0, 1), nh, nc)
    far = [across(shared, (a, b), nh, nc) for a in range(1, nh) for b in range(nc)]
    parts = call_out(scalars, slices, out_weight, ns, nh, nc)
    parts = [parts[0]] + [across(parts[k], (nh - k, 0), nh, nc) for k in range(1, nh)]
    d_out_weight, mark = call_weight(scalars, slices, cots, width, ns, nh, nc)
    layer_out, d_xz, d_bc, d_dt = call_final(
        scalars, firsts, packed, far, parts, mark, raw, QUARTERS + nh * nc
    )
    return (layer_out, d_out_weight, d_xz, d_bc, d_dt)


PRECISE = lax.Precision.HIGHEST


def carried_in(part, axis, combine, identity):
    place = lax.axis_index(axis)
    gathered = jax.tree.map(lambda a: lax.all_gather(a, axis), part)
    state = jax.tree.map(lambda a, e: jnp.zeros_like(a) + jnp.asarray(e, a.dtype), part, identity)

    def one(hop, state):
        return combine(
            state, jax.tree.map(lambda a: lax.dynamic_index_in_dim(a, hop, 0, False), gathered)
        )

    return lax.fori_loop(0, place, one, state)


def carried_in_2(array, axis, combine, identity):
    length, mine = (lax.axis_size(axis), lax.axis_index(axis))
    everything = jax.tree.map(
        lambda part, kind: lax.all_gather(part.astype(kind), axis),
        array,
        jax.tree.map(lambda a: jnp.bfloat16 if a.dtype == jnp.float32 else a.dtype, array),
    )
    start = jax.tree.map(
        lambda part, zero: jnp.broadcast_to(jnp.asarray(zero, part.dtype), part.shape),
        array,
        identity,
    )

    def hop(k, before):
        at = length - 1 - k
        reached = at > mine
        new = combine(
            before, jax.tree.map(lambda part, own: part[at].astype(own.dtype), everything, array)
        )
        return jax.tree.map(lambda a, b: jnp.where(reached, a, b), new, before)

    return lax.fori_loop(0, length, hop, start)


def with_halo(block, sides, width):
    for axis, dim in sides:
        count = lax.axis_size(axis)
        forward = [(i, i + 1) for i in range(count - 1)]
        backward = [(target, source) for source, target in forward]
        low = lax.ppermute(
            lax.slice_in_dim(block, block.shape[dim] - width, None, axis=dim), axis, forward
        )
        high = lax.ppermute(lax.slice_in_dim(block, 0, width, axis=dim), axis, backward)
        block = jnp.concatenate([low, block, high], axis=dim)
    return block


def block_step(carry_state, pieces):
    scaled_x, logdec, b_mat, c_mat = pieces
    block_len = scaled_x.shape[0]
    running = jnp.cumsum(logdec, axis=0)
    by_head = running.T
    causal_mask = (jnp.arange(block_len)[:, None] >= jnp.arange(block_len)[None, :])[None, :, :]
    gap_matrix = by_head[:, :, None] - by_head[:, None, :]
    decay_mat = jnp.where(causal_mask, jnp.exp(jnp.where(causal_mask, gap_matrix, 0.0)), 0.0)
    scores = jnp.einsum("tn,sn->ts", c_mat, b_mat, precision=PRECISE)
    within = jnp.einsum("hts,shp->thp", scores[None, :, :] * decay_mat, scaled_x, precision=PRECISE)
    carried = jnp.exp(running)[:, :, None] * jnp.einsum(
        "tn,hpn->thp", c_mat, carry_state, precision=PRECISE
    )
    to_end = jnp.exp(running[-1][None, :] - running)
    gained = jnp.einsum("shp,sn->hpn", to_end[:, :, None] * scaled_x, b_mat, precision=PRECISE)
    return (jnp.exp(running[-1])[:, None, None] * carry_state + gained, within + carried)


def state_pass(inputs, start_state, block_len):
    scaled_x, logdec, b_mat, c_mat = inputs
    block_count = scaled_x.shape[0] // block_len
    pieces = (
        scaled_x.reshape((block_count, block_len) + scaled_x.shape[1:]),
        logdec.reshape(block_count, block_len, -1),
        b_mat.reshape(block_count, block_len, -1),
        c_mat.reshape(block_count, block_len, -1),
    )
    end_state, outputs = lax.scan(jax.checkpoint(block_step), start_state, pieces)
    return (outputs.reshape(scaled_x.shape), end_state)


def final_state(inputs):
    scaled_x, logdec, b_mat, c_mat = inputs
    running = jnp.cumsum(logdec, axis=0)
    to_end = jnp.exp(running[-1][None, :] - running)
    gained = jnp.einsum("shp,sn->hpn", to_end[:, :, None] * scaled_x, b_mat, precision=PRECISE)
    return (jnp.exp(running[-1]), gained)


def lookup(symbols, table):
    vocab_size = table.shape[0]
    onehot = (symbols[:, None] == jnp.arange(vocab_size, dtype=jnp.int32)[None, :]).astype(
        jnp.float32
    )
    return jnp.dot(onehot, table, precision=PRECISE)


def conv_rows(extended, weight, row_count, forward):
    conv_width = weight.shape[0]
    rim_width = conv_width - 1
    summed = jnp.zeros((row_count, extended.shape[1]), jnp.float32)
    for offset in range(conv_width):
        if forward:
            first_row = rim_width - offset
        else:
            first_row = rim_width + offset
        summed = summed + weight[offset][None, :] * extended[first_row : first_row + row_count]
    return summed


def open_inputs(ext_sym, inside_mask, tables, frozen):
    xz_tab, bc_tab, dt_tab = tables
    conv_inner, conv_shared, log_rates, skip_vals = frozen
    rim_width = conv_inner.shape[0] - 1
    row_count = ext_sym.shape[0] - 2 * rim_width
    vocab_size = xz_tab.shape[0]
    inner_dim = xz_tab.shape[2]
    head_count = dt_tab.shape[1]
    state_dim = bc_tab.shape[2]
    looked = lookup(ext_sym, xz_tab.reshape(vocab_size, 2 * inner_dim)) * inside_mask[:, None]
    pre_x = looked[:, :inner_dim]
    gate_act = jax.nn.silu(looked[rim_width : rim_width + row_count, inner_dim:])
    pre_bc = lookup(ext_sym, bc_tab.reshape(vocab_size, 2 * state_dim)) * inside_mask[:, None]
    dt_step = jax.nn.softplus(lookup(ext_sym[rim_width : rim_width + row_count], dt_tab))
    logdec = -jnp.exp(log_rates)[None, :] * dt_step
    flat_bc = conv_shared.reshape(conv_inner.shape[0], 2 * state_dim)

    def one_way(forward):
        x_conv = jax.nn.silu(conv_rows(pre_x, conv_inner, row_count, forward)).reshape(
            row_count, head_count, -1
        )
        bc_conv = jax.nn.silu(conv_rows(pre_bc, flat_bc, row_count, forward))
        return (x_conv, bc_conv[:, :state_dim], bc_conv[:, state_dim:])

    x_fwd, b_fwd, c_fwd = one_way(True)
    x_back, b_back, c_back = one_way(False)
    ahead_in = (x_fwd * dt_step[:, :, None], logdec, b_fwd, c_fwd)
    behind_in = (
        jnp.flip(x_back * dt_step[:, :, None], 0),
        jnp.flip(logdec, 0),
        jnp.flip(b_back, 0),
        jnp.flip(c_back, 0),
    )
    skip_term = skip_vals[None, :, None] * (x_fwd + x_back)
    return (ahead_in, behind_in, skip_term, gate_act)


def combine(earlier, later):
    decay_early, state_early = earlier
    decay_late, state_late = later
    return (decay_early * decay_late, decay_late[:, None, None] * state_early + state_late)


def carries(ahead_pair, behind_pair):
    ahead_out = carried_in(
        (ahead_pair[0], ahead_pair[1]),
        "seq",
        combine,
        (jnp.ones_like(ahead_pair[0]), jnp.zeros_like(ahead_pair[1])),
    )
    behind_out = carried_in_2(
        (behind_pair[0], behind_pair[1]),
        "seq",
        combine,
        (jnp.ones_like(behind_pair[0]), jnp.zeros_like(behind_pair[1])),
    )
    return (ahead_out[1], behind_out[1])


def decay_weights(adjoint, start_state):
    return jnp.sum(adjoint * start_state, axis=(1, 2))


def shards(
    token_ids,
    basemap,
    xz_table,
    bc_table,
    dt_table,
    conv_x,
    conv_bc,
    a_log,
    skip_gain,
    out_weight,
    cotangent,
):
    row_count = token_ids.shape[0]
    rim_width = conv_x.shape[0] - 1
    ext_ids = with_halo(token_ids, (("seq", 0),), rim_width)
    first_row = lax.axis_index("seq") * row_count - rim_width
    where_global = first_row + jnp.arange(row_count + 2 * rim_width, dtype=jnp.int32)
    inside_mask = jnp.logical_and(
        where_global >= 0, where_global < row_count * lax.axis_size("seq")
    ).astype(jnp.float32)
    vocab_size = basemap.shape[0]
    matches = ext_ids[:, None] == jnp.arange(vocab_size, dtype=jnp.int32)[None, :]
    mapped = jnp.sum(jnp.where(matches, basemap[None, :], 0), axis=1)
    ext_sym = jnp.where(lax.axis_index("sub") == 1, mapped, ext_ids)
    tables = (xz_table.astype(jnp.float32), bc_table.astype(jnp.float32), dt_table)
    frozen = (conv_x.astype(jnp.float32), conv_bc.astype(jnp.float32), a_log, skip_gain)

    def summary(tabs_in):
        ahead_in, behind_in, skip_term, gate_act = open_inputs(
            ext_sym, inside_mask, tabs_in, frozen
        )
        decay_fwd, end_fwd = final_state(ahead_in)
        decay_back, end_back = final_state(behind_in)
        return (decay_fwd, end_fwd, decay_back, end_back)

    (decay_fwd, end_fwd, decay_back, end_back), pull_summary = jax.vjp(summary, tables)
    start_fwd, start_back = carries((decay_fwd, end_fwd), (decay_back, end_back))

    def finished(tabs_in, begin_fwd, begin_back):
        ahead_in, behind_in, skip_term, gate_act = open_inputs(
            ext_sym, inside_mask, tabs_in, frozen
        )
        out_fwd, unused_fwd = state_pass(ahead_in, begin_fwd, BLOCK)
        out_back, unused_back = state_pass(behind_in, begin_back, BLOCK)
        return (out_fwd + jnp.flip(out_back, 0) + skip_term).reshape(row_count, -1) * gate_act

    gated, pull_finished = jax.vjp(finished, tables, start_fwd, start_back)
    gated_bf = gated.astype(jnp.bfloat16)
    products = jnp.dot(gated_bf, out_weight, preferred_element_type=jnp.float32)
    layer_out = lax.psum_scatter(products, ("head", "sub"), scatter_dimension=1, tiled=True).astype(
        jnp.bfloat16
    )
    full_cot = lax.all_gather(cotangent, ("head", "sub"), axis=1, tiled=True)
    d_gated = jnp.einsum(
        "tc,kc->tk", full_cot, out_weight, preferred_element_type=jnp.float32
    ).astype(jnp.bfloat16)
    weight_part = jnp.einsum("tk,tc->kc", gated_bf, full_cot, preferred_element_type=jnp.float32)
    d_gated_wide = lax.optimization_barrier(d_gated).astype(jnp.float32)
    grads_first, direct_fwd, direct_back = pull_finished(d_gated_wide)
    adjoint_back, adjoint_fwd = carries((decay_back, direct_back), (decay_fwd, direct_fwd))
    grads_second = pull_summary(
        (
            decay_weights(adjoint_fwd, start_fwd),
            adjoint_fwd,
            decay_weights(adjoint_back, start_back),
            adjoint_back,
        )
    )[0]
    d_tables = jax.tree.map(lambda former, latter: former + latter, grads_first, grads_second)
    d_xz, d_bc, d_dt = d_tables
    d_bc = lax.psum(d_bc, ("seq", "head", "sub"))
    d_out_weight, d_xz, d_dt = lax.psum((weight_part, d_xz, d_dt), ("seq", "sub"))
    return (layer_out, d_out_weight, d_xz, d_bc, d_dt)


def solution(mesh):
    in_specs = (
        P(("grp", "seq")),
        P(),
        P(None, None, "head"),
        P(),
        P(None, "head"),
        P(None, "head"),
        P(),
        P("head"),
        P("head"),
        P("head", None),
        P(("grp", "seq"), ("head", "sub")),
    )
    out_specs = (
        P(("grp", "seq"), ("head", "sub")),
        P(("grp", "head"), None),
        P("grp", None, "head"),
        P("grp", None, None),
        P("grp", "head"),
    )
    def run(*args):
        ns, nc = mesh.shape["seq"], mesh.shape["sub"]
        rows, inner, heads = args[0].shape[0], args[2].shape[2], args[4].shape[1]
        by_lanes = (
            rows == BLOCK
            and nc == 2
            and ns > 1
            and inner == ns * nc * LANES
            and inner == heads * (LANES // 2)
            and args[3].shape[2] == LANES
            and args[5].shape[0] == 4
            and args[9].shape[1] == args[10].shape[1] * nc * mesh.shape["head"]
        )
        return (by_channel if by_lanes else shards)(*args)

    return jax.shard_map(run, mesh=mesh, in_specs=in_specs, out_specs=out_specs, check_vma=False)
```

```python
import functools

import jax
import jax.numpy as jnp
from jax import lax
from jax.experimental import pallas as pl
from jax.experimental.pallas import tpu as pltpu
from jax.sharding import PartitionSpec as P

BLOCK = 128
LANES = 128
SYM = 8
F32 = jnp.float32
BF16 = jnp.bfloat16
NN = (((1,), (0,)), ((), ()))
NT = (((1,), (1,)), ((), ()))
TN = (((0,), (0,)), ((), ()))
X_ROW, Z_ROW, DT_ROW, MISC_ROW, TAB_ROWS = 0, 8, 16, 24, 32
RAW = 8
XF, XB, ZZ, BCF, BCB, WIDE = 0, 128, 256, 384, 640, 896


def mm(a, b, dims):
    return lax.dot_general(a, b, dims, preferred_element_type=F32)


def halves(a):
    top = a.astype(BF16)
    return top, (a - top.astype(F32)).astype(BF16)


def thirds(a):
    top = a.astype(BF16).astype(F32)
    rest = a - top
    mid = rest.astype(BF16).astype(F32)
    return top, mid, rest - mid


def mm_fine(a, b, dims, terms):
    ah, al = halves(a)
    bh, bl = halves(b)
    (ca,), (cb,) = dims[0]
    left, right = [ah], [bh]
    if terms >= 2:
        left.append(al)
        right.append(bh)
    if terms >= 3:
        left.append(ah)
        right.append(bl)
    return mm(jnp.concatenate(left, ca), jnp.concatenate(right, cb), dims)


def permuted(table, basemap, count):
    row = lax.broadcasted_iota(jnp.int32, table.shape, 0)
    out = jnp.zeros_like(table)
    for k in range(count):
        picked = jnp.zeros_like(table[0:1])
        for m in range(count):
            picked = jnp.where(basemap[k] == m, table[m : m + 1], picked)
        out = jnp.where(row == k, picked, out)
    return out


def sigmoid(v):
    return 0.5 * jnp.tanh(0.5 * v) + 0.5


def gather_tables(j, raw, tabs_ref, bcp_ref, conv, vocab):
    xz_ref, bc_ref, conv_ref, conv_bc_ref, dt_ref, a_log_ref, skip_ref = raw
    lanes = pl.ds(pl.multiple_of(j * LANES, LANES), LANES)
    head0 = lax.broadcasted_iota(jnp.int32, (1, LANES), 1) < 64
    pair = lambda a, b: jnp.where(head0, a, b)
    tabs_ref[...] = jnp.zeros_like(tabs_ref)
    bcp_ref[...] = jnp.zeros_like(bcp_ref)
    for k in range(vocab):
        tabs_ref[X_ROW + k : X_ROW + k + 1, :] = xz_ref[k, 0:1, lanes].astype(F32)
        tabs_ref[Z_ROW + k : Z_ROW + k + 1, :] = xz_ref[k, 1:2, lanes].astype(F32)
        tabs_ref[DT_ROW + k : DT_ROW + k + 1, :] = pair(dt_ref[k, 2 * j], dt_ref[k, 2 * j + 1])
        for i in range(2):
            bcp_ref[k : k + 1, i * 128 : i * 128 + 128] = bc_ref[k, i : i + 1, :].astype(F32)
    for k in range(conv):
        tabs_ref[MISC_ROW + k : MISC_ROW + k + 1, :] = conv_ref[k : k + 1, lanes].astype(F32)
        for i in range(2):
            bcp_ref[SYM + k : SYM + k + 1, i * 128 : i * 128 + 128] = conv_bc_ref[
                k, i : i + 1, :
            ].astype(F32)
    at = MISC_ROW + 4
    tabs_ref[at : at + 1, :] = pair(a_log_ref[2 * j], a_log_ref[2 * j + 1])
    tabs_ref[at + 1 : at + 2, :] = pair(skip_ref[2 * j], skip_ref[2 * j + 1])


def tables_kernel(scalars, *refs, conv, vocab):
    tabs_ref, bcp_ref, dt1_ref, perm_ref, w_ref, w2_out, wf, w2 = refs[RAW : RAW + 8]
    local, sems = refs[RAW + 8 : 2 * RAW + 8], refs[2 * RAW + 8]
    copies = [pltpu.make_async_copy(refs[k], local[k], sems.at[k]) for k in range(RAW)]
    for copy in copies:
        copy.start()
    for copy in copies:
        copy.wait()
    basemap = local[0]
    gather_tables(scalars[0], local[1:], tabs_ref, bcp_ref, conv, vocab)
    row = lax.broadcasted_iota(jnp.int32, perm_ref.shape, 0)
    lane = lax.broadcasted_iota(jnp.int32, perm_ref.shape, 1)
    perm = jnp.zeros(perm_ref.shape, F32)
    for k in range(vocab):
        perm = jnp.where(jnp.logical_and(lane == k, row == basemap[k]), 1.0, perm)
    perm_ref[...] = perm
    wf[...] = jnp.zeros_like(wf)
    w2[...] = jnp.zeros_like(w2)
    for st in range(2):
        fetch = (lambda t: t) if st == 0 else (lambda t: permuted(t, basemap, vocab))
        xt = fetch(tabs_ref[X_ROW : X_ROW + SYM, :])
        zt = fetch(tabs_ref[Z_ROW : Z_ROW + SYM, :])
        dtt = fetch(tabs_ref[DT_ROW : DT_ROW + SYM, :])
        if st == 1:
            dt1_ref[...] = dtt
        bct = fetch(bcp_ref[0:SYM, :])
        base = st * WIDE
        mid = SYM * (conv - 1)
        wf[mid : mid + SYM, base + ZZ : base + ZZ + LANES] = zt
        for k in range(conv):
            cx = tabs_ref[MISC_ROW + k : MISC_ROW + k + 1, :]
            cbc = bcp_ref[SYM + k : SYM + k + 1, :]
            lo, hi = mid - SYM * k, mid + SYM * k
            wf[lo : lo + SYM, base + XF : base + XF + LANES] = xt * cx
            wf[hi : hi + SYM, base + XB : base + XB + LANES] = xt * cx
            wf[lo : lo + SYM, base + BCF : base + BCF + 256] = bct * cbc
            wf[hi : hi + SYM, base + BCB : base + BCB + 256] = bct * cbc
        dt = jnp.maximum(dtt, 0.0) + jnp.log1p(jnp.exp(-jnp.abs(dtt)))
        ld = -jnp.exp(tabs_ref[MISC_ROW + 4 : MISC_ROW + 5, :]) * dt
        ld0 = jnp.broadcast_to(ld[:, 0:1], ld.shape)
        ld1 = jnp.broadcast_to(ld[:, 64:65], ld.shape)
        for i, t in enumerate((ld, ld0, ld1)):
            for k, piece in enumerate(thirds(t)):
                c = st * 384 + i * 128
                w2[SYM * k : SYM * (k + 1), c : c + 128] = piece
                w2[32 + SYM * k : 32 + SYM * (k + 1), 768 + c : 768 + c + 128] = piece
        for k, piece in enumerate(thirds(dt)):
            c = 1536 + st * 128
            w2[64 + SYM * k : 64 + SYM * (k + 1), c : c + 128] = piece
    top, rest = halves(wf[...])
    w_ref[0:64, :] = top
    w_ref[64:128, :] = rest
    w2_out[...] = w2[...].astype(BF16)


def prepare(scalars, tok_refs, w_ref, w2_ref, r, conv):
    ns = len(tok_refs)
    length = ns * BLOCK
    mine = scalars[1]
    for k in range(ns):
        sym = lax.broadcasted_iota(jnp.int32, (SYM, BLOCK), 0).astype(F32)
        tok = jnp.broadcast_to(tok_refs[k][BLOCK : BLOCK + 1, 0:BLOCK].astype(F32), (SYM, BLOCK))
        at = jnp.bitwise_xor(mine, k) * BLOCK
        r.oh[:, pl.ds(pl.multiple_of(at, BLOCK), BLOCK)] = (sym == tok).astype(F32)
    oh = r.oh[...]
    lane = lax.broadcasted_iota(jnp.int32, (SYM, length), 1)
    up = (
        lax.broadcasted_iota(jnp.int32, (BLOCK, BLOCK), 0)
        <= lax.broadcasted_iota(jnp.int32, (BLOCK, BLOCK), 1)
    ).astype(BF16)
    r.rows[...] = jnp.zeros_like(r.rows)
    for d in range(1 - conv, conv):
        shifted = oh if d == 0 else pltpu.roll(oh, (length - d) % length, 1)
        inside = jnp.logical_and(lane + d >= 0, lane + d < length)
        r.rows[SYM * (d + conv - 1) : SYM * (d + conv), :] = jnp.where(inside, shifted, 0.0)
    r.rows[64:128, :] = r.rows[0:64, :]
    oh_b = oh.astype(BF16)
    for b in range(ns):
        cols = slice(b * BLOCK, (b + 1) * BLOCK)
        inc = mm(oh_b[:, cols], up, NN)
        exc = inc - oh[:, cols]
        r.inc[:, cols] = inc
        r.exc[:, cols] = exc
        for k in range(3):
            r.rows[128 + SYM * k : 128 + SYM * (k + 1), cols] = inc
            r.rows[160 + SYM * k : 160 + SYM * (k + 1), cols] = exc
            r.rows[192 + SYM * k : 192 + SYM * (k + 1), cols] = oh[:, cols]
    r.sym[...] = r.rows[0:64, :].astype(BF16)
    turned = jnp.transpose(r.rows[...]).astype(BF16)
    r.pre[...] = mm(turned[:, 0:128], w_ref[...], NN)
    w2 = w2_ref[...]
    r.pd[...] = mm(turned[:, 128:256], w2, NN)
    for st in range(2):
        for part, row0 in ((0, 0), (1, 32)):
            c = part * 768 + st * 384
            flat = mm(
                w2[row0 : row0 + 32, c : c + 128],
                r.rows[128 + row0 : 160 + row0, :].astype(BF16),
                TN,
            )
            for h in range(2):
                i = part * 4 + st * 2 + h
                r.prow[i : i + 1, :] = flat[64 * h : 64 * h + 1, :]


class Unit:
    def __init__(self, r, tabs_ref, st, b, nb):
        self.rows = rows = slice(b * BLOCK, (b + 1) * BLOCK)
        base = st * WIDE
        self.skip = tabs_ref[MISC_ROW + 5 : MISC_ROW + 6, :]
        self.dt = r.pd[rows, 1536 + st * 128 : 1536 + st * 128 + 128]
        self.p = r.pd[rows, st * 384 : st * 384 + 128]
        self.q = r.pd[rows, 768 + st * 384 : 768 + st * 384 + 128]
        self.total = self.p[BLOCK - 1 : BLOCK, :]
        self.r, self.st, self.b, self.base = r, st, b, base
        lane = lax.broadcasted_iota(jnp.int32, (BLOCK, LANES), 1)
        self.head0 = lane < 64
        row = lax.broadcasted_iota(jnp.int32, (BLOCK, BLOCK), 0)
        self.low = row >= lane
        self.upp = row <= lane

    def pre(self, col, width):
        return self.r.pre[self.rows, self.base + col : self.base + col + width]

    def act(self, col, width):
        v = self.pre(col, width)
        return v * sigmoid(v)

    def by_head(self, v):
        zero = jnp.zeros_like(v)
        return jnp.where(self.head0, v, zero), jnp.where(self.head0, zero, v)

    def decay(self, h):
        r, st = self.r, self.st
        c = st * 384 + 128 * (h + 1)
        pc = r.pd[self.rows, c : c + 128]
        qc = r.pd[self.rows, 768 + c : 768 + c + 128]
        pr = r.prow[st * 2 + h : st * 2 + h + 1, self.rows]
        qr = r.prow[4 + st * 2 + h : 4 + st * 2 + h + 1, self.rows]
        return jnp.exp(jnp.where(self.low, pc - pr, qr - qc))


def state_pass_fwd(r, tabs_ref, nb, units):
    for st in range(2):
        for b in range(nb):
            u = units[st][b]
            xf, xb = u.act(XF, 128), u.act(XB, 128)
            bcf, bcb = u.act(BCF, 256), u.act(BCB, 256)
            r.x[u.rows, st * 256 : st * 256 + 128] = xf
            r.x[u.rows, st * 256 + 128 : st * 256 + 256] = xb
            r.bc[u.rows, st * 512 : st * 512 + 256] = bcf
            r.bc[u.rows, st * 512 + 256 : st * 512 + 512] = bcb
            wf = jnp.exp(u.total - u.p) * (u.dt * xf)
            wb = jnp.exp(u.q) * (u.dt * xb)
            if b < nb - 1:
                r.s[st * 2, b + 1] = mm_fine(bcf[:, 0:128], wf, TN, 2)
            if b > 0:
                r.s[st * 2 + 1, b - 1] = mm_fine(bcb[:, 0:128], wb, TN, 2)
        for b in range(2, nb):
            r.s[st * 2, b] += jnp.exp(units[st][b - 1].total) * r.s[st * 2, b - 1]
        for b in range(nb - 3, -1, -1):
            r.s[st * 2 + 1, b] += jnp.exp(units[st][b + 1].total) * r.s[st * 2 + 1, b + 1]


class Names:
    pass


def named(refs, names):
    r = Names()
    for name, ref in zip(names, refs):
        setattr(r, name, ref)
    return r


KEPT = ("inc", "exc", "oh", "sym", "pre", "pd", "x", "bc", "s", "dec", "wts", "ys")


def kept_shapes(length):
    nb = length // BLOCK
    return [
        ((SYM, length), F32),
        ((SYM, length), F32),
        ((SYM, length), F32),
        ((64, length), BF16),
        ((length, 2 * WIDE), F32),
        ((length, 1792), F32),
        ((length, 512), F32),
        ((length, 1024), F32),
        ((4, nb, LANES, LANES), F32),
        ((4 * nb, BLOCK, BLOCK), F32),
        ((8 * nb, BLOCK, BLOCK), BF16),
        ((length, 1024), F32),
    ]


def forward_kernel(scalars, *refs, ns, conv):
    tok_refs, (w_ref, w2_ref, tabs_ref, out_ref) = refs[:ns], refs[ns : ns + 4]
    r = named(refs[ns + 4 :], KEPT + ("rows", "prow"))
    prepare(scalars, tok_refs, w_ref, w2_ref, r, conv)
    units = [[Unit(r, tabs_ref, st, b, ns) for b in range(ns)] for st in range(2)]
    state_pass_fwd(r, tabs_ref, ns, units)
    for b in range(ns):
        gated = []
        for st in range(2):
            u = units[st][b]
            xf = r.x[u.rows, st * 256 : st * 256 + 128]
            xb = r.x[u.rows, st * 256 + 128 : st * 256 + 256]
            decays = (u.decay(0), u.decay(1))
            for h in range(2):
                r.dec[(st * ns + b) * 2 + h] = decays[h]
            y = u.skip * (xf + xb)
            for way, x, mask in ((0, xf, u.low), (1, xb, u.upp)):
                c = st * 512 + way * 256
                bm, cm = r.bc[u.rows, c : c + 128], r.bc[u.rows, c + 128 : c + 256]
                g = jnp.where(mask, mm_fine(cm, bm, NT, 3), 0.0)
                left = [(g * d).astype(BF16) for d in decays]
                for h in range(2):
                    r.wts[((st * ns + b) * 2 + way) * 2 + h] = left[h]
                right = u.by_head((u.dt * x).astype(BF16))
                inner = mm(jnp.concatenate(left, 1), jnp.concatenate(right, 0), NN)
                r.ys[u.rows, c : c + 128] = inner
                y = y + inner
                if (way == 0 and b > 0) or (way == 1 and b < ns - 1):
                    enter = jnp.exp(u.p) if way == 0 else jnp.exp(u.total - u.q)
                    carried = enter * mm_fine(cm, r.s[st * 2 + way, b], NN, 2)
                    r.ys[u.rows, c + 128 : c + 256] = carried
                    y = y + carried
            gated.append(y * u.act(ZZ, 128))
        out_ref[:, units[0][b].rows] = jnp.transpose(gated[0] + gated[1]).astype(BF16)


def backward_kernel(scalars, *refs, ns, nq, conv, vocab):
    tabs_ref, bcp_ref, dt1_ref, perm_ref = refs[:4]
    cot_refs, weight_ref = refs[4 : 4 + nq], refs[4 + nq]
    kept = refs[5 + nq : 5 + nq + len(KEPT)]
    out_ref, *work = refs[5 + nq + len(KEPT) :]
    r = named(list(kept) + work, KEPT + ("ds", "dg", "dpre"))
    cols = cot_refs[0].shape[2]
    cot = jnp.concatenate([a[...].reshape(ns * BLOCK, cols) for a in cot_refs], 1)
    weight = []
    for k in range(nq):
        at = pl.multiple_of(scalars[QUARTERS + k] * cols, LANES)
        rows = pl.ds(pl.multiple_of(scalars[0] * LANES, LANES), LANES)
        weight.append(weight_ref[rows, pl.ds(at, cols)])
    d_gated = mm(cot, jnp.concatenate(weight, 1), NT).astype(BF16).astype(F32)
    mine = scalars[1]
    for k in range(ns):
        at = jnp.bitwise_xor(mine, k)
        r.dg[pl.ds(pl.multiple_of(at * BLOCK, BLOCK), BLOCK), :] = d_gated[
            k * BLOCK : (k + 1) * BLOCK
        ]
    units = [[Unit(r, tabs_ref, st, b, ns) for b in range(ns)] for st in range(2)]
    for st in range(2):
        for b in range(ns):
            u = units[st][b]
            dy = r.dg[u.rows, :] * u.act(ZZ, 128)
            cf = r.bc[u.rows, st * 512 + 128 : st * 512 + 256]
            cb = r.bc[u.rows, st * 512 + 384 : st * 512 + 512]
            if b > 0:
                r.ds[st * 2, b - 1] = mm_fine(cf, jnp.exp(u.p) * dy, TN, 2)
            if b < ns - 1:
                r.ds[st * 2 + 1, b + 1] = mm_fine(cb, jnp.exp(u.total - u.q) * dy, TN, 2)
        for b in range(ns - 3, -1, -1):
            r.ds[st * 2, b] += jnp.exp(units[st][b + 1].total) * r.ds[st * 2, b + 1]
        for b in range(2, ns):
            r.ds[st * 2 + 1, b] += jnp.exp(units[st][b - 1].total) * r.ds[st * 2 + 1, b - 1]
    d_steps, d_decays = [], []
    for st in range(2):
        d_step = jnp.zeros((SYM, LANES), F32)
        d_decay = jnp.zeros((SYM, LANES), F32)
        for b in range(ns):
            u = units[st][b]
            base = st * WIDE
            x = [r.x[u.rows, st * 256 + w * 128 : st * 256 + w * 128 + 128] for w in range(2)]
            dgv = r.dg[u.rows, :]
            pz = u.pre(ZZ, 128)
            sz = sigmoid(pz)
            dy = dgv * (pz * sz)
            dyr = dy.astype(BF16)
            dyw = dyr.astype(F32)
            dy0, dy1 = u.by_head(dyr)
            decays = [r.dec[(st * ns + b) * 2 + h] for h in range(2)]
            inputs = [u.dt * v for v in x]
            ur = [v.astype(BF16) for v in inputs]
            uw = [v.astype(F32) for v in ur]
            uh = [u.by_head(v) for v in ur]
            d_pair = mm(dyr, jnp.concatenate([uh[0][0], uh[0][1], uh[1][0], uh[1][1]], 0), NT)
            masks = (u.low, u.upp)
            ends = (jnp.exp(u.total - u.p), jnp.exp(u.q))
            enters = (jnp.exp(u.p), jnp.exp(u.total - u.q))
            weights, bms, cms = [], [], []
            for w in range(2):
                c = st * 512 + w * 256
                bm, cm = r.bc[u.rows, c : c + 128], r.bc[u.rows, c + 128 : c + 256]
                weights.append([r.wts[((st * ns + b) * 2 + w) * 2 + h] for h in range(2)])
                bms.append(bm)
                cms.append(cm)
            du_both = mm(
                jnp.concatenate(
                    [
                        jnp.concatenate([weights[0][0], weights[1][0]], 1),
                        jnp.concatenate([weights[0][1], weights[1][1]], 1),
                    ],
                    0,
                ),
                jnp.concatenate([dy0, dy1], 0),
                TN,
            )
            y = u.skip * (x[0] + x[1])
            mixes, step_part, flat = [], 0.0, 0.0
            for w in range(2):
                c = st * 512 + w * 256
                inner = r.ys[u.rows, c : c + 128]
                du_in = du_both[w * BLOCK : (w + 1) * BLOCK]
                has_enter = (w == 0 and b > 0) or (w == 1 and b < ns - 1)
                has_leave = (w == 0 and b < ns - 1) or (w == 1 and b > 0)
                y = y + inner
                row = dyw * inner - uw[w] * du_in
                du = du_in
                d_g = jnp.where(
                    masks[w],
                    d_pair[:, w * 256 : w * 256 + 128] * decays[0]
                    + d_pair[:, w * 256 + 128 : w * 256 + 256] * decays[1],
                    0.0,
                ).astype(BF16)
                d_c = mm(d_g, bms[w].astype(BF16), NN)
                d_b = mm(d_g, cms[w].astype(BF16), TN)
                enter_part = gain_part = None
                if has_enter:
                    state = r.s[st * 2 + w, b]
                    carried = r.ys[u.rows, c + 128 : c + 256]
                    y = y + carried
                    enter_part = dy * carried
                    d_c = d_c + mm((enters[w] * dy).astype(BF16), state.astype(BF16), NT)
                if has_leave:
                    d_state = r.ds[st * 2 + w, b]
                    d_gain = mm_fine(bms[w], d_state, NN, 2)
                    du = du + ends[w] * d_gain
                    gain = ends[w] * inputs[w]
                    gain_part = gain * d_gain
                    d_b = d_b + mm(gain.astype(BF16), d_state.astype(BF16), NT)
                if has_enter and has_leave:
                    flat = flat + jnp.exp(u.total) * jnp.sum(state * d_state, 0, keepdims=True)
                if w == 1:
                    row = -row
                if enter_part is not None:
                    row = row + enter_part if w == 0 else row - enter_part
                if gain_part is not None:
                    row = row - gain_part if w == 0 else row + gain_part
                if w == 0 and gain_part is not None:
                    flat = flat + jnp.sum(gain_part, 0, keepdims=True)
                if w == 1 and enter_part is not None:
                    flat = flat + jnp.sum(enter_part, 0, keepdims=True)
                mixes.append(row)
                step_part = step_part + du * x[w]
                dx = du * u.dt + dy * u.skip
                px = u.pre((XF, XB)[w], 128)
                sx = sigmoid(px)
                col = base + (XF, XB)[w]
                r.dpre[u.rows, col : col + 128] = (dx * (sx * (1.0 + px * (1.0 - sx)))).astype(BF16)
                col = (BCF, BCB)[w]
                for i, grad in enumerate((d_b, d_c)):
                    pb = u.pre(col + 128 * i, 128)
                    sb = sigmoid(pb)
                    at = base + col + 128 * i
                    r.dpre[u.rows, at : at + 128] = (
                        grad * (sb * (1.0 + pb * (1.0 - sb)))
                    ).astype(BF16)
            d_z = dgv * y * (sz * (1.0 + pz * (1.0 - sz)))
            r.dpre[u.rows, base + ZZ : base + ZZ + 128] = d_z.astype(BF16)
            inc = r.inc[:, u.rows]
            exc = r.exc[:, u.rows]
            inc_b, exc_b, oh_b = inc.astype(BF16), exc.astype(BF16), r.oh[:, u.rows].astype(BF16)
            right = list(halves(mixes[0])) + list(halves(mixes[1]))
            d_decay = d_decay + mm(
                jnp.concatenate([inc_b, inc_b, exc_b, exc_b], 1), jnp.concatenate(right, 0), NN
            )
            d_decay = d_decay + inc[:, BLOCK - 1 : BLOCK] * flat
            d_step = d_step + mm(
                jnp.concatenate([oh_b, oh_b], 1), jnp.concatenate(halves(step_part), 0), NN
            )
        d_steps.append(d_step)
        d_decays.append(d_decay)
    d_tab = mm(r.sym[...], r.dpre[...], NN)
    mid = SYM * (conv - 1)
    result = None
    for st in range(2):
        base = st * WIDE
        d_x = jnp.zeros((SYM, 128), F32)
        d_bc = jnp.zeros((SYM, 256), F32)
        for k in range(conv):
            cx = tabs_ref[MISC_ROW + k : MISC_ROW + k + 1, :]
            cbc = bcp_ref[SYM + k : SYM + k + 1, :]
            lo, hi = mid - SYM * k, mid + SYM * k
            d_x = d_x + cx * (
                d_tab[lo : lo + SYM, base + XF : base + XF + 128]
                + d_tab[hi : hi + SYM, base + XB : base + XB + 128]
            )
            d_bc = d_bc + cbc * (
                d_tab[lo : lo + SYM, base + BCF : base + BCF + 256]
                + d_tab[hi : hi + SYM, base + BCB : base + BCB + 256]
            )
        d_zt = d_tab[mid : mid + SYM, base + ZZ : base + ZZ + 128]
        dtt = dt1_ref[...] if st else tabs_ref[DT_ROW : DT_ROW + SYM, :]
        rate = -jnp.exp(tabs_ref[MISC_ROW + 4 : MISC_ROW + 5, :])
        d_dt = (d_steps[st] + rate * d_decays[st]) * sigmoid(dtt)
        wide = jnp.concatenate([d_x, d_zt, d_dt, d_bc], 1)
        if st == 0:
            result = wide
        else:
            for k in range(vocab):
                result = result + perm_ref[:, k : k + 1] * wide[k : k + 1]
    out_ref[...] = result


SMEM = pl.BlockSpec(memory_space=pltpu.SMEM)
VMEM = pl.BlockSpec(memory_space=pltpu.VMEM)
HBM = pl.BlockSpec(memory_space=pl.ANY)


def params(mib):
    return pltpu.CompilerParams(vmem_limit_bytes=mib * 1024 * 1024)


def call_tables(scalars, raw):
    conv, vocab = raw[3].shape[0], raw[1].shape[0]
    outs = [
        ((TAB_ROWS, LANES), F32),
        ((2 * SYM, 256), F32),
        ((SYM, LANES), F32),
        ((SYM, LANES), F32),
        ((128, 2 * WIDE), BF16),
        ((128, 1792), BF16),
    ]
    return pl.pallas_call(
        functools.partial(tables_kernel, conv=conv, vocab=vocab),
        out_shape=[jax.ShapeDtypeStruct(*a) for a in outs],
        in_specs=[SMEM] + [pl.BlockSpec(memory_space=pltpu.HBM)] * RAW,
        out_specs=[VMEM] * len(outs),
        scratch_shapes=[pltpu.VMEM((64, 2 * WIDE), F32), pltpu.VMEM((128, 1792), F32)]
        + [pltpu.SMEM(raw[0].shape, raw[0].dtype)]
        + [pltpu.VMEM(a.shape, a.dtype) for a in raw[1:5]]
        + [pltpu.SMEM(a.shape, a.dtype) for a in raw[5:]]
        + [pltpu.SemaphoreType.DMA((RAW,))],
        compiler_params=params(8),
        cost_estimate=pl.CostEstimate(flops=2 * 10**9, transcendentals=0, bytes_accessed=10**6),
        name="tables",
    )(scalars, *raw)


def call_forward(scalars, pays, w, w2, tabs, conv):
    ns = len(pays)
    length = ns * BLOCK
    outs = [((LANES, length), BF16)] + kept_shapes(length)
    return pl.pallas_call(
        functools.partial(forward_kernel, ns=ns, conv=conv),
        out_shape=[jax.ShapeDtypeStruct(*a) for a in outs],
        in_specs=[SMEM] + [VMEM] * (ns + 3),
        out_specs=[VMEM] * len(outs),
        scratch_shapes=[pltpu.VMEM((256, length), F32), pltpu.VMEM((SYM, length), F32)],
        compiler_params=params(8),
        cost_estimate=pl.CostEstimate(
            flops=5 * 10**9, transcendentals=0, bytes_accessed=8 * LANES * length
        ),
        name="mix_forward",
    )(scalars, *pays, w, w2, tabs)


def call_backward(scalars, tables, cots, out_weight, kept, conv, vocab):
    length = kept[0].shape[1]
    ns = length // BLOCK
    return pl.pallas_call(
        functools.partial(backward_kernel, ns=ns, nq=len(cots), conv=conv, vocab=vocab),
        out_shape=jax.ShapeDtypeStruct((SYM, 640), F32),
        in_specs=[SMEM] + [VMEM] * (len(tables) + len(cots) + 1 + len(kept)),
        out_specs=VMEM,
        scratch_shapes=[
            pltpu.VMEM((4, ns, LANES, LANES), F32),
            pltpu.VMEM((length, LANES), F32),
            pltpu.VMEM((length, 2 * WIDE), BF16),
        ],
        compiler_params=params(10),
        cost_estimate=pl.CostEstimate(
            flops=6 * 10**9, transcendentals=0, bytes_accessed=8 * LANES * length
        ),
        name="mix_backward",
    )(scalars, *tables, *cots, out_weight, *kept)


QUARTERS = 3


def out_kernel(scalars, *refs, ns, nh, nc):
    slices, weight_ref, outs = refs[: ns * nc], refs[ns * nc], refs[ns * nc + 1 :]
    here = pl.ds(pl.multiple_of(scalars[1] * BLOCK, BLOCK), BLOCK)
    places = QUARTERS + nh * nc
    cols = outs[0].shape[1]
    left = jnp.concatenate([a[:, here] for a in slices], 0)
    for k in range(nh):
        at = pl.ds(pl.multiple_of(scalars[QUARTERS + k * nc] * cols, LANES), cols)
        right = []
        for i in range(ns * nc):
            rows = pl.ds(pl.multiple_of(scalars[places + i] * LANES, LANES), LANES)
            right.append(weight_ref[rows, at])
        outs[k][...] = mm(left, jnp.concatenate(right, 0), TN)


def call_out(scalars, slices, out_weight, ns, nh, nc):
    cols = out_weight.shape[1] // (nh * nc)
    return pl.pallas_call(
        functools.partial(out_kernel, ns=ns, nh=nh, nc=nc),
        out_shape=[jax.ShapeDtypeStruct((BLOCK, cols), F32)] * nh,
        in_specs=[SMEM] + [VMEM] * (len(slices) + 1),
        out_specs=[VMEM] * nh,
        compiler_params=params(8),
        name="layer_out",
    )(scalars, *slices, out_weight)


def weight_kernel(scalars, *refs, ns, nh, nc):
    slices, cots = refs[: ns * nc], refs[ns * nc : ns * nc + nh * nc]
    out_ref, mark_ref, left, buf, sems = refs[ns * nc + nh * nc :]
    mine = scalars[1]
    places = QUARTERS + nh * nc
    cols = cots[0].shape[2]
    mark_ref[...] = jnp.zeros_like(mark_ref)
    for n in range(ns * nc):
        for k in range(ns):
            at = jnp.bitwise_xor(mine, k)
            left[n * LANES : (n + 1) * LANES, k * BLOCK : (k + 1) * BLOCK] = slices[n][
                :, pl.ds(pl.multiple_of(at * BLOCK, BLOCK), BLOCK)
            ]
    copies = []
    for q in range(nh * nc):
        total = mm(left[...], cots[q][...].reshape(ns * BLOCK, cols), NN)
        for n in range(ns * nc):
            at = pl.multiple_of(scalars[places + n] * LANES, LANES)
            buf[q, pl.ds(at, LANES), :] = total[n * LANES : (n + 1) * LANES]
        at = pl.multiple_of(scalars[QUARTERS + q] * cols, LANES)
        copy = pltpu.make_async_copy(buf.at[q], out_ref.at[:, pl.ds(at, cols)], sems.at[q])
        copy.start()
        copies.append(copy)
    for copy in copies:
        copy.wait()


def call_weight(scalars, slices, cots, width, ns, nh, nc):
    length = slices[0].shape[1]
    rows = ns * nc * LANES
    return pl.pallas_call(
        functools.partial(weight_kernel, ns=ns, nh=nh, nc=nc),
        out_shape=[
            jax.ShapeDtypeStruct((rows, width), F32),
            jax.ShapeDtypeStruct((SYM, LANES), F32),
        ],
        in_specs=[SMEM] + [VMEM] * (len(slices) + len(cots)),
        out_specs=[HBM, VMEM],
        scratch_shapes=[
            pltpu.VMEM((rows, length), BF16),
            pltpu.VMEM((nh * nc, rows, width // (nh * nc)), F32),
            pltpu.SemaphoreType.DMA((nh * nc,)),
        ],
        compiler_params=params(12),
        cost_estimate=pl.CostEstimate(
            flops=2 * rows * width * length, transcendentals=0, bytes_accessed=6 * rows * width
        ),
        name="weight_grad",
    )(scalars, *slices, *cots)


def final_kernel(scalars, *refs, ns, nq, nh, vocab, places):
    firsts, packed, shared = refs[:ns], refs[ns], refs[ns + 1 : ns + nq]
    parts = refs[ns + nq : ns + nq + nh]
    out_ref, xz_ref, bc_ref, dt_ref = refs[ns + nq + nh + 1 :]
    total = parts[0][...]
    for a in parts[1:]:
        total = total + a[...]
    out_ref[...] = total.astype(BF16)
    d_bc = packed[:, ns * 384 : ns * 384 + 256]
    for a in list(firsts) + list(shared):
        d_bc = d_bc + a[:, a.shape[1] - 256 :]
    for i in range(2):
        for k in range(vocab):
            bc_ref[k, i : i + 1, :] = d_bc[k : k + 1, i * 128 : i * 128 + 128]
    lane = lax.broadcasted_iota(jnp.int32, (SYM, dt_ref.shape[1]), 1)
    d_dt = jnp.zeros((SYM, dt_ref.shape[1]), F32)
    for n in range(2 * ns):
        j = scalars[places + n]
        if n < ns:
            piece = firsts[n][:, 0:384]
        else:
            piece = packed[:, (n - ns) * 384 : (n - ns + 1) * 384]
        for i in range(2):
            for k in range(vocab):
                xz_ref[k, i : i + 1, pl.ds(pl.multiple_of(j * LANES, LANES), LANES)] = piece[
                    k : k + 1, i * 128 : i * 128 + 128
                ]
            row = jnp.sum(piece[:, 256 + 64 * i : 320 + 64 * i], 1, keepdims=True)
            d_dt = jnp.where(lane == 2 * j + i, row, d_dt)
    dt_ref[...] = d_dt[:vocab]


def call_final(scalars, firsts, packed, shared, parts, mark, raw, places):
    ns = len(firsts)
    shapes = [raw[1].shape, raw[2].shape, raw[5].shape]
    arrays = list(firsts) + [packed] + list(shared) + list(parts)
    return pl.pallas_call(
        functools.partial(
            final_kernel,
            ns=ns,
            nq=len(shared) + 1,
            nh=len(parts),
            vocab=raw[1].shape[0],
            places=places,
        ),
        out_shape=[jax.ShapeDtypeStruct(parts[0].shape, BF16)]
        + [jax.ShapeDtypeStruct(a, F32) for a in shapes],
        in_specs=[SMEM] + [VMEM] * (len(arrays) + 1),
        out_specs=[VMEM] * (len(shapes) + 1),
        compiler_params=params(8),
        name="place_grads",
    )(scalars, *arrays, mark)


def around(x, axis):
    n = lax.axis_size(axis)
    return [x] + [lax.ppermute(x, axis, [(i, i ^ k) for i in range(n)]) for k in range(1, n)]


def across(x, hops, nh, nc):
    pairs = [
        (a * nc + b, (a + hops[0]) % nh * nc + (b + hops[1]) % nc)
        for a in range(nh)
        for b in range(nc)
    ]
    return lax.ppermute(x, ("head", "sub"), pairs)


def by_channel(
    token_ids, basemap, xz_table, bc_table, dt_table, conv_x, conv_bc, a_log, skip_gain, out_weight, cotangent
):
    ns, nc, nh = lax.axis_size("seq"), lax.axis_size("sub"), lax.axis_size("head")
    s, c, h = lax.axis_index("seq"), lax.axis_index("sub"), lax.axis_index("head")
    width = out_weight.shape[1]
    cols = width // (nh * nc)
    raw = (basemap, xz_table, bc_table, conv_x, conv_bc, dt_table, a_log, skip_gain)
    symbols = jnp.pad(token_ids.astype(BF16).reshape(1, BLOCK), ((0, 15), (0, cols - BLOCK)))
    pays = around(jnp.concatenate([cotangent, symbols], 0), "seq")
    slot = jnp.arange(nh * nc, dtype=jnp.int32)
    quarters = (h - slot // nc) % nh * nc + (c - slot % nc) % nc
    slot = jnp.arange(ns * nc, dtype=jnp.int32)
    places = (c - slot // ns) % nc * ns + jnp.bitwise_xor(s, slot % ns)
    scalars = jnp.concatenate([jnp.stack([c * ns + s, s, c]), quarters, places]).astype(jnp.int32)
    stacked = jnp.stack([a[:BLOCK] for a in pays], 0)
    heads = [stacked] + [across(stacked, (k, 0), nh, nc) for k in range(1, nh)]
    side = across(stacked, (0, 1), nh, nc)
    conv, vocab = conv_x.shape[0], xz_table.shape[0]
    *tables, w, w2 = call_tables(scalars, raw)
    gated, *kept = call_forward(scalars, pays, w, w2, tables[0], conv)
    heads, gated = lax.optimization_barrier((heads, gated))
    cots = [heads[0], side]
    for a in heads[1:]:
        cots += [a, across(a, (0, 1), nh, nc)]
    slices = around(gated, "seq")
    grads = call_backward(scalars, tables, cots, out_weight, kept, conv, vocab)
    slices, _ = lax.optimization_barrier((slices, grads))
    slices = slices + [across(a, (0, 1), nh, nc) for a in slices]
    firsts = around(grads, "seq")
    shared = sum(a[:, 384:] for a in firsts)
    packed = across(jnp.concatenate([a[:, :384] for a in firsts] + [shared], 1), (0, 1), nh, nc)
    far = [across(shared, (a, b), nh, nc) for a in range(1, nh) for b in range(nc)]
    parts = call_out(scalars, slices, out_weight, ns, nh, nc)
    parts = [parts[0]] + [across(parts[k], (nh - k, 0), nh, nc) for k in range(1, nh)]
    d_out_weight, mark = call_weight(scalars, slices, cots, width, ns, nh, nc)
    layer_out, d_xz, d_bc, d_dt = call_final(
        scalars, firsts, packed, far, parts, mark, raw, QUARTERS + nh * nc
    )
    return (layer_out, d_out_weight, d_xz, d_bc, d_dt)


PRECISE = lax.Precision.HIGHEST


def carried_in(part, axis, combine, identity):
    place = lax.axis_index(axis)
    gathered = jax.tree.map(lambda a: lax.all_gather(a, axis), part)
    state = jax.tree.map(lambda a, e: jnp.zeros_like(a) + jnp.asarray(e, a.dtype), part, identity)

    def one(hop, state):
        return combine(
            state, jax.tree.map(lambda a: lax.dynamic_index_in_dim(a, hop, 0, False), gathered)
        )

    return lax.fori_loop(0, place, one, state)


def carried_in_2(array, axis, combine, identity):
    length, mine = (lax.axis_size(axis), lax.axis_index(axis))
    everything = jax.tree.map(
        lambda part, kind: lax.all_gather(part.astype(kind), axis),
        array,
        jax.tree.map(lambda a: jnp.bfloat16 if a.dtype == jnp.float32 else a.dtype, array),
    )
    start = jax.tree.map(
        lambda part, zero: jnp.broadcast_to(jnp.asarray(zero, part.dtype), part.shape),
        array,
        identity,
    )

    def hop(k, before):
        at = length - 1 - k
        reached = at > mine
        new = combine(
            before, jax.tree.map(lambda part, own: part[at].astype(own.dtype), everything, array)
        )
        return jax.tree.map(lambda a, b: jnp.where(reached, a, b), new, before)

    return lax.fori_loop(0, length, hop, start)


def with_halo(block, sides, width):
    for axis, dim in sides:
        count = lax.axis_size(axis)
        forward = [(i, i + 1) for i in range(count - 1)]
        backward = [(target, source) for source, target in forward]
        low = lax.ppermute(
            lax.slice_in_dim(block, block.shape[dim] - width, None, axis=dim), axis, forward
        )
        high = lax.ppermute(lax.slice_in_dim(block, 0, width, axis=dim), axis, backward)
        block = jnp.concatenate([low, block, high], axis=dim)
    return block


def block_step(carry_state, pieces):
    scaled_x, logdec, b_mat, c_mat = pieces
    block_len = scaled_x.shape[0]
    running = jnp.cumsum(logdec, axis=0)
    by_head = running.T
    causal_mask = (jnp.arange(block_len)[:, None] >= jnp.arange(block_len)[None, :])[None, :, :]
    gap_matrix = by_head[:, :, None] - by_head[:, None, :]
    decay_mat = jnp.where(causal_mask, jnp.exp(jnp.where(causal_mask, gap_matrix, 0.0)), 0.0)
    scores = jnp.einsum("tn,sn->ts", c_mat, b_mat, precision=PRECISE)
    within = jnp.einsum("hts,shp->thp", scores[None, :, :] * decay_mat, scaled_x, precision=PRECISE)
    carried = jnp.exp(running)[:, :, None] * jnp.einsum(
        "tn,hpn->thp", c_mat, carry_state, precision=PRECISE
    )
    to_end = jnp.exp(running[-1][None, :] - running)
    gained = jnp.einsum("shp,sn->hpn", to_end[:, :, None] * scaled_x, b_mat, precision=PRECISE)
    return (jnp.exp(running[-1])[:, None, None] * carry_state + gained, within + carried)


def state_pass(inputs, start_state, block_len):
    scaled_x, logdec, b_mat, c_mat = inputs
    block_count = scaled_x.shape[0] // block_len
    pieces = (
        scaled_x.reshape((block_count, block_len) + scaled_x.shape[1:]),
        logdec.reshape(block_count, block_len, -1),
        b_mat.reshape(block_count, block_len, -1),
        c_mat.reshape(block_count, block_len, -1),
    )
    end_state, outputs = lax.scan(jax.checkpoint(block_step), start_state, pieces)
    return (outputs.reshape(scaled_x.shape), end_state)


def final_state(inputs):
    scaled_x, logdec, b_mat, c_mat = inputs
    running = jnp.cumsum(logdec, axis=0)
    to_end = jnp.exp(running[-1][None, :] - running)
    gained = jnp.einsum("shp,sn->hpn", to_end[:, :, None] * scaled_x, b_mat, precision=PRECISE)
    return (jnp.exp(running[-1]), gained)


def lookup(symbols, table):
    vocab_size = table.shape[0]
    onehot = (symbols[:, None] == jnp.arange(vocab_size, dtype=jnp.int32)[None, :]).astype(
        jnp.float32
    )
    return jnp.dot(onehot, table, precision=PRECISE)


def conv_rows(extended, weight, row_count, forward):
    conv_width = weight.shape[0]
    rim_width = conv_width - 1
    summed = jnp.zeros((row_count, extended.shape[1]), jnp.float32)
    for offset in range(conv_width):
        if forward:
            first_row = rim_width - offset
        else:
            first_row = rim_width + offset
        summed = summed + weight[offset][None, :] * extended[first_row : first_row + row_count]
    return summed


def open_inputs(ext_sym, inside_mask, tables, frozen):
    xz_tab, bc_tab, dt_tab = tables
    conv_inner, conv_shared, log_rates, skip_vals = frozen
    rim_width = conv_inner.shape[0] - 1
    row_count = ext_sym.shape[0] - 2 * rim_width
    vocab_size = xz_tab.shape[0]
    inner_dim = xz_tab.shape[2]
    head_count = dt_tab.shape[1]
    state_dim = bc_tab.shape[2]
    looked = lookup(ext_sym, xz_tab.reshape(vocab_size, 2 * inner_dim)) * inside_mask[:, None]
    pre_x = looked[:, :inner_dim]
    gate_act = jax.nn.silu(looked[rim_width : rim_width + row_count, inner_dim:])
    pre_bc = lookup(ext_sym, bc_tab.reshape(vocab_size, 2 * state_dim)) * inside_mask[:, None]
    dt_step = jax.nn.softplus(lookup(ext_sym[rim_width : rim_width + row_count], dt_tab))
    logdec = -jnp.exp(log_rates)[None, :] * dt_step
    flat_bc = conv_shared.reshape(conv_inner.shape[0], 2 * state_dim)

    def one_way(forward):
        x_conv = jax.nn.silu(conv_rows(pre_x, conv_inner, row_count, forward)).reshape(
            row_count, head_count, -1
        )
        bc_conv = jax.nn.silu(conv_rows(pre_bc, flat_bc, row_count, forward))
        return (x_conv, bc_conv[:, :state_dim], bc_conv[:, state_dim:])

    x_fwd, b_fwd, c_fwd = one_way(True)
    x_back, b_back, c_back = one_way(False)
    ahead_in = (x_fwd * dt_step[:, :, None], logdec, b_fwd, c_fwd)
    behind_in = (
        jnp.flip(x_back * dt_step[:, :, None], 0),
        jnp.flip(logdec, 0),
        jnp.flip(b_back, 0),
        jnp.flip(c_back, 0),
    )
    skip_term = skip_vals[None, :, None] * (x_fwd + x_back)
    return (ahead_in, behind_in, skip_term, gate_act)


def combine(earlier, later):
    decay_early, state_early = earlier
    decay_late, state_late = later
    return (decay_early * decay_late, decay_late[:, None, None] * state_early + state_late)


def carries(ahead_pair, behind_pair):
    ahead_out = carried_in(
        (ahead_pair[0], ahead_pair[1]),
        "seq",
        combine,
        (jnp.ones_like(ahead_pair[0]), jnp.zeros_like(ahead_pair[1])),
    )
    behind_out = carried_in_2(
        (behind_pair[0], behind_pair[1]),
        "seq",
        combine,
        (jnp.ones_like(behind_pair[0]), jnp.zeros_like(behind_pair[1])),
    )
    return (ahead_out[1], behind_out[1])


def decay_weights(adjoint, start_state):
    return jnp.sum(adjoint * start_state, axis=(1, 2))


def shards(
    token_ids,
    basemap,
    xz_table,
    bc_table,
    dt_table,
    conv_x,
    conv_bc,
    a_log,
    skip_gain,
    out_weight,
    cotangent,
):
    row_count = token_ids.shape[0]
    rim_width = conv_x.shape[0] - 1
    ext_ids = with_halo(token_ids, (("seq", 0),), rim_width)
    first_row = lax.axis_index("seq") * row_count - rim_width
    where_global = first_row + jnp.arange(row_count + 2 * rim_width, dtype=jnp.int32)
    inside_mask = jnp.logical_and(
        where_global >= 0, where_global < row_count * lax.axis_size("seq")
    ).astype(jnp.float32)
    vocab_size = basemap.shape[0]
    matches = ext_ids[:, None] == jnp.arange(vocab_size, dtype=jnp.int32)[None, :]
    mapped = jnp.sum(jnp.where(matches, basemap[None, :], 0), axis=1)
    ext_sym = jnp.where(lax.axis_index("sub") == 1, mapped, ext_ids)
    tables = (xz_table.astype(jnp.float32), bc_table.astype(jnp.float32), dt_table)
    frozen = (conv_x.astype(jnp.float32), conv_bc.astype(jnp.float32), a_log, skip_gain)

    def summary(tabs_in):
        ahead_in, behind_in, skip_term, gate_act = open_inputs(
            ext_sym, inside_mask, tabs_in, frozen
        )
        decay_fwd, end_fwd = final_state(ahead_in)
        decay_back, end_back = final_state(behind_in)
        return (decay_fwd, end_fwd, decay_back, end_back)

    (decay_fwd, end_fwd, decay_back, end_back), pull_summary = jax.vjp(summary, tables)
    start_fwd, start_back = carries((decay_fwd, end_fwd), (decay_back, end_back))

    def finished(tabs_in, begin_fwd, begin_back):
        ahead_in, behind_in, skip_term, gate_act = open_inputs(
            ext_sym, inside_mask, tabs_in, frozen
        )
        out_fwd, unused_fwd = state_pass(ahead_in, begin_fwd, BLOCK)
        out_back, unused_back = state_pass(behind_in, begin_back, BLOCK)
        return (out_fwd + jnp.flip(out_back, 0) + skip_term).reshape(row_count, -1) * gate_act

    gated, pull_finished = jax.vjp(finished, tables, start_fwd, start_back)
    gated_bf = gated.astype(jnp.bfloat16)
    products = jnp.dot(gated_bf, out_weight, preferred_element_type=jnp.float32)
    layer_out = lax.psum_scatter(products, ("head", "sub"), scatter_dimension=1, tiled=True).astype(
        jnp.bfloat16
    )
    full_cot = lax.all_gather(cotangent, ("head", "sub"), axis=1, tiled=True)
    d_gated = jnp.einsum(
        "tc,kc->tk", full_cot, out_weight, preferred_element_type=jnp.float32
    ).astype(jnp.bfloat16)
    weight_part = jnp.einsum("tk,tc->kc", gated_bf, full_cot, preferred_element_type=jnp.float32)
    d_gated_wide = lax.optimization_barrier(d_gated).astype(jnp.float32)
    grads_first, direct_fwd, direct_back = pull_finished(d_gated_wide)
    adjoint_back, adjoint_fwd = carries((decay_back, direct_back), (decay_fwd, direct_fwd))
    grads_second = pull_summary(
        (
            decay_weights(adjoint_fwd, start_fwd),
            adjoint_fwd,
            decay_weights(adjoint_back, start_back),
            adjoint_back,
        )
    )[0]
    d_tables = jax.tree.map(lambda former, latter: former + latter, grads_first, grads_second)
    d_xz, d_bc, d_dt = d_tables
    d_bc = lax.psum(d_bc, ("seq", "head", "sub"))
    d_out_weight, d_xz, d_dt = lax.psum((weight_part, d_xz, d_dt), ("seq", "sub"))
    return (layer_out, d_out_weight, d_xz, d_bc, d_dt)


def solution(mesh):
    in_specs = (
        P(("grp", "seq")),
        P(),
        P(None, None, "head"),
        P(),
        P(None, "head"),
        P(None, "head"),
        P(),
        P("head"),
        P("head"),
        P("head", None),
        P(("grp", "seq"), ("head", "sub")),
    )
    out_specs = (
        P(("grp", "seq"), ("head", "sub")),
        P(("grp", "head"), None),
        P("grp", None, "head"),
        P("grp", None, None),
        P("grp", "head"),
    )
    def run(*args):
        ns, nc = mesh.shape["seq"], mesh.shape["sub"]
        rows, inner, heads = args[0].shape[0], args[2].shape[2], args[4].shape[1]
        by_lanes = (
            rows == BLOCK
            and nc == 2
            and ns > 1
            and ns & (ns - 1) == 0
            and inner == ns * nc * LANES
            and inner == heads * (LANES // 2)
            and args[3].shape[2] == LANES
            and args[5].shape[0] == 4
            and args[9].shape[1] == args[10].shape[1] * nc * mesh.shape["head"]
        )
        return (by_channel if by_lanes else shards)(*args)

    return jax.shard_map(run, mesh=mesh, in_specs=in_specs, out_specs=out_specs, check_vma=False)
```

```python
import functools

import jax
import jax.numpy as jnp
from jax import lax
from jax.experimental import pallas as pl
from jax.experimental.pallas import tpu as pltpu
from jax.sharding import PartitionSpec as P

BLOCK = 128
LANES = 128
SYM = 8
F32 = jnp.float32
BF16 = jnp.bfloat16
GROUP = 2
GROUP_BACK = 4
NN = (((1,), (0,)), ((), ()))
NT = (((1,), (1,)), ((), ()))
TN = (((0,), (0,)), ((), ()))
X_ROW, Z_ROW, DT_ROW, MISC_ROW, TAB_ROWS = 0, 8, 16, 24, 32
XF, XB, ZZ, BCF, BCB, WIDE = 0, 128, 256, 384, 640, 896


def mm(a, b, dims):
    return lax.dot_general(a, b, dims, preferred_element_type=F32)


def halves(a):
    top = a.astype(BF16)
    return top, (a - top.astype(F32)).astype(BF16)


def thirds(a):
    top = a.astype(BF16).astype(F32)
    rest = a - top
    mid = rest.astype(BF16).astype(F32)
    return top, mid, rest - mid


def mm_fine(a, b, dims, terms):
    ah, al = halves(a)
    bh, bl = halves(b)
    (ca,), (cb,) = dims[0]
    left, right = [ah], [bh]
    if terms >= 2:
        left.append(al)
        right.append(bh)
    if terms >= 3:
        left.append(ah)
        right.append(bl)
    return mm(jnp.concatenate(left, ca), jnp.concatenate(right, cb), dims)


def permuted(table, basemap, count):
    row = lax.broadcasted_iota(jnp.int32, table.shape, 0)
    out = jnp.zeros_like(table)
    for k in range(count):
        picked = jnp.zeros_like(table[0:1])
        for m in range(count):
            picked = jnp.where(basemap[k] == m, table[m : m + 1], picked)
        out = jnp.where(row == k, picked, out)
    return out


def sigmoid(v):
    return 0.5 * jnp.tanh(0.5 * v) + 0.5


def gather_tables(j, raw, tabs_ref, bcp_ref, conv, vocab):
    wide_ref, bc_ref, dt_ref = raw
    lanes = pl.ds(pl.multiple_of(j * LANES, LANES), LANES)
    head0 = lax.broadcasted_iota(jnp.int32, (1, LANES), 1) < 64
    pair = lambda a, b: jnp.where(head0, a, b)
    tabs_ref[...] = jnp.zeros_like(tabs_ref)
    bcp_ref[...] = jnp.zeros_like(bcp_ref)
    for k in range(vocab):
        tabs_ref[X_ROW + k : X_ROW + k + 1, :] = wide_ref[2 * k : 2 * k + 1, lanes].astype(F32)
        tabs_ref[Z_ROW + k : Z_ROW + k + 1, :] = wide_ref[2 * k + 1 : 2 * k + 2, lanes].astype(F32)
        tabs_ref[DT_ROW + k : DT_ROW + k + 1, :] = pair(dt_ref[k, 2 * j], dt_ref[k, 2 * j + 1])
        for i in range(2):
            bcp_ref[k : k + 1, i * 128 : i * 128 + 128] = bc_ref[k, i : i + 1, :].astype(F32)
    for k in range(conv):
        tabs_ref[MISC_ROW + k : MISC_ROW + k + 1, :] = wide_ref[2 * vocab + k : 2 * vocab + k + 1, lanes].astype(F32)
        for i in range(2):
            bcp_ref[SYM + k : SYM + k + 1, i * 128 : i * 128 + 128] = bc_ref[
                vocab + k, i : i + 1, :
            ].astype(F32)
    at = MISC_ROW + 4
    tabs_ref[at : at + 1, :] = pair(dt_ref[vocab, 2 * j], dt_ref[vocab, 2 * j + 1])
    tabs_ref[at + 1 : at + 2, :] = pair(
        dt_ref[vocab + 1, 2 * j], dt_ref[vocab + 1, 2 * j + 1]
    )


def tables_kernel(scalars, basemap, *refs, conv, vocab):
    tabs_ref, bcp_ref, dt1_ref, perm_ref, w_ref, w2_out, rate_ref, wf, w2 = refs[3:]
    gather_tables(scalars[0], refs[:3], tabs_ref, bcp_ref, conv, vocab)
    row = lax.broadcasted_iota(jnp.int32, perm_ref.shape, 0)
    lane = lax.broadcasted_iota(jnp.int32, perm_ref.shape, 1)
    perm = jnp.zeros(perm_ref.shape, F32)
    for k in range(vocab):
        perm = jnp.where(jnp.logical_and(lane == k, row == basemap[k]), 1.0, perm)
    perm_ref[...] = perm
    wf[...] = jnp.zeros_like(wf)
    w2[...] = jnp.zeros_like(w2)
    for st in range(2):
        fetch = (lambda t: t) if st == 0 else (lambda t: permuted(t, basemap, vocab))
        xt = fetch(tabs_ref[X_ROW : X_ROW + SYM, :])
        zt = fetch(tabs_ref[Z_ROW : Z_ROW + SYM, :])
        dtt = fetch(tabs_ref[DT_ROW : DT_ROW + SYM, :])
        if st == 1:
            dt1_ref[...] = dtt
        bct = fetch(bcp_ref[0:SYM, :])
        base = st * WIDE
        mid = SYM * (conv - 1)
        wf[mid : mid + SYM, base + ZZ : base + ZZ + LANES] = zt
        for k in range(conv):
            cx = tabs_ref[MISC_ROW + k : MISC_ROW + k + 1, :]
            cbc = bcp_ref[SYM + k : SYM + k + 1, :]
            lo, hi = mid - SYM * k, mid + SYM * k
            wf[lo : lo + SYM, base + XF : base + XF + LANES] = xt * cx
            wf[hi : hi + SYM, base + XB : base + XB + LANES] = xt * cx
            wf[lo : lo + SYM, base + BCF : base + BCF + 256] = bct * cbc
            wf[hi : hi + SYM, base + BCB : base + BCB + 256] = bct * cbc
        dt = jnp.maximum(dtt, 0.0) + jnp.log1p(jnp.exp(-jnp.abs(dtt)))
        ld = -jnp.exp(tabs_ref[MISC_ROW + 4 : MISC_ROW + 5, :]) * dt
        for k, piece in enumerate(thirds(ld)):
            w2[SYM * k : SYM * (k + 1), st * 128 : st * 128 + 128] = piece
            w2[32 + SYM * k : 32 + SYM * (k + 1), 256 + st * 128 : 384 + st * 128] = piece
            for h in range(2):
                at = 24 * (st * 2 + h) + SYM * k
                rate_ref[at : at + SYM, :] = jnp.broadcast_to(
                    piece[:, 64 * h : 64 * h + 1], piece.shape
                )
        for k, piece in enumerate(thirds(dt)):
            c = 512 + st * 128
            w2[64 + SYM * k : 64 + SYM * (k + 1), c : c + 128] = piece
    top, rest = halves(wf[...])
    w_ref[0:64, :] = top
    w_ref[64:128, :] = rest
    w2_out[...] = w2[...].astype(BF16)


def prepare(scalars, tok_refs, w_ref, w2_ref, r, conv):
    ns = len(tok_refs)
    length = ns * BLOCK
    mine = scalars[1]
    for k in range(ns):
        sym = lax.broadcasted_iota(jnp.int32, (SYM, BLOCK), 0).astype(F32)
        tok = jnp.broadcast_to(tok_refs[k][BLOCK : BLOCK + 1, 0:BLOCK].astype(F32), (SYM, BLOCK))
        at = jnp.bitwise_xor(mine, k) * BLOCK
        r.oh[:, pl.ds(pl.multiple_of(at, BLOCK), BLOCK)] = (sym == tok).astype(F32)
    oh = r.oh[...]
    lane = lax.broadcasted_iota(jnp.int32, (SYM, length), 1)
    up = (
        lax.broadcasted_iota(jnp.int32, (BLOCK, BLOCK), 0)
        <= lax.broadcasted_iota(jnp.int32, (BLOCK, BLOCK), 1)
    ).astype(BF16)
    r.rows[...] = jnp.zeros_like(r.rows)
    for d in range(1 - conv, conv):
        shifted = oh if d == 0 else pltpu.roll(oh, (length - d) % length, 1)
        inside = jnp.logical_and(lane + d >= 0, lane + d < length)
        r.rows[SYM * (d + conv - 1) : SYM * (d + conv), :] = jnp.where(inside, shifted, 0.0)
    r.rows[64:128, :] = r.rows[0:64, :]
    one = lax.broadcasted_iota(jnp.int32, (SYM, length), 0) < 3
    r.rows[152:160, :] = one.astype(F32)
    r.rows[184:192, :] = one.astype(F32)
    r.prow[...] = jnp.zeros_like(r.prow)
    oh_b = oh.astype(BF16)
    for b in range(ns):
        cols = slice(b * BLOCK, (b + 1) * BLOCK)
        inc = mm(oh_b[:, cols], up, NN)
        exc = inc - oh[:, cols]
        r.inc[:, cols] = inc
        r.exc[:, cols] = exc
        for k in range(3):
            r.rows[128 + SYM * k : 128 + SYM * (k + 1), cols] = inc
            r.rows[160 + SYM * k : 160 + SYM * (k + 1), cols] = exc
            r.rows[192 + SYM * k : 192 + SYM * (k + 1), cols] = oh[:, cols]
    r.sym[...] = r.rows[0:64, :].astype(BF16)
    turned = jnp.transpose(r.rows[...].astype(BF16))
    r.pre[...] = mm(turned[:, 0:128], w_ref[...], NN)
    w2 = w2_ref[...]
    r.pd[...] = mm(turned[:, 128:256], w2[:, 0:768], NN)
    r.count[...] = turned[:, 128:192]
    for st in range(2):
        for part, row0 in ((0, 0), (1, 32)):
            c = part * 256 + st * 128
            flat = mm(
                w2[row0 : row0 + 32, c : c + 128],
                r.rows[128 + row0 : 160 + row0, :].astype(BF16),
                TN,
            )
            for h in range(2):
                i = part * 4 + st * 2 + h
                row = flat[64 * h : 64 * h + 1, :]
                if part == 0:
                    row = -row
                for k, piece in enumerate(thirds(row)):
                    r.prow[SYM * i + k : SYM * i + k + 1, :] = piece


class Unit:
    def __init__(self, r, tabs_ref, st, b, nb):
        self.rows = rows = slice(b * BLOCK, (b + 1) * BLOCK)
        base = st * WIDE
        self.skip = tabs_ref[MISC_ROW + 5 : MISC_ROW + 6, :]
        self.dt = r.pd[rows, 512 + st * 128 : 512 + st * 128 + 128]
        self.p = r.pd[rows, st * 128 : st * 128 + 128]
        self.q = r.pd[rows, 256 + st * 128 : 256 + st * 128 + 128]
        self.total = self.p[BLOCK - 1 : BLOCK, :]
        self.r, self.st, self.b, self.base = r, st, b, base
        lane = lax.broadcasted_iota(jnp.int32, (BLOCK, LANES), 1)
        self.head0 = lane < 64
        row = lax.broadcasted_iota(jnp.int32, (BLOCK, BLOCK), 0)
        self.low = row >= lane
        self.upp = row <= lane

    def pre(self, col, width):
        return self.r.pre[self.rows, self.base + col : self.base + col + width]

    def act(self, col, width):
        v = self.pre(col, width)
        return v * sigmoid(v)

    def by_head(self, v):
        zero = jnp.zeros_like(v)
        return jnp.where(self.head0, v, zero), jnp.where(self.head0, zero, v)

    def decay(self, h):
        r, st = self.r, self.st
        i = st * 2 + h
        rate = r.rate[24 * i : 24 * i + 24, :]
        ends = r.prow[SYM * i : SYM * (i + 1), self.rows]
        starts = r.prow[SYM * (4 + i) : SYM * (5 + i), self.rows]
        zero = jnp.zeros((32, LANES), F32)
        below = jnp.concatenate([rate, ends, zero], 0)
        above = jnp.concatenate([zero, -rate, starts], 0)
        gap = mm(r.count[self.rows, :], jnp.concatenate([below, above], 1).astype(BF16), NN)
        return jnp.exp(jnp.where(self.low, gap[:, 0:LANES], gap[:, LANES : 2 * LANES]))


def state_pass_fwd(r, tabs_ref, nb, units):
    for st in range(2):
        for b in range(nb):
            u = units[st][b]
            xf, xb = u.act(XF, 128), u.act(XB, 128)
            bcf, bcb = u.act(BCF, 256), u.act(BCB, 256)
            r.x[u.rows, st * 256 : st * 256 + 128] = xf
            r.x[u.rows, st * 256 + 128 : st * 256 + 256] = xb
            r.bc[u.rows, st * 512 : st * 512 + 256] = bcf
            r.bc[u.rows, st * 512 + 256 : st * 512 + 512] = bcb
            wf = jnp.exp(u.total - u.p) * (u.dt * xf)
            wb = jnp.exp(u.q) * (u.dt * xb)
            if b < nb - 1:
                r.s[st * 2, b + 1] = mm_fine(bcf[:, 0:128], wf, TN, 2)
            if b > 0:
                r.s[st * 2 + 1, b - 1] = mm_fine(bcb[:, 0:128], wb, TN, 2)
        for b in range(2, nb):
            r.s[st * 2, b] += jnp.exp(units[st][b - 1].total) * r.s[st * 2, b - 1]
        for b in range(nb - 3, -1, -1):
            r.s[st * 2 + 1, b] += jnp.exp(units[st][b + 1].total) * r.s[st * 2 + 1, b + 1]


def together(bodies):
    bodies = list(bodies)
    while bodies:
        bodies = [b for b in bodies if next(b, True) is None]


class Names:
    pass


def named(refs, names):
    r = Names()
    for name, ref in zip(names, refs):
        setattr(r, name, ref)
    return r


KEPT = ("inc", "exc", "oh", "sym", "pre", "pd", "x", "bc", "s", "dec", "wts", "ys")


def kept_shapes(length):
    nb = length // BLOCK
    return [
        ((SYM, length), F32),
        ((SYM, length), F32),
        ((SYM, length), F32),
        ((64, length), BF16),
        ((length, 2 * WIDE), F32),
        ((length, 768), F32),
        ((length, 512), F32),
        ((length, 1024), F32),
        ((4, nb, LANES, LANES), F32),
        ((4 * nb, BLOCK, BLOCK), F32),
        ((8 * nb, BLOCK, BLOCK), BF16),
        ((length, 1024), F32),
    ]


def forward_kernel(scalars, *refs, ns, conv):
    tok_refs, (w_ref, w2_ref, rate_ref, tabs_ref, out_ref) = refs[:ns], refs[ns : ns + 5]
    r = named(refs[ns + 5 :], KEPT + ("rows", "prow", "count"))
    r.rate = rate_ref
    prepare(scalars, tok_refs, w_ref, w2_ref, r, conv)
    units = [[Unit(r, tabs_ref, st, b, ns) for b in range(ns)] for st in range(2)]
    state_pass_fwd(r, tabs_ref, ns, units)
    gated = {}

    def body(st, b):
        u = units[st][b]
        x = [r.x[u.rows, st * 256 + w * 128 : st * 256 + w * 128 + 128] for w in range(2)]
        decays = (u.decay(0), u.decay(1))
        yield
        masks, lefts, cms = (u.low, u.upp), [], []
        for w in range(2):
            c = st * 512 + w * 256
            bm, cm = r.bc[u.rows, c : c + 128], r.bc[u.rows, c + 128 : c + 256]
            lefts.append(mm_fine(cm, bm, NT, 3))
            cms.append(cm)
        yield
        y = u.skip * (x[0] + x[1])
        for w in range(2):
            if (w == 0 and b > 0) or (w == 1 and b < ns - 1):
                enter = jnp.exp(u.p) if w == 0 else jnp.exp(u.total - u.q)
                carried = enter * mm_fine(cms[w], r.s[st * 2 + w, b], NN, 2)
                r.ys[u.rows, st * 512 + w * 256 + 128 : st * 512 + w * 256 + 256] = carried
                y = y + carried
        yield
        for h in range(2):
            r.dec[(st * ns + b) * 2 + h] = decays[h]
        for w in range(2):
            g = jnp.where(masks[w], lefts[w], 0.0)
            lefts[w] = [(g * d).astype(BF16) for d in decays]
            for h in range(2):
                r.wts[((st * ns + b) * 2 + w) * 2 + h] = lefts[w][h]
        yield
        for w in range(2):
            right = u.by_head((u.dt * x[w]).astype(BF16))
            inner = mm(jnp.concatenate(lefts[w], 1), jnp.concatenate(right, 0), NN)
            r.ys[u.rows, st * 512 + w * 256 : st * 512 + w * 256 + 128] = inner
            y = y + inner
        gated[st, b] = y * u.act(ZZ, 128)

    for b0 in range(0, ns, GROUP):
        together(body(st, b) for b in range(b0, min(b0 + GROUP, ns)) for st in range(2))
        for b in range(b0, min(b0 + GROUP, ns)):
            out_ref[:, units[0][b].rows] = jnp.transpose(gated[0, b] + gated[1, b]).astype(BF16)


def backward_kernel(scalars, *refs, ns, nq, conv, vocab):
    tabs_ref, bcp_ref, dt1_ref, perm_ref = refs[:4]
    cot_refs, weight_ref = refs[4 : 4 + nq], refs[4 + nq]
    kept = refs[5 + nq : 5 + nq + len(KEPT)]
    out_ref, *work = refs[5 + nq + len(KEPT) :]
    r = named(list(kept) + work, KEPT + ("ds", "dg", "dpre"))
    cols = cot_refs[0].shape[2]
    cot = jnp.concatenate([a[...].reshape(ns * BLOCK, cols) for a in cot_refs], 1)
    weight = []
    for k in range(nq):
        at = pl.multiple_of(scalars[QUARTERS + k] * cols, LANES)
        rows = pl.ds(pl.multiple_of(scalars[0] * LANES, LANES), LANES)
        weight.append(weight_ref[rows, pl.ds(at, cols)])
    d_gated = mm(cot, jnp.concatenate(weight, 1), NT).astype(BF16).astype(F32)
    mine = scalars[1]
    for k in range(ns):
        at = jnp.bitwise_xor(mine, k)
        r.dg[pl.ds(pl.multiple_of(at * BLOCK, BLOCK), BLOCK), :] = d_gated[
            k * BLOCK : (k + 1) * BLOCK
        ]
    units = [[Unit(r, tabs_ref, st, b, ns) for b in range(ns)] for st in range(2)]
    for st in range(2):
        for b in range(ns):
            u = units[st][b]
            dy = r.dg[u.rows, :] * u.act(ZZ, 128)
            cf = r.bc[u.rows, st * 512 + 128 : st * 512 + 256]
            cb = r.bc[u.rows, st * 512 + 384 : st * 512 + 512]
            if b > 0:
                r.ds[st * 2, b - 1] = mm_fine(cf, jnp.exp(u.p) * dy, TN, 2)
            if b < ns - 1:
                r.ds[st * 2 + 1, b + 1] = mm_fine(cb, jnp.exp(u.total - u.q) * dy, TN, 2)
        for b in range(ns - 3, -1, -1):
            r.ds[st * 2, b] += jnp.exp(units[st][b + 1].total) * r.ds[st * 2, b + 1]
        for b in range(2, ns):
            r.ds[st * 2 + 1, b] += jnp.exp(units[st][b - 1].total) * r.ds[st * 2 + 1, b - 1]
    d_steps = [jnp.zeros((SYM, LANES), F32)] * 2
    d_decays = [jnp.zeros((SYM, LANES), F32)] * 2
    d_tab = 0.0

    def body(st, b):
        u = units[st][b]
        base = st * WIDE
        x = [r.x[u.rows, st * 256 + w * 128 : st * 256 + w * 128 + 128] for w in range(2)]
        dgv = r.dg[u.rows, :]
        pz = u.pre(ZZ, 128)
        sz = sigmoid(pz)
        dy = dgv * (pz * sz)
        dyr = dy.astype(BF16)
        dyw = dyr.astype(F32)
        dy0, dy1 = u.by_head(dyr)
        decays = [r.dec[(st * ns + b) * 2 + h] for h in range(2)]
        inputs = [u.dt * v for v in x]
        ur = [v.astype(BF16) for v in inputs]
        uw = [v.astype(F32) for v in ur]
        uh = [u.by_head(v) for v in ur]
        d_pair = mm(dyr, jnp.concatenate([uh[0][0], uh[0][1], uh[1][0], uh[1][1]], 0), NT)
        yield
        masks = (u.low, u.upp)
        ends = (jnp.exp(u.total - u.p), jnp.exp(u.q))
        enters = (jnp.exp(u.p), jnp.exp(u.total - u.q))
        weights, bms, cms = [], [], []
        for w in range(2):
            c = st * 512 + w * 256
            bm, cm = r.bc[u.rows, c : c + 128], r.bc[u.rows, c + 128 : c + 256]
            weights.append([r.wts[((st * ns + b) * 2 + w) * 2 + h] for h in range(2)])
            bms.append(bm)
            cms.append(cm)
        du_both = mm(
            jnp.concatenate(
                [
                    jnp.concatenate([weights[0][0], weights[1][0]], 1),
                    jnp.concatenate([weights[0][1], weights[1][1]], 1),
                ],
                0,
            ),
            jnp.concatenate([dy0, dy1], 0),
            TN,
        )
        yield
        y = u.skip * (x[0] + x[1])
        mixes, step_part, flat = [], 0.0, 0.0
        for w in range(2):
            yield
            c = st * 512 + w * 256
            inner = r.ys[u.rows, c : c + 128]
            du_in = du_both[w * BLOCK : (w + 1) * BLOCK]
            has_enter = (w == 0 and b > 0) or (w == 1 and b < ns - 1)
            has_leave = (w == 0 and b < ns - 1) or (w == 1 and b > 0)
            y = y + inner
            row = dyw * inner - uw[w] * du_in
            du = du_in
            d_g = jnp.where(
                masks[w],
                d_pair[:, w * 256 : w * 256 + 128] * decays[0]
                + d_pair[:, w * 256 + 128 : w * 256 + 256] * decays[1],
                0.0,
            ).astype(BF16)
            d_c = mm(d_g, bms[w].astype(BF16), NN)
            d_b = mm(d_g, cms[w].astype(BF16), TN)
            enter_part = gain_part = None
            if has_enter:
                state = r.s[st * 2 + w, b]
                carried = r.ys[u.rows, c + 128 : c + 256]
                y = y + carried
                enter_part = dy * carried
                d_c = d_c + mm((enters[w] * dy).astype(BF16), state.astype(BF16), NT)
            if has_leave:
                d_state = r.ds[st * 2 + w, b]
                d_gain = mm_fine(bms[w], d_state, NN, 2)
                du = du + ends[w] * d_gain
                gain = ends[w] * inputs[w]
                gain_part = gain * d_gain
                d_b = d_b + mm(gain.astype(BF16), d_state.astype(BF16), NT)
            if has_enter and has_leave:
                flat = flat + jnp.exp(u.total) * jnp.sum(state * d_state, 0, keepdims=True)
            if w == 1:
                row = -row
            if enter_part is not None:
                row = row + enter_part if w == 0 else row - enter_part
            if gain_part is not None:
                row = row - gain_part if w == 0 else row + gain_part
            if w == 0 and gain_part is not None:
                flat = flat + jnp.sum(gain_part, 0, keepdims=True)
            if w == 1 and enter_part is not None:
                flat = flat + jnp.sum(enter_part, 0, keepdims=True)
            mixes.append(row)
            step_part = step_part + du * x[w]
            dx = du * u.dt + dy * u.skip
            px = u.pre((XF, XB)[w], 128)
            sx = sigmoid(px)
            col = base + (XF, XB)[w]
            r.dpre[u.rows, col : col + 128] = (dx * (sx * (1.0 + px * (1.0 - sx)))).astype(BF16)
            col = (BCF, BCB)[w]
            for i, grad in enumerate((d_b, d_c)):
                pb = u.pre(col + 128 * i, 128)
                sb = sigmoid(pb)
                at = base + col + 128 * i
                r.dpre[u.rows, at : at + 128] = (
                    grad * (sb * (1.0 + pb * (1.0 - sb)))
                ).astype(BF16)
        yield
        d_z = dgv * y * (sz * (1.0 + pz * (1.0 - sz)))
        r.dpre[u.rows, base + ZZ : base + ZZ + 128] = d_z.astype(BF16)
        inc = r.inc[:, u.rows]
        exc = r.exc[:, u.rows]
        inc_b, exc_b, oh_b = inc.astype(BF16), exc.astype(BF16), r.oh[:, u.rows].astype(BF16)
        right = list(halves(mixes[0])) + list(halves(mixes[1]))
        decay_part = mm(
            jnp.concatenate([inc_b, inc_b, exc_b, exc_b], 1), jnp.concatenate(right, 0), NN
        )
        decay_part = decay_part + inc[:, BLOCK - 1 : BLOCK] * flat
        step_sum = mm(
            jnp.concatenate([oh_b, oh_b], 1), jnp.concatenate(halves(step_part), 0), NN
        )
        d_steps[st] = d_steps[st] + step_sum
        d_decays[st] = d_decays[st] + decay_part

    for b0 in range(0, ns, GROUP_BACK):
        last = min(b0 + GROUP_BACK, ns)
        together(body(st, b) for b in range(b0, last) for st in range(2))
        span = slice(b0 * BLOCK, last * BLOCK)
        d_tab = d_tab + mm(r.sym[:, span], r.dpre[span, :], NN)
    mid = SYM * (conv - 1)
    result = None
    for st in range(2):
        base = st * WIDE
        d_x = jnp.zeros((SYM, 128), F32)
        d_bc = jnp.zeros((SYM, 256), F32)
        for k in range(conv):
            cx = tabs_ref[MISC_ROW + k : MISC_ROW + k + 1, :]
            cbc = bcp_ref[SYM + k : SYM + k + 1, :]
            lo, hi = mid - SYM * k, mid + SYM * k
            d_x = d_x + cx * (
                d_tab[lo : lo + SYM, base + XF : base + XF + 128]
                + d_tab[hi : hi + SYM, base + XB : base + XB + 128]
            )
            d_bc = d_bc + cbc * (
                d_tab[lo : lo + SYM, base + BCF : base + BCF + 256]
                + d_tab[hi : hi + SYM, base + BCB : base + BCB + 256]
            )
        d_zt = d_tab[mid : mid + SYM, base + ZZ : base + ZZ + 128]
        dtt = dt1_ref[...] if st else tabs_ref[DT_ROW : DT_ROW + SYM, :]
        rate = -jnp.exp(tabs_ref[MISC_ROW + 4 : MISC_ROW + 5, :])
        d_dt = (d_steps[st] + rate * d_decays[st]) * sigmoid(dtt)
        wide = jnp.concatenate([d_x, d_zt, d_dt, d_bc], 1)
        if st == 0:
            result = wide
        else:
            for k in range(vocab):
                result = result + perm_ref[:, k : k + 1] * wide[k : k + 1]
    out_ref[...] = result


SMEM = pl.BlockSpec(memory_space=pltpu.SMEM)
VMEM = pl.BlockSpec(memory_space=pltpu.VMEM)
HBM = pl.BlockSpec(memory_space=pl.ANY)


def params(mib):
    return pltpu.CompilerParams(vmem_limit_bytes=mib * 1024 * 1024)


def call_tables(scalars, raw):
    basemap, xz_table, bc_table, conv_x, conv_bc, dt_table, a_log, skip_gain = raw
    conv, vocab = conv_x.shape[0], xz_table.shape[0]
    outs = [
        ((TAB_ROWS, LANES), F32),
        ((2 * SYM, 256), F32),
        ((SYM, LANES), F32),
        ((SYM, LANES), F32),
        ((128, 2 * WIDE), BF16),
        ((128, 768), BF16),
        ((96, LANES), F32),
    ]
    return pl.pallas_call(
        functools.partial(tables_kernel, conv=conv, vocab=vocab),
        out_shape=[jax.ShapeDtypeStruct(*a) for a in outs],
        in_specs=[SMEM, SMEM, VMEM, VMEM, SMEM],
        out_specs=[VMEM] * len(outs),
        scratch_shapes=[pltpu.VMEM((64, 2 * WIDE), F32), pltpu.VMEM((128, 768), F32)],
        compiler_params=params(8),
        cost_estimate=pl.CostEstimate(flops=2 * 10**9, transcendentals=0, bytes_accessed=10**6),
        name="tables",
    )(
        scalars,
        basemap,
        jnp.concatenate([xz_table.reshape(2 * vocab, -1), conv_x], 0),
        jnp.concatenate([bc_table, conv_bc], 0),
        jnp.concatenate([dt_table, a_log[None], skip_gain[None]], 0),
    )


def call_forward(scalars, pays, w, w2, rate, tabs, conv):
    ns = len(pays)
    length = ns * BLOCK
    outs = [((LANES, length), BF16)] + kept_shapes(length)
    return pl.pallas_call(
        functools.partial(forward_kernel, ns=ns, conv=conv),
        out_shape=[jax.ShapeDtypeStruct(*a) for a in outs],
        in_specs=[SMEM] + [VMEM] * (ns + 4),
        out_specs=[VMEM] * len(outs),
        scratch_shapes=[
            pltpu.VMEM((256, length), F32),
            pltpu.VMEM((64, length), F32),
            pltpu.VMEM((length, 64), BF16),
        ],
        compiler_params=params(8),
        cost_estimate=pl.CostEstimate(
            flops=5 * 10**9, transcendentals=0, bytes_accessed=8 * LANES * length
        ),
        name="mix_forward",
    )(scalars, *pays, w, w2, rate, tabs)


def call_backward(scalars, tables, cots, out_weight, kept, conv, vocab):
    length = kept[0].shape[1]
    ns = length // BLOCK
    return pl.pallas_call(
        functools.partial(backward_kernel, ns=ns, nq=len(cots), conv=conv, vocab=vocab),
        out_shape=jax.ShapeDtypeStruct((SYM, 640), F32),
        in_specs=[SMEM] + [VMEM] * (len(tables) + len(cots) + 1 + len(kept)),
        out_specs=VMEM,
        scratch_shapes=[
            pltpu.VMEM((4, ns, LANES, LANES), F32),
            pltpu.VMEM((length, LANES), F32),
            pltpu.VMEM((length, 2 * WIDE), BF16),
        ],
        compiler_params=params(10),
        cost_estimate=pl.CostEstimate(
            flops=6 * 10**9, transcendentals=0, bytes_accessed=8 * LANES * length
        ),
        name="mix_backward",
    )(scalars, *tables, *cots, out_weight, *kept)


QUARTERS = 3


def out_kernel(scalars, *refs, ns, nh, nc):
    slices, weight_ref, outs = refs[: ns * nc], refs[ns * nc], refs[ns * nc + 1 :]
    here = pl.ds(pl.multiple_of(scalars[1] * BLOCK, BLOCK), BLOCK)
    places = QUARTERS + nh * nc
    cols = outs[0].shape[1]
    left = jnp.concatenate([a[:, here] for a in slices], 0)
    for k in range(nh):
        at = pl.ds(pl.multiple_of(scalars[QUARTERS + k * nc] * cols, LANES), cols)
        right = []
        for i in range(ns * nc):
            rows = pl.ds(pl.multiple_of(scalars[places + i] * LANES, LANES), LANES)
            right.append(weight_ref[rows, at])
        outs[k][...] = mm(left, jnp.concatenate(right, 0), TN)


def call_out(scalars, slices, out_weight, ns, nh, nc):
    cols = out_weight.shape[1] // (nh * nc)
    return pl.pallas_call(
        functools.partial(out_kernel, ns=ns, nh=nh, nc=nc),
        out_shape=[jax.ShapeDtypeStruct((BLOCK, cols), F32)] * nh,
        in_specs=[SMEM] + [VMEM] * (len(slices) + 1),
        out_specs=[VMEM] * nh,
        compiler_params=params(8),
        name="layer_out",
    )(scalars, *slices, out_weight)


def weight_kernel(scalars, *refs, ns, nh, nc, vocab):
    slices, cots = refs[: ns * nc], refs[ns * nc : ns * nc + nh * nc]
    packs = refs[ns * nc + nh * nc : ns * nc + nh * nc + ns]
    out_ref, xz_ref, bc_ref, dt_ref, left, buf, sems = refs[ns * nc + nh * nc + ns :]
    mine = scalars[1]
    places = QUARTERS + nh * nc
    cols = cots[0].shape[2]
    for n in range(ns * nc):
        for k in range(ns):
            at = jnp.bitwise_xor(mine, k)
            left[n * LANES : (n + 1) * LANES, k * BLOCK : (k + 1) * BLOCK] = slices[n][
                :, pl.ds(pl.multiple_of(at * BLOCK, BLOCK), BLOCK)
            ]
    copies = []
    for q in range(nh * nc):
        total = mm(left[...], cots[q][...].reshape(ns * BLOCK, cols), NN)
        for n in range(ns * nc):
            at = pl.multiple_of(scalars[places + n] * LANES, LANES)
            buf[q, pl.ds(at, LANES), :] = total[n * LANES : (n + 1) * LANES]
        at = pl.multiple_of(scalars[QUARTERS + q] * cols, LANES)
        copy = pltpu.make_async_copy(buf.at[q], out_ref.at[:, pl.ds(at, cols)], sems.at[q])
        copy.start()
        copies.append(copy)
    d_bc = packs[0][:, 768:1024]
    for a in packs[1:]:
        d_bc = d_bc + a[:, 768:1024]
    for i in range(2):
        for k in range(vocab):
            bc_ref[k, i : i + 1, :] = d_bc[k : k + 1, i * 128 : i * 128 + 128]
    lane = lax.broadcasted_iota(jnp.int32, (SYM, dt_ref.shape[1]), 1)
    d_dt = jnp.zeros((SYM, dt_ref.shape[1]), F32)
    for n in range(2 * ns):
        j = scalars[places + n]
        piece = packs[n % ns][:, n // ns * 384 : n // ns * 384 + 384]
        for i in range(2):
            for k in range(vocab):
                xz_ref[k, i : i + 1, pl.ds(pl.multiple_of(j * LANES, LANES), LANES)] = piece[
                    k : k + 1, i * 128 : i * 128 + 128
                ]
            row = jnp.sum(piece[:, 256 + 64 * i : 320 + 64 * i], 1, keepdims=True)
            d_dt = jnp.where(lane == 2 * j + i, row, d_dt)
    dt_ref[...] = d_dt[:vocab]
    for copy in copies:
        copy.wait()


def call_weight(scalars, slices, cots, packs, raw, width, ns, nh, nc):
    length = slices[0].shape[1]
    rows = ns * nc * LANES
    return pl.pallas_call(
        functools.partial(weight_kernel, ns=ns, nh=nh, nc=nc, vocab=raw[1].shape[0]),
        out_shape=[
            jax.ShapeDtypeStruct(a, F32)
            for a in ((rows, width), raw[1].shape, raw[2].shape, raw[5].shape)
        ],
        in_specs=[SMEM] + [VMEM] * (len(slices) + len(cots) + len(packs)),
        out_specs=[HBM] + [VMEM] * 3,
        scratch_shapes=[
            pltpu.VMEM((rows, length), BF16),
            pltpu.VMEM((nh * nc, rows, width // (nh * nc)), F32),
            pltpu.SemaphoreType.DMA((nh * nc,)),
        ],
        compiler_params=params(12),
        cost_estimate=pl.CostEstimate(
            flops=2 * rows * width * length, transcendentals=0, bytes_accessed=6 * rows * width
        ),
        name="weight_grad",
    )(scalars, *slices, *cots, *packs)


def around(x, axis):
    n = lax.axis_size(axis)
    return [x] + [lax.ppermute(x, axis, [(i, i ^ k) for i in range(n)]) for k in range(1, n)]


def across(x, hops, nh, nc):
    pairs = [
        (a * nc + b, (a + hops[0]) % nh * nc + (b + hops[1]) % nc)
        for a in range(nh)
        for b in range(nc)
    ]
    return lax.ppermute(x, ("head", "sub"), pairs)


def by_channel(
    token_ids, basemap, xz_table, bc_table, dt_table, conv_x, conv_bc, a_log, skip_gain, out_weight, cotangent
):
    ns, nc, nh = lax.axis_size("seq"), lax.axis_size("sub"), lax.axis_size("head")
    s, c, h = lax.axis_index("seq"), lax.axis_index("sub"), lax.axis_index("head")
    width = out_weight.shape[1]
    cols = width // (nh * nc)
    raw = (basemap, xz_table, bc_table, conv_x, conv_bc, dt_table, a_log, skip_gain)
    symbols = jnp.pad(token_ids.astype(BF16).reshape(1, BLOCK), ((0, 15), (0, cols - BLOCK)))
    pays = around(jnp.concatenate([cotangent, symbols], 0), "seq")
    slot = jnp.arange(nh * nc, dtype=jnp.int32)
    quarters = (h - slot // nc) % nh * nc + (c - slot % nc) % nc
    slot = jnp.arange(ns * nc, dtype=jnp.int32)
    places = (c - slot // ns) % nc * ns + jnp.bitwise_xor(s, slot % ns)
    scalars = jnp.concatenate([jnp.stack([c * ns + s, s, c]), quarters, places]).astype(jnp.int32)
    stacked = jnp.stack([a[:BLOCK] for a in pays], 0)
    heads = [stacked] + [across(stacked, (k, 0), nh, nc) for k in range(1, nh)]
    side = across(stacked, (0, 1), nh, nc)
    conv, vocab = conv_x.shape[0], xz_table.shape[0]
    *tables, w, w2, rate = call_tables(scalars, raw)
    gated, *kept = call_forward(scalars, pays, w, w2, rate, tables[0], conv)
    heads, gated = lax.optimization_barrier((heads, gated))
    cots = [heads[0], side]
    for a in heads[1:]:
        cots += [a, across(a, (0, 1), nh, nc)]
    slices = around(gated, "seq")
    grads = call_backward(scalars, tables, cots, out_weight, kept, conv, vocab)
    slices, _ = lax.optimization_barrier((slices, grads))
    slices = slices + [across(a, (0, 1), nh, nc) for a in slices]
    shared = grads[:, 384:]
    beside = across(grads, (0, 1), nh, nc)
    for a in range(1, nh):
        for b in range(nc):
            shared = shared + across(grads[:, 384:], (a, b), nh, nc)
    packed = jnp.concatenate([grads[:, :384], beside[:, :384], shared + beside[:, 384:]], 1)
    packs = around(packed, "seq")
    parts = call_out(scalars, slices, out_weight, ns, nh, nc)
    total = parts[0]
    for k in range(1, nh):
        total = total + across(parts[k], (nh - k, 0), nh, nc)
    layer_out = total.astype(BF16)
    d_out_weight, d_xz, d_bc, d_dt = call_weight(
        scalars, slices, cots, packs, raw, width, ns, nh, nc
    )
    return (layer_out, d_out_weight, d_xz, d_bc, d_dt)


PRECISE = lax.Precision.HIGHEST


def carried_in(part, axis, combine, identity):
    place = lax.axis_index(axis)
    gathered = jax.tree.map(lambda a: lax.all_gather(a, axis), part)
    state = jax.tree.map(lambda a, e: jnp.zeros_like(a) + jnp.asarray(e, a.dtype), part, identity)

    def one(hop, state):
        return combine(
            state, jax.tree.map(lambda a: lax.dynamic_index_in_dim(a, hop, 0, False), gathered)
        )

    return lax.fori_loop(0, place, one, state)


def carried_in_2(array, axis, combine, identity):
    length, mine = (lax.axis_size(axis), lax.axis_index(axis))
    everything = jax.tree.map(
        lambda part, kind: lax.all_gather(part.astype(kind), axis),
        array,
        jax.tree.map(lambda a: jnp.bfloat16 if a.dtype == jnp.float32 else a.dtype, array),
    )
    start = jax.tree.map(
        lambda part, zero: jnp.broadcast_to(jnp.asarray(zero, part.dtype), part.shape),
        array,
        identity,
    )

    def hop(k, before):
        at = length - 1 - k
        reached = at > mine
        new = combine(
            before, jax.tree.map(lambda part, own: part[at].astype(own.dtype), everything, array)
        )
        return jax.tree.map(lambda a, b: jnp.where(reached, a, b), new, before)

    return lax.fori_loop(0, length, hop, start)


def with_halo(block, sides, width):
    for axis, dim in sides:
        count = lax.axis_size(axis)
        forward = [(i, i + 1) for i in range(count - 1)]
        backward = [(target, source) for source, target in forward]
        low = lax.ppermute(
            lax.slice_in_dim(block, block.shape[dim] - width, None, axis=dim), axis, forward
        )
        high = lax.ppermute(lax.slice_in_dim(block, 0, width, axis=dim), axis, backward)
        block = jnp.concatenate([low, block, high], axis=dim)
    return block


def block_step(carry_state, pieces):
    scaled_x, logdec, b_mat, c_mat = pieces
    block_len = scaled_x.shape[0]
    running = jnp.cumsum(logdec, axis=0)
    by_head = running.T
    causal_mask = (jnp.arange(block_len)[:, None] >= jnp.arange(block_len)[None, :])[None, :, :]
    gap_matrix = by_head[:, :, None] - by_head[:, None, :]
    decay_mat = jnp.where(causal_mask, jnp.exp(jnp.where(causal_mask, gap_matrix, 0.0)), 0.0)
    scores = jnp.einsum("tn,sn->ts", c_mat, b_mat, precision=PRECISE)
    within = jnp.einsum("hts,shp->thp", scores[None, :, :] * decay_mat, scaled_x, precision=PRECISE)
    carried = jnp.exp(running)[:, :, None] * jnp.einsum(
        "tn,hpn->thp", c_mat, carry_state, precision=PRECISE
    )
    to_end = jnp.exp(running[-1][None, :] - running)
    gained = jnp.einsum("shp,sn->hpn", to_end[:, :, None] * scaled_x, b_mat, precision=PRECISE)
    return (jnp.exp(running[-1])[:, None, None] * carry_state + gained, within + carried)


def state_pass(inputs, start_state, block_len):
    scaled_x, logdec, b_mat, c_mat = inputs
    block_count = scaled_x.shape[0] // block_len
    pieces = (
        scaled_x.reshape((block_count, block_len) + scaled_x.shape[1:]),
        logdec.reshape(block_count, block_len, -1),
        b_mat.reshape(block_count, block_len, -1),
        c_mat.reshape(block_count, block_len, -1),
    )
    end_state, outputs = lax.scan(jax.checkpoint(block_step), start_state, pieces)
    return (outputs.reshape(scaled_x.shape), end_state)


def final_state(inputs):
    scaled_x, logdec, b_mat, c_mat = inputs
    running = jnp.cumsum(logdec, axis=0)
    to_end = jnp.exp(running[-1][None, :] - running)
    gained = jnp.einsum("shp,sn->hpn", to_end[:, :, None] * scaled_x, b_mat, precision=PRECISE)
    return (jnp.exp(running[-1]), gained)


def lookup(symbols, table):
    vocab_size = table.shape[0]
    onehot = (symbols[:, None] == jnp.arange(vocab_size, dtype=jnp.int32)[None, :]).astype(
        jnp.float32
    )
    return jnp.dot(onehot, table, precision=PRECISE)


def conv_rows(extended, weight, row_count, forward):
    conv_width = weight.shape[0]
    rim_width = conv_width - 1
    summed = jnp.zeros((row_count, extended.shape[1]), jnp.float32)
    for offset in range(conv_width):
        if forward:
            first_row = rim_width - offset
        else:
            first_row = rim_width + offset
        summed = summed + weight[offset][None, :] * extended[first_row : first_row + row_count]
    return summed


def open_inputs(ext_sym, inside_mask, tables, frozen):
    xz_tab, bc_tab, dt_tab = tables
    conv_inner, conv_shared, log_rates, skip_vals = frozen
    rim_width = conv_inner.shape[0] - 1
    row_count = ext_sym.shape[0] - 2 * rim_width
    vocab_size = xz_tab.shape[0]
    inner_dim = xz_tab.shape[2]
    head_count = dt_tab.shape[1]
    state_dim = bc_tab.shape[2]
    looked = lookup(ext_sym, xz_tab.reshape(vocab_size, 2 * inner_dim)) * inside_mask[:, None]
    pre_x = looked[:, :inner_dim]
    gate_act = jax.nn.silu(looked[rim_width : rim_width + row_count, inner_dim:])
    pre_bc = lookup(ext_sym, bc_tab.reshape(vocab_size, 2 * state_dim)) * inside_mask[:, None]
    dt_step = jax.nn.softplus(lookup(ext_sym[rim_width : rim_width + row_count], dt_tab))
    logdec = -jnp.exp(log_rates)[None, :] * dt_step
    flat_bc = conv_shared.reshape(conv_inner.shape[0], 2 * state_dim)

    def one_way(forward):
        x_conv = jax.nn.silu(conv_rows(pre_x, conv_inner, row_count, forward)).reshape(
            row_count, head_count, -1
        )
        bc_conv = jax.nn.silu(conv_rows(pre_bc, flat_bc, row_count, forward))
        return (x_conv, bc_conv[:, :state_dim], bc_conv[:, state_dim:])

    x_fwd, b_fwd, c_fwd = one_way(True)
    x_back, b_back, c_back = one_way(False)
    ahead_in = (x_fwd * dt_step[:, :, None], logdec, b_fwd, c_fwd)
    behind_in = (
        jnp.flip(x_back * dt_step[:, :, None], 0),
        jnp.flip(logdec, 0),
        jnp.flip(b_back, 0),
        jnp.flip(c_back, 0),
    )
    skip_term = skip_vals[None, :, None] * (x_fwd + x_back)
    return (ahead_in, behind_in, skip_term, gate_act)


def combine(earlier, later):
    decay_early, state_early = earlier
    decay_late, state_late = later
    return (decay_early * decay_late, decay_late[:, None, None] * state_early + state_late)


def carries(ahead_pair, behind_pair):
    ahead_out = carried_in(
        (ahead_pair[0], ahead_pair[1]),
        "seq",
        combine,
        (jnp.ones_like(ahead_pair[0]), jnp.zeros_like(ahead_pair[1])),
    )
    behind_out = carried_in_2(
        (behind_pair[0], behind_pair[1]),
        "seq",
        combine,
        (jnp.ones_like(behind_pair[0]), jnp.zeros_like(behind_pair[1])),
    )
    return (ahead_out[1], behind_out[1])


def decay_weights(adjoint, start_state):
    return jnp.sum(adjoint * start_state, axis=(1, 2))


def shards(
    token_ids,
    basemap,
    xz_table,
    bc_table,
    dt_table,
    conv_x,
    conv_bc,
    a_log,
    skip_gain,
    out_weight,
    cotangent,
):
    row_count = token_ids.shape[0]
    rim_width = conv_x.shape[0] - 1
    ext_ids = with_halo(token_ids, (("seq", 0),), rim_width)
    first_row = lax.axis_index("seq") * row_count - rim_width
    where_global = first_row + jnp.arange(row_count + 2 * rim_width, dtype=jnp.int32)
    inside_mask = jnp.logical_and(
        where_global >= 0, where_global < row_count * lax.axis_size("seq")
    ).astype(jnp.float32)
    vocab_size = basemap.shape[0]
    matches = ext_ids[:, None] == jnp.arange(vocab_size, dtype=jnp.int32)[None, :]
    mapped = jnp.sum(jnp.where(matches, basemap[None, :], 0), axis=1)
    ext_sym = jnp.where(lax.axis_index("sub") == 1, mapped, ext_ids)
    tables = (xz_table.astype(jnp.float32), bc_table.astype(jnp.float32), dt_table)
    frozen = (conv_x.astype(jnp.float32), conv_bc.astype(jnp.float32), a_log, skip_gain)

    def summary(tabs_in):
        ahead_in, behind_in, skip_term, gate_act = open_inputs(
            ext_sym, inside_mask, tabs_in, frozen
        )
        decay_fwd, end_fwd = final_state(ahead_in)
        decay_back, end_back = final_state(behind_in)
        return (decay_fwd, end_fwd, decay_back, end_back)

    (decay_fwd, end_fwd, decay_back, end_back), pull_summary = jax.vjp(summary, tables)
    start_fwd, start_back = carries((decay_fwd, end_fwd), (decay_back, end_back))

    def finished(tabs_in, begin_fwd, begin_back):
        ahead_in, behind_in, skip_term, gate_act = open_inputs(
            ext_sym, inside_mask, tabs_in, frozen
        )
        out_fwd, unused_fwd = state_pass(ahead_in, begin_fwd, BLOCK)
        out_back, unused_back = state_pass(behind_in, begin_back, BLOCK)
        return (out_fwd + jnp.flip(out_back, 0) + skip_term).reshape(row_count, -1) * gate_act

    gated, pull_finished = jax.vjp(finished, tables, start_fwd, start_back)
    gated_bf = gated.astype(jnp.bfloat16)
    products = jnp.dot(gated_bf, out_weight, preferred_element_type=jnp.float32)
    layer_out = lax.psum_scatter(products, ("head", "sub"), scatter_dimension=1, tiled=True).astype(
        jnp.bfloat16
    )
    full_cot = lax.all_gather(cotangent, ("head", "sub"), axis=1, tiled=True)
    d_gated = jnp.einsum(
        "tc,kc->tk", full_cot, out_weight, preferred_element_type=jnp.float32
    ).astype(jnp.bfloat16)
    weight_part = jnp.einsum("tk,tc->kc", gated_bf, full_cot, preferred_element_type=jnp.float32)
    d_gated_wide = lax.optimization_barrier(d_gated).astype(jnp.float32)
    grads_first, direct_fwd, direct_back = pull_finished(d_gated_wide)
    adjoint_back, adjoint_fwd = carries((decay_back, direct_back), (decay_fwd, direct_fwd))
    grads_second = pull_summary(
        (
            decay_weights(adjoint_fwd, start_fwd),
            adjoint_fwd,
            decay_weights(adjoint_back, start_back),
            adjoint_back,
        )
    )[0]
    d_tables = jax.tree.map(lambda former, latter: former + latter, grads_first, grads_second)
    d_xz, d_bc, d_dt = d_tables
    d_bc = lax.psum(d_bc, ("seq", "head", "sub"))
    d_out_weight, d_xz, d_dt = lax.psum((weight_part, d_xz, d_dt), ("seq", "sub"))
    return (layer_out, d_out_weight, d_xz, d_bc, d_dt)


def solution(mesh):
    in_specs = (
        P(("grp", "seq")),
        P(),
        P(None, None, "head"),
        P(),
        P(None, "head"),
        P(None, "head"),
        P(),
        P("head"),
        P("head"),
        P("head", None),
        P(("grp", "seq"), ("head", "sub")),
    )
    out_specs = (
        P(("grp", "seq"), ("head", "sub")),
        P(("grp", "head"), None),
        P("grp", None, "head"),
        P("grp", None, None),
        P("grp", "head"),
    )
    def run(*args):
        ns, nc = mesh.shape["seq"], mesh.shape["sub"]
        rows, inner, heads = args[0].shape[0], args[2].shape[2], args[4].shape[1]
        by_lanes = (
            rows == BLOCK
            and nc == 2
            and ns > 1
            and ns & (ns - 1) == 0
            and inner == ns * nc * LANES
            and inner == heads * (LANES // 2)
            and args[3].shape[2] == LANES
            and args[5].shape[0] == 4
            and args[9].shape[1] == args[10].shape[1] * nc * mesh.shape["head"]
        )
        return (by_channel if by_lanes else shards)(*args)

    return jax.shard_map(run, mesh=mesh, in_specs=in_specs, out_specs=out_specs, check_vma=False)
```

```python
import functools

import jax
import jax.numpy as jnp
from jax import lax
from jax.experimental import pallas as pl
from jax.experimental.pallas import tpu as pltpu
from jax.sharding import PartitionSpec as P

BLOCK = 128
LANES = 128
SYM = 8
F32 = jnp.float32
BF16 = jnp.bfloat16
GROUP = 2
GROUP_BACK = 4
NN = (((1,), (0,)), ((), ()))
NT = (((1,), (1,)), ((), ()))
TN = (((0,), (0,)), ((), ()))
X_ROW, Z_ROW, DT_ROW, MISC_ROW, TAB_ROWS = 0, 8, 16, 24, 32
XF, XB, ZZ, BCF, BCB, WIDE = 0, 128, 256, 384, 640, 896


def mm(a, b, dims):
    return lax.dot_general(a, b, dims, preferred_element_type=F32)


def halves(a):
    top = a.astype(BF16)
    return top, (a - top.astype(F32)).astype(BF16)


def thirds(a):
    top = a.astype(BF16).astype(F32)
    rest = a - top
    mid = rest.astype(BF16).astype(F32)
    return top, mid, rest - mid


def mm_fine(a, b, dims, terms):
    ah, al = halves(a)
    bh, bl = halves(b)
    (ca,), (cb,) = dims[0]
    left, right = [ah], [bh]
    if terms >= 2:
        left.append(al)
        right.append(bh)
    if terms >= 3:
        left.append(ah)
        right.append(bl)
    return mm(jnp.concatenate(left, ca), jnp.concatenate(right, cb), dims)


def permuted(table, basemap, count):
    row = lax.broadcasted_iota(jnp.int32, table.shape, 0)
    out = jnp.zeros_like(table)
    for k in range(count):
        picked = jnp.zeros_like(table[0:1])
        for m in range(count):
            picked = jnp.where(basemap[k] == m, table[m : m + 1], picked)
        out = jnp.where(row == k, picked, out)
    return out


def sigmoid(v):
    return 0.5 * jnp.tanh(0.5 * v) + 0.5


def gather_tables(j, raw, tabs_ref, bcp_ref, conv, vocab):
    wide_ref, bc_ref, dt_ref = raw
    lanes = pl.ds(pl.multiple_of(j * LANES, LANES), LANES)
    head0 = lax.broadcasted_iota(jnp.int32, (1, LANES), 1) < 64
    pair = lambda a, b: jnp.where(head0, a, b)
    tabs_ref[...] = jnp.zeros_like(tabs_ref)
    bcp_ref[...] = jnp.zeros_like(bcp_ref)
    for k in range(vocab):
        tabs_ref[X_ROW + k : X_ROW + k + 1, :] = wide_ref[2 * k : 2 * k + 1, lanes].astype(F32)
        tabs_ref[Z_ROW + k : Z_ROW + k + 1, :] = wide_ref[2 * k + 1 : 2 * k + 2, lanes].astype(F32)
        tabs_ref[DT_ROW + k : DT_ROW + k + 1, :] = pair(dt_ref[k, 2 * j], dt_ref[k, 2 * j + 1])
        for i in range(2):
            bcp_ref[k : k + 1, i * 128 : i * 128 + 128] = bc_ref[k, i : i + 1, :].astype(F32)
    for k in range(conv):
        tabs_ref[MISC_ROW + k : MISC_ROW + k + 1, :] = wide_ref[2 * vocab + k : 2 * vocab + k + 1, lanes].astype(F32)
        for i in range(2):
            bcp_ref[SYM + k : SYM + k + 1, i * 128 : i * 128 + 128] = bc_ref[
                vocab + k, i : i + 1, :
            ].astype(F32)
    at = MISC_ROW + 4
    tabs_ref[at : at + 1, :] = pair(dt_ref[vocab, 2 * j], dt_ref[vocab, 2 * j + 1])
    tabs_ref[at + 1 : at + 2, :] = pair(
        dt_ref[vocab + 1, 2 * j], dt_ref[vocab + 1, 2 * j + 1]
    )


def tables_kernel(scalars, basemap, *refs, conv, vocab):
    tabs_ref, bcp_ref, dt1_ref, perm_ref, w_ref, w2_out, rate_ref, wf, w2 = refs[3:]
    gather_tables(scalars[0], refs[:3], tabs_ref, bcp_ref, conv, vocab)
    row = lax.broadcasted_iota(jnp.int32, perm_ref.shape, 0)
    lane = lax.broadcasted_iota(jnp.int32, perm_ref.shape, 1)
    perm = jnp.zeros(perm_ref.shape, F32)
    for k in range(vocab):
        perm = jnp.where(jnp.logical_and(lane == k, row == basemap[k]), 1.0, perm)
    perm_ref[...] = perm
    wf[...] = jnp.zeros_like(wf)
    w2[...] = jnp.zeros_like(w2)
    for st in range(2):
        fetch = (lambda t: t) if st == 0 else (lambda t: permuted(t, basemap, vocab))
        xt = fetch(tabs_ref[X_ROW : X_ROW + SYM, :])
        zt = fetch(tabs_ref[Z_ROW : Z_ROW + SYM, :])
        dtt = fetch(tabs_ref[DT_ROW : DT_ROW + SYM, :])
        if st == 1:
            dt1_ref[...] = dtt
        bct = fetch(bcp_ref[0:SYM, :])
        base = st * WIDE
        mid = SYM * (conv - 1)
        wf[mid : mid + SYM, base + ZZ : base + ZZ + LANES] = zt
        for k in range(conv):
            cx = tabs_ref[MISC_ROW + k : MISC_ROW + k + 1, :]
            cbc = bcp_ref[SYM + k : SYM + k + 1, :]
            lo, hi = mid - SYM * k, mid + SYM * k
            wf[lo : lo + SYM, base + XF : base + XF + LANES] = xt * cx
            wf[hi : hi + SYM, base + XB : base + XB + LANES] = xt * cx
            wf[lo : lo + SYM, base + BCF : base + BCF + 256] = bct * cbc
            wf[hi : hi + SYM, base + BCB : base + BCB + 256] = bct * cbc
        dt = jnp.maximum(dtt, 0.0) + jnp.log1p(jnp.exp(-jnp.abs(dtt)))
        ld = -jnp.exp(tabs_ref[MISC_ROW + 4 : MISC_ROW + 5, :]) * dt
        for k, piece in enumerate(thirds(ld)):
            w2[SYM * k : SYM * (k + 1), st * 128 : st * 128 + 128] = piece
            w2[32 + SYM * k : 32 + SYM * (k + 1), 256 + st * 128 : 384 + st * 128] = piece
            for h in range(2):
                at = 24 * (st * 2 + h) + SYM * k
                rate_ref[at : at + SYM, :] = jnp.broadcast_to(
                    piece[:, 64 * h : 64 * h + 1], piece.shape
                )
        for k, piece in enumerate(thirds(dt)):
            c = 512 + st * 128
            w2[64 + SYM * k : 64 + SYM * (k + 1), c : c + 128] = piece
    top, rest = halves(wf[...])
    w_ref[0:64, :] = top
    w_ref[64:128, :] = rest
    w2_out[...] = w2[...].astype(BF16)


def prepare(scalars, tok_refs, w_ref, w2_ref, r, conv):
    ns = len(tok_refs)
    length = ns * BLOCK
    mine = scalars[1]
    for k in range(ns):
        sym = lax.broadcasted_iota(jnp.int32, (SYM, BLOCK), 0).astype(F32)
        tok = jnp.broadcast_to(tok_refs[k][BLOCK : BLOCK + 1, 0:BLOCK].astype(F32), (SYM, BLOCK))
        at = jnp.bitwise_xor(mine, k) * BLOCK
        r.oh[:, pl.ds(pl.multiple_of(at, BLOCK), BLOCK)] = (sym == tok).astype(F32)
    oh = r.oh[...]
    lane = lax.broadcasted_iota(jnp.int32, (SYM, length), 1)
    up = (
        lax.broadcasted_iota(jnp.int32, (BLOCK, BLOCK), 0)
        <= lax.broadcasted_iota(jnp.int32, (BLOCK, BLOCK), 1)
    ).astype(BF16)
    r.rows[...] = jnp.zeros_like(r.rows)
    for d in range(1 - conv, conv):
        shifted = oh if d == 0 else pltpu.roll(oh, (length - d) % length, 1)
        inside = jnp.logical_and(lane + d >= 0, lane + d < length)
        r.rows[SYM * (d + conv - 1) : SYM * (d + conv), :] = jnp.where(inside, shifted, 0.0)
    r.rows[64:128, :] = r.rows[0:64, :]
    one = lax.broadcasted_iota(jnp.int32, (SYM, length), 0) < 3
    r.rows[152:160, :] = one.astype(F32)
    r.rows[184:192, :] = one.astype(F32)
    r.prow[...] = jnp.zeros_like(r.prow)
    oh_b = oh.astype(BF16)
    for b in range(ns):
        cols = slice(b * BLOCK, (b + 1) * BLOCK)
        inc = mm(oh_b[:, cols], up, NN)
        exc = inc - oh[:, cols]
        r.inc[:, cols] = inc
        r.exc[:, cols] = exc
        for k in range(3):
            r.rows[128 + SYM * k : 128 + SYM * (k + 1), cols] = inc
            r.rows[160 + SYM * k : 160 + SYM * (k + 1), cols] = exc
            r.rows[192 + SYM * k : 192 + SYM * (k + 1), cols] = oh[:, cols]
    r.sym[...] = r.rows[0:64, :].astype(BF16)
    turned = jnp.transpose(r.rows[...].astype(BF16))
    r.pre[...] = mm(turned[:, 0:128], w_ref[...], NN)
    w2 = w2_ref[...]
    r.pd[...] = mm(turned[:, 128:256], w2[:, 0:768], NN)
    r.count[...] = turned[:, 128:192]
    for st in range(2):
        for part, row0 in ((0, 0), (1, 32)):
            c = part * 256 + st * 128
            flat = mm(
                w2[row0 : row0 + 32, c : c + 128],
                r.rows[128 + row0 : 160 + row0, :].astype(BF16),
                TN,
            )
            for h in range(2):
                i = part * 4 + st * 2 + h
                row = flat[64 * h : 64 * h + 1, :]
                if part == 0:
                    row = -row
                for k, piece in enumerate(thirds(row)):
                    r.prow[SYM * i + k : SYM * i + k + 1, :] = piece


class Unit:
    def __init__(self, r, tabs_ref, st, b, nb):
        self.rows = rows = slice(b * BLOCK, (b + 1) * BLOCK)
        base = st * WIDE
        self.skip = tabs_ref[MISC_ROW + 5 : MISC_ROW + 6, :]
        self.dt = r.pd[rows, 512 + st * 128 : 512 + st * 128 + 128]
        self.p = r.pd[rows, st * 128 : st * 128 + 128]
        self.q = r.pd[rows, 256 + st * 128 : 256 + st * 128 + 128]
        self.total = self.p[BLOCK - 1 : BLOCK, :]
        self.r, self.st, self.b, self.base = r, st, b, base
        lane = lax.broadcasted_iota(jnp.int32, (BLOCK, LANES), 1)
        self.head0 = lane < 64
        row = lax.broadcasted_iota(jnp.int32, (BLOCK, BLOCK), 0)
        self.low = row >= lane
        self.upp = row <= lane

    def pre(self, col, width):
        return self.r.pre[self.rows, self.base + col : self.base + col + width]

    def act(self, col, width):
        v = self.pre(col, width)
        return v * sigmoid(v)

    def by_head(self, v):
        zero = jnp.zeros_like(v)
        return jnp.where(self.head0, v, zero), jnp.where(self.head0, zero, v)

    def decay(self, h):
        r, st = self.r, self.st
        i = st * 2 + h
        rate = r.rate[24 * i : 24 * i + 24, :]
        ends = r.prow[SYM * i : SYM * (i + 1), self.rows]
        starts = r.prow[SYM * (4 + i) : SYM * (5 + i), self.rows]
        zero = jnp.zeros((32, LANES), F32)
        below = jnp.concatenate([rate, ends, zero], 0)
        above = jnp.concatenate([zero, -rate, starts], 0)
        gap = mm(r.count[self.rows, :], jnp.concatenate([below, above], 1).astype(BF16), NN)
        return jnp.exp(jnp.where(self.low, gap[:, 0:LANES], gap[:, LANES : 2 * LANES]))


def state_pass_fwd(r, tabs_ref, nb, units):
    for st in range(2):
        for b in range(nb):
            u = units[st][b]
            xf, xb = u.act(XF, 128), u.act(XB, 128)
            bcf, bcb = u.act(BCF, 256), u.act(BCB, 256)
            r.x[u.rows, st * 256 : st * 256 + 128] = xf
            r.x[u.rows, st * 256 + 128 : st * 256 + 256] = xb
            r.bc[u.rows, st * 512 : st * 512 + 256] = bcf
            r.bc[u.rows, st * 512 + 256 : st * 512 + 512] = bcb
            wf = jnp.exp(u.total - u.p) * (u.dt * xf)
            wb = jnp.exp(u.q) * (u.dt * xb)
            if b < nb - 1:
                r.s[st * 2, b + 1] = mm_fine(bcf[:, 0:128], wf, TN, 2)
            if b > 0:
                r.s[st * 2 + 1, b - 1] = mm_fine(bcb[:, 0:128], wb, TN, 2)
        for b in range(2, nb):
            r.s[st * 2, b] += jnp.exp(units[st][b - 1].total) * r.s[st * 2, b - 1]
        for b in range(nb - 3, -1, -1):
            r.s[st * 2 + 1, b] += jnp.exp(units[st][b + 1].total) * r.s[st * 2 + 1, b + 1]


def together(bodies):
    bodies = list(bodies)
    while bodies:
        bodies = [b for b in bodies if next(b, True) is None]


class Names:
    pass


def named(refs, names):
    r = Names()
    for name, ref in zip(names, refs):
        setattr(r, name, ref)
    return r


KEPT = ("inc", "exc", "oh", "sym", "pre", "pd", "x", "bc", "s", "dec", "wts", "ys")


def kept_shapes(length):
    nb = length // BLOCK
    return [
        ((SYM, length), F32),
        ((SYM, length), F32),
        ((SYM, length), F32),
        ((64, length), BF16),
        ((length, 2 * WIDE), F32),
        ((length, 768), F32),
        ((length, 512), F32),
        ((length, 1024), F32),
        ((4, nb, LANES, LANES), F32),
        ((4 * nb, BLOCK, BLOCK), F32),
        ((8 * nb, BLOCK, BLOCK), BF16),
        ((length, 1024), F32),
    ]


def forward_kernel(scalars, *refs, ns, conv):
    tok_refs, (w_ref, w2_ref, rate_ref, tabs_ref, out_ref) = refs[:ns], refs[ns : ns + 5]
    r = named(refs[ns + 5 :], KEPT + ("rows", "prow", "count"))
    r.rate = rate_ref
    prepare(scalars, tok_refs, w_ref, w2_ref, r, conv)
    units = [[Unit(r, tabs_ref, st, b, ns) for b in range(ns)] for st in range(2)]
    state_pass_fwd(r, tabs_ref, ns, units)
    gated = {}

    def body(st, b):
        u = units[st][b]
        x = [r.x[u.rows, st * 256 + w * 128 : st * 256 + w * 128 + 128] for w in range(2)]
        decays = (u.decay(0), u.decay(1))
        yield
        masks, lefts, cms = (u.low, u.upp), [], []
        for w in range(2):
            c = st * 512 + w * 256
            bm, cm = r.bc[u.rows, c : c + 128], r.bc[u.rows, c + 128 : c + 256]
            lefts.append(mm_fine(cm, bm, NT, 3))
            cms.append(cm)
        yield
        y = u.skip * (x[0] + x[1])
        for w in range(2):
            if (w == 0 and b > 0) or (w == 1 and b < ns - 1):
                enter = jnp.exp(u.p) if w == 0 else jnp.exp(u.total - u.q)
                carried = enter * mm_fine(cms[w], r.s[st * 2 + w, b], NN, 2)
                r.ys[u.rows, st * 512 + w * 256 + 128 : st * 512 + w * 256 + 256] = carried
                y = y + carried
        yield
        for h in range(2):
            r.dec[(st * ns + b) * 2 + h] = decays[h]
        for w in range(2):
            g = jnp.where(masks[w], lefts[w], 0.0)
            lefts[w] = [(g * d).astype(BF16) for d in decays]
            for h in range(2):
                r.wts[((st * ns + b) * 2 + w) * 2 + h] = lefts[w][h]
        yield
        for w in range(2):
            right = u.by_head((u.dt * x[w]).astype(BF16))
            inner = mm(jnp.concatenate(lefts[w], 1), jnp.concatenate(right, 0), NN)
            r.ys[u.rows, st * 512 + w * 256 : st * 512 + w * 256 + 128] = inner
            y = y + inner
        gated[st, b] = y * u.act(ZZ, 128)

    for b0 in range(0, ns, GROUP):
        together(body(st, b) for b in range(b0, min(b0 + GROUP, ns)) for st in range(2))
        for b in range(b0, min(b0 + GROUP, ns)):
            out_ref[:, units[0][b].rows] = jnp.transpose(gated[0, b] + gated[1, b]).astype(BF16)


def backward_kernel(scalars, *refs, ns, nq, conv, vocab):
    tabs_ref, bcp_ref, dt1_ref, perm_ref = refs[:4]
    cot_refs, weight_ref = refs[4 : 4 + nq], refs[4 + nq]
    kept = refs[5 + nq : 5 + nq + len(KEPT)]
    out_ref, *work = refs[5 + nq + len(KEPT) :]
    r = named(list(kept) + work, KEPT + ("ds", "dg", "dpre"))
    cols = cot_refs[0].shape[2]
    cot = jnp.concatenate([a[...].reshape(ns * BLOCK, cols) for a in cot_refs], 1)
    weight = []
    for k in range(nq):
        at = pl.multiple_of(scalars[QUARTERS + k] * cols, LANES)
        rows = pl.ds(pl.multiple_of(scalars[0] * LANES, LANES), LANES)
        weight.append(weight_ref[rows, pl.ds(at, cols)])
    d_gated = mm(cot, jnp.concatenate(weight, 1), NT).astype(BF16).astype(F32)
    mine = scalars[1]
    for k in range(ns):
        at = jnp.bitwise_xor(mine, k)
        r.dg[pl.ds(pl.multiple_of(at * BLOCK, BLOCK), BLOCK), :] = d_gated[
            k * BLOCK : (k + 1) * BLOCK
        ]
    units = [[Unit(r, tabs_ref, st, b, ns) for b in range(ns)] for st in range(2)]
    for st in range(2):
        for b in range(ns):
            u = units[st][b]
            dy = r.dg[u.rows, :] * u.act(ZZ, 128)
            cf = r.bc[u.rows, st * 512 + 128 : st * 512 + 256]
            cb = r.bc[u.rows, st * 512 + 384 : st * 512 + 512]
            if b > 0:
                r.ds[st * 2, b - 1] = mm_fine(cf, jnp.exp(u.p) * dy, TN, 2)
            if b < ns - 1:
                r.ds[st * 2 + 1, b + 1] = mm_fine(cb, jnp.exp(u.total - u.q) * dy, TN, 2)
        for b in range(ns - 3, -1, -1):
            r.ds[st * 2, b] += jnp.exp(units[st][b + 1].total) * r.ds[st * 2, b + 1]
        for b in range(2, ns):
            r.ds[st * 2 + 1, b] += jnp.exp(units[st][b - 1].total) * r.ds[st * 2 + 1, b - 1]
    d_steps = [jnp.zeros((SYM, LANES), F32)] * 2
    d_decays = [jnp.zeros((SYM, LANES), F32)] * 2
    d_tab = 0.0

    def body(st, b):
        u = units[st][b]
        base = st * WIDE
        x = [r.x[u.rows, st * 256 + w * 128 : st * 256 + w * 128 + 128] for w in range(2)]
        dgv = r.dg[u.rows, :]
        pz = u.pre(ZZ, 128)
        sz = sigmoid(pz)
        dy = dgv * (pz * sz)
        dyr = dy.astype(BF16)
        dyw = dyr.astype(F32)
        dy0, dy1 = u.by_head(dyr)
        decays = [r.dec[(st * ns + b) * 2 + h] for h in range(2)]
        inputs = [u.dt * v for v in x]
        ur = [v.astype(BF16) for v in inputs]
        uw = [v.astype(F32) for v in ur]
        uh = [u.by_head(v) for v in ur]
        d_pair = mm(dyr, jnp.concatenate([uh[0][0], uh[0][1], uh[1][0], uh[1][1]], 0), NT)
        yield
        masks = (u.low, u.upp)
        ends = (jnp.exp(u.total - u.p), jnp.exp(u.q))
        enters = (jnp.exp(u.p), jnp.exp(u.total - u.q))
        weights, bms, cms = [], [], []
        for w in range(2):
            c = st * 512 + w * 256
            bm, cm = r.bc[u.rows, c : c + 128], r.bc[u.rows, c + 128 : c + 256]
            weights.append([r.wts[((st * ns + b) * 2 + w) * 2 + h] for h in range(2)])
            bms.append(bm)
            cms.append(cm)
        du_both = mm(
            jnp.concatenate(
                [
                    jnp.concatenate([weights[0][0], weights[1][0]], 1),
                    jnp.concatenate([weights[0][1], weights[1][1]], 1),
                ],
                0,
            ),
            jnp.concatenate([dy0, dy1], 0),
            TN,
        )
        yield
        y = u.skip * (x[0] + x[1])
        mixes, step_part, flat = [], 0.0, 0.0
        for w in range(2):
            yield
            c = st * 512 + w * 256
            inner = r.ys[u.rows, c : c + 128]
            du_in = du_both[w * BLOCK : (w + 1) * BLOCK]
            has_enter = (w == 0 and b > 0) or (w == 1 and b < ns - 1)
            has_leave = (w == 0 and b < ns - 1) or (w == 1 and b > 0)
            y = y + inner
            row = dyw * inner - uw[w] * du_in
            du = du_in
            d_g = jnp.where(
                masks[w],
                d_pair[:, w * 256 : w * 256 + 128] * decays[0]
                + d_pair[:, w * 256 + 128 : w * 256 + 256] * decays[1],
                0.0,
            ).astype(BF16)
            d_c = mm(d_g, bms[w].astype(BF16), NN)
            d_b = mm(d_g, cms[w].astype(BF16), TN)
            enter_part = gain_part = None
            if has_enter:
                state = r.s[st * 2 + w, b]
                carried = r.ys[u.rows, c + 128 : c + 256]
                y = y + carried
                enter_part = dy * carried
                d_c = d_c + mm((enters[w] * dy).astype(BF16), state.astype(BF16), NT)
            if has_leave:
                d_state = r.ds[st * 2 + w, b]
                d_gain = mm_fine(bms[w], d_state, NN, 2)
                du = du + ends[w] * d_gain
                gain = ends[w] * inputs[w]
                gain_part = gain * d_gain
                d_b = d_b + mm(gain.astype(BF16), d_state.astype(BF16), NT)
            if has_enter and has_leave:
                flat = flat + jnp.exp(u.total) * jnp.sum(state * d_state, 0, keepdims=True)
            if w == 1:
                row = -row
            if enter_part is not None:
                row = row + enter_part if w == 0 else row - enter_part
            if gain_part is not None:
                row = row - gain_part if w == 0 else row + gain_part
            if w == 0 and gain_part is not None:
                flat = flat + jnp.sum(gain_part, 0, keepdims=True)
            if w == 1 and enter_part is not None:
                flat = flat + jnp.sum(enter_part, 0, keepdims=True)
            mixes.append(row)
            step_part = step_part + du * x[w]
            dx = du * u.dt + dy * u.skip
            px = u.pre((XF, XB)[w], 128)
            sx = sigmoid(px)
            col = base + (XF, XB)[w]
            r.dpre[u.rows, col : col + 128] = (dx * (sx * (1.0 + px * (1.0 - sx)))).astype(BF16)
            col = (BCF, BCB)[w]
            for i, grad in enumerate((d_b, d_c)):
                pb = u.pre(col + 128 * i, 128)
                sb = sigmoid(pb)
                at = base + col + 128 * i
                r.dpre[u.rows, at : at + 128] = (
                    grad * (sb * (1.0 + pb * (1.0 - sb)))
                ).astype(BF16)
        yield
        d_z = dgv * y * (sz * (1.0 + pz * (1.0 - sz)))
        r.dpre[u.rows, base + ZZ : base + ZZ + 128] = d_z.astype(BF16)
        inc = r.inc[:, u.rows]
        exc = r.exc[:, u.rows]
        inc_b, exc_b, oh_b = inc.astype(BF16), exc.astype(BF16), r.oh[:, u.rows].astype(BF16)
        right = list(halves(mixes[0])) + list(halves(mixes[1]))
        decay_part = mm(
            jnp.concatenate([inc_b, inc_b, exc_b, exc_b], 1), jnp.concatenate(right, 0), NN
        )
        decay_part = decay_part + inc[:, BLOCK - 1 : BLOCK] * flat
        step_sum = mm(
            jnp.concatenate([oh_b, oh_b], 1), jnp.concatenate(halves(step_part), 0), NN
        )
        d_steps[st] = d_steps[st] + step_sum
        d_decays[st] = d_decays[st] + decay_part

    for b0 in range(0, ns, GROUP_BACK):
        last = min(b0 + GROUP_BACK, ns)
        together(body(st, b) for b in range(b0, last) for st in range(2))
        span = slice(b0 * BLOCK, last * BLOCK)
        d_tab = d_tab + mm(r.sym[:, span], r.dpre[span, :], NN)
    mid = SYM * (conv - 1)
    result = None
    for st in range(2):
        base = st * WIDE
        d_x = jnp.zeros((SYM, 128), F32)
        d_bc = jnp.zeros((SYM, 256), F32)
        for k in range(conv):
            cx = tabs_ref[MISC_ROW + k : MISC_ROW + k + 1, :]
            cbc = bcp_ref[SYM + k : SYM + k + 1, :]
            lo, hi = mid - SYM * k, mid + SYM * k
            d_x = d_x + cx * (
                d_tab[lo : lo + SYM, base + XF : base + XF + 128]
                + d_tab[hi : hi + SYM, base + XB : base + XB + 128]
            )
            d_bc = d_bc + cbc * (
                d_tab[lo : lo + SYM, base + BCF : base + BCF + 256]
                + d_tab[hi : hi + SYM, base + BCB : base + BCB + 256]
            )
        d_zt = d_tab[mid : mid + SYM, base + ZZ : base + ZZ + 128]
        dtt = dt1_ref[...] if st else tabs_ref[DT_ROW : DT_ROW + SYM, :]
        rate = -jnp.exp(tabs_ref[MISC_ROW + 4 : MISC_ROW + 5, :])
        d_dt = (d_steps[st] + rate * d_decays[st]) * sigmoid(dtt)
        wide = jnp.concatenate([d_x, d_zt, d_dt, d_bc], 1)
        if st == 0:
            result = wide
        else:
            for k in range(vocab):
                result = result + perm_ref[:, k : k + 1] * wide[k : k + 1]
    out_ref[...] = result


SMEM = pl.BlockSpec(memory_space=pltpu.SMEM)
VMEM = pl.BlockSpec(memory_space=pltpu.VMEM)
HBM = pl.BlockSpec(memory_space=pl.ANY)


def params(mib):
    return pltpu.CompilerParams(vmem_limit_bytes=mib * 1024 * 1024)


def call_tables(scalars, raw):
    basemap, xz_table, bc_table, conv_x, conv_bc, dt_table, a_log, skip_gain = raw
    conv, vocab = conv_x.shape[0], xz_table.shape[0]
    outs = [
        ((TAB_ROWS, LANES), F32),
        ((2 * SYM, 256), F32),
        ((SYM, LANES), F32),
        ((SYM, LANES), F32),
        ((128, 2 * WIDE), BF16),
        ((128, 768), BF16),
        ((96, LANES), F32),
    ]
    return pl.pallas_call(
        functools.partial(tables_kernel, conv=conv, vocab=vocab),
        out_shape=[jax.ShapeDtypeStruct(*a) for a in outs],
        in_specs=[SMEM, SMEM, VMEM, VMEM, SMEM],
        out_specs=[VMEM] * len(outs),
        scratch_shapes=[pltpu.VMEM((64, 2 * WIDE), F32), pltpu.VMEM((128, 768), F32)],
        compiler_params=params(8),
        cost_estimate=pl.CostEstimate(flops=2 * 10**9, transcendentals=0, bytes_accessed=10**6),
        name="tables",
    )(
        scalars,
        basemap,
        jnp.concatenate([xz_table.reshape(2 * vocab, -1), conv_x], 0),
        jnp.concatenate([bc_table, conv_bc], 0),
        jnp.concatenate([dt_table, a_log[None], skip_gain[None]], 0),
    )


def call_forward(scalars, pays, w, w2, rate, tabs, conv):
    ns = len(pays)
    length = ns * BLOCK
    outs = [((LANES, length), BF16)] + kept_shapes(length)
    return pl.pallas_call(
        functools.partial(forward_kernel, ns=ns, conv=conv),
        out_shape=[jax.ShapeDtypeStruct(*a) for a in outs],
        in_specs=[SMEM] + [VMEM] * (ns + 4),
        out_specs=[VMEM] * len(outs),
        scratch_shapes=[
            pltpu.VMEM((256, length), F32),
            pltpu.VMEM((64, length), F32),
            pltpu.VMEM((length, 64), BF16),
        ],
        compiler_params=params(8),
        cost_estimate=pl.CostEstimate(
            flops=5 * 10**9, transcendentals=0, bytes_accessed=8 * LANES * length
        ),
        name="mix_forward",
    )(scalars, *pays, w, w2, rate, tabs)


def call_backward(scalars, tables, cots, out_weight, kept, conv, vocab):
    length = kept[0].shape[1]
    ns = length // BLOCK
    return pl.pallas_call(
        functools.partial(backward_kernel, ns=ns, nq=len(cots), conv=conv, vocab=vocab),
        out_shape=jax.ShapeDtypeStruct((SYM, 640), F32),
        in_specs=[SMEM] + [VMEM] * (len(tables) + len(cots) + 1 + len(kept)),
        out_specs=VMEM,
        scratch_shapes=[
            pltpu.VMEM((4, ns, LANES, LANES), F32),
            pltpu.VMEM((length, LANES), F32),
            pltpu.VMEM((length, 2 * WIDE), BF16),
        ],
        compiler_params=params(10),
        cost_estimate=pl.CostEstimate(
            flops=6 * 10**9, transcendentals=0, bytes_accessed=8 * LANES * length
        ),
        name="mix_backward",
    )(scalars, *tables, *cots, out_weight, *kept)


QUARTERS = 3


def out_kernel(scalars, *refs, ns, nh, nc):
    slices, weight_ref, outs = refs[: ns * nc], refs[ns * nc], refs[ns * nc + 1 :]
    here = pl.ds(pl.multiple_of(scalars[1] * BLOCK, BLOCK), BLOCK)
    places = QUARTERS + nh * nc
    cols = outs[0].shape[1]
    left = jnp.concatenate([a[:, here] for a in slices], 0)
    for k in range(nh):
        at = pl.ds(pl.multiple_of(scalars[QUARTERS + k * nc] * cols, LANES), cols)
        right = []
        for i in range(ns * nc):
            rows = pl.ds(pl.multiple_of(scalars[places + i] * LANES, LANES), LANES)
            right.append(weight_ref[rows, at])
        outs[k][...] = mm(left, jnp.concatenate(right, 0), TN)


def call_out(scalars, slices, out_weight, ns, nh, nc):
    cols = out_weight.shape[1] // (nh * nc)
    return pl.pallas_call(
        functools.partial(out_kernel, ns=ns, nh=nh, nc=nc),
        out_shape=[jax.ShapeDtypeStruct((BLOCK, cols), F32)] * nh,
        in_specs=[SMEM] + [VMEM] * (len(slices) + 1),
        out_specs=[VMEM] * nh,
        compiler_params=params(8),
        name="layer_out",
    )(scalars, *slices, out_weight)


def weight_kernel(scalars, *refs, ns, nh, nc):
    slices, cots = refs[: ns * nc], refs[ns * nc : ns * nc + nh * nc]
    out_ref, mark_ref, left, buf, sems = refs[ns * nc + nh * nc :]
    mine = scalars[1]
    places = QUARTERS + nh * nc
    cols = cots[0].shape[2]
    mark_ref[...] = jnp.zeros_like(mark_ref)
    for n in range(ns * nc):
        for k in range(ns):
            at = jnp.bitwise_xor(mine, k)
            left[n * LANES : (n + 1) * LANES, k * BLOCK : (k + 1) * BLOCK] = slices[n][
                :, pl.ds(pl.multiple_of(at * BLOCK, BLOCK), BLOCK)
            ]
    copies = []
    for q in range(nh * nc):
        total = mm(left[...], cots[q][...].reshape(ns * BLOCK, cols), NN)
        for n in range(ns * nc):
            at = pl.multiple_of(scalars[places + n] * LANES, LANES)
            buf[q, pl.ds(at, LANES), :] = total[n * LANES : (n + 1) * LANES]
        at = pl.multiple_of(scalars[QUARTERS + q] * cols, LANES)
        copy = pltpu.make_async_copy(buf.at[q], out_ref.at[:, pl.ds(at, cols)], sems.at[q])
        copy.start()
        copies.append(copy)
    for copy in copies:
        copy.wait()


def call_weight(scalars, slices, cots, width, ns, nh, nc):
    length = slices[0].shape[1]
    rows = ns * nc * LANES
    return pl.pallas_call(
        functools.partial(weight_kernel, ns=ns, nh=nh, nc=nc),
        out_shape=[
            jax.ShapeDtypeStruct((rows, width), F32),
            jax.ShapeDtypeStruct((SYM, LANES), F32),
        ],
        in_specs=[SMEM] + [VMEM] * (len(slices) + len(cots)),
        out_specs=[HBM, VMEM],
        scratch_shapes=[
            pltpu.VMEM((rows, length), BF16),
            pltpu.VMEM((nh * nc, rows, width // (nh * nc)), F32),
            pltpu.SemaphoreType.DMA((nh * nc,)),
        ],
        compiler_params=params(12),
        cost_estimate=pl.CostEstimate(
            flops=2 * rows * width * length, transcendentals=0, bytes_accessed=6 * rows * width
        ),
        name="weight_grad",
    )(scalars, *slices, *cots)


def final_kernel(scalars, *refs, ns, nh, vocab, places):
    packs, parts = refs[:ns], refs[ns : ns + nh]
    out_ref, xz_ref, bc_ref, dt_ref = refs[ns + nh + 1 :]
    total = parts[0][...]
    for a in parts[1:]:
        total = total + a[...]
    out_ref[...] = total.astype(BF16)
    d_bc = packs[0][:, 768:1024]
    for a in packs[1:]:
        d_bc = d_bc + a[:, 768:1024]
    for i in range(2):
        for k in range(vocab):
            bc_ref[k, i : i + 1, :] = d_bc[k : k + 1, i * 128 : i * 128 + 128]
    lane = lax.broadcasted_iota(jnp.int32, (SYM, dt_ref.shape[1]), 1)
    d_dt = jnp.zeros((SYM, dt_ref.shape[1]), F32)
    for n in range(2 * ns):
        j = scalars[places + n]
        piece = packs[n % ns][:, n // ns * 384 : n // ns * 384 + 384]
        for i in range(2):
            for k in range(vocab):
                xz_ref[k, i : i + 1, pl.ds(pl.multiple_of(j * LANES, LANES), LANES)] = piece[
                    k : k + 1, i * 128 : i * 128 + 128
                ]
            row = jnp.sum(piece[:, 256 + 64 * i : 320 + 64 * i], 1, keepdims=True)
            d_dt = jnp.where(lane == 2 * j + i, row, d_dt)
    dt_ref[...] = d_dt[:vocab]


def call_final(scalars, packs, parts, mark, raw, places):
    shapes = [raw[1].shape, raw[2].shape, raw[5].shape]
    arrays = list(packs) + list(parts)
    return pl.pallas_call(
        functools.partial(
            final_kernel, ns=len(packs), nh=len(parts), vocab=raw[1].shape[0], places=places
        ),
        out_shape=[jax.ShapeDtypeStruct(parts[0].shape, BF16)]
        + [jax.ShapeDtypeStruct(a, F32) for a in shapes],
        in_specs=[SMEM] + [VMEM] * (len(arrays) + 1),
        out_specs=[VMEM] * (len(shapes) + 1),
        compiler_params=params(8),
        name="place_grads",
    )(scalars, *arrays, mark)


def around(x, axis):
    n = lax.axis_size(axis)
    return [x] + [lax.ppermute(x, axis, [(i, i ^ k) for i in range(n)]) for k in range(1, n)]


def across(x, hops, nh, nc):
    pairs = [
        (a * nc + b, (a + hops[0]) % nh * nc + (b + hops[1]) % nc)
        for a in range(nh)
        for b in range(nc)
    ]
    return lax.ppermute(x, ("head", "sub"), pairs)


def by_channel(
    token_ids, basemap, xz_table, bc_table, dt_table, conv_x, conv_bc, a_log, skip_gain, out_weight, cotangent
):
    ns, nc, nh = lax.axis_size("seq"), lax.axis_size("sub"), lax.axis_size("head")
    s, c, h = lax.axis_index("seq"), lax.axis_index("sub"), lax.axis_index("head")
    width = out_weight.shape[1]
    cols = width // (nh * nc)
    raw = (basemap, xz_table, bc_table, conv_x, conv_bc, dt_table, a_log, skip_gain)
    symbols = jnp.pad(token_ids.astype(BF16).reshape(1, BLOCK), ((0, 15), (0, cols - BLOCK)))
    pays = around(jnp.concatenate([cotangent, symbols], 0), "seq")
    slot = jnp.arange(nh * nc, dtype=jnp.int32)
    quarters = (h - slot // nc) % nh * nc + (c - slot % nc) % nc
    slot = jnp.arange(ns * nc, dtype=jnp.int32)
    places = (c - slot // ns) % nc * ns + jnp.bitwise_xor(s, slot % ns)
    scalars = jnp.concatenate([jnp.stack([c * ns + s, s, c]), quarters, places]).astype(jnp.int32)
    stacked = jnp.stack([a[:BLOCK] for a in pays], 0)
    heads = [stacked] + [across(stacked, (k, 0), nh, nc) for k in range(1, nh)]
    side = across(stacked, (0, 1), nh, nc)
    conv, vocab = conv_x.shape[0], xz_table.shape[0]
    *tables, w, w2, rate = call_tables(scalars, raw)
    gated, *kept = call_forward(scalars, pays, w, w2, rate, tables[0], conv)
    heads, _ = lax.optimization_barrier((heads, gated))
    cots = [heads[0], side]
    for a in heads[1:]:
        cots += [a, across(a, (0, 1), nh, nc)]
    hop = lambda x, k: lax.ppermute(x, "seq", [(i, i ^ k) for i in range(ns)])
    direct = {k: hop(gated, k) for k in (1 << n for n in range(ns.bit_length() - 1))}
    grads = call_backward(scalars, tables, cots, out_weight, kept, conv, vocab)
    direct, _ = lax.optimization_barrier((direct, grads))
    held = {0: gated, **direct}
    for k in range(3, ns):
        if k not in held:
            held[k] = hop(held[k & (k - 1)], k & -k)
    slices = [held[k] for k in range(ns)]
    slices = slices + [across(a, (0, 1), nh, nc) for a in slices]
    shared = grads[:, 384:]
    beside = across(grads, (0, 1), nh, nc)
    for a in range(1, nh):
        for b in range(nc):
            shared = shared + across(grads[:, 384:], (a, b), nh, nc)
    packed = jnp.concatenate([grads[:, :384], beside[:, :384], shared + beside[:, 384:]], 1)
    packs = around(packed, "seq")
    parts = call_out(scalars, slices, out_weight, ns, nh, nc)
    parts = [parts[0]] + [across(parts[k], (nh - k, 0), nh, nc) for k in range(1, nh)]
    d_out_weight, mark = call_weight(scalars, slices, cots, width, ns, nh, nc)
    layer_out, d_xz, d_bc, d_dt = call_final(
        scalars, packs, parts, mark, raw, QUARTERS + nh * nc
    )
    return (layer_out, d_out_weight, d_xz, d_bc, d_dt)


PRECISE = lax.Precision.HIGHEST


def carried_in(part, axis, combine, identity):
    place = lax.axis_index(axis)
    gathered = jax.tree.map(lambda a: lax.all_gather(a, axis), part)
    state = jax.tree.map(lambda a, e: jnp.zeros_like(a) + jnp.asarray(e, a.dtype), part, identity)

    def one(hop, state):
        return combine(
            state, jax.tree.map(lambda a: lax.dynamic_index_in_dim(a, hop, 0, False), gathered)
        )

    return lax.fori_loop(0, place, one, state)


def carried_in_2(array, axis, combine, identity):
    length, mine = (lax.axis_size(axis), lax.axis_index(axis))
    everything = jax.tree.map(
        lambda part, kind: lax.all_gather(part.astype(kind), axis),
        array,
        jax.tree.map(lambda a: jnp.bfloat16 if a.dtype == jnp.float32 else a.dtype, array),
    )
    start = jax.tree.map(
        lambda part, zero: jnp.broadcast_to(jnp.asarray(zero, part.dtype), part.shape),
        array,
        identity,
    )

    def hop(k, before):
        at = length - 1 - k
        reached = at > mine
        new = combine(
            before, jax.tree.map(lambda part, own: part[at].astype(own.dtype), everything, array)
        )
        return jax.tree.map(lambda a, b: jnp.where(reached, a, b), new, before)

    return lax.fori_loop(0, length, hop, start)


def with_halo(block, sides, width):
    for axis, dim in sides:
        count = lax.axis_size(axis)
        forward = [(i, i + 1) for i in range(count - 1)]
        backward = [(target, source) for source, target in forward]
        low = lax.ppermute(
            lax.slice_in_dim(block, block.shape[dim] - width, None, axis=dim), axis, forward
        )
        high = lax.ppermute(lax.slice_in_dim(block, 0, width, axis=dim), axis, backward)
        block = jnp.concatenate([low, block, high], axis=dim)
    return block


def block_step(carry_state, pieces):
    scaled_x, logdec, b_mat, c_mat = pieces
    block_len = scaled_x.shape[0]
    running = jnp.cumsum(logdec, axis=0)
    by_head = running.T
    causal_mask = (jnp.arange(block_len)[:, None] >= jnp.arange(block_len)[None, :])[None, :, :]
    gap_matrix = by_head[:, :, None] - by_head[:, None, :]
    decay_mat = jnp.where(causal_mask, jnp.exp(jnp.where(causal_mask, gap_matrix, 0.0)), 0.0)
    scores = jnp.einsum("tn,sn->ts", c_mat, b_mat, precision=PRECISE)
    within = jnp.einsum("hts,shp->thp", scores[None, :, :] * decay_mat, scaled_x, precision=PRECISE)
    carried = jnp.exp(running)[:, :, None] * jnp.einsum(
        "tn,hpn->thp", c_mat, carry_state, precision=PRECISE
    )
    to_end = jnp.exp(running[-1][None, :] - running)
    gained = jnp.einsum("shp,sn->hpn", to_end[:, :, None] * scaled_x, b_mat, precision=PRECISE)
    return (jnp.exp(running[-1])[:, None, None] * carry_state + gained, within + carried)


def state_pass(inputs, start_state, block_len):
    scaled_x, logdec, b_mat, c_mat = inputs
    block_count = scaled_x.shape[0] // block_len
    pieces = (
        scaled_x.reshape((block_count, block_len) + scaled_x.shape[1:]),
        logdec.reshape(block_count, block_len, -1),
        b_mat.reshape(block_count, block_len, -1),
        c_mat.reshape(block_count, block_len, -1),
    )
    end_state, outputs = lax.scan(jax.checkpoint(block_step), start_state, pieces)
    return (outputs.reshape(scaled_x.shape), end_state)


def final_state(inputs):
    scaled_x, logdec, b_mat, c_mat = inputs
    running = jnp.cumsum(logdec, axis=0)
    to_end = jnp.exp(running[-1][None, :] - running)
    gained = jnp.einsum("shp,sn->hpn", to_end[:, :, None] * scaled_x, b_mat, precision=PRECISE)
    return (jnp.exp(running[-1]), gained)


def lookup(symbols, table):
    vocab_size = table.shape[0]
    onehot = (symbols[:, None] == jnp.arange(vocab_size, dtype=jnp.int32)[None, :]).astype(
        jnp.float32
    )
    return jnp.dot(onehot, table, precision=PRECISE)


def conv_rows(extended, weight, row_count, forward):
    conv_width = weight.shape[0]
    rim_width = conv_width - 1
    summed = jnp.zeros((row_count, extended.shape[1]), jnp.float32)
    for offset in range(conv_width):
        if forward:
            first_row = rim_width - offset
        else:
            first_row = rim_width + offset
        summed = summed + weight[offset][None, :] * extended[first_row : first_row + row_count]
    return summed


def open_inputs(ext_sym, inside_mask, tables, frozen):
    xz_tab, bc_tab, dt_tab = tables
    conv_inner, conv_shared, log_rates, skip_vals = frozen
    rim_width = conv_inner.shape[0] - 1
    row_count = ext_sym.shape[0] - 2 * rim_width
    vocab_size = xz_tab.shape[0]
    inner_dim = xz_tab.shape[2]
    head_count = dt_tab.shape[1]
    state_dim = bc_tab.shape[2]
    looked = lookup(ext_sym, xz_tab.reshape(vocab_size, 2 * inner_dim)) * inside_mask[:, None]
    pre_x = looked[:, :inner_dim]
    gate_act = jax.nn.silu(looked[rim_width : rim_width + row_count, inner_dim:])
    pre_bc = lookup(ext_sym, bc_tab.reshape(vocab_size, 2 * state_dim)) * inside_mask[:, None]
    dt_step = jax.nn.softplus(lookup(ext_sym[rim_width : rim_width + row_count], dt_tab))
    logdec = -jnp.exp(log_rates)[None, :] * dt_step
    flat_bc = conv_shared.reshape(conv_inner.shape[0], 2 * state_dim)

    def one_way(forward):
        x_conv = jax.nn.silu(conv_rows(pre_x, conv_inner, row_count, forward)).reshape(
            row_count, head_count, -1
        )
        bc_conv = jax.nn.silu(conv_rows(pre_bc, flat_bc, row_count, forward))
        return (x_conv, bc_conv[:, :state_dim], bc_conv[:, state_dim:])

    x_fwd, b_fwd, c_fwd = one_way(True)
    x_back, b_back, c_back = one_way(False)
    ahead_in = (x_fwd * dt_step[:, :, None], logdec, b_fwd, c_fwd)
    behind_in = (
        jnp.flip(x_back * dt_step[:, :, None], 0),
        jnp.flip(logdec, 0),
        jnp.flip(b_back, 0),
        jnp.flip(c_back, 0),
    )
    skip_term = skip_vals[None, :, None] * (x_fwd + x_back)
    return (ahead_in, behind_in, skip_term, gate_act)


def combine(earlier, later):
    decay_early, state_early = earlier
    decay_late, state_late = later
    return (decay_early * decay_late, decay_late[:, None, None] * state_early + state_late)


def carries(ahead_pair, behind_pair):
    ahead_out = carried_in(
        (ahead_pair[0], ahead_pair[1]),
        "seq",
        combine,
        (jnp.ones_like(ahead_pair[0]), jnp.zeros_like(ahead_pair[1])),
    )
    behind_out = carried_in_2(
        (behind_pair[0], behind_pair[1]),
        "seq",
        combine,
        (jnp.ones_like(behind_pair[0]), jnp.zeros_like(behind_pair[1])),
    )
    return (ahead_out[1], behind_out[1])


def decay_weights(adjoint, start_state):
    return jnp.sum(adjoint * start_state, axis=(1, 2))


def shards(
    token_ids,
    basemap,
    xz_table,
    bc_table,
    dt_table,
    conv_x,
    conv_bc,
    a_log,
    skip_gain,
    out_weight,
    cotangent,
):
    row_count = token_ids.shape[0]
    rim_width = conv_x.shape[0] - 1
    ext_ids = with_halo(token_ids, (("seq", 0),), rim_width)
    first_row = lax.axis_index("seq") * row_count - rim_width
    where_global = first_row + jnp.arange(row_count + 2 * rim_width, dtype=jnp.int32)
    inside_mask = jnp.logical_and(
        where_global >= 0, where_global < row_count * lax.axis_size("seq")
    ).astype(jnp.float32)
    vocab_size = basemap.shape[0]
    matches = ext_ids[:, None] == jnp.arange(vocab_size, dtype=jnp.int32)[None, :]
    mapped = jnp.sum(jnp.where(matches, basemap[None, :], 0), axis=1)
    ext_sym = jnp.where(lax.axis_index("sub") == 1, mapped, ext_ids)
    tables = (xz_table.astype(jnp.float32), bc_table.astype(jnp.float32), dt_table)
    frozen = (conv_x.astype(jnp.float32), conv_bc.astype(jnp.float32), a_log, skip_gain)

    def summary(tabs_in):
        ahead_in, behind_in, skip_term, gate_act = open_inputs(
            ext_sym, inside_mask, tabs_in, frozen
        )
        decay_fwd, end_fwd = final_state(ahead_in)
        decay_back, end_back = final_state(behind_in)
        return (decay_fwd, end_fwd, decay_back, end_back)

    (decay_fwd, end_fwd, decay_back, end_back), pull_summary = jax.vjp(summary, tables)
    start_fwd, start_back = carries((decay_fwd, end_fwd), (decay_back, end_back))

    def finished(tabs_in, begin_fwd, begin_back):
        ahead_in, behind_in, skip_term, gate_act = open_inputs(
            ext_sym, inside_mask, tabs_in, frozen
        )
        out_fwd, unused_fwd = state_pass(ahead_in, begin_fwd, BLOCK)
        out_back, unused_back = state_pass(behind_in, begin_back, BLOCK)
        return (out_fwd + jnp.flip(out_back, 0) + skip_term).reshape(row_count, -1) * gate_act

    gated, pull_finished = jax.vjp(finished, tables, start_fwd, start_back)
    gated_bf = gated.astype(jnp.bfloat16)
    products = jnp.dot(gated_bf, out_weight, preferred_element_type=jnp.float32)
    layer_out = lax.psum_scatter(products, ("head", "sub"), scatter_dimension=1, tiled=True).astype(
        jnp.bfloat16
    )
    full_cot = lax.all_gather(cotangent, ("head", "sub"), axis=1, tiled=True)
    d_gated = jnp.einsum(
        "tc,kc->tk", full_cot, out_weight, preferred_element_type=jnp.float32
    ).astype(jnp.bfloat16)
    weight_part = jnp.einsum("tk,tc->kc", gated_bf, full_cot, preferred_element_type=jnp.float32)
    d_gated_wide = lax.optimization_barrier(d_gated).astype(jnp.float32)
    grads_first, direct_fwd, direct_back = pull_finished(d_gated_wide)
    adjoint_back, adjoint_fwd = carries((decay_back, direct_back), (decay_fwd, direct_fwd))
    grads_second = pull_summary(
        (
            decay_weights(adjoint_fwd, start_fwd),
            adjoint_fwd,
            decay_weights(adjoint_back, start_back),
            adjoint_back,
        )
    )[0]
    d_tables = jax.tree.map(lambda former, latter: former + latter, grads_first, grads_second)
    d_xz, d_bc, d_dt = d_tables
    d_bc = lax.psum(d_bc, ("seq", "head", "sub"))
    d_out_weight, d_xz, d_dt = lax.psum((weight_part, d_xz, d_dt), ("seq", "sub"))
    return (layer_out, d_out_weight, d_xz, d_bc, d_dt)


def solution(mesh):
    in_specs = (
        P(("grp", "seq")),
        P(),
        P(None, None, "head"),
        P(),
        P(None, "head"),
        P(None, "head"),
        P(),
        P("head"),
        P("head"),
        P("head", None),
        P(("grp", "seq"), ("head", "sub")),
    )
    out_specs = (
        P(("grp", "seq"), ("head", "sub")),
        P(("grp", "head"), None),
        P("grp", None, "head"),
        P("grp", None, None),
        P("grp", "head"),
    )
    def run(*args):
        ns, nc = mesh.shape["seq"], mesh.shape["sub"]
        rows, inner, heads = args[0].shape[0], args[2].shape[2], args[4].shape[1]
        by_lanes = (
            rows == BLOCK
            and nc == 2
            and ns > 1
            and ns & (ns - 1) == 0
            and inner == ns * nc * LANES
            and inner == heads * (LANES // 2)
            and args[3].shape[2] == LANES
            and args[5].shape[0] == 4
            and args[9].shape[1] == args[10].shape[1] * nc * mesh.shape["head"]
        )
        return (by_channel if by_lanes else shards)(*args)

    return jax.shard_map(run, mesh=mesh, in_specs=in_specs, out_specs=out_specs, check_vma=False)
```

```python
import functools

import jax
import jax.numpy as jnp
from jax import lax
from jax.experimental import pallas as pl
from jax.experimental.pallas import tpu as pltpu
from jax.sharding import PartitionSpec as P

BLOCK = 128
LANES = 128
SYM = 8
F32 = jnp.float32
BF16 = jnp.bfloat16
GROUP = 2
GROUP_BACK = 4
NN = (((1,), (0,)), ((), ()))
NT = (((1,), (1,)), ((), ()))
TN = (((0,), (0,)), ((), ()))
X_ROW, Z_ROW, DT_ROW, MISC_ROW, TAB_ROWS = 0, 8, 16, 24, 32
XF, XB, ZZ, BCF, BCB, WIDE = 0, 128, 256, 384, 640, 896


def mm(a, b, dims):
    return lax.dot_general(a, b, dims, preferred_element_type=F32)


def halves(a):
    top = a.astype(BF16)
    return top, (a - top.astype(F32)).astype(BF16)


def thirds(a):
    top = a.astype(BF16).astype(F32)
    rest = a - top
    mid = rest.astype(BF16).astype(F32)
    return top, mid, rest - mid


def mm_fine(a, b, dims, terms):
    ah, al = halves(a)
    bh, bl = halves(b)
    (ca,), (cb,) = dims[0]
    left, right = [ah], [bh]
    if terms >= 2:
        left.append(al)
        right.append(bh)
    if terms >= 3:
        left.append(ah)
        right.append(bl)
    return mm(jnp.concatenate(left, ca), jnp.concatenate(right, cb), dims)


def permuted(table, basemap, count):
    row = lax.broadcasted_iota(jnp.int32, table.shape, 0)
    out = jnp.zeros_like(table)
    for k in range(count):
        picked = jnp.zeros_like(table[0:1])
        for m in range(count):
            picked = jnp.where(basemap[k] == m, table[m : m + 1], picked)
        out = jnp.where(row == k, picked, out)
    return out


def sigmoid(v):
    return 0.5 * jnp.tanh(0.5 * v) + 0.5


def gather_tables(j, raw, tabs_ref, bcp_ref, conv, vocab):
    wide_ref, bc_ref, dt_ref = raw
    lanes = pl.ds(pl.multiple_of(j * LANES, LANES), LANES)
    head0 = lax.broadcasted_iota(jnp.int32, (1, LANES), 1) < 64
    pair = lambda a, b: jnp.where(head0, a, b)
    tabs_ref[...] = jnp.zeros_like(tabs_ref)
    bcp_ref[...] = jnp.zeros_like(bcp_ref)
    for k in range(vocab):
        tabs_ref[X_ROW + k : X_ROW + k + 1, :] = wide_ref[2 * k : 2 * k + 1, lanes].astype(F32)
        tabs_ref[Z_ROW + k : Z_ROW + k + 1, :] = wide_ref[2 * k + 1 : 2 * k + 2, lanes].astype(F32)
        tabs_ref[DT_ROW + k : DT_ROW + k + 1, :] = pair(dt_ref[k, 2 * j], dt_ref[k, 2 * j + 1])
        for i in range(2):
            bcp_ref[k : k + 1, i * 128 : i * 128 + 128] = bc_ref[k, i : i + 1, :].astype(F32)
    for k in range(conv):
        tabs_ref[MISC_ROW + k : MISC_ROW + k + 1, :] = wide_ref[2 * vocab + k : 2 * vocab + k + 1, lanes].astype(F32)
        for i in range(2):
            bcp_ref[SYM + k : SYM + k + 1, i * 128 : i * 128 + 128] = bc_ref[
                vocab + k, i : i + 1, :
            ].astype(F32)
    at = MISC_ROW + 4
    tabs_ref[at : at + 1, :] = pair(dt_ref[vocab, 2 * j], dt_ref[vocab, 2 * j + 1])
    tabs_ref[at + 1 : at + 2, :] = pair(
        dt_ref[vocab + 1, 2 * j], dt_ref[vocab + 1, 2 * j + 1]
    )


def tables_kernel(scalars, basemap, *refs, conv, vocab):
    tabs_ref, bcp_ref, dt1_ref, perm_ref, w_ref, w2_out, rate_ref, wf, w2 = refs[3:]
    gather_tables(scalars[0], refs[:3], tabs_ref, bcp_ref, conv, vocab)
    row = lax.broadcasted_iota(jnp.int32, perm_ref.shape, 0)
    lane = lax.broadcasted_iota(jnp.int32, perm_ref.shape, 1)
    perm = jnp.zeros(perm_ref.shape, F32)
    for k in range(vocab):
        perm = jnp.where(jnp.logical_and(lane == k, row == basemap[k]), 1.0, perm)
    perm_ref[...] = perm
    wf[...] = jnp.zeros_like(wf)
    w2[...] = jnp.zeros_like(w2)
    for st in range(2):
        fetch = (lambda t: t) if st == 0 else (lambda t: permuted(t, basemap, vocab))
        xt = fetch(tabs_ref[X_ROW : X_ROW + SYM, :])
        zt = fetch(tabs_ref[Z_ROW : Z_ROW + SYM, :])
        dtt = fetch(tabs_ref[DT_ROW : DT_ROW + SYM, :])
        if st == 1:
            dt1_ref[...] = dtt
        bct = fetch(bcp_ref[0:SYM, :])
        base = st * WIDE
        mid = SYM * (conv - 1)
        wf[mid : mid + SYM, base + ZZ : base + ZZ + LANES] = zt
        for k in range(conv):
            cx = tabs_ref[MISC_ROW + k : MISC_ROW + k + 1, :]
            cbc = bcp_ref[SYM + k : SYM + k + 1, :]
            lo, hi = mid - SYM * k, mid + SYM * k
            wf[lo : lo + SYM, base + XF : base + XF + LANES] = xt * cx
            wf[hi : hi + SYM, base + XB : base + XB + LANES] = xt * cx
            wf[lo : lo + SYM, base + BCF : base + BCF + 256] = bct * cbc
            wf[hi : hi + SYM, base + BCB : base + BCB + 256] = bct * cbc
        dt = jnp.maximum(dtt, 0.0) + jnp.log1p(jnp.exp(-jnp.abs(dtt)))
        ld = -jnp.exp(tabs_ref[MISC_ROW + 4 : MISC_ROW + 5, :]) * dt
        for k, piece in enumerate(thirds(ld)):
            w2[SYM * k : SYM * (k + 1), st * 128 : st * 128 + 128] = piece
            w2[32 + SYM * k : 32 + SYM * (k + 1), 256 + st * 128 : 384 + st * 128] = piece
            for h in range(2):
                at = 24 * (st * 2 + h) + SYM * k
                rate_ref[at : at + SYM, :] = jnp.broadcast_to(
                    piece[:, 64 * h : 64 * h + 1], piece.shape
                )
        for k, piece in enumerate(thirds(dt)):
            c = 512 + st * 128
            w2[64 + SYM * k : 64 + SYM * (k + 1), c : c + 128] = piece
    top, rest = halves(wf[...])
    w_ref[0:64, :] = top
    w_ref[64:128, :] = rest
    w2_out[...] = w2[...].astype(BF16)


def prepare(scalars, tok_refs, w_ref, w2_ref, r, conv):
    ns = len(tok_refs)
    length = ns * BLOCK
    mine = scalars[1]
    for k in range(ns):
        sym = lax.broadcasted_iota(jnp.int32, (SYM, BLOCK), 0).astype(F32)
        tok = jnp.broadcast_to(tok_refs[k][BLOCK : BLOCK + 1, 0:BLOCK].astype(F32), (SYM, BLOCK))
        at = jnp.bitwise_xor(mine, k) * BLOCK
        r.oh[:, pl.ds(pl.multiple_of(at, BLOCK), BLOCK)] = (sym == tok).astype(F32)
    oh = r.oh[...]
    lane = lax.broadcasted_iota(jnp.int32, (SYM, length), 1)
    up = (
        lax.broadcasted_iota(jnp.int32, (BLOCK, BLOCK), 0)
        <= lax.broadcasted_iota(jnp.int32, (BLOCK, BLOCK), 1)
    ).astype(BF16)
    r.rows[...] = jnp.zeros_like(r.rows)
    for d in range(1 - conv, conv):
        shifted = oh if d == 0 else pltpu.roll(oh, (length - d) % length, 1)
        inside = jnp.logical_and(lane + d >= 0, lane + d < length)
        r.rows[SYM * (d + conv - 1) : SYM * (d + conv), :] = jnp.where(inside, shifted, 0.0)
    r.rows[64:128, :] = r.rows[0:64, :]
    one = lax.broadcasted_iota(jnp.int32, (SYM, length), 0) < 3
    r.rows[152:160, :] = one.astype(F32)
    r.rows[184:192, :] = one.astype(F32)
    r.prow[...] = jnp.zeros_like(r.prow)
    oh_b = oh.astype(BF16)
    for b in range(ns):
        cols = slice(b * BLOCK, (b + 1) * BLOCK)
        inc = mm(oh_b[:, cols], up, NN)
        exc = inc - oh[:, cols]
        r.inc[:, cols] = inc
        r.exc[:, cols] = exc
        for k in range(3):
            r.rows[128 + SYM * k : 128 + SYM * (k + 1), cols] = inc
            r.rows[160 + SYM * k : 160 + SYM * (k + 1), cols] = exc
            r.rows[192 + SYM * k : 192 + SYM * (k + 1), cols] = oh[:, cols]
    r.sym[...] = r.rows[0:64, :].astype(BF16)
    turned = jnp.transpose(r.rows[...].astype(BF16))
    r.pre[...] = mm(turned[:, 0:128], w_ref[...], NN)
    w2 = w2_ref[...]
    r.pd[...] = mm(turned[:, 128:256], w2[:, 0:768], NN)
    r.count[...] = turned[:, 128:192]
    for st in range(2):
        for part, row0 in ((0, 0), (1, 32)):
            c = part * 256 + st * 128
            flat = mm(
                w2[row0 : row0 + 32, c : c + 128],
                r.rows[128 + row0 : 160 + row0, :].astype(BF16),
                TN,
            )
            for h in range(2):
                i = part * 4 + st * 2 + h
                row = flat[64 * h : 64 * h + 1, :]
                if part == 0:
                    row = -row
                for k, piece in enumerate(thirds(row)):
                    r.prow[SYM * i + k : SYM * i + k + 1, :] = piece


class Unit:
    def __init__(self, r, tabs_ref, st, b, nb):
        self.rows = rows = slice(b * BLOCK, (b + 1) * BLOCK)
        base = st * WIDE
        self.skip = tabs_ref[MISC_ROW + 5 : MISC_ROW + 6, :]
        self.dt = r.pd[rows, 512 + st * 128 : 512 + st * 128 + 128]
        self.p = r.pd[rows, st * 128 : st * 128 + 128]
        self.q = r.pd[rows, 256 + st * 128 : 256 + st * 128 + 128]
        self.total = self.p[BLOCK - 1 : BLOCK, :]
        self.r, self.st, self.b, self.base = r, st, b, base
        lane = lax.broadcasted_iota(jnp.int32, (BLOCK, LANES), 1)
        self.head0 = lane < 64
        row = lax.broadcasted_iota(jnp.int32, (BLOCK, BLOCK), 0)
        self.low = row >= lane
        self.upp = row <= lane

    def pre(self, col, width):
        return self.r.pre[self.rows, self.base + col : self.base + col + width]

    def act(self, col, width):
        v = self.pre(col, width)
        s = sigmoid(v)
        at = self.base + col
        self.r.slope[self.rows, at : at + width] = s * (1.0 + v * (1.0 - s))
        return v * s

    def slope(self, col, width):
        return self.r.slope[self.rows, self.base + col : self.base + col + width]

    def by_head(self, v):
        zero = jnp.zeros_like(v)
        return jnp.where(self.head0, v, zero), jnp.where(self.head0, zero, v)

    def decay(self, h):
        r, st = self.r, self.st
        i = st * 2 + h
        rate = r.rate[24 * i : 24 * i + 24, :]
        ends = r.prow[SYM * i : SYM * (i + 1), self.rows]
        starts = r.prow[SYM * (4 + i) : SYM * (5 + i), self.rows]
        zero = jnp.zeros((32, LANES), F32)
        below = jnp.concatenate([rate, ends, zero], 0)
        above = jnp.concatenate([zero, -rate, starts], 0)
        gap = mm(r.count[self.rows, :], jnp.concatenate([below, above], 1).astype(BF16), NN)
        return jnp.exp(jnp.where(self.low, gap[:, 0:LANES], gap[:, LANES : 2 * LANES]))


def state_pass_fwd(r, tabs_ref, nb, units):
    for st in range(2):
        for b in range(nb):
            u = units[st][b]
            xf, xb = u.act(XF, 128), u.act(XB, 128)
            bcf, bcb = u.act(BCF, 256), u.act(BCB, 256)
            r.x[u.rows, st * 256 : st * 256 + 128] = xf
            r.x[u.rows, st * 256 + 128 : st * 256 + 256] = xb
            r.bc[u.rows, st * 512 : st * 512 + 256] = bcf
            r.bc[u.rows, st * 512 + 256 : st * 512 + 512] = bcb
            wf = jnp.exp(u.total - u.p) * (u.dt * xf)
            wb = jnp.exp(u.q) * (u.dt * xb)
            if b < nb - 1:
                r.s[st * 2, b + 1] = mm_fine(bcf[:, 0:128], wf, TN, 2)
            if b > 0:
                r.s[st * 2 + 1, b - 1] = mm_fine(bcb[:, 0:128], wb, TN, 2)
        for b in range(2, nb):
            r.s[st * 2, b] += jnp.exp(units[st][b - 1].total) * r.s[st * 2, b - 1]
        for b in range(nb - 3, -1, -1):
            r.s[st * 2 + 1, b] += jnp.exp(units[st][b + 1].total) * r.s[st * 2 + 1, b + 1]


def together(bodies):
    bodies = list(bodies)
    while bodies:
        bodies = [b for b in bodies if next(b, True) is None]


class Names:
    pass


def named(refs, names):
    r = Names()
    for name, ref in zip(names, refs):
        setattr(r, name, ref)
    return r


KEPT = ("inc", "exc", "oh", "sym", "slope", "z", "pd", "x", "bc", "s", "dec", "wts", "ys")


def kept_shapes(length):
    nb = length // BLOCK
    return [
        ((SYM, length), F32),
        ((SYM, length), F32),
        ((SYM, length), F32),
        ((64, length), BF16),
        ((length, 2 * WIDE), F32),
        ((length, 256), F32),
        ((length, 768), F32),
        ((length, 512), F32),
        ((length, 1024), F32),
        ((4, nb, LANES, LANES), F32),
        ((4 * nb, BLOCK, BLOCK), F32),
        ((8 * nb, BLOCK, BLOCK), BF16),
        ((length, 1024), F32),
    ]


def forward_kernel(scalars, *refs, ns, conv):
    tok_refs, (w_ref, w2_ref, rate_ref, tabs_ref, out_ref) = refs[:ns], refs[ns : ns + 5]
    r = named(refs[ns + 5 :], KEPT + ("rows", "prow", "count", "pre"))
    r.rate = rate_ref
    prepare(scalars, tok_refs, w_ref, w2_ref, r, conv)
    units = [[Unit(r, tabs_ref, st, b, ns) for b in range(ns)] for st in range(2)]
    state_pass_fwd(r, tabs_ref, ns, units)
    gated = {}

    def body(st, b):
        u = units[st][b]
        x = [r.x[u.rows, st * 256 + w * 128 : st * 256 + w * 128 + 128] for w in range(2)]
        decays = (u.decay(0), u.decay(1))
        yield
        masks, lefts, cms = (u.low, u.upp), [], []
        for w in range(2):
            c = st * 512 + w * 256
            bm, cm = r.bc[u.rows, c : c + 128], r.bc[u.rows, c + 128 : c + 256]
            lefts.append(mm_fine(cm, bm, NT, 3))
            cms.append(cm)
        yield
        y = u.skip * (x[0] + x[1])
        for w in range(2):
            if (w == 0 and b > 0) or (w == 1 and b < ns - 1):
                enter = jnp.exp(u.p) if w == 0 else jnp.exp(u.total - u.q)
                carried = enter * mm_fine(cms[w], r.s[st * 2 + w, b], NN, 2)
                r.ys[u.rows, st * 512 + w * 256 + 128 : st * 512 + w * 256 + 256] = carried
                y = y + carried
        yield
        for h in range(2):
            r.dec[(st * ns + b) * 2 + h] = decays[h]
        for w in range(2):
            g = jnp.where(masks[w], lefts[w], 0.0)
            lefts[w] = [(g * d).astype(BF16) for d in decays]
            for h in range(2):
                r.wts[((st * ns + b) * 2 + w) * 2 + h] = lefts[w][h]
        yield
        for w in range(2):
            right = u.by_head((u.dt * x[w]).astype(BF16))
            inner = mm(jnp.concatenate(lefts[w], 1), jnp.concatenate(right, 0), NN)
            r.ys[u.rows, st * 512 + w * 256 : st * 512 + w * 256 + 128] = inner
            y = y + inner
        z = u.act(ZZ, 128)
        r.z[u.rows, st * 128 : st * 128 + 128] = z
        gated[st, b] = y * z

    for b0 in range(0, ns, GROUP):
        together(body(st, b) for b in range(b0, min(b0 + GROUP, ns)) for st in range(2))
        for b in range(b0, min(b0 + GROUP, ns)):
            out_ref[:, units[0][b].rows] = jnp.transpose(gated[0, b] + gated[1, b]).astype(BF16)


def backward_kernel(scalars, *refs, ns, nq, conv, vocab):
    tabs_ref, bcp_ref, dt1_ref, perm_ref = refs[:4]
    cot_refs, weight_ref = refs[4 : 4 + nq], refs[4 + nq]
    kept = refs[5 + nq : 5 + nq + len(KEPT)]
    out_ref, *work = refs[5 + nq + len(KEPT) :]
    r = named(list(kept) + work, KEPT + ("ds", "dg", "dpre"))
    cols = cot_refs[0].shape[2]
    cot = jnp.concatenate([a[...].reshape(ns * BLOCK, cols) for a in cot_refs], 1)
    weight = []
    for k in range(nq):
        at = pl.multiple_of(scalars[QUARTERS + k] * cols, LANES)
        rows = pl.ds(pl.multiple_of(scalars[0] * LANES, LANES), LANES)
        weight.append(weight_ref[rows, pl.ds(at, cols)])
    d_gated = mm(cot, jnp.concatenate(weight, 1), NT).astype(BF16).astype(F32)
    mine = scalars[1]
    for k in range(ns):
        at = jnp.bitwise_xor(mine, k)
        r.dg[pl.ds(pl.multiple_of(at * BLOCK, BLOCK), BLOCK), :] = d_gated[
            k * BLOCK : (k + 1) * BLOCK
        ]
    units = [[Unit(r, tabs_ref, st, b, ns) for b in range(ns)] for st in range(2)]

    def spread(st):
        backs, aheads = {}, {}
        for b in range(ns):
            u = units[st][b]
            dy = r.dg[u.rows, :] * r.z[u.rows, st * 128 : st * 128 + 128]
            cf = r.bc[u.rows, st * 512 + 128 : st * 512 + 256]
            cb = r.bc[u.rows, st * 512 + 384 : st * 512 + 512]
            if b > 0:
                backs[b - 1] = mm_fine(cf, jnp.exp(u.p) * dy, TN, 2)
            if b < ns - 1:
                aheads[b + 1] = mm_fine(cb, jnp.exp(u.total - u.q) * dy, TN, 2)
        yield
        for b in range(ns - 2, -1, -1):
            if b < ns - 2:
                backs[b] = backs[b] + jnp.exp(units[st][b + 1].total) * backs[b + 1]
            r.ds[st * 2, b] = backs[b]
        for b in range(1, ns):
            if b > 1:
                aheads[b] = aheads[b] + jnp.exp(units[st][b - 1].total) * aheads[b - 1]
            r.ds[st * 2 + 1, b] = aheads[b]

    d_steps = [jnp.zeros((SYM, LANES), F32)] * 2
    d_decays = [jnp.zeros((SYM, LANES), F32)] * 2
    d_tab = 0.0

    def body(st, b):
        u = units[st][b]
        base = st * WIDE
        x = [r.x[u.rows, st * 256 + w * 128 : st * 256 + w * 128 + 128] for w in range(2)]
        dgv = r.dg[u.rows, :]
        dy = dgv * r.z[u.rows, st * 128 : st * 128 + 128]
        dyr = dy.astype(BF16)
        dyw = dyr.astype(F32)
        dy0, dy1 = u.by_head(dyr)
        decays = [r.dec[(st * ns + b) * 2 + h] for h in range(2)]
        inputs = [u.dt * v for v in x]
        ur = [v.astype(BF16) for v in inputs]
        uw = [v.astype(F32) for v in ur]
        uh = [u.by_head(v) for v in ur]
        d_pair = mm(dyr, jnp.concatenate([uh[0][0], uh[0][1], uh[1][0], uh[1][1]], 0), NT)
        yield
        masks = (u.low, u.upp)
        ends = (jnp.exp(u.total - u.p), jnp.exp(u.q))
        enters = (jnp.exp(u.p), jnp.exp(u.total - u.q))
        weights, bms, cms = [], [], []
        for w in range(2):
            c = st * 512 + w * 256
            bm, cm = r.bc[u.rows, c : c + 128], r.bc[u.rows, c + 128 : c + 256]
            weights.append([r.wts[((st * ns + b) * 2 + w) * 2 + h] for h in range(2)])
            bms.append(bm)
            cms.append(cm)
        du_both = mm(
            jnp.concatenate(
                [
                    jnp.concatenate([weights[0][0], weights[1][0]], 1),
                    jnp.concatenate([weights[0][1], weights[1][1]], 1),
                ],
                0,
            ),
            jnp.concatenate([dy0, dy1], 0),
            TN,
        )
        yield
        y = u.skip * (x[0] + x[1])
        mixes, step_part, flat = [], 0.0, 0.0
        for w in range(2):
            yield
            c = st * 512 + w * 256
            inner = r.ys[u.rows, c : c + 128]
            du_in = du_both[w * BLOCK : (w + 1) * BLOCK]
            has_enter = (w == 0 and b > 0) or (w == 1 and b < ns - 1)
            has_leave = (w == 0 and b < ns - 1) or (w == 1 and b > 0)
            y = y + inner
            row = dyw * inner - uw[w] * du_in
            du = du_in
            d_g = jnp.where(
                masks[w],
                d_pair[:, w * 256 : w * 256 + 128] * decays[0]
                + d_pair[:, w * 256 + 128 : w * 256 + 256] * decays[1],
                0.0,
            ).astype(BF16)
            d_c = mm(d_g, bms[w].astype(BF16), NN)
            d_b = mm(d_g, cms[w].astype(BF16), TN)
            enter_part = gain_part = None
            if has_enter:
                state = r.s[st * 2 + w, b]
                carried = r.ys[u.rows, c + 128 : c + 256]
                y = y + carried
                enter_part = dy * carried
                d_c = d_c + mm((enters[w] * dy).astype(BF16), state.astype(BF16), NT)
            if has_leave:
                d_state = r.ds[st * 2 + w, b]
                d_gain = mm_fine(bms[w], d_state, NN, 2)
                du = du + ends[w] * d_gain
                gain = ends[w] * inputs[w]
                gain_part = gain * d_gain
                d_b = d_b + mm(gain.astype(BF16), d_state.astype(BF16), NT)
            if has_enter and has_leave:
                flat = flat + jnp.exp(u.total) * jnp.sum(state * d_state, 0, keepdims=True)
            if w == 1:
                row = -row
            if enter_part is not None:
                row = row + enter_part if w == 0 else row - enter_part
            if gain_part is not None:
                row = row - gain_part if w == 0 else row + gain_part
            if w == 0 and gain_part is not None:
                flat = flat + jnp.sum(gain_part, 0, keepdims=True)
            if w == 1 and enter_part is not None:
                flat = flat + jnp.sum(enter_part, 0, keepdims=True)
            mixes.append(row)
            step_part = step_part + du * x[w]
            dx = du * u.dt + dy * u.skip
            col = (XF, XB)[w]
            grad = dx * u.slope(col, 128)
            r.dpre[u.rows, base + col : base + col + 128] = grad.astype(BF16)
            col = (BCF, BCB)[w]
            for i, grad in enumerate((d_b, d_c)):
                at = base + col + 128 * i
                r.dpre[u.rows, at : at + 128] = (grad * u.slope(col + 128 * i, 128)).astype(BF16)
        yield
        d_z = dgv * y * u.slope(ZZ, 128)
        r.dpre[u.rows, base + ZZ : base + ZZ + 128] = d_z.astype(BF16)
        inc = r.inc[:, u.rows]
        exc = r.exc[:, u.rows]
        inc_b, exc_b, oh_b = inc.astype(BF16), exc.astype(BF16), r.oh[:, u.rows].astype(BF16)
        right = list(halves(mixes[0])) + list(halves(mixes[1]))
        decay_part = mm(
            jnp.concatenate([inc_b, inc_b, exc_b, exc_b], 1), jnp.concatenate(right, 0), NN
        )
        decay_part = decay_part + inc[:, BLOCK - 1 : BLOCK] * flat
        step_sum = mm(
            jnp.concatenate([oh_b, oh_b], 1), jnp.concatenate(halves(step_part), 0), NN
        )
        d_steps[st] = d_steps[st] + step_sum
        d_decays[st] = d_decays[st] + decay_part

    for b0 in range(0, ns, GROUP_BACK):
        last = min(b0 + GROUP_BACK, ns)
        bodies = [body(st, b) for b in range(b0, last) for st in range(2)]
        together([spread(0), spread(1)] * (b0 == 0) + bodies)
        span = slice(b0 * BLOCK, last * BLOCK)
        d_tab = d_tab + mm(r.sym[:, span], r.dpre[span, :], NN)
    mid = SYM * (conv - 1)
    result = None
    for st in range(2):
        base = st * WIDE
        d_x = jnp.zeros((SYM, 128), F32)
        d_bc = jnp.zeros((SYM, 256), F32)
        for k in range(conv):
            cx = tabs_ref[MISC_ROW + k : MISC_ROW + k + 1, :]
            cbc = bcp_ref[SYM + k : SYM + k + 1, :]
            lo, hi = mid - SYM * k, mid + SYM * k
            d_x = d_x + cx * (
                d_tab[lo : lo + SYM, base + XF : base + XF + 128]
                + d_tab[hi : hi + SYM, base + XB : base + XB + 128]
            )
            d_bc = d_bc + cbc * (
                d_tab[lo : lo + SYM, base + BCF : base + BCF + 256]
                + d_tab[hi : hi + SYM, base + BCB : base + BCB + 256]
            )
        d_zt = d_tab[mid : mid + SYM, base + ZZ : base + ZZ + 128]
        dtt = dt1_ref[...] if st else tabs_ref[DT_ROW : DT_ROW + SYM, :]
        rate = -jnp.exp(tabs_ref[MISC_ROW + 4 : MISC_ROW + 5, :])
        d_dt = (d_steps[st] + rate * d_decays[st]) * sigmoid(dtt)
        wide = jnp.concatenate([d_x, d_zt, d_dt, d_bc], 1)
        if st == 0:
            result = wide
        else:
            for k in range(vocab):
                result = result + perm_ref[:, k : k + 1] * wide[k : k + 1]
    out_ref[...] = result


SMEM = pl.BlockSpec(memory_space=pltpu.SMEM)
VMEM = pl.BlockSpec(memory_space=pltpu.VMEM)
HBM = pl.BlockSpec(memory_space=pl.ANY)


def params(mib):
    return pltpu.CompilerParams(vmem_limit_bytes=mib * 1024 * 1024)


def call_tables(scalars, raw):
    basemap, xz_table, bc_table, conv_x, conv_bc, dt_table, a_log, skip_gain = raw
    conv, vocab = conv_x.shape[0], xz_table.shape[0]
    outs = [
        ((TAB_ROWS, LANES), F32),
        ((2 * SYM, 256), F32),
        ((SYM, LANES), F32),
        ((SYM, LANES), F32),
        ((128, 2 * WIDE), BF16),
        ((128, 768), BF16),
        ((96, LANES), F32),
    ]
    return pl.pallas_call(
        functools.partial(tables_kernel, conv=conv, vocab=vocab),
        out_shape=[jax.ShapeDtypeStruct(*a) for a in outs],
        in_specs=[SMEM, SMEM, VMEM, VMEM, SMEM],
        out_specs=[VMEM] * len(outs),
        scratch_shapes=[pltpu.VMEM((64, 2 * WIDE), F32), pltpu.VMEM((128, 768), F32)],
        compiler_params=params(8),
        cost_estimate=pl.CostEstimate(flops=2 * 10**9, transcendentals=0, bytes_accessed=10**6),
        name="tables",
    )(
        scalars,
        basemap,
        jnp.concatenate([xz_table.reshape(2 * vocab, -1), conv_x], 0),
        jnp.concatenate([bc_table, conv_bc], 0),
        jnp.concatenate([dt_table, a_log[None], skip_gain[None]], 0),
    )


def call_forward(scalars, pays, w, w2, rate, tabs, conv):
    ns = len(pays)
    length = ns * BLOCK
    outs = [((LANES, length), BF16)] + kept_shapes(length)
    return pl.pallas_call(
        functools.partial(forward_kernel, ns=ns, conv=conv),
        out_shape=[jax.ShapeDtypeStruct(*a) for a in outs],
        in_specs=[SMEM] + [VMEM] * (ns + 4),
        out_specs=[VMEM] * len(outs),
        scratch_shapes=[
            pltpu.VMEM((256, length), F32),
            pltpu.VMEM((64, length), F32),
            pltpu.VMEM((length, 64), BF16),
            pltpu.VMEM((length, 2 * WIDE), F32),
        ],
        compiler_params=params(12),
        cost_estimate=pl.CostEstimate(
            flops=5 * 10**9, transcendentals=0, bytes_accessed=8 * LANES * length
        ),
        name="mix_forward",
    )(scalars, *pays, w, w2, rate, tabs)


def call_backward(scalars, tables, cots, out_weight, kept, conv, vocab):
    length = kept[0].shape[1]
    ns = length // BLOCK
    return pl.pallas_call(
        functools.partial(backward_kernel, ns=ns, nq=len(cots), conv=conv, vocab=vocab),
        out_shape=jax.ShapeDtypeStruct((SYM, 640), F32),
        in_specs=[SMEM] + [VMEM] * (len(tables) + len(cots) + 1 + len(kept)),
        out_specs=VMEM,
        scratch_shapes=[
            pltpu.VMEM((4, ns, LANES, LANES), F32),
            pltpu.VMEM((length, LANES), F32),
            pltpu.VMEM((length, 2 * WIDE), BF16),
        ],
        compiler_params=params(10),
        cost_estimate=pl.CostEstimate(
            flops=6 * 10**9, transcendentals=0, bytes_accessed=8 * LANES * length
        ),
        name="mix_backward",
    )(scalars, *tables, *cots, out_weight, *kept)


QUARTERS = 3


def out_kernel(scalars, *refs, ns, nh, nc):
    slices, weight_ref, outs = refs[: ns * nc], refs[ns * nc], refs[ns * nc + 1 :]
    here = pl.ds(pl.multiple_of(scalars[1] * BLOCK, BLOCK), BLOCK)
    places = QUARTERS + nh * nc
    cols = outs[0].shape[1]
    left = jnp.concatenate([a[:, here] for a in slices], 0)
    for k in range(nh):
        at = pl.ds(pl.multiple_of(scalars[QUARTERS + k * nc] * cols, LANES), cols)
        right = []
        for i in range(ns * nc):
            rows = pl.ds(pl.multiple_of(scalars[places + i] * LANES, LANES), LANES)
            right.append(weight_ref[rows, at])
        outs[k][...] = mm(left, jnp.concatenate(right, 0), TN)


def call_out(scalars, slices, out_weight, ns, nh, nc):
    cols = out_weight.shape[1] // (nh * nc)
    return pl.pallas_call(
        functools.partial(out_kernel, ns=ns, nh=nh, nc=nc),
        out_shape=[jax.ShapeDtypeStruct((BLOCK, cols), F32)] * nh,
        in_specs=[SMEM] + [VMEM] * (len(slices) + 1),
        out_specs=[VMEM] * nh,
        compiler_params=params(8),
        name="layer_out",
    )(scalars, *slices, out_weight)


def weight_kernel(scalars, *refs, ns, nh, nc):
    slices, cots = refs[: ns * nc], refs[ns * nc : ns * nc + nh * nc]
    out_ref, mark_ref, left, buf, sems = refs[ns * nc + nh * nc :]
    mine = scalars[1]
    places = QUARTERS + nh * nc
    cols = cots[0].shape[2]
    mark_ref[...] = jnp.zeros_like(mark_ref)
    for n in range(ns * nc):
        for k in range(ns):
            at = jnp.bitwise_xor(mine, k)
            left[n * LANES : (n + 1) * LANES, k * BLOCK : (k + 1) * BLOCK] = slices[n][
                :, pl.ds(pl.multiple_of(at * BLOCK, BLOCK), BLOCK)
            ]
    copies = []
    for q in range(nh * nc):
        total = mm(left[...], cots[q][...].reshape(ns * BLOCK, cols), NN)
        for n in range(ns * nc):
            at = pl.multiple_of(scalars[places + n] * LANES, LANES)
            buf[q, pl.ds(at, LANES), :] = total[n * LANES : (n + 1) * LANES]
        at = pl.multiple_of(scalars[QUARTERS + q] * cols, LANES)
        copy = pltpu.make_async_copy(buf.at[q], out_ref.at[:, pl.ds(at, cols)], sems.at[q])
        copy.start()
        copies.append(copy)
    for copy in copies:
        copy.wait()


def call_weight(scalars, slices, cots, width, ns, nh, nc):
    length = slices[0].shape[1]
    rows = ns * nc * LANES
    return pl.pallas_call(
        functools.partial(weight_kernel, ns=ns, nh=nh, nc=nc),
        out_shape=[
            jax.ShapeDtypeStruct((rows, width), F32),
            jax.ShapeDtypeStruct((SYM, LANES), F32),
        ],
        in_specs=[SMEM] + [VMEM] * (len(slices) + len(cots)),
        out_specs=[HBM, VMEM],
        scratch_shapes=[
            pltpu.VMEM((rows, length), BF16),
            pltpu.VMEM((nh * nc, rows, width // (nh * nc)), F32),
            pltpu.SemaphoreType.DMA((nh * nc,)),
        ],
        compiler_params=params(12),
        cost_estimate=pl.CostEstimate(
            flops=2 * rows * width * length, transcendentals=0, bytes_accessed=6 * rows * width
        ),
        name="weight_grad",
    )(scalars, *slices, *cots)


def final_kernel(scalars, *refs, ns, nh, vocab, places):
    packs, parts = refs[:ns], refs[ns : ns + nh]
    out_ref, xz_ref, bc_ref, dt_ref = refs[ns + nh + 1 :]
    total = parts[0][...]
    for a in parts[1:]:
        total = total + a[...]
    out_ref[...] = total.astype(BF16)
    d_bc = packs[0][:, 768:1024]
    for a in packs[1:]:
        d_bc = d_bc + a[:, 768:1024]
    for i in range(2):
        for k in range(vocab):
            bc_ref[k, i : i + 1, :] = d_bc[k : k + 1, i * 128 : i * 128 + 128]
    lane = lax.broadcasted_iota(jnp.int32, (SYM, dt_ref.shape[1]), 1)
    d_dt = jnp.zeros((SYM, dt_ref.shape[1]), F32)
    for n in range(2 * ns):
        j = scalars[places + n]
        piece = packs[n % ns][:, n // ns * 384 : n // ns * 384 + 384]
        for i in range(2):
            for k in range(vocab):
                xz_ref[k, i : i + 1, pl.ds(pl.multiple_of(j * LANES, LANES), LANES)] = piece[
                    k : k + 1, i * 128 : i * 128 + 128
                ]
            row = jnp.sum(piece[:, 256 + 64 * i : 320 + 64 * i], 1, keepdims=True)
            d_dt = jnp.where(lane == 2 * j + i, row, d_dt)
    dt_ref[...] = d_dt[:vocab]


def call_final(scalars, packs, parts, mark, raw, places):
    shapes = [raw[1].shape, raw[2].shape, raw[5].shape]
    arrays = list(packs) + list(parts)
    return pl.pallas_call(
        functools.partial(
            final_kernel, ns=len(packs), nh=len(parts), vocab=raw[1].shape[0], places=places
        ),
        out_shape=[jax.ShapeDtypeStruct(parts[0].shape, BF16)]
        + [jax.ShapeDtypeStruct(a, F32) for a in shapes],
        in_specs=[SMEM] + [VMEM] * (len(arrays) + 1),
        out_specs=[VMEM] * (len(shapes) + 1),
        compiler_params=params(8),
        name="place_grads",
    )(scalars, *arrays, mark)


def around(x, axis):
    n = lax.axis_size(axis)
    return [x] + [lax.ppermute(x, axis, [(i, i ^ k) for i in range(n)]) for k in range(1, n)]


def across(x, hops, nh, nc):
    pairs = [
        (a * nc + b, (a + hops[0]) % nh * nc + (b + hops[1]) % nc)
        for a in range(nh)
        for b in range(nc)
    ]
    return lax.ppermute(x, ("head", "sub"), pairs)


def by_channel(
    token_ids, basemap, xz_table, bc_table, dt_table, conv_x, conv_bc, a_log, skip_gain, out_weight, cotangent
):
    ns, nc, nh = lax.axis_size("seq"), lax.axis_size("sub"), lax.axis_size("head")
    s, c, h = lax.axis_index("seq"), lax.axis_index("sub"), lax.axis_index("head")
    width = out_weight.shape[1]
    cols = width // (nh * nc)
    raw = (basemap, xz_table, bc_table, conv_x, conv_bc, dt_table, a_log, skip_gain)
    symbols = jnp.pad(token_ids.astype(BF16).reshape(1, BLOCK), ((0, 15), (0, cols - BLOCK)))
    pays = around(jnp.concatenate([cotangent, symbols], 0), "seq")
    slot = jnp.arange(nh * nc, dtype=jnp.int32)
    quarters = (h - slot // nc) % nh * nc + (c - slot % nc) % nc
    slot = jnp.arange(ns * nc, dtype=jnp.int32)
    places = (c - slot // ns) % nc * ns + jnp.bitwise_xor(s, slot % ns)
    scalars = jnp.concatenate([jnp.stack([c * ns + s, s, c]), quarters, places]).astype(jnp.int32)
    stacked = jnp.stack([a[:BLOCK] for a in pays], 0)
    heads = [stacked] + [across(stacked, (k, 0), nh, nc) for k in range(1, nh)]
    side = across(stacked, (0, 1), nh, nc)
    conv, vocab = conv_x.shape[0], xz_table.shape[0]
    *tables, w, w2, rate = call_tables(scalars, raw)
    gated, *kept = call_forward(scalars, pays, w, w2, rate, tables[0], conv)
    heads, _ = lax.optimization_barrier((heads, gated))
    cots = [heads[0], side]
    for a in heads[1:]:
        cots += [a, across(a, (0, 1), nh, nc)]
    hop = lambda x, k: lax.ppermute(x, "seq", [(i, i ^ k) for i in range(ns)])
    direct = {k: hop(gated, k) for k in (1 << n for n in range(ns.bit_length() - 1))}
    grads = call_backward(scalars, tables, cots, out_weight, kept, conv, vocab)
    direct, _ = lax.optimization_barrier((direct, grads))
    held = {0: gated, **direct}
    for k in range(3, ns):
        if k not in held:
            held[k] = hop(held[k & (k - 1)], k & -k)
    slices = [held[k] for k in range(ns)]
    slices = slices + [across(a, (0, 1), nh, nc) for a in slices]
    shared = grads[:, 384:]
    beside = across(grads, (0, 1), nh, nc)
    for a in range(1, nh):
        for b in range(nc):
            shared = shared + across(grads[:, 384:], (a, b), nh, nc)
    packed = jnp.concatenate([grads[:, :384], beside[:, :384], shared + beside[:, 384:]], 1)
    packs = around(packed, "seq")
    parts = call_out(scalars, slices, out_weight, ns, nh, nc)
    parts = [parts[0]] + [across(parts[k], (nh - k, 0), nh, nc) for k in range(1, nh)]
    d_out_weight, mark = call_weight(scalars, slices, cots, width, ns, nh, nc)
    layer_out, d_xz, d_bc, d_dt = call_final(
        scalars, packs, parts, mark, raw, QUARTERS + nh * nc
    )
    return (layer_out, d_out_weight, d_xz, d_bc, d_dt)


PRECISE = lax.Precision.HIGHEST


def carried_in(part, axis, combine, identity):
    place = lax.axis_index(axis)
    gathered = jax.tree.map(lambda a: lax.all_gather(a, axis), part)
    state = jax.tree.map(lambda a, e: jnp.zeros_like(a) + jnp.asarray(e, a.dtype), part, identity)

    def one(hop, state):
        return combine(
            state, jax.tree.map(lambda a: lax.dynamic_index_in_dim(a, hop, 0, False), gathered)
        )

    return lax.fori_loop(0, place, one, state)


def carried_in_2(array, axis, combine, identity):
    length, mine = (lax.axis_size(axis), lax.axis_index(axis))
    everything = jax.tree.map(
        lambda part, kind: lax.all_gather(part.astype(kind), axis),
        array,
        jax.tree.map(lambda a: jnp.bfloat16 if a.dtype == jnp.float32 else a.dtype, array),
    )
    start = jax.tree.map(
        lambda part, zero: jnp.broadcast_to(jnp.asarray(zero, part.dtype), part.shape),
        array,
        identity,
    )

    def hop(k, before):
        at = length - 1 - k
        reached = at > mine
        new = combine(
            before, jax.tree.map(lambda part, own: part[at].astype(own.dtype), everything, array)
        )
        return jax.tree.map(lambda a, b: jnp.where(reached, a, b), new, before)

    return lax.fori_loop(0, length, hop, start)


def with_halo(block, sides, width):
    for axis, dim in sides:
        count = lax.axis_size(axis)
        forward = [(i, i + 1) for i in range(count - 1)]
        backward = [(target, source) for source, target in forward]
        low = lax.ppermute(
            lax.slice_in_dim(block, block.shape[dim] - width, None, axis=dim), axis, forward
        )
        high = lax.ppermute(lax.slice_in_dim(block, 0, width, axis=dim), axis, backward)
        block = jnp.concatenate([low, block, high], axis=dim)
    return block


def block_step(carry_state, pieces):
    scaled_x, logdec, b_mat, c_mat = pieces
    block_len = scaled_x.shape[0]
    running = jnp.cumsum(logdec, axis=0)
    by_head = running.T
    causal_mask = (jnp.arange(block_len)[:, None] >= jnp.arange(block_len)[None, :])[None, :, :]
    gap_matrix = by_head[:, :, None] - by_head[:, None, :]
    decay_mat = jnp.where(causal_mask, jnp.exp(jnp.where(causal_mask, gap_matrix, 0.0)), 0.0)
    scores = jnp.einsum("tn,sn->ts", c_mat, b_mat, precision=PRECISE)
    within = jnp.einsum("hts,shp->thp", scores[None, :, :] * decay_mat, scaled_x, precision=PRECISE)
    carried = jnp.exp(running)[:, :, None] * jnp.einsum(
        "tn,hpn->thp", c_mat, carry_state, precision=PRECISE
    )
    to_end = jnp.exp(running[-1][None, :] - running)
    gained = jnp.einsum("shp,sn->hpn", to_end[:, :, None] * scaled_x, b_mat, precision=PRECISE)
    return (jnp.exp(running[-1])[:, None, None] * carry_state + gained, within + carried)


def state_pass(inputs, start_state, block_len):
    scaled_x, logdec, b_mat, c_mat = inputs
    block_count = scaled_x.shape[0] // block_len
    pieces = (
        scaled_x.reshape((block_count, block_len) + scaled_x.shape[1:]),
        logdec.reshape(block_count, block_len, -1),
        b_mat.reshape(block_count, block_len, -1),
        c_mat.reshape(block_count, block_len, -1),
    )
    end_state, outputs = lax.scan(jax.checkpoint(block_step), start_state, pieces)
    return (outputs.reshape(scaled_x.shape), end_state)


def final_state(inputs):
    scaled_x, logdec, b_mat, c_mat = inputs
    running = jnp.cumsum(logdec, axis=0)
    to_end = jnp.exp(running[-1][None, :] - running)
    gained = jnp.einsum("shp,sn->hpn", to_end[:, :, None] * scaled_x, b_mat, precision=PRECISE)
    return (jnp.exp(running[-1]), gained)


def lookup(symbols, table):
    vocab_size = table.shape[0]
    onehot = (symbols[:, None] == jnp.arange(vocab_size, dtype=jnp.int32)[None, :]).astype(
        jnp.float32
    )
    return jnp.dot(onehot, table, precision=PRECISE)


def conv_rows(extended, weight, row_count, forward):
    conv_width = weight.shape[0]
    rim_width = conv_width - 1
    summed = jnp.zeros((row_count, extended.shape[1]), jnp.float32)
    for offset in range(conv_width):
        if forward:
            first_row = rim_width - offset
        else:
            first_row = rim_width + offset
        summed = summed + weight[offset][None, :] * extended[first_row : first_row + row_count]
    return summed


def open_inputs(ext_sym, inside_mask, tables, frozen):
    xz_tab, bc_tab, dt_tab = tables
    conv_inner, conv_shared, log_rates, skip_vals = frozen
    rim_width = conv_inner.shape[0] - 1
    row_count = ext_sym.shape[0] - 2 * rim_width
    vocab_size = xz_tab.shape[0]
    inner_dim = xz_tab.shape[2]
    head_count = dt_tab.shape[1]
    state_dim = bc_tab.shape[2]
    looked = lookup(ext_sym, xz_tab.reshape(vocab_size, 2 * inner_dim)) * inside_mask[:, None]
    pre_x = looked[:, :inner_dim]
    gate_act = jax.nn.silu(looked[rim_width : rim_width + row_count, inner_dim:])
    pre_bc = lookup(ext_sym, bc_tab.reshape(vocab_size, 2 * state_dim)) * inside_mask[:, None]
    dt_step = jax.nn.softplus(lookup(ext_sym[rim_width : rim_width + row_count], dt_tab))
    logdec = -jnp.exp(log_rates)[None, :] * dt_step
    flat_bc = conv_shared.reshape(conv_inner.shape[0], 2 * state_dim)

    def one_way(forward):
        x_conv = jax.nn.silu(conv_rows(pre_x, conv_inner, row_count, forward)).reshape(
            row_count, head_count, -1
        )
        bc_conv = jax.nn.silu(conv_rows(pre_bc, flat_bc, row_count, forward))
        return (x_conv, bc_conv[:, :state_dim], bc_conv[:, state_dim:])

    x_fwd, b_fwd, c_fwd = one_way(True)
    x_back, b_back, c_back = one_way(False)
    ahead_in = (x_fwd * dt_step[:, :, None], logdec, b_fwd, c_fwd)
    behind_in = (
        jnp.flip(x_back * dt_step[:, :, None], 0),
        jnp.flip(logdec, 0),
        jnp.flip(b_back, 0),
        jnp.flip(c_back, 0),
    )
    skip_term = skip_vals[None, :, None] * (x_fwd + x_back)
    return (ahead_in, behind_in, skip_term, gate_act)


def combine(earlier, later):
    decay_early, state_early = earlier
    decay_late, state_late = later
    return (decay_early * decay_late, decay_late[:, None, None] * state_early + state_late)


def carries(ahead_pair, behind_pair):
    ahead_out = carried_in(
        (ahead_pair[0], ahead_pair[1]),
        "seq",
        combine,
        (jnp.ones_like(ahead_pair[0]), jnp.zeros_like(ahead_pair[1])),
    )
    behind_out = carried_in_2(
        (behind_pair[0], behind_pair[1]),
        "seq",
        combine,
        (jnp.ones_like(behind_pair[0]), jnp.zeros_like(behind_pair[1])),
    )
    return (ahead_out[1], behind_out[1])


def decay_weights(adjoint, start_state):
    return jnp.sum(adjoint * start_state, axis=(1, 2))


def shards(
    token_ids,
    basemap,
    xz_table,
    bc_table,
    dt_table,
    conv_x,
    conv_bc,
    a_log,
    skip_gain,
    out_weight,
    cotangent,
):
    row_count = token_ids.shape[0]
    rim_width = conv_x.shape[0] - 1
    ext_ids = with_halo(token_ids, (("seq", 0),), rim_width)
    first_row = lax.axis_index("seq") * row_count - rim_width
    where_global = first_row + jnp.arange(row_count + 2 * rim_width, dtype=jnp.int32)
    inside_mask = jnp.logical_and(
        where_global >= 0, where_global < row_count * lax.axis_size("seq")
    ).astype(jnp.float32)
    vocab_size = basemap.shape[0]
    matches = ext_ids[:, None] == jnp.arange(vocab_size, dtype=jnp.int32)[None, :]
    mapped = jnp.sum(jnp.where(matches, basemap[None, :], 0), axis=1)
    ext_sym = jnp.where(lax.axis_index("sub") == 1, mapped, ext_ids)
    tables = (xz_table.astype(jnp.float32), bc_table.astype(jnp.float32), dt_table)
    frozen = (conv_x.astype(jnp.float32), conv_bc.astype(jnp.float32), a_log, skip_gain)

    def summary(tabs_in):
        ahead_in, behind_in, skip_term, gate_act = open_inputs(
            ext_sym, inside_mask, tabs_in, frozen
        )
        decay_fwd, end_fwd = final_state(ahead_in)
        decay_back, end_back = final_state(behind_in)
        return (decay_fwd, end_fwd, decay_back, end_back)

    (decay_fwd, end_fwd, decay_back, end_back), pull_summary = jax.vjp(summary, tables)
    start_fwd, start_back = carries((decay_fwd, end_fwd), (decay_back, end_back))

    def finished(tabs_in, begin_fwd, begin_back):
        ahead_in, behind_in, skip_term, gate_act = open_inputs(
            ext_sym, inside_mask, tabs_in, frozen
        )
        out_fwd, unused_fwd = state_pass(ahead_in, begin_fwd, BLOCK)
        out_back, unused_back = state_pass(behind_in, begin_back, BLOCK)
        return (out_fwd + jnp.flip(out_back, 0) + skip_term).reshape(row_count, -1) * gate_act

    gated, pull_finished = jax.vjp(finished, tables, start_fwd, start_back)
    gated_bf = gated.astype(jnp.bfloat16)
    products = jnp.dot(gated_bf, out_weight, preferred_element_type=jnp.float32)
    layer_out = lax.psum_scatter(products, ("head", "sub"), scatter_dimension=1, tiled=True).astype(
        jnp.bfloat16
    )
    full_cot = lax.all_gather(cotangent, ("head", "sub"), axis=1, tiled=True)
    d_gated = jnp.einsum(
        "tc,kc->tk", full_cot, out_weight, preferred_element_type=jnp.float32
    ).astype(jnp.bfloat16)
    weight_part = jnp.einsum("tk,tc->kc", gated_bf, full_cot, preferred_element_type=jnp.float32)
    d_gated_wide = lax.optimization_barrier(d_gated).astype(jnp.float32)
    grads_first, direct_fwd, direct_back = pull_finished(d_gated_wide)
    adjoint_back, adjoint_fwd = carries((decay_back, direct_back), (decay_fwd, direct_fwd))
    grads_second = pull_summary(
        (
            decay_weights(adjoint_fwd, start_fwd),
            adjoint_fwd,
            decay_weights(adjoint_back, start_back),
            adjoint_back,
        )
    )[0]
    d_tables = jax.tree.map(lambda former, latter: former + latter, grads_first, grads_second)
    d_xz, d_bc, d_dt = d_tables
    d_bc = lax.psum(d_bc, ("seq", "head", "sub"))
    d_out_weight, d_xz, d_dt = lax.psum((weight_part, d_xz, d_dt), ("seq", "sub"))
    return (layer_out, d_out_weight, d_xz, d_bc, d_dt)


def solution(mesh):
    in_specs = (
        P(("grp", "seq")),
        P(),
        P(None, None, "head"),
        P(),
        P(None, "head"),
        P(None, "head"),
        P(),
        P("head"),
        P("head"),
        P("head", None),
        P(("grp", "seq"), ("head", "sub")),
    )
    out_specs = (
        P(("grp", "seq"), ("head", "sub")),
        P(("grp", "head"), None),
        P("grp", None, "head"),
        P("grp", None, None),
        P("grp", "head"),
    )
    def run(*args):
        ns, nc = mesh.shape["seq"], mesh.shape["sub"]
        rows, inner, heads = args[0].shape[0], args[2].shape[2], args[4].shape[1]
        by_lanes = (
            rows == BLOCK
            and nc == 2
            and ns > 1
            and ns & (ns - 1) == 0
            and inner == ns * nc * LANES
            and inner == heads * (LANES // 2)
            and args[3].shape[2] == LANES
            and args[5].shape[0] == 4
            and args[9].shape[1] == args[10].shape[1] * nc * mesh.shape["head"]
        )
        return (by_channel if by_lanes else shards)(*args)

    return jax.shard_map(run, mesh=mesh, in_specs=in_specs, out_specs=out_specs, check_vma=False)
```

```python
import functools

import jax
import jax.numpy as jnp
from jax import lax
from jax.experimental import pallas as pl
from jax.experimental.pallas import tpu as pltpu
from jax.sharding import PartitionSpec as P

BLOCK = 128
LANES = 128
SYM = 8
F32 = jnp.float32
BF16 = jnp.bfloat16
GROUP = 1
GROUP_BACK = 4
NN = (((1,), (0,)), ((), ()))
NT = (((1,), (1,)), ((), ()))
TN = (((0,), (0,)), ((), ()))
X_ROW, Z_ROW, DT_ROW, MISC_ROW, TAB_ROWS = 0, 8, 16, 24, 32
XF, XB, ZZ, BCF, BCB, WIDE = 0, 128, 256, 384, 640, 896


def mm(a, b, dims):
    return lax.dot_general(a, b, dims, preferred_element_type=F32)


def halves(a):
    top = a.astype(BF16)
    return top, (a - top.astype(F32)).astype(BF16)


def thirds(a):
    top = a.astype(BF16).astype(F32)
    rest = a - top
    mid = rest.astype(BF16).astype(F32)
    return top, mid, rest - mid


def mm_fine(a, b, dims, terms):
    ah, al = halves(a)
    bh, bl = halves(b)
    (ca,), (cb,) = dims[0]
    left, right = [ah], [bh]
    if terms >= 2:
        left.append(al)
        right.append(bh)
    if terms >= 3:
        left.append(ah)
        right.append(bl)
    return mm(jnp.concatenate(left, ca), jnp.concatenate(right, cb), dims)


def permuted(table, basemap, count):
    row = lax.broadcasted_iota(jnp.int32, table.shape, 0)
    out = jnp.zeros_like(table)
    for k in range(count):
        picked = jnp.zeros_like(table[0:1])
        for m in range(count):
            picked = jnp.where(basemap[k] == m, table[m : m + 1], picked)
        out = jnp.where(row == k, picked, out)
    return out


def sigmoid(v):
    return 0.5 * jnp.tanh(0.5 * v) + 0.5


def gather_tables(j, raw, tabs_ref, bcp_ref, conv, vocab):
    wide_ref, bc_ref, dt_ref = raw
    lanes = pl.ds(pl.multiple_of(j * LANES, LANES), LANES)
    head0 = lax.broadcasted_iota(jnp.int32, (1, LANES), 1) < 64
    pair = lambda a, b: jnp.where(head0, a, b)
    tabs_ref[...] = jnp.zeros_like(tabs_ref)
    bcp_ref[...] = jnp.zeros_like(bcp_ref)
    for k in range(vocab):
        tabs_ref[X_ROW + k : X_ROW + k + 1, :] = wide_ref[2 * k : 2 * k + 1, lanes].astype(F32)
        tabs_ref[Z_ROW + k : Z_ROW + k + 1, :] = wide_ref[2 * k + 1 : 2 * k + 2, lanes].astype(F32)
        tabs_ref[DT_ROW + k : DT_ROW + k + 1, :] = pair(dt_ref[k, 2 * j], dt_ref[k, 2 * j + 1])
        for i in range(2):
            bcp_ref[k : k + 1, i * 128 : i * 128 + 128] = bc_ref[k, i : i + 1, :].astype(F32)
    for k in range(conv):
        tabs_ref[MISC_ROW + k : MISC_ROW + k + 1, :] = wide_ref[2 * vocab + k : 2 * vocab + k + 1, lanes].astype(F32)
        for i in range(2):
            bcp_ref[SYM + k : SYM + k + 1, i * 128 : i * 128 + 128] = bc_ref[
                vocab + k, i : i + 1, :
            ].astype(F32)
    at = MISC_ROW + 4
    tabs_ref[at : at + 1, :] = pair(dt_ref[vocab, 2 * j], dt_ref[vocab, 2 * j + 1])
    tabs_ref[at + 1 : at + 2, :] = pair(
        dt_ref[vocab + 1, 2 * j], dt_ref[vocab + 1, 2 * j + 1]
    )


def tables_kernel(scalars, basemap, *refs, conv, vocab):
    tabs_ref, bcp_ref, dt1_ref, perm_ref, w_ref, w2_out, rate_ref, wf, w2 = refs[3:]
    gather_tables(scalars[0], refs[:3], tabs_ref, bcp_ref, conv, vocab)
    row = lax.broadcasted_iota(jnp.int32, perm_ref.shape, 0)
    lane = lax.broadcasted_iota(jnp.int32, perm_ref.shape, 1)
    perm = jnp.zeros(perm_ref.shape, F32)
    for k in range(vocab):
        perm = jnp.where(jnp.logical_and(lane == k, row == basemap[k]), 1.0, perm)
    perm_ref[...] = perm
    wf[...] = jnp.zeros_like(wf)
    w2[...] = jnp.zeros_like(w2)
    for st in range(2):
        fetch = (lambda t: t) if st == 0 else (lambda t: permuted(t, basemap, vocab))
        xt = fetch(tabs_ref[X_ROW : X_ROW + SYM, :])
        zt = fetch(tabs_ref[Z_ROW : Z_ROW + SYM, :])
        dtt = fetch(tabs_ref[DT_ROW : DT_ROW + SYM, :])
        if st == 1:
            dt1_ref[...] = dtt
        bct = fetch(bcp_ref[0:SYM, :])
        base = st * WIDE
        mid = SYM * (conv - 1)
        wf[mid : mid + SYM, base + ZZ : base + ZZ + LANES] = zt
        for k in range(conv):
            cx = tabs_ref[MISC_ROW + k : MISC_ROW + k + 1, :]
            cbc = bcp_ref[SYM + k : SYM + k + 1, :]
            lo, hi = mid - SYM * k, mid + SYM * k
            wf[lo : lo + SYM, base + XF : base + XF + LANES] = xt * cx
            wf[hi : hi + SYM, base + XB : base + XB + LANES] = xt * cx
            wf[lo : lo + SYM, base + BCF : base + BCF + 256] = bct * cbc
            wf[hi : hi + SYM, base + BCB : base + BCB + 256] = bct * cbc
        dt = jnp.maximum(dtt, 0.0) + jnp.log1p(jnp.exp(-jnp.abs(dtt)))
        ld = -jnp.exp(tabs_ref[MISC_ROW + 4 : MISC_ROW + 5, :]) * dt
        for k, piece in enumerate(thirds(ld)):
            w2[SYM * k : SYM * (k + 1), st * 128 : st * 128 + 128] = piece
            w2[32 + SYM * k : 32 + SYM * (k + 1), 256 + st * 128 : 384 + st * 128] = piece
            for h in range(2):
                at = 24 * (st * 2 + h) + SYM * k
                rate_ref[at : at + SYM, :] = jnp.broadcast_to(
                    piece[:, 64 * h : 64 * h + 1], piece.shape
                )
        for k, piece in enumerate(thirds(dt)):
            c = 512 + st * 128
            w2[64 + SYM * k : 64 + SYM * (k + 1), c : c + 128] = piece
    top, rest = halves(wf[...])
    w_ref[0:64, :] = top
    w_ref[64:128, :] = rest
    w2_out[...] = w2[...].astype(BF16)


def prepare(scalars, tok_refs, w_ref, w2_ref, r, conv):
    ns = len(tok_refs)
    length = ns * BLOCK
    mine = scalars[1]
    for k in range(ns):
        sym = lax.broadcasted_iota(jnp.int32, (SYM, BLOCK), 0).astype(F32)
        tok = jnp.broadcast_to(tok_refs[k][BLOCK : BLOCK + 1, 0:BLOCK].astype(F32), (SYM, BLOCK))
        at = jnp.bitwise_xor(mine, k) * BLOCK
        r.oh[:, pl.ds(pl.multiple_of(at, BLOCK), BLOCK)] = (sym == tok).astype(F32)
    oh = r.oh[...]
    lane = lax.broadcasted_iota(jnp.int32, (SYM, length), 1)
    up = (
        lax.broadcasted_iota(jnp.int32, (BLOCK, BLOCK), 0)
        <= lax.broadcasted_iota(jnp.int32, (BLOCK, BLOCK), 1)
    ).astype(BF16)
    r.rows[...] = jnp.zeros_like(r.rows)
    for d in range(1 - conv, conv):
        shifted = oh if d == 0 else pltpu.roll(oh, (length - d) % length, 1)
        inside = jnp.logical_and(lane + d >= 0, lane + d < length)
        r.rows[SYM * (d + conv - 1) : SYM * (d + conv), :] = jnp.where(inside, shifted, 0.0)
    r.rows[64:128, :] = r.rows[0:64, :]
    one = lax.broadcasted_iota(jnp.int32, (SYM, length), 0) < 3
    r.rows[152:160, :] = one.astype(F32)
    r.rows[184:192, :] = one.astype(F32)
    r.prow[...] = jnp.zeros_like(r.prow)
    oh_b = oh.astype(BF16)
    for b in range(ns):
        cols = slice(b * BLOCK, (b + 1) * BLOCK)
        inc = mm(oh_b[:, cols], up, NN)
        exc = inc - oh[:, cols]
        r.inc[:, cols] = inc
        r.exc[:, cols] = exc
        for k in range(3):
            r.rows[128 + SYM * k : 128 + SYM * (k + 1), cols] = inc
            r.rows[160 + SYM * k : 160 + SYM * (k + 1), cols] = exc
            r.rows[192 + SYM * k : 192 + SYM * (k + 1), cols] = oh[:, cols]
    r.sym[...] = r.rows[0:64, :].astype(BF16)
    turned = jnp.transpose(r.rows[...].astype(BF16))
    r.pre[...] = mm(turned[:, 0:128], w_ref[...], NN)
    w2 = w2_ref[...]
    r.pd[...] = mm(turned[:, 128:256], w2[:, 0:768], NN)
    r.count[...] = turned[:, 128:192]
    for st in range(2):
        for part, row0 in ((0, 0), (1, 32)):
            c = part * 256 + st * 128
            flat = mm(
                w2[row0 : row0 + 32, c : c + 128],
                r.rows[128 + row0 : 160 + row0, :].astype(BF16),
                TN,
            )
            for h in range(2):
                i = part * 4 + st * 2 + h
                row = flat[64 * h : 64 * h + 1, :]
                if part == 0:
                    row = -row
                for k, piece in enumerate(thirds(row)):
                    r.prow[SYM * i + k : SYM * i + k + 1, :] = piece


class Unit:
    def __init__(self, r, tabs_ref, st, b, nb):
        self.rows = rows = slice(b * BLOCK, (b + 1) * BLOCK)
        base = st * WIDE
        self.skip = tabs_ref[MISC_ROW + 5 : MISC_ROW + 6, :]
        self.dt = r.pd[rows, 512 + st * 128 : 512 + st * 128 + 128]
        self.p = r.pd[rows, st * 128 : st * 128 + 128]
        self.q = r.pd[rows, 256 + st * 128 : 256 + st * 128 + 128]
        self.total = self.p[BLOCK - 1 : BLOCK, :]
        self.r, self.st, self.b, self.base = r, st, b, base
        lane = lax.broadcasted_iota(jnp.int32, (BLOCK, LANES), 1)
        self.head0 = lane < 64
        row = lax.broadcasted_iota(jnp.int32, (BLOCK, BLOCK), 0)
        self.low = row >= lane
        self.upp = row <= lane

    def pre(self, col, width):
        return self.r.pre[self.rows, self.base + col : self.base + col + width]

    def act(self, col, width):
        v = self.pre(col, width)
        return v * sigmoid(v)

    def by_head(self, v):
        zero = jnp.zeros_like(v)
        return jnp.where(self.head0, v, zero), jnp.where(self.head0, zero, v)

    def decay(self, h):
        r, st = self.r, self.st
        i = st * 2 + h
        rate = r.rate[24 * i : 24 * i + 24, :]
        ends = r.prow[SYM * i : SYM * (i + 1), self.rows]
        starts = r.prow[SYM * (4 + i) : SYM * (5 + i), self.rows]
        zero = jnp.zeros((32, LANES), F32)
        below = jnp.concatenate([rate, ends, zero], 0)
        above = jnp.concatenate([zero, -rate, starts], 0)
        gap = mm(r.count[self.rows, :], jnp.concatenate([below, above], 1).astype(BF16), NN)
        return jnp.exp(jnp.where(self.low, gap[:, 0:LANES], gap[:, LANES : 2 * LANES]))


def state_pass_fwd(r, tabs_ref, nb, units):
    for st in range(2):
        for b in range(nb):
            u = units[st][b]
            xf, xb = u.act(XF, 128), u.act(XB, 128)
            bcf, bcb = u.act(BCF, 256), u.act(BCB, 256)
            r.x[u.rows, st * 256 : st * 256 + 128] = xf
            r.x[u.rows, st * 256 + 128 : st * 256 + 256] = xb
            r.bc[u.rows, st * 512 : st * 512 + 256] = bcf
            r.bc[u.rows, st * 512 + 256 : st * 512 + 512] = bcb
            wf = jnp.exp(u.total - u.p) * (u.dt * xf)
            wb = jnp.exp(u.q) * (u.dt * xb)
            if b < nb - 1:
                r.s[st * 2, b + 1] = mm_fine(bcf[:, 0:128], wf, TN, 2)
            if b > 0:
                r.s[st * 2 + 1, b - 1] = mm_fine(bcb[:, 0:128], wb, TN, 2)
        for b in range(2, nb):
            r.s[st * 2, b] += jnp.exp(units[st][b - 1].total) * r.s[st * 2, b - 1]
        for b in range(nb - 3, -1, -1):
            r.s[st * 2 + 1, b] += jnp.exp(units[st][b + 1].total) * r.s[st * 2 + 1, b + 1]


def together(bodies):
    bodies = list(bodies)
    while bodies:
        bodies = [b for b in bodies if next(b, True) is None]


class Names:
    pass


def named(refs, names):
    r = Names()
    for name, ref in zip(names, refs):
        setattr(r, name, ref)
    return r


KEPT = ("inc", "exc", "oh", "sym", "pre", "pd", "x", "bc", "s", "dec", "wts", "ys")


def kept_shapes(length):
    nb = length // BLOCK
    return [
        ((SYM, length), F32),
        ((SYM, length), F32),
        ((SYM, length), F32),
        ((64, length), BF16),
        ((length, 2 * WIDE), F32),
        ((length, 768), F32),
        ((length, 512), F32),
        ((length, 1024), F32),
        ((4, nb, LANES, LANES), F32),
        ((4 * nb, BLOCK, BLOCK), F32),
        ((8 * nb, BLOCK, BLOCK), BF16),
        ((length, 1024), F32),
    ]


def forward_kernel(scalars, *refs, ns, conv):
    tok_refs, (w_ref, w2_ref, rate_ref, tabs_ref, out_ref) = refs[:ns], refs[ns : ns + 5]
    r = named(refs[ns + 5 :], KEPT + ("rows", "prow", "count"))
    r.rate = rate_ref
    prepare(scalars, tok_refs, w_ref, w2_ref, r, conv)
    units = [[Unit(r, tabs_ref, st, b, ns) for b in range(ns)] for st in range(2)]
    state_pass_fwd(r, tabs_ref, ns, units)
    gated = {}

    def body(st, b):
        u = units[st][b]
        x = [r.x[u.rows, st * 256 + w * 128 : st * 256 + w * 128 + 128] for w in range(2)]
        decays = (u.decay(0), u.decay(1))
        yield
        masks, lefts, cms = (u.low, u.upp), [], []
        for w in range(2):
            c = st * 512 + w * 256
            bm, cm = r.bc[u.rows, c : c + 128], r.bc[u.rows, c + 128 : c + 256]
            lefts.append(mm_fine(cm, bm, NT, 3))
            cms.append(cm)
        yield
        y = u.skip * (x[0] + x[1])
        for w in range(2):
            if (w == 0 and b > 0) or (w == 1 and b < ns - 1):
                enter = jnp.exp(u.p) if w == 0 else jnp.exp(u.total - u.q)
                carried = enter * mm_fine(cms[w], r.s[st * 2 + w, b], NN, 2)
                r.ys[u.rows, st * 512 + w * 256 + 128 : st * 512 + w * 256 + 256] = carried
                y = y + carried
        yield
        for h in range(2):
            r.dec[(st * ns + b) * 2 + h] = decays[h]
        for w in range(2):
            g = jnp.where(masks[w], lefts[w], 0.0)
            lefts[w] = [(g * d).astype(BF16) for d in decays]
            for h in range(2):
                r.wts[((st * ns + b) * 2 + w) * 2 + h] = lefts[w][h]
        yield
        for w in range(2):
            right = u.by_head((u.dt * x[w]).astype(BF16))
            inner = mm(jnp.concatenate(lefts[w], 1), jnp.concatenate(right, 0), NN)
            r.ys[u.rows, st * 512 + w * 256 : st * 512 + w * 256 + 128] = inner
            y = y + inner
        gated[st, b] = y * u.act(ZZ, 128)

    for b0 in range(0, ns, GROUP):
        together(body(st, b) for b in range(b0, min(b0 + GROUP, ns)) for st in range(2))
        for b in range(b0, min(b0 + GROUP, ns)):
            out_ref[:, units[0][b].rows] = jnp.transpose(gated[0, b] + gated[1, b]).astype(BF16)


def backward_kernel(scalars, *refs, ns, nq, conv, vocab):
    tabs_ref, bcp_ref, dt1_ref, perm_ref = refs[:4]
    cot_refs, weight_ref = refs[4 : 4 + nq], refs[4 + nq]
    kept = refs[5 + nq : 5 + nq + len(KEPT)]
    out_ref, *work = refs[5 + nq + len(KEPT) :]
    r = named(list(kept) + work, KEPT + ("ds", "dg", "dpre"))
    cols = cot_refs[0].shape[2]
    cot = jnp.concatenate([a[...].reshape(ns * BLOCK, cols) for a in cot_refs], 1)
    weight = []
    for k in range(nq):
        at = pl.multiple_of(scalars[QUARTERS + k] * cols, LANES)
        rows = pl.ds(pl.multiple_of(scalars[0] * LANES, LANES), LANES)
        weight.append(weight_ref[rows, pl.ds(at, cols)])
    d_gated = mm(cot, jnp.concatenate(weight, 1), NT).astype(BF16).astype(F32)
    mine = scalars[1]
    for k in range(ns):
        at = jnp.bitwise_xor(mine, k)
        r.dg[pl.ds(pl.multiple_of(at * BLOCK, BLOCK), BLOCK), :] = d_gated[
            k * BLOCK : (k + 1) * BLOCK
        ]
    units = [[Unit(r, tabs_ref, st, b, ns) for b in range(ns)] for st in range(2)]

    def spread(st):
        backs, aheads = {}, {}
        for b in range(ns):
            u = units[st][b]
            dy = r.dg[u.rows, :] * u.act(ZZ, 128)
            cf = r.bc[u.rows, st * 512 + 128 : st * 512 + 256]
            cb = r.bc[u.rows, st * 512 + 384 : st * 512 + 512]
            if b > 0:
                backs[b - 1] = mm_fine(cf, jnp.exp(u.p) * dy, TN, 2)
            if b < ns - 1:
                aheads[b + 1] = mm_fine(cb, jnp.exp(u.total - u.q) * dy, TN, 2)
        yield
        for b in range(ns - 2, -1, -1):
            if b < ns - 2:
                backs[b] = backs[b] + jnp.exp(units[st][b + 1].total) * backs[b + 1]
            r.ds[st * 2, b] = backs[b]
        for b in range(1, ns):
            if b > 1:
                aheads[b] = aheads[b] + jnp.exp(units[st][b - 1].total) * aheads[b - 1]
            r.ds[st * 2 + 1, b] = aheads[b]

    d_steps = [jnp.zeros((SYM, LANES), F32)] * 2
    d_decays = [jnp.zeros((SYM, LANES), F32)] * 2
    d_tab = 0.0

    def body(st, b):
        u = units[st][b]
        base = st * WIDE
        x = [r.x[u.rows, st * 256 + w * 128 : st * 256 + w * 128 + 128] for w in range(2)]
        dgv = r.dg[u.rows, :]
        pz = u.pre(ZZ, 128)
        sz = sigmoid(pz)
        dy = dgv * (pz * sz)
        dyr = dy.astype(BF16)
        dyw = dyr.astype(F32)
        dy0, dy1 = u.by_head(dyr)
        decays = [r.dec[(st * ns + b) * 2 + h] for h in range(2)]
        inputs = [u.dt * v for v in x]
        ur = [v.astype(BF16) for v in inputs]
        uw = [v.astype(F32) for v in ur]
        uh = [u.by_head(v) for v in ur]
        d_pair = mm(dyr, jnp.concatenate([uh[0][0], uh[0][1], uh[1][0], uh[1][1]], 0), NT)
        yield
        masks = (u.low, u.upp)
        ends = (jnp.exp(u.total - u.p), jnp.exp(u.q))
        enters = (jnp.exp(u.p), jnp.exp(u.total - u.q))
        weights, bms, cms = [], [], []
        for w in range(2):
            c = st * 512 + w * 256
            bm, cm = r.bc[u.rows, c : c + 128], r.bc[u.rows, c + 128 : c + 256]
            weights.append([r.wts[((st * ns + b) * 2 + w) * 2 + h] for h in range(2)])
            bms.append(bm)
            cms.append(cm)
        du_both = mm(
            jnp.concatenate(
                [
                    jnp.concatenate([weights[0][0], weights[1][0]], 1),
                    jnp.concatenate([weights[0][1], weights[1][1]], 1),
                ],
                0,
            ),
            jnp.concatenate([dy0, dy1], 0),
            TN,
        )
        yield
        y = u.skip * (x[0] + x[1])
        mixes, step_part, flat = [], 0.0, 0.0
        for w in range(2):
            yield
            c = st * 512 + w * 256
            inner = r.ys[u.rows, c : c + 128]
            du_in = du_both[w * BLOCK : (w + 1) * BLOCK]
            has_enter = (w == 0 and b > 0) or (w == 1 and b < ns - 1)
            has_leave = (w == 0 and b < ns - 1) or (w == 1 and b > 0)
            y = y + inner
            row = dyw * inner - uw[w] * du_in
            du = du_in
            d_g = jnp.where(
                masks[w],
                d_pair[:, w * 256 : w * 256 + 128] * decays[0]
                + d_pair[:, w * 256 + 128 : w * 256 + 256] * decays[1],
                0.0,
            ).astype(BF16)
            d_c = mm(d_g, bms[w].astype(BF16), NN)
            d_b = mm(d_g, cms[w].astype(BF16), TN)
            enter_part = gain_part = None
            if has_enter:
                state = r.s[st * 2 + w, b]
                carried = r.ys[u.rows, c + 128 : c + 256]
                y = y + carried
                enter_part = dy * carried
                d_c = d_c + mm((enters[w] * dy).astype(BF16), state.astype(BF16), NT)
            if has_leave:
                d_state = r.ds[st * 2 + w, b]
                d_gain = mm_fine(bms[w], d_state, NN, 2)
                du = du + ends[w] * d_gain
                gain = ends[w] * inputs[w]
                gain_part = gain * d_gain
                d_b = d_b + mm(gain.astype(BF16), d_state.astype(BF16), NT)
            if has_enter and has_leave:
                flat = flat + jnp.exp(u.total) * jnp.sum(state * d_state, 0, keepdims=True)
            if w == 1:
                row = -row
            if enter_part is not None:
                row = row + enter_part if w == 0 else row - enter_part
            if gain_part is not None:
                row = row - gain_part if w == 0 else row + gain_part
            if w == 0 and gain_part is not None:
                flat = flat + jnp.sum(gain_part, 0, keepdims=True)
            if w == 1 and enter_part is not None:
                flat = flat + jnp.sum(enter_part, 0, keepdims=True)
            mixes.append(row)
            step_part = step_part + du * x[w]
            dx = du * u.dt + dy * u.skip
            px = u.pre((XF, XB)[w], 128)
            sx = sigmoid(px)
            col = base + (XF, XB)[w]
            r.dpre[u.rows, col : col + 128] = (dx * (sx * (1.0 + px * (1.0 - sx)))).astype(BF16)
            col = (BCF, BCB)[w]
            for i, grad in enumerate((d_b, d_c)):
                pb = u.pre(col + 128 * i, 128)
                sb = sigmoid(pb)
                at = base + col + 128 * i
                r.dpre[u.rows, at : at + 128] = (
                    grad * (sb * (1.0 + pb * (1.0 - sb)))
                ).astype(BF16)
        yield
        d_z = dgv * y * (sz * (1.0 + pz * (1.0 - sz)))
        r.dpre[u.rows, base + ZZ : base + ZZ + 128] = d_z.astype(BF16)
        inc = r.inc[:, u.rows]
        exc = r.exc[:, u.rows]
        inc_b, exc_b, oh_b = inc.astype(BF16), exc.astype(BF16), r.oh[:, u.rows].astype(BF16)
        right = list(halves(mixes[0])) + list(halves(mixes[1]))
        decay_part = mm(
            jnp.concatenate([inc_b, inc_b, exc_b, exc_b], 1), jnp.concatenate(right, 0), NN
        )
        decay_part = decay_part + inc[:, BLOCK - 1 : BLOCK] * flat
        step_sum = mm(
            jnp.concatenate([oh_b, oh_b], 1), jnp.concatenate(halves(step_part), 0), NN
        )
        d_steps[st] = d_steps[st] + step_sum
        d_decays[st] = d_decays[st] + decay_part

    for b0 in range(0, ns, GROUP_BACK):
        last = min(b0 + GROUP_BACK, ns)
        bodies = [body(st, b) for b in range(b0, last) for st in range(2)]
        together([spread(0), spread(1)] * (b0 == 0) + bodies)
        span = slice(b0 * BLOCK, last * BLOCK)
        d_tab = d_tab + mm(r.sym[:, span], r.dpre[span, :], NN)
    mid = SYM * (conv - 1)
    result = None
    for st in range(2):
        base = st * WIDE
        d_x = jnp.zeros((SYM, 128), F32)
        d_bc = jnp.zeros((SYM, 256), F32)
        for k in range(conv):
            cx = tabs_ref[MISC_ROW + k : MISC_ROW + k + 1, :]
            cbc = bcp_ref[SYM + k : SYM + k + 1, :]
            lo, hi = mid - SYM * k, mid + SYM * k
            d_x = d_x + cx * (
                d_tab[lo : lo + SYM, base + XF : base + XF + 128]
                + d_tab[hi : hi + SYM, base + XB : base + XB + 128]
            )
            d_bc = d_bc + cbc * (
                d_tab[lo : lo + SYM, base + BCF : base + BCF + 256]
                + d_tab[hi : hi + SYM, base + BCB : base + BCB + 256]
            )
        d_zt = d_tab[mid : mid + SYM, base + ZZ : base + ZZ + 128]
        dtt = dt1_ref[...] if st else tabs_ref[DT_ROW : DT_ROW + SYM, :]
        rate = -jnp.exp(tabs_ref[MISC_ROW + 4 : MISC_ROW + 5, :])
        d_dt = (d_steps[st] + rate * d_decays[st]) * sigmoid(dtt)
        wide = jnp.concatenate([d_x, d_zt, d_dt, d_bc], 1)
        if st == 0:
            result = wide
        else:
            for k in range(vocab):
                result = result + perm_ref[:, k : k + 1] * wide[k : k + 1]
    out_ref[...] = result


SMEM = pl.BlockSpec(memory_space=pltpu.SMEM)
VMEM = pl.BlockSpec(memory_space=pltpu.VMEM)
HBM = pl.BlockSpec(memory_space=pl.ANY)


def params(mib):
    return pltpu.CompilerParams(vmem_limit_bytes=mib * 1024 * 1024)


def call_tables(scalars, raw):
    basemap, xz_table, bc_table, conv_x, conv_bc, dt_table, a_log, skip_gain = raw
    conv, vocab = conv_x.shape[0], xz_table.shape[0]
    outs = [
        ((TAB_ROWS, LANES), F32),
        ((2 * SYM, 256), F32),
        ((SYM, LANES), F32),
        ((SYM, LANES), F32),
        ((128, 2 * WIDE), BF16),
        ((128, 768), BF16),
        ((96, LANES), F32),
    ]
    return pl.pallas_call(
        functools.partial(tables_kernel, conv=conv, vocab=vocab),
        out_shape=[jax.ShapeDtypeStruct(*a) for a in outs],
        in_specs=[SMEM, SMEM, VMEM, VMEM, SMEM],
        out_specs=[VMEM] * len(outs),
        scratch_shapes=[pltpu.VMEM((64, 2 * WIDE), F32), pltpu.VMEM((128, 768), F32)],
        compiler_params=params(8),
        cost_estimate=pl.CostEstimate(flops=2 * 10**9, transcendentals=0, bytes_accessed=10**6),
        name="tables",
    )(
        scalars,
        basemap,
        jnp.concatenate([xz_table.reshape(2 * vocab, -1), conv_x], 0),
        jnp.concatenate([bc_table, conv_bc], 0),
        jnp.concatenate([dt_table, a_log[None], skip_gain[None]], 0),
    )


def call_forward(scalars, pays, w, w2, rate, tabs, conv):
    ns = len(pays)
    length = ns * BLOCK
    outs = [((LANES, length), BF16)] + kept_shapes(length)
    return pl.pallas_call(
        functools.partial(forward_kernel, ns=ns, conv=conv),
        out_shape=[jax.ShapeDtypeStruct(*a) for a in outs],
        in_specs=[SMEM] + [VMEM] * (ns + 4),
        out_specs=[VMEM] * len(outs),
        scratch_shapes=[
            pltpu.VMEM((256, length), F32),
            pltpu.VMEM((64, length), F32),
            pltpu.VMEM((length, 64), BF16),
        ],
        compiler_params=params(8),
        cost_estimate=pl.CostEstimate(
            flops=5 * 10**9, transcendentals=0, bytes_accessed=8 * LANES * length
        ),
        name="mix_forward",
    )(scalars, *pays, w, w2, rate, tabs)


def call_backward(scalars, tables, cots, out_weight, kept, conv, vocab):
    length = kept[0].shape[1]
    ns = length // BLOCK
    return pl.pallas_call(
        functools.partial(backward_kernel, ns=ns, nq=len(cots), conv=conv, vocab=vocab),
        out_shape=jax.ShapeDtypeStruct((SYM, 640), F32),
        in_specs=[SMEM] + [VMEM] * (len(tables) + len(cots) + 1 + len(kept)),
        out_specs=VMEM,
        scratch_shapes=[
            pltpu.VMEM((4, ns, LANES, LANES), F32),
            pltpu.VMEM((length, LANES), F32),
            pltpu.VMEM((length, 2 * WIDE), BF16),
        ],
        compiler_params=params(10),
        cost_estimate=pl.CostEstimate(
            flops=6 * 10**9, transcendentals=0, bytes_accessed=8 * LANES * length
        ),
        name="mix_backward",
    )(scalars, *tables, *cots, out_weight, *kept)


QUARTERS = 3


def out_kernel(scalars, *refs, ns, nh, nc):
    slices, weight_ref, outs = refs[: ns * nc], refs[ns * nc], refs[ns * nc + 1 :]
    here = pl.ds(pl.multiple_of(scalars[1] * BLOCK, BLOCK), BLOCK)
    places = QUARTERS + nh * nc
    cols = outs[0].shape[1]
    left = jnp.concatenate([a[:, here] for a in slices], 0)
    for k in range(nh):
        at = pl.ds(pl.multiple_of(scalars[QUARTERS + k * nc] * cols, LANES), cols)
        right = []
        for i in range(ns * nc):
            rows = pl.ds(pl.multiple_of(scalars[places + i] * LANES, LANES), LANES)
            right.append(weight_ref[rows, at])
        outs[k][...] = mm(left, jnp.concatenate(right, 0), TN)


def call_out(scalars, slices, out_weight, ns, nh, nc):
    cols = out_weight.shape[1] // (nh * nc)
    return pl.pallas_call(
        functools.partial(out_kernel, ns=ns, nh=nh, nc=nc),
        out_shape=[jax.ShapeDtypeStruct((BLOCK, cols), F32)] * nh,
        in_specs=[SMEM] + [VMEM] * (len(slices) + 1),
        out_specs=[VMEM] * nh,
        compiler_params=params(8),
        name="layer_out",
    )(scalars, *slices, out_weight)


def weight_kernel(scalars, *refs, ns, nh, nc):
    slices, cots = refs[: ns * nc], refs[ns * nc : ns * nc + nh * nc]
    out_ref, mark_ref, left, buf, sems = refs[ns * nc + nh * nc :]
    mine = scalars[1]
    places = QUARTERS + nh * nc
    cols = cots[0].shape[2]
    mark_ref[...] = jnp.zeros_like(mark_ref)
    copies = []
    for n in range(ns * nc):
        span = slice(n * LANES, (n + 1) * LANES)
        for k in range(ns):
            at = pl.multiple_of(jnp.bitwise_xor(mine, k) * BLOCK, BLOCK)
            left[span, k * BLOCK : (k + 1) * BLOCK] = slices[n][:, pl.ds(at, BLOCK)]
        for q in range(nh * nc):
            at = pl.multiple_of(scalars[QUARTERS + q] * cols, LANES)
            right = cots[q][...].reshape(ns * BLOCK, cols)
            buf[span, pl.ds(at, cols)] = mm(left[span, :], right, NN)
        to = pl.multiple_of(scalars[places + n] * LANES, LANES)
        copy = pltpu.make_async_copy(
            buf.at[pl.ds(n * LANES, LANES), :], out_ref.at[pl.ds(to, LANES), :], sems.at[n]
        )
        copy.start()
        copies.append(copy)
    for copy in copies:
        copy.wait()


def call_weight(scalars, slices, cots, width, ns, nh, nc):
    length = slices[0].shape[1]
    rows = ns * nc * LANES
    return pl.pallas_call(
        functools.partial(weight_kernel, ns=ns, nh=nh, nc=nc),
        out_shape=[
            jax.ShapeDtypeStruct((rows, width), F32),
            jax.ShapeDtypeStruct((SYM, LANES), F32),
        ],
        in_specs=[SMEM] + [VMEM] * (len(slices) + len(cots)),
        out_specs=[HBM, VMEM],
        scratch_shapes=[
            pltpu.VMEM((rows, length), BF16),
            pltpu.VMEM((rows, width), F32),
            pltpu.SemaphoreType.DMA((ns * nc,)),
        ],
        compiler_params=params(12),
        cost_estimate=pl.CostEstimate(
            flops=2 * rows * width * length, transcendentals=0, bytes_accessed=6 * rows * width
        ),
        name="weight_grad",
    )(scalars, *slices, *cots)


def final_kernel(scalars, *refs, ns, nh, vocab, places):
    packs, parts = refs[:ns], refs[ns : ns + nh]
    out_ref, xz_ref, bc_ref, dt_ref = refs[ns + nh + 1 :]
    total = parts[0][...]
    for a in parts[1:]:
        total = total + a[...]
    out_ref[...] = total.astype(BF16)
    d_bc = packs[0][:, 768:1024]
    for a in packs[1:]:
        d_bc = d_bc + a[:, 768:1024]
    for i in range(2):
        for k in range(vocab):
            bc_ref[k, i : i + 1, :] = d_bc[k : k + 1, i * 128 : i * 128 + 128]
    lane = lax.broadcasted_iota(jnp.int32, (SYM, dt_ref.shape[1]), 1)
    d_dt = jnp.zeros((SYM, dt_ref.shape[1]), F32)
    for n in range(2 * ns):
        j = scalars[places + n]
        piece = packs[n % ns][:, n // ns * 384 : n // ns * 384 + 384]
        for i in range(2):
            for k in range(vocab):
                xz_ref[k, i : i + 1, pl.ds(pl.multiple_of(j * LANES, LANES), LANES)] = piece[
                    k : k + 1, i * 128 : i * 128 + 128
                ]
            row = jnp.sum(piece[:, 256 + 64 * i : 320 + 64 * i], 1, keepdims=True)
            d_dt = jnp.where(lane == 2 * j + i, row, d_dt)
    dt_ref[...] = d_dt[:vocab]


def call_final(scalars, packs, parts, mark, raw, places):
    shapes = [raw[1].shape, raw[2].shape, raw[5].shape]
    arrays = list(packs) + list(parts)
    return pl.pallas_call(
        functools.partial(
            final_kernel, ns=len(packs), nh=len(parts), vocab=raw[1].shape[0], places=places
        ),
        out_shape=[jax.ShapeDtypeStruct(parts[0].shape, BF16)]
        + [jax.ShapeDtypeStruct(a, F32) for a in shapes],
        in_specs=[SMEM] + [VMEM] * (len(arrays) + 1),
        out_specs=[VMEM] * (len(shapes) + 1),
        compiler_params=params(8),
        name="place_grads",
    )(scalars, *arrays, mark)


def around(x, axis):
    n = lax.axis_size(axis)
    return [x] + [lax.ppermute(x, axis, [(i, i ^ k) for i in range(n)]) for k in range(1, n)]


def across(x, hops, nh, nc):
    pairs = [
        (a * nc + b, (a + hops[0]) % nh * nc + (b + hops[1]) % nc)
        for a in range(nh)
        for b in range(nc)
    ]
    return lax.ppermute(x, ("head", "sub"), pairs)


def by_channel(
    token_ids, basemap, xz_table, bc_table, dt_table, conv_x, conv_bc, a_log, skip_gain, out_weight, cotangent
):
    ns, nc, nh = lax.axis_size("seq"), lax.axis_size("sub"), lax.axis_size("head")
    s, c, h = lax.axis_index("seq"), lax.axis_index("sub"), lax.axis_index("head")
    width = out_weight.shape[1]
    cols = width // (nh * nc)
    raw = (basemap, xz_table, bc_table, conv_x, conv_bc, dt_table, a_log, skip_gain)
    symbols = jnp.pad(token_ids.astype(BF16).reshape(1, BLOCK), ((0, 15), (0, cols - BLOCK)))
    pays = around(jnp.concatenate([cotangent, symbols], 0), "seq")
    slot = jnp.arange(nh * nc, dtype=jnp.int32)
    quarters = (h - slot // nc) % nh * nc + (c - slot % nc) % nc
    slot = jnp.arange(ns * nc, dtype=jnp.int32)
    places = (c - slot // ns) % nc * ns + jnp.bitwise_xor(s, slot % ns)
    scalars = jnp.concatenate([jnp.stack([c * ns + s, s, c]), quarters, places]).astype(jnp.int32)
    stacked = jnp.stack([a[:BLOCK] for a in pays], 0)
    heads = [stacked] + [across(stacked, (k, 0), nh, nc) for k in range(1, nh)]
    side = across(stacked, (0, 1), nh, nc)
    conv, vocab = conv_x.shape[0], xz_table.shape[0]
    *tables, w, w2, rate = call_tables(scalars, raw)
    gated, *kept = call_forward(scalars, pays, w, w2, rate, tables[0], conv)
    heads, _ = lax.optimization_barrier((heads, gated))
    cots = [heads[0], side]
    for a in heads[1:]:
        cots += [a, across(a, (0, 1), nh, nc)]
    hop = lambda x, k: lax.ppermute(x, "seq", [(i, i ^ k) for i in range(ns)])
    direct = {k: hop(gated, k) for k in (ns >> n for n in range(1, ns.bit_length()))}
    grads = call_backward(scalars, tables, cots, out_weight, kept, conv, vocab)
    direct, _ = lax.optimization_barrier((direct, grads))
    held = {0: gated, **direct}
    for k in range(3, ns):
        if k not in held:
            held[k] = hop(held[k & (k - 1)], k & -k)
    slices = [held[k] for k in range(ns)]
    slices = slices + [across(a, (0, 1), nh, nc) for a in slices]
    shared = grads[:, 384:]
    beside = across(grads, (0, 1), nh, nc)
    for a in range(1, nh):
        for b in range(nc):
            shared = shared + across(grads[:, 384:], (a, b), nh, nc)
    packed = jnp.concatenate([grads[:, :384], beside[:, :384], shared + beside[:, 384:]], 1)
    packs = around(packed, "seq")
    parts = call_out(scalars, slices, out_weight, ns, nh, nc)
    parts = [parts[0]] + [across(parts[k], (nh - k, 0), nh, nc) for k in range(1, nh)]
    d_out_weight, mark = call_weight(scalars, slices, cots, width, ns, nh, nc)
    layer_out, d_xz, d_bc, d_dt = call_final(
        scalars, packs, parts, mark, raw, QUARTERS + nh * nc
    )
    return (layer_out, d_out_weight, d_xz, d_bc, d_dt)


PRECISE = lax.Precision.HIGHEST


def carried_in(part, axis, combine, identity):
    place = lax.axis_index(axis)
    gathered = jax.tree.map(lambda a: lax.all_gather(a, axis), part)
    state = jax.tree.map(lambda a, e: jnp.zeros_like(a) + jnp.asarray(e, a.dtype), part, identity)

    def one(hop, state):
        return combine(
            state, jax.tree.map(lambda a: lax.dynamic_index_in_dim(a, hop, 0, False), gathered)
        )

    return lax.fori_loop(0, place, one, state)


def carried_in_2(array, axis, combine, identity):
    length, mine = (lax.axis_size(axis), lax.axis_index(axis))
    everything = jax.tree.map(
        lambda part, kind: lax.all_gather(part.astype(kind), axis),
        array,
        jax.tree.map(lambda a: jnp.bfloat16 if a.dtype == jnp.float32 else a.dtype, array),
    )
    start = jax.tree.map(
        lambda part, zero: jnp.broadcast_to(jnp.asarray(zero, part.dtype), part.shape),
        array,
        identity,
    )

    def hop(k, before):
        at = length - 1 - k
        reached = at > mine
        new = combine(
            before, jax.tree.map(lambda part, own: part[at].astype(own.dtype), everything, array)
        )
        return jax.tree.map(lambda a, b: jnp.where(reached, a, b), new, before)

    return lax.fori_loop(0, length, hop, start)


def with_halo(block, sides, width):
    for axis, dim in sides:
        count = lax.axis_size(axis)
        forward = [(i, i + 1) for i in range(count - 1)]
        backward = [(target, source) for source, target in forward]
        low = lax.ppermute(
            lax.slice_in_dim(block, block.shape[dim] - width, None, axis=dim), axis, forward
        )
        high = lax.ppermute(lax.slice_in_dim(block, 0, width, axis=dim), axis, backward)
        block = jnp.concatenate([low, block, high], axis=dim)
    return block


def block_step(carry_state, pieces):
    scaled_x, logdec, b_mat, c_mat = pieces
    block_len = scaled_x.shape[0]
    running = jnp.cumsum(logdec, axis=0)
    by_head = running.T
    causal_mask = (jnp.arange(block_len)[:, None] >= jnp.arange(block_len)[None, :])[None, :, :]
    gap_matrix = by_head[:, :, None] - by_head[:, None, :]
    decay_mat = jnp.where(causal_mask, jnp.exp(jnp.where(causal_mask, gap_matrix, 0.0)), 0.0)
    scores = jnp.einsum("tn,sn->ts", c_mat, b_mat, precision=PRECISE)
    within = jnp.einsum("hts,shp->thp", scores[None, :, :] * decay_mat, scaled_x, precision=PRECISE)
    carried = jnp.exp(running)[:, :, None] * jnp.einsum(
        "tn,hpn->thp", c_mat, carry_state, precision=PRECISE
    )
    to_end = jnp.exp(running[-1][None, :] - running)
    gained = jnp.einsum("shp,sn->hpn", to_end[:, :, None] * scaled_x, b_mat, precision=PRECISE)
    return (jnp.exp(running[-1])[:, None, None] * carry_state + gained, within + carried)


def state_pass(inputs, start_state, block_len):
    scaled_x, logdec, b_mat, c_mat = inputs
    block_count = scaled_x.shape[0] // block_len
    pieces = (
        scaled_x.reshape((block_count, block_len) + scaled_x.shape[1:]),
        logdec.reshape(block_count, block_len, -1),
        b_mat.reshape(block_count, block_len, -1),
        c_mat.reshape(block_count, block_len, -1),
    )
    end_state, outputs = lax.scan(jax.checkpoint(block_step), start_state, pieces)
    return (outputs.reshape(scaled_x.shape), end_state)


def final_state(inputs):
    scaled_x, logdec, b_mat, c_mat = inputs
    running = jnp.cumsum(logdec, axis=0)
    to_end = jnp.exp(running[-1][None, :] - running)
    gained = jnp.einsum("shp,sn->hpn", to_end[:, :, None] * scaled_x, b_mat, precision=PRECISE)
    return (jnp.exp(running[-1]), gained)


def lookup(symbols, table):
    vocab_size = table.shape[0]
    onehot = (symbols[:, None] == jnp.arange(vocab_size, dtype=jnp.int32)[None, :]).astype(
        jnp.float32
    )
    return jnp.dot(onehot, table, precision=PRECISE)


def conv_rows(extended, weight, row_count, forward):
    conv_width = weight.shape[0]
    rim_width = conv_width - 1
    summed = jnp.zeros((row_count, extended.shape[1]), jnp.float32)
    for offset in range(conv_width):
        if forward:
            first_row = rim_width - offset
        else:
            first_row = rim_width + offset
        summed = summed + weight[offset][None, :] * extended[first_row : first_row + row_count]
    return summed


def open_inputs(ext_sym, inside_mask, tables, frozen):
    xz_tab, bc_tab, dt_tab = tables
    conv_inner, conv_shared, log_rates, skip_vals = frozen
    rim_width = conv_inner.shape[0] - 1
    row_count = ext_sym.shape[0] - 2 * rim_width
    vocab_size = xz_tab.shape[0]
    inner_dim = xz_tab.shape[2]
    head_count = dt_tab.shape[1]
    state_dim = bc_tab.shape[2]
    looked = lookup(ext_sym, xz_tab.reshape(vocab_size, 2 * inner_dim)) * inside_mask[:, None]
    pre_x = looked[:, :inner_dim]
    gate_act = jax.nn.silu(looked[rim_width : rim_width + row_count, inner_dim:])
    pre_bc = lookup(ext_sym, bc_tab.reshape(vocab_size, 2 * state_dim)) * inside_mask[:, None]
    dt_step = jax.nn.softplus(lookup(ext_sym[rim_width : rim_width + row_count], dt_tab))
    logdec = -jnp.exp(log_rates)[None, :] * dt_step
    flat_bc = conv_shared.reshape(conv_inner.shape[0], 2 * state_dim)

    def one_way(forward):
        x_conv = jax.nn.silu(conv_rows(pre_x, conv_inner, row_count, forward)).reshape(
            row_count, head_count, -1
        )
        bc_conv = jax.nn.silu(conv_rows(pre_bc, flat_bc, row_count, forward))
        return (x_conv, bc_conv[:, :state_dim], bc_conv[:, state_dim:])

    x_fwd, b_fwd, c_fwd = one_way(True)
    x_back, b_back, c_back = one_way(False)
    ahead_in = (x_fwd * dt_step[:, :, None], logdec, b_fwd, c_fwd)
    behind_in = (
        jnp.flip(x_back * dt_step[:, :, None], 0),
        jnp.flip(logdec, 0),
        jnp.flip(b_back, 0),
        jnp.flip(c_back, 0),
    )
    skip_term = skip_vals[None, :, None] * (x_fwd + x_back)
    return (ahead_in, behind_in, skip_term, gate_act)


def combine(earlier, later):
    decay_early, state_early = earlier
    decay_late, state_late = later
    return (decay_early * decay_late, decay_late[:, None, None] * state_early + state_late)


def carries(ahead_pair, behind_pair):
    ahead_out = carried_in(
        (ahead_pair[0], ahead_pair[1]),
        "seq",
        combine,
        (jnp.ones_like(ahead_pair[0]), jnp.zeros_like(ahead_pair[1])),
    )
    behind_out = carried_in_2(
        (behind_pair[0], behind_pair[1]),
        "seq",
        combine,
        (jnp.ones_like(behind_pair[0]), jnp.zeros_like(behind_pair[1])),
    )
    return (ahead_out[1], behind_out[1])


def decay_weights(adjoint, start_state):
    return jnp.sum(adjoint * start_state, axis=(1, 2))


def shards(
    token_ids,
    basemap,
    xz_table,
    bc_table,
    dt_table,
    conv_x,
    conv_bc,
    a_log,
    skip_gain,
    out_weight,
    cotangent,
):
    row_count = token_ids.shape[0]
    rim_width = conv_x.shape[0] - 1
    ext_ids = with_halo(token_ids, (("seq", 0),), rim_width)
    first_row = lax.axis_index("seq") * row_count - rim_width
    where_global = first_row + jnp.arange(row_count + 2 * rim_width, dtype=jnp.int32)
    inside_mask = jnp.logical_and(
        where_global >= 0, where_global < row_count * lax.axis_size("seq")
    ).astype(jnp.float32)
    vocab_size = basemap.shape[0]
    matches = ext_ids[:, None] == jnp.arange(vocab_size, dtype=jnp.int32)[None, :]
    mapped = jnp.sum(jnp.where(matches, basemap[None, :], 0), axis=1)
    ext_sym = jnp.where(lax.axis_index("sub") == 1, mapped, ext_ids)
    tables = (xz_table.astype(jnp.float32), bc_table.astype(jnp.float32), dt_table)
    frozen = (conv_x.astype(jnp.float32), conv_bc.astype(jnp.float32), a_log, skip_gain)

    def summary(tabs_in):
        ahead_in, behind_in, skip_term, gate_act = open_inputs(
            ext_sym, inside_mask, tabs_in, frozen
        )
        decay_fwd, end_fwd = final_state(ahead_in)
        decay_back, end_back = final_state(behind_in)
        return (decay_fwd, end_fwd, decay_back, end_back)

    (decay_fwd, end_fwd, decay_back, end_back), pull_summary = jax.vjp(summary, tables)
    start_fwd, start_back = carries((decay_fwd, end_fwd), (decay_back, end_back))

    def finished(tabs_in, begin_fwd, begin_back):
        ahead_in, behind_in, skip_term, gate_act = open_inputs(
            ext_sym, inside_mask, tabs_in, frozen
        )
        out_fwd, unused_fwd = state_pass(ahead_in, begin_fwd, BLOCK)
        out_back, unused_back = state_pass(behind_in, begin_back, BLOCK)
        return (out_fwd + jnp.flip(out_back, 0) + skip_term).reshape(row_count, -1) * gate_act

    gated, pull_finished = jax.vjp(finished, tables, start_fwd, start_back)
    gated_bf = gated.astype(jnp.bfloat16)
    products = jnp.dot(gated_bf, out_weight, preferred_element_type=jnp.float32)
    layer_out = lax.psum_scatter(products, ("head", "sub"), scatter_dimension=1, tiled=True).astype(
        jnp.bfloat16
    )
    full_cot = lax.all_gather(cotangent, ("head", "sub"), axis=1, tiled=True)
    d_gated = jnp.einsum(
        "tc,kc->tk", full_cot, out_weight, preferred_element_type=jnp.float32
    ).astype(jnp.bfloat16)
    weight_part = jnp.einsum("tk,tc->kc", gated_bf, full_cot, preferred_element_type=jnp.float32)
    d_gated_wide = lax.optimization_barrier(d_gated).astype(jnp.float32)
    grads_first, direct_fwd, direct_back = pull_finished(d_gated_wide)
    adjoint_back, adjoint_fwd = carries((decay_back, direct_back), (decay_fwd, direct_fwd))
    grads_second = pull_summary(
        (
            decay_weights(adjoint_fwd, start_fwd),
            adjoint_fwd,
            decay_weights(adjoint_back, start_back),
            adjoint_back,
        )
    )[0]
    d_tables = jax.tree.map(lambda former, latter: former + latter, grads_first, grads_second)
    d_xz, d_bc, d_dt = d_tables
    d_bc = lax.psum(d_bc, ("seq", "head", "sub"))
    d_out_weight, d_xz, d_dt = lax.psum((weight_part, d_xz, d_dt), ("seq", "sub"))
    return (layer_out, d_out_weight, d_xz, d_bc, d_dt)


def solution(mesh):
    in_specs = (
        P(("grp", "seq")),
        P(),
        P(None, None, "head"),
        P(),
        P(None, "head"),
        P(None, "head"),
        P(),
        P("head"),
        P("head"),
        P("head", None),
        P(("grp", "seq"), ("head", "sub")),
    )
    out_specs = (
        P(("grp", "seq"), ("head", "sub")),
        P(("grp", "head"), None),
        P("grp", None, "head"),
        P("grp", None, None),
        P("grp", "head"),
    )
    def run(*args):
        ns, nc = mesh.shape["seq"], mesh.shape["sub"]
        rows, inner, heads = args[0].shape[0], args[2].shape[2], args[4].shape[1]
        by_lanes = (
            rows == BLOCK
            and nc == 2
            and ns > 1
            and ns & (ns - 1) == 0
            and inner == ns * nc * LANES
            and inner == heads * (LANES // 2)
            and args[3].shape[2] == LANES
            and args[5].shape[0] == 4
            and args[9].shape[1] == args[10].shape[1] * nc * mesh.shape["head"]
        )
        return (by_channel if by_lanes else shards)(*args)

    return jax.shard_map(run, mesh=mesh, in_specs=in_specs, out_specs=out_specs, check_vma=False)
```

```python
import functools

import jax
import jax.numpy as jnp
from jax import lax
from jax.experimental import pallas as pl
from jax.experimental.pallas import tpu as pltpu
from jax.sharding import PartitionSpec as P

BLOCK = 128
LANES = 128
SYM = 8
F32 = jnp.float32
BF16 = jnp.bfloat16
GROUP = 2
GROUP_BACK = 4
NN = (((1,), (0,)), ((), ()))
NT = (((1,), (1,)), ((), ()))
TN = (((0,), (0,)), ((), ()))
X_ROW, Z_ROW, DT_ROW, MISC_ROW, TAB_ROWS = 0, 8, 16, 24, 32
XF, XB, ZZ, BCF, BCB, WIDE = 0, 128, 256, 384, 640, 896


def mm(a, b, dims):
    return lax.dot_general(a, b, dims, preferred_element_type=F32)


def halves(a):
    top = a.astype(BF16)
    return top, (a - top.astype(F32)).astype(BF16)


def thirds(a):
    top = a.astype(BF16).astype(F32)
    rest = a - top
    mid = rest.astype(BF16).astype(F32)
    return top, mid, rest - mid


def mm_fine(a, b, dims, terms):
    ah, al = halves(a)
    bh, bl = halves(b)
    (ca,), (cb,) = dims[0]
    left, right = [ah], [bh]
    if terms >= 2:
        left.append(al)
        right.append(bh)
    if terms >= 3:
        left.append(ah)
        right.append(bl)
    return mm(jnp.concatenate(left, ca), jnp.concatenate(right, cb), dims)


def permuted(table, basemap, count):
    row = lax.broadcasted_iota(jnp.int32, table.shape, 0)
    out = jnp.zeros_like(table)
    for k in range(count):
        picked = jnp.zeros_like(table[0:1])
        for m in range(count):
            picked = jnp.where(basemap[k] == m, table[m : m + 1], picked)
        out = jnp.where(row == k, picked, out)
    return out


def sigmoid(v):
    return 0.5 * jnp.tanh(0.5 * v) + 0.5


def gather_tables(j, raw, tabs_ref, bcp_ref, conv, vocab):
    wide_ref, bc_ref, dt_ref = raw
    lanes = pl.ds(pl.multiple_of(j * LANES, LANES), LANES)
    head0 = lax.broadcasted_iota(jnp.int32, (1, LANES), 1) < 64
    pair = lambda a, b: jnp.where(head0, a, b)
    tabs_ref[...] = jnp.zeros_like(tabs_ref)
    bcp_ref[...] = jnp.zeros_like(bcp_ref)
    for k in range(vocab):
        tabs_ref[X_ROW + k : X_ROW + k + 1, :] = wide_ref[2 * k : 2 * k + 1, lanes].astype(F32)
        tabs_ref[Z_ROW + k : Z_ROW + k + 1, :] = wide_ref[2 * k + 1 : 2 * k + 2, lanes].astype(F32)
        tabs_ref[DT_ROW + k : DT_ROW + k + 1, :] = pair(dt_ref[k, 2 * j], dt_ref[k, 2 * j + 1])
        for i in range(2):
            bcp_ref[k : k + 1, i * 128 : i * 128 + 128] = bc_ref[k, i : i + 1, :].astype(F32)
    for k in range(conv):
        tabs_ref[MISC_ROW + k : MISC_ROW + k + 1, :] = wide_ref[2 * vocab + k : 2 * vocab + k + 1, lanes].astype(F32)
        for i in range(2):
            bcp_ref[SYM + k : SYM + k + 1, i * 128 : i * 128 + 128] = bc_ref[
                vocab + k, i : i + 1, :
            ].astype(F32)
    at = MISC_ROW + 4
    tabs_ref[at : at + 1, :] = pair(dt_ref[vocab, 2 * j], dt_ref[vocab, 2 * j + 1])
    tabs_ref[at + 1 : at + 2, :] = pair(
        dt_ref[vocab + 1, 2 * j], dt_ref[vocab + 1, 2 * j + 1]
    )


def tables_kernel(scalars, basemap, *refs, conv, vocab):
    tabs_ref, bcp_ref, dt1_ref, perm_ref, w_ref, w2_out, rate_ref, wf, w2 = refs[3:]
    gather_tables(scalars[0], refs[:3], tabs_ref, bcp_ref, conv, vocab)
    row = lax.broadcasted_iota(jnp.int32, perm_ref.shape, 0)
    lane = lax.broadcasted_iota(jnp.int32, perm_ref.shape, 1)
    perm = jnp.zeros(perm_ref.shape, F32)
    for k in range(vocab):
        perm = jnp.where(jnp.logical_and(lane == k, row == basemap[k]), 1.0, perm)
    perm_ref[...] = perm
    wf[...] = jnp.zeros_like(wf)
    w2[...] = jnp.zeros_like(w2)
    for st in range(2):
        fetch = (lambda t: t) if st == 0 else (lambda t: permuted(t, basemap, vocab))
        xt = fetch(tabs_ref[X_ROW : X_ROW + SYM, :])
        zt = fetch(tabs_ref[Z_ROW : Z_ROW + SYM, :])
        dtt = fetch(tabs_ref[DT_ROW : DT_ROW + SYM, :])
        if st == 1:
            dt1_ref[...] = dtt
        bct = fetch(bcp_ref[0:SYM, :])
        base = st * WIDE
        mid = SYM * (conv - 1)
        wf[mid : mid + SYM, base + ZZ : base + ZZ + LANES] = zt
        for k in range(conv):
            cx = tabs_ref[MISC_ROW + k : MISC_ROW + k + 1, :]
            cbc = bcp_ref[SYM + k : SYM + k + 1, :]
            lo, hi = mid - SYM * k, mid + SYM * k
            wf[lo : lo + SYM, base + XF : base + XF + LANES] = xt * cx
            wf[hi : hi + SYM, base + XB : base + XB + LANES] = xt * cx
            wf[lo : lo + SYM, base + BCF : base + BCF + 256] = bct * cbc
            wf[hi : hi + SYM, base + BCB : base + BCB + 256] = bct * cbc
        dt = jnp.maximum(dtt, 0.0) + jnp.log1p(jnp.exp(-jnp.abs(dtt)))
        ld = -jnp.exp(tabs_ref[MISC_ROW + 4 : MISC_ROW + 5, :]) * dt
        for k, piece in enumerate(thirds(ld)):
            w2[SYM * k : SYM * (k + 1), st * 128 : st * 128 + 128] = piece
            w2[32 + SYM * k : 32 + SYM * (k + 1), 256 + st * 128 : 384 + st * 128] = piece
            for h in range(2):
                at = 24 * (st * 2 + h) + SYM * k
                rate_ref[at : at + SYM, :] = jnp.broadcast_to(
                    piece[:, 64 * h : 64 * h + 1], piece.shape
                )
        for k, piece in enumerate(thirds(dt)):
            c = 512 + st * 128
            w2[64 + SYM * k : 64 + SYM * (k + 1), c : c + 128] = piece
    top, rest = halves(wf[...])
    w_ref[0:64, :] = top
    w_ref[64:128, :] = rest
    w2_out[...] = w2[...].astype(BF16)


def prepare(scalars, tok_refs, w_ref, w2_ref, r, conv):
    ns = len(tok_refs)
    length = ns * BLOCK
    mine = scalars[1]
    for k in range(ns):
        sym = lax.broadcasted_iota(jnp.int32, (SYM, BLOCK), 0).astype(F32)
        tok = jnp.broadcast_to(tok_refs[k][BLOCK : BLOCK + 1, 0:BLOCK].astype(F32), (SYM, BLOCK))
        at = jnp.bitwise_xor(mine, k) * BLOCK
        r.oh[:, pl.ds(pl.multiple_of(at, BLOCK), BLOCK)] = (sym == tok).astype(F32)
    oh = r.oh[...]
    lane = lax.broadcasted_iota(jnp.int32, (SYM, length), 1)
    up = (
        lax.broadcasted_iota(jnp.int32, (BLOCK, BLOCK), 0)
        <= lax.broadcasted_iota(jnp.int32, (BLOCK, BLOCK), 1)
    ).astype(BF16)
    r.rows[...] = jnp.zeros_like(r.rows)
    for d in range(1 - conv, conv):
        shifted = oh if d == 0 else pltpu.roll(oh, (length - d) % length, 1)
        inside = jnp.logical_and(lane + d >= 0, lane + d < length)
        r.rows[SYM * (d + conv - 1) : SYM * (d + conv), :] = jnp.where(inside, shifted, 0.0)
    r.rows[64:128, :] = r.rows[0:64, :]
    one = lax.broadcasted_iota(jnp.int32, (SYM, length), 0) < 3
    r.rows[152:160, :] = one.astype(F32)
    r.rows[184:192, :] = one.astype(F32)
    r.prow[...] = jnp.zeros_like(r.prow)
    oh_b = oh.astype(BF16)
    for b in range(ns):
        cols = slice(b * BLOCK, (b + 1) * BLOCK)
        inc = mm(oh_b[:, cols], up, NN)
        exc = inc - oh[:, cols]
        r.inc[:, cols] = inc
        r.exc[:, cols] = exc
        for k in range(3):
            r.rows[128 + SYM * k : 128 + SYM * (k + 1), cols] = inc
            r.rows[160 + SYM * k : 160 + SYM * (k + 1), cols] = exc
            r.rows[192 + SYM * k : 192 + SYM * (k + 1), cols] = oh[:, cols]
    r.sym[...] = r.rows[0:64, :].astype(BF16)
    turned = jnp.transpose(r.rows[...].astype(BF16))
    r.pre[...] = mm(turned[:, 0:128], w_ref[...], NN)
    w2 = w2_ref[...]
    r.pd[...] = mm(turned[:, 128:256], w2[:, 0:768], NN)
    r.count[...] = turned[:, 128:192]
    for st in range(2):
        for part, row0 in ((0, 0), (1, 32)):
            c = part * 256 + st * 128
            flat = mm(
                w2[row0 : row0 + 32, c : c + 128],
                r.rows[128 + row0 : 160 + row0, :].astype(BF16),
                TN,
            )
            for h in range(2):
                i = part * 4 + st * 2 + h
                row = flat[64 * h : 64 * h + 1, :]
                if part == 0:
                    row = -row
                for k, piece in enumerate(thirds(row)):
                    r.prow[SYM * i + k : SYM * i + k + 1, :] = piece


class Unit:
    def __init__(self, r, tabs_ref, st, b, nb):
        self.rows = rows = slice(b * BLOCK, (b + 1) * BLOCK)
        base = st * WIDE
        self.skip = tabs_ref[MISC_ROW + 5 : MISC_ROW + 6, :]
        self.dt = r.pd[rows, 512 + st * 128 : 512 + st * 128 + 128]
        self.p = r.pd[rows, st * 128 : st * 128 + 128]
        self.q = r.pd[rows, 256 + st * 128 : 256 + st * 128 + 128]
        self.total = self.p[BLOCK - 1 : BLOCK, :]
        self.r, self.st, self.b, self.base = r, st, b, base
        lane = lax.broadcasted_iota(jnp.int32, (BLOCK, LANES), 1)
        self.head0 = lane < 64
        row = lax.broadcasted_iota(jnp.int32, (BLOCK, BLOCK), 0)
        self.low = row >= lane
        self.upp = row <= lane

    def pre(self, col, width):
        return self.r.pre[self.rows, self.base + col : self.base + col + width]

    def act(self, col, width):
        v = self.pre(col, width)
        return v * sigmoid(v)

    def by_head(self, v):
        zero = jnp.zeros_like(v)
        return jnp.where(self.head0, v, zero), jnp.where(self.head0, zero, v)

    def decay(self, h):
        r, st = self.r, self.st
        i = st * 2 + h
        rate = r.rate[24 * i : 24 * i + 24, :]
        ends = r.prow[SYM * i : SYM * (i + 1), self.rows]
        starts = r.prow[SYM * (4 + i) : SYM * (5 + i), self.rows]
        zero = jnp.zeros((32, LANES), F32)
        below = jnp.concatenate([rate, ends, zero], 0)
        above = jnp.concatenate([zero, -rate, starts], 0)
        gap = mm(r.count[self.rows, :], jnp.concatenate([below, above], 1).astype(BF16), NN)
        return jnp.exp(jnp.where(self.low, gap[:, 0:LANES], gap[:, LANES : 2 * LANES]))


def state_pass_fwd(r, tabs_ref, nb, units):
    for st in range(2):
        for b in range(nb):
            u = units[st][b]
            xf, xb = u.act(XF, 128), u.act(XB, 128)
            bcf, bcb = u.act(BCF, 256), u.act(BCB, 256)
            r.x[u.rows, st * 256 : st * 256 + 128] = xf
            r.x[u.rows, st * 256 + 128 : st * 256 + 256] = xb
            r.bc[u.rows, st * 512 : st * 512 + 256] = bcf
            r.bc[u.rows, st * 512 + 256 : st * 512 + 512] = bcb
            wf = jnp.exp(u.total - u.p) * (u.dt * xf)
            wb = jnp.exp(u.q) * (u.dt * xb)
            if b < nb - 1:
                r.s[st * 2, b + 1] = mm_fine(bcf[:, 0:128], wf, TN, 2)
            if b > 0:
                r.s[st * 2 + 1, b - 1] = mm_fine(bcb[:, 0:128], wb, TN, 2)
        for b in range(2, nb):
            r.s[st * 2, b] += jnp.exp(units[st][b - 1].total) * r.s[st * 2, b - 1]
        for b in range(nb - 3, -1, -1):
            r.s[st * 2 + 1, b] += jnp.exp(units[st][b + 1].total) * r.s[st * 2 + 1, b + 1]


def together(bodies):
    bodies = list(bodies)
    while bodies:
        bodies = [b for b in bodies if next(b, True) is None]


class Names:
    pass


def named(refs, names):
    r = Names()
    for name, ref in zip(names, refs):
        setattr(r, name, ref)
    return r


KEPT = ("inc", "exc", "oh", "sym", "pre", "pd", "x", "bc", "s", "dec", "wts", "ys")


def kept_shapes(length):
    nb = length // BLOCK
    return [
        ((SYM, length), F32),
        ((SYM, length), F32),
        ((SYM, length), F32),
        ((64, length), BF16),
        ((length, 2 * WIDE), F32),
        ((length, 768), F32),
        ((length, 512), F32),
        ((length, 1024), F32),
        ((4, nb, LANES, LANES), F32),
        ((4 * nb, BLOCK, BLOCK), F32),
        ((8 * nb, BLOCK, BLOCK), BF16),
        ((length, 1024), F32),
    ]


def forward_kernel(scalars, *refs, ns, conv):
    tok_refs, (w_ref, w2_ref, rate_ref, tabs_ref, out_ref) = refs[:ns], refs[ns : ns + 5]
    r = named(refs[ns + 5 :], KEPT + ("rows", "prow", "count"))
    r.rate = rate_ref
    prepare(scalars, tok_refs, w_ref, w2_ref, r, conv)
    units = [[Unit(r, tabs_ref, st, b, ns) for b in range(ns)] for st in range(2)]
    state_pass_fwd(r, tabs_ref, ns, units)
    gated = {}

    def body(st, b):
        u = units[st][b]
        x = [r.x[u.rows, st * 256 + w * 128 : st * 256 + w * 128 + 128] for w in range(2)]
        decays = (u.decay(0), u.decay(1))
        yield
        masks, lefts, cms = (u.low, u.upp), [], []
        for w in range(2):
            c = st * 512 + w * 256
            bm, cm = r.bc[u.rows, c : c + 128], r.bc[u.rows, c + 128 : c + 256]
            lefts.append(mm_fine(cm, bm, NT, 3))
            cms.append(cm)
        yield
        y = u.skip * (x[0] + x[1])
        for w in range(2):
            if (w == 0 and b > 0) or (w == 1 and b < ns - 1):
                enter = jnp.exp(u.p) if w == 0 else jnp.exp(u.total - u.q)
                carried = enter * mm_fine(cms[w], r.s[st * 2 + w, b], NN, 2)
                r.ys[u.rows, st * 512 + w * 256 + 128 : st * 512 + w * 256 + 256] = carried
                y = y + carried
        yield
        for h in range(2):
            r.dec[(st * ns + b) * 2 + h] = decays[h]
        for w in range(2):
            g = jnp.where(masks[w], lefts[w], 0.0)
            lefts[w] = [(g * d).astype(BF16) for d in decays]
            for h in range(2):
                r.wts[((st * ns + b) * 2 + w) * 2 + h] = lefts[w][h]
        yield
        for w in range(2):
            right = u.by_head((u.dt * x[w]).astype(BF16))
            inner = mm(jnp.concatenate(lefts[w], 1), jnp.concatenate(right, 0), NN)
            r.ys[u.rows, st * 512 + w * 256 : st * 512 + w * 256 + 128] = inner
            y = y + inner
        gated[st, b] = y * u.act(ZZ, 128)

    for b0 in range(0, ns, GROUP):
        together(body(st, b) for b in range(b0, min(b0 + GROUP, ns)) for st in range(2))
        for b in range(b0, min(b0 + GROUP, ns)):
            out_ref[:, units[0][b].rows] = jnp.transpose(gated[0, b] + gated[1, b]).astype(BF16)


def backward_kernel(scalars, *refs, ns, nq, conv, vocab):
    tabs_ref, bcp_ref, dt1_ref, perm_ref = refs[:4]
    cot_refs, weight_ref = refs[4 : 4 + nq], refs[4 + nq]
    kept = refs[5 + nq : 5 + nq + len(KEPT)]
    out_ref, *work = refs[5 + nq + len(KEPT) :]
    r = named(list(kept) + work, KEPT + ("ds", "dg", "dpre"))
    cols = cot_refs[0].shape[2]
    cot = jnp.concatenate([a[...].reshape(ns * BLOCK, cols) for a in cot_refs], 1)
    weight = []
    for k in range(nq):
        at = pl.multiple_of(scalars[QUARTERS + k] * cols, LANES)
        rows = pl.ds(pl.multiple_of(scalars[0] * LANES, LANES), LANES)
        weight.append(weight_ref[rows, pl.ds(at, cols)])
    d_gated = mm(cot, jnp.concatenate(weight, 1), NT).astype(BF16).astype(F32)
    mine = scalars[1]
    for k in range(ns):
        at = jnp.bitwise_xor(mine, k)
        r.dg[pl.ds(pl.multiple_of(at * BLOCK, BLOCK), BLOCK), :] = d_gated[
            k * BLOCK : (k + 1) * BLOCK
        ]
    units = [[Unit(r, tabs_ref, st, b, ns) for b in range(ns)] for st in range(2)]
    for st in range(2):
        for b in range(ns):
            u = units[st][b]
            dy = r.dg[u.rows, :] * u.act(ZZ, 128)
            cf = r.bc[u.rows, st * 512 + 128 : st * 512 + 256]
            cb = r.bc[u.rows, st * 512 + 384 : st * 512 + 512]
            if b > 0:
                r.ds[st * 2, b - 1] = mm_fine(cf, jnp.exp(u.p) * dy, TN, 2)
            if b < ns - 1:
                r.ds[st * 2 + 1, b + 1] = mm_fine(cb, jnp.exp(u.total - u.q) * dy, TN, 2)
        for b in range(ns - 3, -1, -1):
            r.ds[st * 2, b] += jnp.exp(units[st][b + 1].total) * r.ds[st * 2, b + 1]
        for b in range(2, ns):
            r.ds[st * 2 + 1, b] += jnp.exp(units[st][b - 1].total) * r.ds[st * 2 + 1, b - 1]
    d_steps = [jnp.zeros((SYM, LANES), F32)] * 2
    d_decays = [jnp.zeros((SYM, LANES), F32)] * 2
    d_tab = 0.0

    def body(st, b):
        u = units[st][b]
        base = st * WIDE
        x = [r.x[u.rows, st * 256 + w * 128 : st * 256 + w * 128 + 128] for w in range(2)]
        dgv = r.dg[u.rows, :]
        pz = u.pre(ZZ, 128)
        sz = sigmoid(pz)
        dy = dgv * (pz * sz)
        dyr = dy.astype(BF16)
        dyw = dyr.astype(F32)
        dy0, dy1 = u.by_head(dyr)
        decays = [r.dec[(st * ns + b) * 2 + h] for h in range(2)]
        inputs = [u.dt * v for v in x]
        ur = [v.astype(BF16) for v in inputs]
        uw = [v.astype(F32) for v in ur]
        uh = [u.by_head(v) for v in ur]
        d_pair = mm(dyr, jnp.concatenate([uh[0][0], uh[0][1], uh[1][0], uh[1][1]], 0), NT)
        yield
        masks = (u.low, u.upp)
        ends = (jnp.exp(u.total - u.p), jnp.exp(u.q))
        enters = (jnp.exp(u.p), jnp.exp(u.total - u.q))
        weights, bms, cms = [], [], []
        for w in range(2):
            c = st * 512 + w * 256
            bm, cm = r.bc[u.rows, c : c + 128], r.bc[u.rows, c + 128 : c + 256]
            weights.append([r.wts[((st * ns + b) * 2 + w) * 2 + h] for h in range(2)])
            bms.append(bm)
            cms.append(cm)
        du_both = mm(
            jnp.concatenate(
                [
                    jnp.concatenate([weights[0][0], weights[1][0]], 1),
                    jnp.concatenate([weights[0][1], weights[1][1]], 1),
                ],
                0,
            ),
            jnp.concatenate([dy0, dy1], 0),
            TN,
        )
        yield
        y = u.skip * (x[0] + x[1])
        mixes, step_part, flat = [], 0.0, 0.0
        for w in range(2):
            yield
            c = st * 512 + w * 256
            inner = r.ys[u.rows, c : c + 128]
            du_in = du_both[w * BLOCK : (w + 1) * BLOCK]
            has_enter = (w == 0 and b > 0) or (w == 1 and b < ns - 1)
            has_leave = (w == 0 and b < ns - 1) or (w == 1 and b > 0)
            y = y + inner
            row = dyw * inner - uw[w] * du_in
            du = du_in
            d_g = jnp.where(
                masks[w],
                d_pair[:, w * 256 : w * 256 + 128] * decays[0]
                + d_pair[:, w * 256 + 128 : w * 256 + 256] * decays[1],
                0.0,
            ).astype(BF16)
            d_c = mm(d_g, bms[w].astype(BF16), NN)
            d_b = mm(d_g, cms[w].astype(BF16), TN)
            enter_part = gain_part = None
            if has_enter:
                state = r.s[st * 2 + w, b]
                carried = r.ys[u.rows, c + 128 : c + 256]
                y = y + carried
                enter_part = dy * carried
                d_c = d_c + mm((enters[w] * dy).astype(BF16), state.astype(BF16), NT)
            if has_leave:
                d_state = r.ds[st * 2 + w, b]
                d_gain = mm_fine(bms[w], d_state, NN, 2)
                du = du + ends[w] * d_gain
                gain = ends[w] * inputs[w]
                gain_part = gain * d_gain
                d_b = d_b + mm(gain.astype(BF16), d_state.astype(BF16), NT)
            if has_enter and has_leave:
                flat = flat + jnp.exp(u.total) * jnp.sum(state * d_state, 0, keepdims=True)
            if w == 1:
                row = -row
            if enter_part is not None:
                row = row + enter_part if w == 0 else row - enter_part
            if gain_part is not None:
                row = row - gain_part if w == 0 else row + gain_part
            if w == 0 and gain_part is not None:
                flat = flat + jnp.sum(gain_part, 0, keepdims=True)
            if w == 1 and enter_part is not None:
                flat = flat + jnp.sum(enter_part, 0, keepdims=True)
            mixes.append(row)
            step_part = step_part + du * x[w]
            dx = du * u.dt + dy * u.skip
            px = u.pre((XF, XB)[w], 128)
            sx = sigmoid(px)
            col = base + (XF, XB)[w]
            r.dpre[u.rows, col : col + 128] = (dx * (sx * (1.0 + px * (1.0 - sx)))).astype(BF16)
            col = (BCF, BCB)[w]
            for i, grad in enumerate((d_b, d_c)):
                pb = u.pre(col + 128 * i, 128)
                sb = sigmoid(pb)
                at = base + col + 128 * i
                r.dpre[u.rows, at : at + 128] = (
                    grad * (sb * (1.0 + pb * (1.0 - sb)))
                ).astype(BF16)
        yield
        d_z = dgv * y * (sz * (1.0 + pz * (1.0 - sz)))
        r.dpre[u.rows, base + ZZ : base + ZZ + 128] = d_z.astype(BF16)
        inc = r.inc[:, u.rows]
        exc = r.exc[:, u.rows]
        inc_b, exc_b, oh_b = inc.astype(BF16), exc.astype(BF16), r.oh[:, u.rows].astype(BF16)
        right = list(halves(mixes[0])) + list(halves(mixes[1]))
        decay_part = mm(
            jnp.concatenate([inc_b, inc_b, exc_b, exc_b], 1), jnp.concatenate(right, 0), NN
        )
        decay_part = decay_part + inc[:, BLOCK - 1 : BLOCK] * flat
        step_sum = mm(
            jnp.concatenate([oh_b, oh_b], 1), jnp.concatenate(halves(step_part), 0), NN
        )
        d_steps[st] = d_steps[st] + step_sum
        d_decays[st] = d_decays[st] + decay_part

    for b0 in range(0, ns, GROUP_BACK):
        last = min(b0 + GROUP_BACK, ns)
        together(body(st, b) for b in range(b0, last) for st in range(2))
        span = slice(b0 * BLOCK, last * BLOCK)
        d_tab = d_tab + mm(r.sym[:, span], r.dpre[span, :], NN)
    mid = SYM * (conv - 1)
    result = None
    for st in range(2):
        base = st * WIDE
        d_x = jnp.zeros((SYM, 128), F32)
        d_bc = jnp.zeros((SYM, 256), F32)
        for k in range(conv):
            cx = tabs_ref[MISC_ROW + k : MISC_ROW + k + 1, :]
            cbc = bcp_ref[SYM + k : SYM + k + 1, :]
            lo, hi = mid - SYM * k, mid + SYM * k
            d_x = d_x + cx * (
                d_tab[lo : lo + SYM, base + XF : base + XF + 128]
                + d_tab[hi : hi + SYM, base + XB : base + XB + 128]
            )
            d_bc = d_bc + cbc * (
                d_tab[lo : lo + SYM, base + BCF : base + BCF + 256]
                + d_tab[hi : hi + SYM, base + BCB : base + BCB + 256]
            )
        d_zt = d_tab[mid : mid + SYM, base + ZZ : base + ZZ + 128]
        dtt = dt1_ref[...] if st else tabs_ref[DT_ROW : DT_ROW + SYM, :]
        rate = -jnp.exp(tabs_ref[MISC_ROW + 4 : MISC_ROW + 5, :])
        d_dt = (d_steps[st] + rate * d_decays[st]) * sigmoid(dtt)
        wide = jnp.concatenate([d_x, d_zt, d_dt, d_bc], 1)
        if st == 0:
            result = wide
        else:
            for k in range(vocab):
                result = result + perm_ref[:, k : k + 1] * wide[k : k + 1]
    out_ref[...] = result


SMEM = pl.BlockSpec(memory_space=pltpu.SMEM)
VMEM = pl.BlockSpec(memory_space=pltpu.VMEM)
HBM = pl.BlockSpec(memory_space=pl.ANY)


def params(mib):
    return pltpu.CompilerParams(vmem_limit_bytes=mib * 1024 * 1024)


def call_tables(scalars, raw):
    basemap, xz_table, bc_table, conv_x, conv_bc, dt_table, a_log, skip_gain = raw
    conv, vocab = conv_x.shape[0], xz_table.shape[0]
    outs = [
        ((TAB_ROWS, LANES), F32),
        ((2 * SYM, 256), F32),
        ((SYM, LANES), F32),
        ((SYM, LANES), F32),
        ((128, 2 * WIDE), BF16),
        ((128, 768), BF16),
        ((96, LANES), F32),
    ]
    return pl.pallas_call(
        functools.partial(tables_kernel, conv=conv, vocab=vocab),
        out_shape=[jax.ShapeDtypeStruct(*a) for a in outs],
        in_specs=[SMEM, SMEM, VMEM, VMEM, SMEM],
        out_specs=[VMEM] * len(outs),
        scratch_shapes=[pltpu.VMEM((64, 2 * WIDE), F32), pltpu.VMEM((128, 768), F32)],
        compiler_params=params(8),
        cost_estimate=pl.CostEstimate(flops=2 * 10**9, transcendentals=0, bytes_accessed=10**6),
        name="tables",
    )(
        scalars,
        basemap,
        jnp.concatenate([xz_table.reshape(2 * vocab, -1), conv_x], 0),
        jnp.concatenate([bc_table, conv_bc], 0),
        jnp.concatenate([dt_table, a_log[None], skip_gain[None]], 0),
    )


def call_forward(scalars, pays, w, w2, rate, tabs, conv):
    ns = len(pays)
    length = ns * BLOCK
    outs = [((LANES, length), BF16)] + kept_shapes(length)
    return pl.pallas_call(
        functools.partial(forward_kernel, ns=ns, conv=conv),
        out_shape=[jax.ShapeDtypeStruct(*a) for a in outs],
        in_specs=[SMEM] + [VMEM] * (ns + 4),
        out_specs=[VMEM] * len(outs),
        scratch_shapes=[
            pltpu.VMEM((256, length), F32),
            pltpu.VMEM((64, length), F32),
            pltpu.VMEM((length, 64), BF16),
        ],
        compiler_params=params(8),
        cost_estimate=pl.CostEstimate(
            flops=5 * 10**9, transcendentals=0, bytes_accessed=8 * LANES * length
        ),
        name="mix_forward",
    )(scalars, *pays, w, w2, rate, tabs)


def call_backward(scalars, tables, cots, out_weight, kept, conv, vocab):
    length = kept[0].shape[1]
    ns = length // BLOCK
    return pl.pallas_call(
        functools.partial(backward_kernel, ns=ns, nq=len(cots), conv=conv, vocab=vocab),
        out_shape=jax.ShapeDtypeStruct((SYM, 640), F32),
        in_specs=[SMEM] + [VMEM] * (len(tables) + len(cots) + 1 + len(kept)),
        out_specs=VMEM,
        scratch_shapes=[
            pltpu.VMEM((4, ns, LANES, LANES), F32),
            pltpu.VMEM((length, LANES), F32),
            pltpu.VMEM((length, 2 * WIDE), BF16),
        ],
        compiler_params=params(10),
        cost_estimate=pl.CostEstimate(
            flops=6 * 10**9, transcendentals=0, bytes_accessed=8 * LANES * length
        ),
        name="mix_backward",
    )(scalars, *tables, *cots, out_weight, *kept)


QUARTERS = 3


def out_kernel(scalars, *refs, ns, nh, nc):
    slices, weight_ref, outs = refs[: ns * nc], refs[ns * nc], refs[ns * nc + 1 :]
    here = pl.ds(pl.multiple_of(scalars[1] * BLOCK, BLOCK), BLOCK)
    places = QUARTERS + nh * nc
    cols = outs[0].shape[1]
    left = jnp.concatenate([a[:, here] for a in slices], 0)
    for k in range(nh):
        at = pl.ds(pl.multiple_of(scalars[QUARTERS + k * nc] * cols, LANES), cols)
        right = []
        for i in range(ns * nc):
            rows = pl.ds(pl.multiple_of(scalars[places + i] * LANES, LANES), LANES)
            right.append(weight_ref[rows, at])
        outs[k][...] = mm(left, jnp.concatenate(right, 0), TN)


def call_out(scalars, slices, out_weight, ns, nh, nc):
    cols = out_weight.shape[1] // (nh * nc)
    return pl.pallas_call(
        functools.partial(out_kernel, ns=ns, nh=nh, nc=nc),
        out_shape=[jax.ShapeDtypeStruct((BLOCK, cols), F32)] * nh,
        in_specs=[SMEM] + [VMEM] * (len(slices) + 1),
        out_specs=[VMEM] * nh,
        compiler_params=params(8),
        name="layer_out",
    )(scalars, *slices, out_weight)


def weight_kernel(scalars, *refs, ns, nh, nc):
    slices, cots = refs[: ns * nc], refs[ns * nc : ns * nc + nh * nc]
    out_ref, mark_ref, left, buf, sems = refs[ns * nc + nh * nc :]
    mine = scalars[1]
    places = QUARTERS + nh * nc
    cols = cots[0].shape[2]
    mark_ref[...] = jnp.zeros_like(mark_ref)
    copies = []
    for n in range(ns * nc):
        span = slice(n * LANES, (n + 1) * LANES)
        for k in range(ns):
            at = pl.multiple_of(jnp.bitwise_xor(mine, k) * BLOCK, BLOCK)
            left[span, k * BLOCK : (k + 1) * BLOCK] = slices[n][:, pl.ds(at, BLOCK)]
        for q in range(nh * nc):
            at = pl.multiple_of(scalars[QUARTERS + q] * cols, LANES)
            right = cots[q][...].reshape(ns * BLOCK, cols)
            buf[span, pl.ds(at, cols)] = mm(left[span, :], right, NN)
        to = pl.multiple_of(scalars[places + n] * LANES, LANES)
        copy = pltpu.make_async_copy(
            buf.at[pl.ds(n * LANES, LANES), :], out_ref.at[pl.ds(to, LANES), :], sems.at[n]
        )
        copy.start()
        copies.append(copy)
    for copy in copies:
        copy.wait()


def call_weight(scalars, slices, cots, width, ns, nh, nc):
    length = slices[0].shape[1]
    rows = ns * nc * LANES
    return pl.pallas_call(
        functools.partial(weight_kernel, ns=ns, nh=nh, nc=nc),
        out_shape=[
            jax.ShapeDtypeStruct((rows, width), F32),
            jax.ShapeDtypeStruct((SYM, LANES), F32),
        ],
        in_specs=[SMEM] + [VMEM] * (len(slices) + len(cots)),
        out_specs=[HBM, VMEM],
        scratch_shapes=[
            pltpu.VMEM((rows, length), BF16),
            pltpu.VMEM((rows, width), F32),
            pltpu.SemaphoreType.DMA((ns * nc,)),
        ],
        compiler_params=params(12),
        cost_estimate=pl.CostEstimate(
            flops=2 * rows * width * length, transcendentals=0, bytes_accessed=6 * rows * width
        ),
        name="weight_grad",
    )(scalars, *slices, *cots)


def final_kernel(scalars, *refs, ns, nh, vocab, places):
    packs, parts = refs[:ns], refs[ns : ns + nh]
    out_ref, xz_ref, bc_ref, dt_ref = refs[ns + nh + 1 :]
    total = parts[0][...]
    for a in parts[1:]:
        total = total + a[...]
    out_ref[...] = total.astype(BF16)
    d_bc = packs[0][:, 768:1024]
    for a in packs[1:]:
        d_bc = d_bc + a[:, 768:1024]
    for i in range(2):
        for k in range(vocab):
            bc_ref[k, i : i + 1, :] = d_bc[k : k + 1, i * 128 : i * 128 + 128]
    lane = lax.broadcasted_iota(jnp.int32, (SYM, dt_ref.shape[1]), 1)
    d_dt = jnp.zeros((SYM, dt_ref.shape[1]), F32)
    for n in range(2 * ns):
        j = scalars[places + n]
        piece = packs[n % ns][:, n // ns * 384 : n // ns * 384 + 384]
        for i in range(2):
            for k in range(vocab):
                xz_ref[k, i : i + 1, pl.ds(pl.multiple_of(j * LANES, LANES), LANES)] = piece[
                    k : k + 1, i * 128 : i * 128 + 128
                ]
            row = jnp.sum(piece[:, 256 + 64 * i : 320 + 64 * i], 1, keepdims=True)
            d_dt = jnp.where(lane == 2 * j + i, row, d_dt)
    dt_ref[...] = d_dt[:vocab]


def call_final(scalars, packs, parts, mark, raw, places):
    shapes = [raw[1].shape, raw[2].shape, raw[5].shape]
    arrays = list(packs) + list(parts)
    return pl.pallas_call(
        functools.partial(
            final_kernel, ns=len(packs), nh=len(parts), vocab=raw[1].shape[0], places=places
        ),
        out_shape=[jax.ShapeDtypeStruct(parts[0].shape, BF16)]
        + [jax.ShapeDtypeStruct(a, F32) for a in shapes],
        in_specs=[SMEM] + [VMEM] * (len(arrays) + 1),
        out_specs=[VMEM] * (len(shapes) + 1),
        compiler_params=params(8),
        name="place_grads",
    )(scalars, *arrays, mark)


def around(x, axis):
    n = lax.axis_size(axis)
    return [x] + [lax.ppermute(x, axis, [(i, i ^ k) for i in range(n)]) for k in range(1, n)]


def across(x, hops, nh, nc):
    pairs = [
        (a * nc + b, (a + hops[0]) % nh * nc + (b + hops[1]) % nc)
        for a in range(nh)
        for b in range(nc)
    ]
    return lax.ppermute(x, ("head", "sub"), pairs)


def by_channel(
    token_ids, basemap, xz_table, bc_table, dt_table, conv_x, conv_bc, a_log, skip_gain, out_weight, cotangent
):
    ns, nc, nh = lax.axis_size("seq"), lax.axis_size("sub"), lax.axis_size("head")
    s, c, h = lax.axis_index("seq"), lax.axis_index("sub"), lax.axis_index("head")
    width = out_weight.shape[1]
    cols = width // (nh * nc)
    raw = (basemap, xz_table, bc_table, conv_x, conv_bc, dt_table, a_log, skip_gain)
    symbols = jnp.pad(token_ids.astype(BF16).reshape(1, BLOCK), ((0, 15), (0, cols - BLOCK)))
    pays = around(jnp.concatenate([cotangent, symbols], 0), "seq")
    slot = jnp.arange(nh * nc, dtype=jnp.int32)
    quarters = (h - slot // nc) % nh * nc + (c - slot % nc) % nc
    slot = jnp.arange(ns * nc, dtype=jnp.int32)
    places = (c - slot // ns) % nc * ns + jnp.bitwise_xor(s, slot % ns)
    scalars = jnp.concatenate([jnp.stack([c * ns + s, s, c]), quarters, places]).astype(jnp.int32)
    stacked = jnp.stack([a[:BLOCK] for a in pays], 0)
    heads = [stacked] + [across(stacked, (k, 0), nh, nc) for k in range(1, nh)]
    side = across(stacked, (0, 1), nh, nc)
    conv, vocab = conv_x.shape[0], xz_table.shape[0]
    *tables, w, w2, rate = call_tables(scalars, raw)
    gated, *kept = call_forward(scalars, pays, w, w2, rate, tables[0], conv)
    heads, _ = lax.optimization_barrier((heads, gated))
    cots = [heads[0], side]
    for a in heads[1:]:
        cots += [a, across(a, (0, 1), nh, nc)]
    hop = lambda x, k: lax.ppermute(x, "seq", [(i, i ^ k) for i in range(ns)])
    direct = {k: hop(gated, k) for k in (1 << n for n in range(ns.bit_length() - 1))}
    grads = call_backward(scalars, tables, cots, out_weight, kept, conv, vocab)
    direct, _ = lax.optimization_barrier((direct, grads))
    held = {0: gated, **direct}
    for k in range(3, ns):
        if k not in held:
            held[k] = hop(held[k & (k - 1)], k & -k)
    slices = [held[k] for k in range(ns)]
    slices = slices + [across(a, (0, 1), nh, nc) for a in slices]
    shared = grads[:, 384:]
    beside = across(grads, (0, 1), nh, nc)
    for a in range(1, nh):
        for b in range(nc):
            shared = shared + across(grads[:, 384:], (a, b), nh, nc)
    packed = jnp.concatenate([grads[:, :384], beside[:, :384], shared + beside[:, 384:]], 1)
    packs = around(packed, "seq")
    parts = call_out(scalars, slices, out_weight, ns, nh, nc)
    parts = [parts[0]] + [across(parts[k], (nh - k, 0), nh, nc) for k in range(1, nh)]
    d_out_weight, mark = call_weight(scalars, slices, cots, width, ns, nh, nc)
    layer_out, d_xz, d_bc, d_dt = call_final(
        scalars, packs, parts, mark, raw, QUARTERS + nh * nc
    )
    return (layer_out, d_out_weight, d_xz, d_bc, d_dt)


PRECISE = lax.Precision.HIGHEST


def carried_in(part, axis, combine, identity):
    place = lax.axis_index(axis)
    gathered = jax.tree.map(lambda a: lax.all_gather(a, axis), part)
    state = jax.tree.map(lambda a, e: jnp.zeros_like(a) + jnp.asarray(e, a.dtype), part, identity)

    def one(hop, state):
        return combine(
            state, jax.tree.map(lambda a: lax.dynamic_index_in_dim(a, hop, 0, False), gathered)
        )

    return lax.fori_loop(0, place, one, state)


def carried_in_2(array, axis, combine, identity):
    length, mine = (lax.axis_size(axis), lax.axis_index(axis))
    everything = jax.tree.map(
        lambda part, kind: lax.all_gather(part.astype(kind), axis),
        array,
        jax.tree.map(lambda a: jnp.bfloat16 if a.dtype == jnp.float32 else a.dtype, array),
    )
    start = jax.tree.map(
        lambda part, zero: jnp.broadcast_to(jnp.asarray(zero, part.dtype), part.shape),
        array,
        identity,
    )

    def hop(k, before):
        at = length - 1 - k
        reached = at > mine
        new = combine(
            before, jax.tree.map(lambda part, own: part[at].astype(own.dtype), everything, array)
        )
        return jax.tree.map(lambda a, b: jnp.where(reached, a, b), new, before)

    return lax.fori_loop(0, length, hop, start)


def with_halo(block, sides, width):
    for axis, dim in sides:
        count = lax.axis_size(axis)
        forward = [(i, i + 1) for i in range(count - 1)]
        backward = [(target, source) for source, target in forward]
        low = lax.ppermute(
            lax.slice_in_dim(block, block.shape[dim] - width, None, axis=dim), axis, forward
        )
        high = lax.ppermute(lax.slice_in_dim(block, 0, width, axis=dim), axis, backward)
        block = jnp.concatenate([low, block, high], axis=dim)
    return block


def block_step(carry_state, pieces):
    scaled_x, logdec, b_mat, c_mat = pieces
    block_len = scaled_x.shape[0]
    running = jnp.cumsum(logdec, axis=0)
    by_head = running.T
    causal_mask = (jnp.arange(block_len)[:, None] >= jnp.arange(block_len)[None, :])[None, :, :]
    gap_matrix = by_head[:, :, None] - by_head[:, None, :]
    decay_mat = jnp.where(causal_mask, jnp.exp(jnp.where(causal_mask, gap_matrix, 0.0)), 0.0)
    scores = jnp.einsum("tn,sn->ts", c_mat, b_mat, precision=PRECISE)
    within = jnp.einsum("hts,shp->thp", scores[None, :, :] * decay_mat, scaled_x, precision=PRECISE)
    carried = jnp.exp(running)[:, :, None] * jnp.einsum(
        "tn,hpn->thp", c_mat, carry_state, precision=PRECISE
    )
    to_end = jnp.exp(running[-1][None, :] - running)
    gained = jnp.einsum("shp,sn->hpn", to_end[:, :, None] * scaled_x, b_mat, precision=PRECISE)
    return (jnp.exp(running[-1])[:, None, None] * carry_state + gained, within + carried)


def state_pass(inputs, start_state, block_len):
    scaled_x, logdec, b_mat, c_mat = inputs
    block_count = scaled_x.shape[0] // block_len
    pieces = (
        scaled_x.reshape((block_count, block_len) + scaled_x.shape[1:]),
        logdec.reshape(block_count, block_len, -1),
        b_mat.reshape(block_count, block_len, -1),
        c_mat.reshape(block_count, block_len, -1),
    )
    end_state, outputs = lax.scan(jax.checkpoint(block_step), start_state, pieces)
    return (outputs.reshape(scaled_x.shape), end_state)


def final_state(inputs):
    scaled_x, logdec, b_mat, c_mat = inputs
    running = jnp.cumsum(logdec, axis=0)
    to_end = jnp.exp(running[-1][None, :] - running)
    gained = jnp.einsum("shp,sn->hpn", to_end[:, :, None] * scaled_x, b_mat, precision=PRECISE)
    return (jnp.exp(running[-1]), gained)


def lookup(symbols, table):
    vocab_size = table.shape[0]
    onehot = (symbols[:, None] == jnp.arange(vocab_size, dtype=jnp.int32)[None, :]).astype(
        jnp.float32
    )
    return jnp.dot(onehot, table, precision=PRECISE)


def conv_rows(extended, weight, row_count, forward):
    conv_width = weight.shape[0]
    rim_width = conv_width - 1
    summed = jnp.zeros((row_count, extended.shape[1]), jnp.float32)
    for offset in range(conv_width):
        if forward:
            first_row = rim_width - offset
        else:
            first_row = rim_width + offset
        summed = summed + weight[offset][None, :] * extended[first_row : first_row + row_count]
    return summed


def open_inputs(ext_sym, inside_mask, tables, frozen):
    xz_tab, bc_tab, dt_tab = tables
    conv_inner, conv_shared, log_rates, skip_vals = frozen
    rim_width = conv_inner.shape[0] - 1
    row_count = ext_sym.shape[0] - 2 * rim_width
    vocab_size = xz_tab.shape[0]
    inner_dim = xz_tab.shape[2]
    head_count = dt_tab.shape[1]
    state_dim = bc_tab.shape[2]
    looked = lookup(ext_sym, xz_tab.reshape(vocab_size, 2 * inner_dim)) * inside_mask[:, None]
    pre_x = looked[:, :inner_dim]
    gate_act = jax.nn.silu(looked[rim_width : rim_width + row_count, inner_dim:])
    pre_bc = lookup(ext_sym, bc_tab.reshape(vocab_size, 2 * state_dim)) * inside_mask[:, None]
    dt_step = jax.nn.softplus(lookup(ext_sym[rim_width : rim_width + row_count], dt_tab))
    logdec = -jnp.exp(log_rates)[None, :] * dt_step
    flat_bc = conv_shared.reshape(conv_inner.shape[0], 2 * state_dim)

    def one_way(forward):
        x_conv = jax.nn.silu(conv_rows(pre_x, conv_inner, row_count, forward)).reshape(
            row_count, head_count, -1
        )
        bc_conv = jax.nn.silu(conv_rows(pre_bc, flat_bc, row_count, forward))
        return (x_conv, bc_conv[:, :state_dim], bc_conv[:, state_dim:])

    x_fwd, b_fwd, c_fwd = one_way(True)
    x_back, b_back, c_back = one_way(False)
    ahead_in = (x_fwd * dt_step[:, :, None], logdec, b_fwd, c_fwd)
    behind_in = (
        jnp.flip(x_back * dt_step[:, :, None], 0),
        jnp.flip(logdec, 0),
        jnp.flip(b_back, 0),
        jnp.flip(c_back, 0),
    )
    skip_term = skip_vals[None, :, None] * (x_fwd + x_back)
    return (ahead_in, behind_in, skip_term, gate_act)


def combine(earlier, later):
    decay_early, state_early = earlier
    decay_late, state_late = later
    return (decay_early * decay_late, decay_late[:, None, None] * state_early + state_late)


def carries(ahead_pair, behind_pair):
    ahead_out = carried_in(
        (ahead_pair[0], ahead_pair[1]),
        "seq",
        combine,
        (jnp.ones_like(ahead_pair[0]), jnp.zeros_like(ahead_pair[1])),
    )
    behind_out = carried_in_2(
        (behind_pair[0], behind_pair[1]),
        "seq",
        combine,
        (jnp.ones_like(behind_pair[0]), jnp.zeros_like(behind_pair[1])),
    )
    return (ahead_out[1], behind_out[1])


def decay_weights(adjoint, start_state):
    return jnp.sum(adjoint * start_state, axis=(1, 2))


def shards(
    token_ids,
    basemap,
    xz_table,
    bc_table,
    dt_table,
    conv_x,
    conv_bc,
    a_log,
    skip_gain,
    out_weight,
    cotangent,
):
    row_count = token_ids.shape[0]
    rim_width = conv_x.shape[0] - 1
    ext_ids = with_halo(token_ids, (("seq", 0),), rim_width)
    first_row = lax.axis_index("seq") * row_count - rim_width
    where_global = first_row + jnp.arange(row_count + 2 * rim_width, dtype=jnp.int32)
    inside_mask = jnp.logical_and(
        where_global >= 0, where_global < row_count * lax.axis_size("seq")
    ).astype(jnp.float32)
    vocab_size = basemap.shape[0]
    matches = ext_ids[:, None] == jnp.arange(vocab_size, dtype=jnp.int32)[None, :]
    mapped = jnp.sum(jnp.where(matches, basemap[None, :], 0), axis=1)
    ext_sym = jnp.where(lax.axis_index("sub") == 1, mapped, ext_ids)
    tables = (xz_table.astype(jnp.float32), bc_table.astype(jnp.float32), dt_table)
    frozen = (conv_x.astype(jnp.float32), conv_bc.astype(jnp.float32), a_log, skip_gain)

    def summary(tabs_in):
        ahead_in, behind_in, skip_term, gate_act = open_inputs(
            ext_sym, inside_mask, tabs_in, frozen
        )
        decay_fwd, end_fwd = final_state(ahead_in)
        decay_back, end_back = final_state(behind_in)
        return (decay_fwd, end_fwd, decay_back, end_back)

    (decay_fwd, end_fwd, decay_back, end_back), pull_summary = jax.vjp(summary, tables)
    start_fwd, start_back = carries((decay_fwd, end_fwd), (decay_back, end_back))

    def finished(tabs_in, begin_fwd, begin_back):
        ahead_in, behind_in, skip_term, gate_act = open_inputs(
            ext_sym, inside_mask, tabs_in, frozen
        )
        out_fwd, unused_fwd = state_pass(ahead_in, begin_fwd, BLOCK)
        out_back, unused_back = state_pass(behind_in, begin_back, BLOCK)
        return (out_fwd + jnp.flip(out_back, 0) + skip_term).reshape(row_count, -1) * gate_act

    gated, pull_finished = jax.vjp(finished, tables, start_fwd, start_back)
    gated_bf = gated.astype(jnp.bfloat16)
    products = jnp.dot(gated_bf, out_weight, preferred_element_type=jnp.float32)
    layer_out = lax.psum_scatter(products, ("head", "sub"), scatter_dimension=1, tiled=True).astype(
        jnp.bfloat16
    )
    full_cot = lax.all_gather(cotangent, ("head", "sub"), axis=1, tiled=True)
    d_gated = jnp.einsum(
        "tc,kc->tk", full_cot, out_weight, preferred_element_type=jnp.float32
    ).astype(jnp.bfloat16)
    weight_part = jnp.einsum("tk,tc->kc", gated_bf, full_cot, preferred_element_type=jnp.float32)
    d_gated_wide = lax.optimization_barrier(d_gated).astype(jnp.float32)
    grads_first, direct_fwd, direct_back = pull_finished(d_gated_wide)
    adjoint_back, adjoint_fwd = carries((decay_back, direct_back), (decay_fwd, direct_fwd))
    grads_second = pull_summary(
        (
            decay_weights(adjoint_fwd, start_fwd),
            adjoint_fwd,
            decay_weights(adjoint_back, start_back),
            adjoint_back,
        )
    )[0]
    d_tables = jax.tree.map(lambda former, latter: former + latter, grads_first, grads_second)
    d_xz, d_bc, d_dt = d_tables
    d_bc = lax.psum(d_bc, ("seq", "head", "sub"))
    d_out_weight, d_xz, d_dt = lax.psum((weight_part, d_xz, d_dt), ("seq", "sub"))
    return (layer_out, d_out_weight, d_xz, d_bc, d_dt)


def solution(mesh):
    in_specs = (
        P(("grp", "seq")),
        P(),
        P(None, None, "head"),
        P(),
        P(None, "head"),
        P(None, "head"),
        P(),
        P("head"),
        P("head"),
        P("head", None),
        P(("grp", "seq"), ("head", "sub")),
    )
    out_specs = (
        P(("grp", "seq"), ("head", "sub")),
        P(("grp", "head"), None),
        P("grp", None, "head"),
        P("grp", None, None),
        P("grp", "head"),
    )
    def run(*args):
        ns, nc = mesh.shape["seq"], mesh.shape["sub"]
        rows, inner, heads = args[0].shape[0], args[2].shape[2], args[4].shape[1]
        by_lanes = (
            rows == BLOCK
            and nc == 2
            and ns > 1
            and ns & (ns - 1) == 0
            and inner == ns * nc * LANES
            and inner == heads * (LANES // 2)
            and args[3].shape[2] == LANES
            and args[5].shape[0] == 4
            and args[9].shape[1] == args[10].shape[1] * nc * mesh.shape["head"]
        )
        return (by_channel if by_lanes else shards)(*args)

    return jax.shard_map(run, mesh=mesh, in_specs=in_specs, out_specs=out_specs, check_vma=False)
```

```python
import functools

import jax
import jax.numpy as jnp
from jax import lax
from jax.experimental import pallas as pl
from jax.experimental.pallas import tpu as pltpu
from jax.sharding import PartitionSpec as P

BLOCK = 128
LANES = 128
SYM = 8
F32 = jnp.float32
BF16 = jnp.bfloat16
GROUP = 2
GROUP_BACK = 4
NN = (((1,), (0,)), ((), ()))
NT = (((1,), (1,)), ((), ()))
TN = (((0,), (0,)), ((), ()))
X_ROW, Z_ROW, DT_ROW, MISC_ROW, TAB_ROWS = 0, 8, 16, 24, 32
XF, XB, ZZ, BCF, BCB, WIDE = 0, 128, 256, 384, 640, 896


def mm(a, b, dims):
    return lax.dot_general(a, b, dims, preferred_element_type=F32)


def halves(a):
    top = a.astype(BF16)
    return top, (a - top.astype(F32)).astype(BF16)


def thirds(a):
    top = a.astype(BF16).astype(F32)
    rest = a - top
    mid = rest.astype(BF16).astype(F32)
    return top, mid, rest - mid


def mm_fine(a, b, dims, terms):
    ah, al = halves(a)
    bh, bl = halves(b)
    (ca,), (cb,) = dims[0]
    left, right = [ah], [bh]
    if terms >= 2:
        left.append(al)
        right.append(bh)
    if terms >= 3:
        left.append(ah)
        right.append(bl)
    return mm(jnp.concatenate(left, ca), jnp.concatenate(right, cb), dims)


def permuted(table, basemap, count):
    row = lax.broadcasted_iota(jnp.int32, table.shape, 0)
    out = jnp.zeros_like(table)
    for k in range(count):
        picked = jnp.zeros_like(table[0:1])
        for m in range(count):
            picked = jnp.where(basemap[k] == m, table[m : m + 1], picked)
        out = jnp.where(row == k, picked, out)
    return out


def sigmoid(v):
    return 0.5 * jnp.tanh(0.5 * v) + 0.5


def gather_tables(j, raw, tabs_ref, bcp_ref, conv, vocab):
    wide_ref, bc_ref, dt_ref = raw
    lanes = pl.ds(pl.multiple_of(j * LANES, LANES), LANES)
    head0 = lax.broadcasted_iota(jnp.int32, (1, LANES), 1) < 64
    pair = lambda a, b: jnp.where(head0, a, b)
    tabs_ref[...] = jnp.zeros_like(tabs_ref)
    bcp_ref[...] = jnp.zeros_like(bcp_ref)
    for k in range(vocab):
        tabs_ref[X_ROW + k : X_ROW + k + 1, :] = wide_ref[2 * k : 2 * k + 1, lanes].astype(F32)
        tabs_ref[Z_ROW + k : Z_ROW + k + 1, :] = wide_ref[2 * k + 1 : 2 * k + 2, lanes].astype(F32)
        tabs_ref[DT_ROW + k : DT_ROW + k + 1, :] = pair(dt_ref[k, 2 * j], dt_ref[k, 2 * j + 1])
        for i in range(2):
            bcp_ref[k : k + 1, i * 128 : i * 128 + 128] = bc_ref[k, i : i + 1, :].astype(F32)
    for k in range(conv):
        tabs_ref[MISC_ROW + k : MISC_ROW + k + 1, :] = wide_ref[2 * vocab + k : 2 * vocab + k + 1, lanes].astype(F32)
        for i in range(2):
            bcp_ref[SYM + k : SYM + k + 1, i * 128 : i * 128 + 128] = bc_ref[
                vocab + k, i : i + 1, :
            ].astype(F32)
    at = MISC_ROW + 4
    tabs_ref[at : at + 1, :] = pair(dt_ref[vocab, 2 * j], dt_ref[vocab, 2 * j + 1])
    tabs_ref[at + 1 : at + 2, :] = pair(
        dt_ref[vocab + 1, 2 * j], dt_ref[vocab + 1, 2 * j + 1]
    )


def tables_kernel(scalars, basemap, *refs, conv, vocab):
    tabs_ref, bcp_ref, dt1_ref, perm_ref, w_ref, w2_out, rate_ref, wf, w2 = refs[3:]
    gather_tables(scalars[0], refs[:3], tabs_ref, bcp_ref, conv, vocab)
    row = lax.broadcasted_iota(jnp.int32, perm_ref.shape, 0)
    lane = lax.broadcasted_iota(jnp.int32, perm_ref.shape, 1)
    perm = jnp.zeros(perm_ref.shape, F32)
    for k in range(vocab):
        perm = jnp.where(jnp.logical_and(lane == k, row == basemap[k]), 1.0, perm)
    perm_ref[...] = perm
    wf[...] = jnp.zeros_like(wf)
    w2[...] = jnp.zeros_like(w2)
    for st in range(2):
        fetch = (lambda t: t) if st == 0 else (lambda t: permuted(t, basemap, vocab))
        xt = fetch(tabs_ref[X_ROW : X_ROW + SYM, :])
        zt = fetch(tabs_ref[Z_ROW : Z_ROW + SYM, :])
        dtt = fetch(tabs_ref[DT_ROW : DT_ROW + SYM, :])
        if st == 1:
            dt1_ref[...] = dtt
        bct = fetch(bcp_ref[0:SYM, :])
        base = st * WIDE
        mid = SYM * (conv - 1)
        wf[mid : mid + SYM, base + ZZ : base + ZZ + LANES] = zt
        for k in range(conv):
            cx = tabs_ref[MISC_ROW + k : MISC_ROW + k + 1, :]
            cbc = bcp_ref[SYM + k : SYM + k + 1, :]
            lo, hi = mid - SYM * k, mid + SYM * k
            wf[lo : lo + SYM, base + XF : base + XF + LANES] = xt * cx
            wf[hi : hi + SYM, base + XB : base + XB + LANES] = xt * cx
            wf[lo : lo + SYM, base + BCF : base + BCF + 256] = bct * cbc
            wf[hi : hi + SYM, base + BCB : base + BCB + 256] = bct * cbc
        dt = jnp.maximum(dtt, 0.0) + jnp.log1p(jnp.exp(-jnp.abs(dtt)))
        ld = -jnp.exp(tabs_ref[MISC_ROW + 4 : MISC_ROW + 5, :]) * dt
        for k, piece in enumerate(thirds(ld)):
            w2[SYM * k : SYM * (k + 1), st * 128 : st * 128 + 128] = piece
            w2[32 + SYM * k : 32 + SYM * (k + 1), 256 + st * 128 : 384 + st * 128] = piece
            for h in range(2):
                at = 24 * (st * 2 + h) + SYM * k
                rate_ref[at : at + SYM, :] = jnp.broadcast_to(
                    piece[:, 64 * h : 64 * h + 1], piece.shape
                )
        for k, piece in enumerate(thirds(dt)):
            c = 512 + st * 128
            w2[64 + SYM * k : 64 + SYM * (k + 1), c : c + 128] = piece
    top, rest = halves(wf[...])
    w_ref[0:64, :] = top
    w_ref[64:128, :] = rest
    w2_out[...] = w2[...].astype(BF16)


def prepare(scalars, tok_refs, w_ref, w2_ref, r, conv):
    ns = len(tok_refs)
    length = ns * BLOCK
    mine = scalars[1]
    for k in range(ns):
        sym = lax.broadcasted_iota(jnp.int32, (SYM, BLOCK), 0).astype(F32)
        tok = jnp.broadcast_to(tok_refs[k][BLOCK : BLOCK + 1, 0:BLOCK].astype(F32), (SYM, BLOCK))
        at = jnp.bitwise_xor(mine, k) * BLOCK
        r.oh[:, pl.ds(pl.multiple_of(at, BLOCK), BLOCK)] = (sym == tok).astype(F32)
    oh = r.oh[...]
    lane = lax.broadcasted_iota(jnp.int32, (SYM, length), 1)
    up = (
        lax.broadcasted_iota(jnp.int32, (BLOCK, BLOCK), 0)
        <= lax.broadcasted_iota(jnp.int32, (BLOCK, BLOCK), 1)
    ).astype(BF16)
    r.rows[...] = jnp.zeros_like(r.rows)
    for d in range(1 - conv, conv):
        shifted = oh if d == 0 else pltpu.roll(oh, (length - d) % length, 1)
        inside = jnp.logical_and(lane + d >= 0, lane + d < length)
        r.rows[SYM * (d + conv - 1) : SYM * (d + conv), :] = jnp.where(inside, shifted, 0.0)
    r.rows[64:128, :] = r.rows[0:64, :]
    one = lax.broadcasted_iota(jnp.int32, (SYM, length), 0) < 3
    r.rows[152:160, :] = one.astype(F32)
    r.rows[184:192, :] = one.astype(F32)
    r.prow[...] = jnp.zeros_like(r.prow)
    oh_b = oh.astype(BF16)
    for b in range(ns):
        cols = slice(b * BLOCK, (b + 1) * BLOCK)
        inc = mm(oh_b[:, cols], up, NN)
        exc = inc - oh[:, cols]
        r.inc[:, cols] = inc
        r.exc[:, cols] = exc
        for k in range(3):
            r.rows[128 + SYM * k : 128 + SYM * (k + 1), cols] = inc
            r.rows[160 + SYM * k : 160 + SYM * (k + 1), cols] = exc
            r.rows[192 + SYM * k : 192 + SYM * (k + 1), cols] = oh[:, cols]
    r.sym[...] = r.rows[0:64, :].astype(BF16)
    turned = jnp.transpose(r.rows[...].astype(BF16))
    r.pre[...] = mm(turned[:, 0:128], w_ref[...], NN)
    w2 = w2_ref[...]
    r.pd[...] = mm(turned[:, 128:256], w2[:, 0:768], NN)
    r.count[...] = turned[:, 128:192]
    for st in range(2):
        for part, row0 in ((0, 0), (1, 32)):
            c = part * 256 + st * 128
            flat = mm(
                w2[row0 : row0 + 32, c : c + 128],
                r.rows[128 + row0 : 160 + row0, :].astype(BF16),
                TN,
            )
            for h in range(2):
                i = part * 4 + st * 2 + h
                row = flat[64 * h : 64 * h + 1, :]
                if part == 0:
                    row = -row
                for k, piece in enumerate(thirds(row)):
                    r.prow[SYM * i + k : SYM * i + k + 1, :] = piece


class Unit:
    def __init__(self, r, tabs_ref, st, b, nb):
        self.rows = rows = slice(b * BLOCK, (b + 1) * BLOCK)
        base = st * WIDE
        self.skip = tabs_ref[MISC_ROW + 5 : MISC_ROW + 6, :]
        self.dt = r.pd[rows, 512 + st * 128 : 512 + st * 128 + 128]
        self.p = r.pd[rows, st * 128 : st * 128 + 128]
        self.q = r.pd[rows, 256 + st * 128 : 256 + st * 128 + 128]
        self.total = self.p[BLOCK - 1 : BLOCK, :]
        self.r, self.st, self.b, self.base = r, st, b, base
        lane = lax.broadcasted_iota(jnp.int32, (BLOCK, LANES), 1)
        self.head0 = lane < 64
        row = lax.broadcasted_iota(jnp.int32, (BLOCK, BLOCK), 0)
        self.low = row >= lane
        self.upp = row <= lane

    def pre(self, col, width):
        return self.r.pre[self.rows, self.base + col : self.base + col + width]

    def act(self, col, width):
        v = self.pre(col, width)
        return v * sigmoid(v)

    def by_head(self, v):
        zero = jnp.zeros_like(v)
        return jnp.where(self.head0, v, zero), jnp.where(self.head0, zero, v)

    def decay(self, h):
        r, st = self.r, self.st
        i = st * 2 + h
        rate = r.rate[24 * i : 24 * i + 24, :]
        ends = r.prow[SYM * i : SYM * (i + 1), self.rows]
        starts = r.prow[SYM * (4 + i) : SYM * (5 + i), self.rows]
        zero = jnp.zeros((32, LANES), F32)
        below = jnp.concatenate([rate, ends, zero], 0)
        above = jnp.concatenate([zero, -rate, starts], 0)
        gap = mm(r.count[self.rows, :], jnp.concatenate([below, above], 1).astype(BF16), NN)
        return jnp.exp(jnp.where(self.low, gap[:, 0:LANES], gap[:, LANES : 2 * LANES]))


def state_pass_fwd(r, tabs_ref, nb, units):
    for st in range(2):
        for b in range(nb):
            u = units[st][b]
            xf, xb = u.act(XF, 128), u.act(XB, 128)
            bcf, bcb = u.act(BCF, 256), u.act(BCB, 256)
            r.x[u.rows, st * 256 : st * 256 + 128] = xf
            r.x[u.rows, st * 256 + 128 : st * 256 + 256] = xb
            r.bc[u.rows, st * 512 : st * 512 + 256] = bcf
            r.bc[u.rows, st * 512 + 256 : st * 512 + 512] = bcb
            wf = jnp.exp(u.total - u.p) * (u.dt * xf)
            wb = jnp.exp(u.q) * (u.dt * xb)
            if b < nb - 1:
                r.s[st * 2, b + 1] = mm_fine(bcf[:, 0:128], wf, TN, 2)
            if b > 0:
                r.s[st * 2 + 1, b - 1] = mm_fine(bcb[:, 0:128], wb, TN, 2)
        for b in range(2, nb):
            r.s[st * 2, b] += jnp.exp(units[st][b - 1].total) * r.s[st * 2, b - 1]
        for b in range(nb - 3, -1, -1):
            r.s[st * 2 + 1, b] += jnp.exp(units[st][b + 1].total) * r.s[st * 2 + 1, b + 1]


def together(bodies):
    bodies = list(bodies)
    while bodies:
        bodies = [b for b in bodies if next(b, True) is None]


class Names:
    pass


def named(refs, names):
    r = Names()
    for name, ref in zip(names, refs):
        setattr(r, name, ref)
    return r


KEPT = ("inc", "exc", "oh", "sym", "pre", "pd", "x", "bc", "s", "dec", "wts", "ys")


def kept_shapes(length):
    nb = length // BLOCK
    return [
        ((SYM, length), F32),
        ((SYM, length), F32),
        ((SYM, length), F32),
        ((64, length), BF16),
        ((length, 2 * WIDE), F32),
        ((length, 768), F32),
        ((length, 512), F32),
        ((length, 1024), F32),
        ((4, nb, LANES, LANES), F32),
        ((4 * nb, BLOCK, BLOCK), F32),
        ((8 * nb, BLOCK, BLOCK), BF16),
        ((length, 1024), F32),
    ]


def forward_kernel(scalars, *refs, ns, conv):
    tok_refs, (w_ref, w2_ref, rate_ref, tabs_ref, out_ref) = refs[:ns], refs[ns : ns + 5]
    r = named(refs[ns + 5 :], KEPT + ("rows", "prow", "count"))
    r.rate = rate_ref
    prepare(scalars, tok_refs, w_ref, w2_ref, r, conv)
    units = [[Unit(r, tabs_ref, st, b, ns) for b in range(ns)] for st in range(2)]
    state_pass_fwd(r, tabs_ref, ns, units)
    gated = {}

    def body(st, b):
        u = units[st][b]
        x = [r.x[u.rows, st * 256 + w * 128 : st * 256 + w * 128 + 128] for w in range(2)]
        decays = (u.decay(0), u.decay(1))
        yield
        masks, lefts, cms = (u.low, u.upp), [], []
        for w in range(2):
            c = st * 512 + w * 256
            bm, cm = r.bc[u.rows, c : c + 128], r.bc[u.rows, c + 128 : c + 256]
            lefts.append(mm_fine(cm, bm, NT, 3))
            cms.append(cm)
        yield
        y = u.skip * (x[0] + x[1])
        for w in range(2):
            if (w == 0 and b > 0) or (w == 1 and b < ns - 1):
                enter = jnp.exp(u.p) if w == 0 else jnp.exp(u.total - u.q)
                carried = enter * mm_fine(cms[w], r.s[st * 2 + w, b], NN, 2)
                r.ys[u.rows, st * 512 + w * 256 + 128 : st * 512 + w * 256 + 256] = carried
                y = y + carried
        yield
        for h in range(2):
            r.dec[(st * ns + b) * 2 + h] = decays[h]
        for w in range(2):
            g = jnp.where(masks[w], lefts[w], 0.0)
            lefts[w] = [(g * d).astype(BF16) for d in decays]
            for h in range(2):
                r.wts[((st * ns + b) * 2 + w) * 2 + h] = lefts[w][h]
        yield
        for w in range(2):
            right = u.by_head((u.dt * x[w]).astype(BF16))
            inner = mm(jnp.concatenate(lefts[w], 1), jnp.concatenate(right, 0), NN)
            r.ys[u.rows, st * 512 + w * 256 : st * 512 + w * 256 + 128] = inner
            y = y + inner
        gated[st, b] = y * u.act(ZZ, 128)

    for b0 in range(0, ns, GROUP):
        together(body(st, b) for b in range(b0, min(b0 + GROUP, ns)) for st in range(2))
        for b in range(b0, min(b0 + GROUP, ns)):
            out_ref[:, units[0][b].rows] = jnp.transpose(gated[0, b] + gated[1, b]).astype(BF16)


def backward_kernel(scalars, *refs, ns, nq, conv, vocab):
    tabs_ref, bcp_ref, dt1_ref, perm_ref = refs[:4]
    cot_refs, weight_ref = refs[4 : 4 + nq], refs[4 + nq]
    kept = refs[5 + nq : 5 + nq + len(KEPT)]
    out_ref, *work = refs[5 + nq + len(KEPT) :]
    r = named(list(kept) + work, KEPT + ("ds", "dg", "dpre"))
    cols = cot_refs[0].shape[2]
    cot = jnp.concatenate([a[...].reshape(ns * BLOCK, cols) for a in cot_refs], 1)
    weight = []
    for k in range(nq):
        at = pl.multiple_of(scalars[QUARTERS + k] * cols, LANES)
        rows = pl.ds(pl.multiple_of(scalars[0] * LANES, LANES), LANES)
        weight.append(weight_ref[rows, pl.ds(at, cols)])
    d_gated = mm(cot, jnp.concatenate(weight, 1), NT).astype(BF16).astype(F32)
    mine = scalars[1]
    for k in range(ns):
        at = jnp.bitwise_xor(mine, k)
        r.dg[pl.ds(pl.multiple_of(at * BLOCK, BLOCK), BLOCK), :] = d_gated[
            k * BLOCK : (k + 1) * BLOCK
        ]
    units = [[Unit(r, tabs_ref, st, b, ns) for b in range(ns)] for st in range(2)]
    for st in range(2):
        for b in range(ns):
            u = units[st][b]
            dy = r.dg[u.rows, :] * u.act(ZZ, 128)
            cf = r.bc[u.rows, st * 512 + 128 : st * 512 + 256]
            cb = r.bc[u.rows, st * 512 + 384 : st * 512 + 512]
            if b > 0:
                r.ds[st * 2, b - 1] = mm_fine(cf, jnp.exp(u.p) * dy, TN, 2)
            if b < ns - 1:
                r.ds[st * 2 + 1, b + 1] = mm_fine(cb, jnp.exp(u.total - u.q) * dy, TN, 2)
        for b in range(ns - 3, -1, -1):
            r.ds[st * 2, b] += jnp.exp(units[st][b + 1].total) * r.ds[st * 2, b + 1]
        for b in range(2, ns):
            r.ds[st * 2 + 1, b] += jnp.exp(units[st][b - 1].total) * r.ds[st * 2 + 1, b - 1]
    d_steps = [jnp.zeros((SYM, LANES), F32)] * 2
    d_decays = [jnp.zeros((SYM, LANES), F32)] * 2
    d_tab = 0.0

    def body(st, b):
        u = units[st][b]
        base = st * WIDE
        x = [r.x[u.rows, st * 256 + w * 128 : st * 256 + w * 128 + 128] for w in range(2)]
        dgv = r.dg[u.rows, :]
        pz = u.pre(ZZ, 128)
        sz = sigmoid(pz)
        dy = dgv * (pz * sz)
        dyr = dy.astype(BF16)
        dyw = dyr.astype(F32)
        dy0, dy1 = u.by_head(dyr)
        decays = [r.dec[(st * ns + b) * 2 + h] for h in range(2)]
        inputs = [u.dt * v for v in x]
        ur = [v.astype(BF16) for v in inputs]
        uw = [v.astype(F32) for v in ur]
        uh = [u.by_head(v) for v in ur]
        d_pair = mm(dyr, jnp.concatenate([uh[0][0], uh[0][1], uh[1][0], uh[1][1]], 0), NT)
        yield
        masks = (u.low, u.upp)
        ends = (jnp.exp(u.total - u.p), jnp.exp(u.q))
        enters = (jnp.exp(u.p), jnp.exp(u.total - u.q))
        weights, bms, cms = [], [], []
        for w in range(2):
            c = st * 512 + w * 256
            bm, cm = r.bc[u.rows, c : c + 128], r.bc[u.rows, c + 128 : c + 256]
            weights.append([r.wts[((st * ns + b) * 2 + w) * 2 + h] for h in range(2)])
            bms.append(bm)
            cms.append(cm)
        du_both = mm(
            jnp.concatenate(
                [
                    jnp.concatenate([weights[0][0], weights[1][0]], 1),
                    jnp.concatenate([weights[0][1], weights[1][1]], 1),
                ],
                0,
            ),
            jnp.concatenate([dy0, dy1], 0),
            TN,
        )
        yield
        y = u.skip * (x[0] + x[1])
        mixes, step_part, flat = [], 0.0, 0.0
        for w in range(2):
            yield
            c = st * 512 + w * 256
            inner = r.ys[u.rows, c : c + 128]
            du_in = du_both[w * BLOCK : (w + 1) * BLOCK]
            has_enter = (w == 0 and b > 0) or (w == 1 and b < ns - 1)
            has_leave = (w == 0 and b < ns - 1) or (w == 1 and b > 0)
            y = y + inner
            row = dyw * inner - uw[w] * du_in
            du = du_in
            d_g = jnp.where(
                masks[w],
                d_pair[:, w * 256 : w * 256 + 128] * decays[0]
                + d_pair[:, w * 256 + 128 : w * 256 + 256] * decays[1],
                0.0,
            ).astype(BF16)
            d_c = mm(d_g, bms[w].astype(BF16), NN)
            d_b = mm(d_g, cms[w].astype(BF16), TN)
            enter_part = gain_part = None
            if has_enter:
                state = r.s[st * 2 + w, b]
                carried = r.ys[u.rows, c + 128 : c + 256]
                y = y + carried
                enter_part = dy * carried
                d_c = d_c + mm((enters[w] * dy).astype(BF16), state.astype(BF16), NT)
            if has_leave:
                d_state = r.ds[st * 2 + w, b]
                d_gain = mm_fine(bms[w], d_state, NN, 2)
                du = du + ends[w] * d_gain
                gain = ends[w] * inputs[w]
                gain_part = gain * d_gain
                d_b = d_b + mm(gain.astype(BF16), d_state.astype(BF16), NT)
            if has_enter and has_leave:
                flat = flat + jnp.exp(u.total) * jnp.sum(state * d_state, 0, keepdims=True)
            if w == 1:
                row = -row
            if enter_part is not None:
                row = row + enter_part if w == 0 else row - enter_part
            if gain_part is not None:
                row = row - gain_part if w == 0 else row + gain_part
            if w == 0 and gain_part is not None:
                flat = flat + jnp.sum(gain_part, 0, keepdims=True)
            if w == 1 and enter_part is not None:
                flat = flat + jnp.sum(enter_part, 0, keepdims=True)
            mixes.append(row)
            step_part = step_part + du * x[w]
            dx = du * u.dt + dy * u.skip
            px = u.pre((XF, XB)[w], 128)
            sx = sigmoid(px)
            col = base + (XF, XB)[w]
            r.dpre[u.rows, col : col + 128] = (dx * (sx * (1.0 + px * (1.0 - sx)))).astype(BF16)
            col = (BCF, BCB)[w]
            for i, grad in enumerate((d_b, d_c)):
                pb = u.pre(col + 128 * i, 128)
                sb = sigmoid(pb)
                at = base + col + 128 * i
                r.dpre[u.rows, at : at + 128] = (
                    grad * (sb * (1.0 + pb * (1.0 - sb)))
                ).astype(BF16)
        yield
        d_z = dgv * y * (sz * (1.0 + pz * (1.0 - sz)))
        r.dpre[u.rows, base + ZZ : base + ZZ + 128] = d_z.astype(BF16)
        inc = r.inc[:, u.rows]
        exc = r.exc[:, u.rows]
        inc_b, exc_b, oh_b = inc.astype(BF16), exc.astype(BF16), r.oh[:, u.rows].astype(BF16)
        right = list(halves(mixes[0])) + list(halves(mixes[1]))
        decay_part = mm(
            jnp.concatenate([inc_b, inc_b, exc_b, exc_b], 1), jnp.concatenate(right, 0), NN
        )
        decay_part = decay_part + inc[:, BLOCK - 1 : BLOCK] * flat
        step_sum = mm(
            jnp.concatenate([oh_b, oh_b], 1), jnp.concatenate(halves(step_part), 0), NN
        )
        d_steps[st] = d_steps[st] + step_sum
        d_decays[st] = d_decays[st] + decay_part

    for b0 in range(0, ns, GROUP_BACK):
        last = min(b0 + GROUP_BACK, ns)
        together(body(st, b) for b in range(b0, last) for st in range(2))
        span = slice(b0 * BLOCK, last * BLOCK)
        d_tab = d_tab + mm(r.sym[:, span], r.dpre[span, :], NN)
    mid = SYM * (conv - 1)
    result = None
    for st in range(2):
        base = st * WIDE
        d_x = jnp.zeros((SYM, 128), F32)
        d_bc = jnp.zeros((SYM, 256), F32)
        for k in range(conv):
            cx = tabs_ref[MISC_ROW + k : MISC_ROW + k + 1, :]
            cbc = bcp_ref[SYM + k : SYM + k + 1, :]
            lo, hi = mid - SYM * k, mid + SYM * k
            d_x = d_x + cx * (
                d_tab[lo : lo + SYM, base + XF : base + XF + 128]
                + d_tab[hi : hi + SYM, base + XB : base + XB + 128]
            )
            d_bc = d_bc + cbc * (
                d_tab[lo : lo + SYM, base + BCF : base + BCF + 256]
                + d_tab[hi : hi + SYM, base + BCB : base + BCB + 256]
            )
        d_zt = d_tab[mid : mid + SYM, base + ZZ : base + ZZ + 128]
        dtt = dt1_ref[...] if st else tabs_ref[DT_ROW : DT_ROW + SYM, :]
        rate = -jnp.exp(tabs_ref[MISC_ROW + 4 : MISC_ROW + 5, :])
        d_dt = (d_steps[st] + rate * d_decays[st]) * sigmoid(dtt)
        wide = jnp.concatenate([d_x, d_zt, d_dt, d_bc], 1)
        if st == 0:
            result = wide
        else:
            for k in range(vocab):
                result = result + perm_ref[:, k : k + 1] * wide[k : k + 1]
    out_ref[...] = result


SMEM = pl.BlockSpec(memory_space=pltpu.SMEM)
VMEM = pl.BlockSpec(memory_space=pltpu.VMEM)
HBM = pl.BlockSpec(memory_space=pl.ANY)


def params(mib):
    return pltpu.CompilerParams(vmem_limit_bytes=mib * 1024 * 1024)


def call_tables(scalars, raw):
    basemap, xz_table, bc_table, conv_x, conv_bc, dt_table, a_log, skip_gain = raw
    conv, vocab = conv_x.shape[0], xz_table.shape[0]
    outs = [
        ((TAB_ROWS, LANES), F32),
        ((2 * SYM, 256), F32),
        ((SYM, LANES), F32),
        ((SYM, LANES), F32),
        ((128, 2 * WIDE), BF16),
        ((128, 768), BF16),
        ((96, LANES), F32),
    ]
    return pl.pallas_call(
        functools.partial(tables_kernel, conv=conv, vocab=vocab),
        out_shape=[jax.ShapeDtypeStruct(*a) for a in outs],
        in_specs=[SMEM, SMEM, VMEM, VMEM, SMEM],
        out_specs=[VMEM] * len(outs),
        scratch_shapes=[pltpu.VMEM((64, 2 * WIDE), F32), pltpu.VMEM((128, 768), F32)],
        compiler_params=params(8),
        cost_estimate=pl.CostEstimate(flops=2 * 10**9, transcendentals=0, bytes_accessed=10**6),
        name="tables",
    )(
        scalars,
        basemap,
        jnp.concatenate([xz_table.reshape(2 * vocab, -1), conv_x], 0),
        jnp.concatenate([bc_table, conv_bc], 0),
        jnp.concatenate([dt_table, a_log[None], skip_gain[None]], 0),
    )


def call_forward(scalars, pays, w, w2, rate, tabs, conv):
    ns = len(pays)
    length = ns * BLOCK
    outs = [((LANES, length), BF16)] + kept_shapes(length)
    return pl.pallas_call(
        functools.partial(forward_kernel, ns=ns, conv=conv),
        out_shape=[jax.ShapeDtypeStruct(*a) for a in outs],
        in_specs=[SMEM] + [VMEM] * (ns + 4),
        out_specs=[VMEM] * len(outs),
        scratch_shapes=[
            pltpu.VMEM((256, length), F32),
            pltpu.VMEM((64, length), F32),
            pltpu.VMEM((length, 64), BF16),
        ],
        compiler_params=params(8),
        cost_estimate=pl.CostEstimate(
            flops=5 * 10**9, transcendentals=0, bytes_accessed=8 * LANES * length
        ),
        name="mix_forward",
    )(scalars, *pays, w, w2, rate, tabs)


def call_backward(scalars, tables, cots, out_weight, kept, conv, vocab):
    length = kept[0].shape[1]
    ns = length // BLOCK
    return pl.pallas_call(
        functools.partial(backward_kernel, ns=ns, nq=len(cots), conv=conv, vocab=vocab),
        out_shape=jax.ShapeDtypeStruct((SYM, 640), F32),
        in_specs=[SMEM] + [VMEM] * (len(tables) + len(cots) + 1 + len(kept)),
        out_specs=VMEM,
        scratch_shapes=[
            pltpu.VMEM((4, ns, LANES, LANES), F32),
            pltpu.VMEM((length, LANES), F32),
            pltpu.VMEM((length, 2 * WIDE), BF16),
        ],
        compiler_params=params(10),
        cost_estimate=pl.CostEstimate(
            flops=6 * 10**9, transcendentals=0, bytes_accessed=8 * LANES * length
        ),
        name="mix_backward",
    )(scalars, *tables, *cots, out_weight, *kept)


QUARTERS = 3


def out_kernel(scalars, *refs, ns, nh, nc):
    slices, weight_ref, outs = refs[: ns * nc], refs[ns * nc], refs[ns * nc + 1 :]
    here = pl.ds(pl.multiple_of(scalars[1] * BLOCK, BLOCK), BLOCK)
    places = QUARTERS + nh * nc
    cols = outs[0].shape[1]
    left = jnp.concatenate([a[:, here] for a in slices], 0)
    for k in range(nh):
        at = pl.ds(pl.multiple_of(scalars[QUARTERS + k * nc] * cols, LANES), cols)
        right = []
        for i in range(ns * nc):
            rows = pl.ds(pl.multiple_of(scalars[places + i] * LANES, LANES), LANES)
            right.append(weight_ref[rows, at])
        outs[k][...] = mm(left, jnp.concatenate(right, 0), TN)


def call_out(scalars, slices, out_weight, ns, nh, nc):
    cols = out_weight.shape[1] // (nh * nc)
    return pl.pallas_call(
        functools.partial(out_kernel, ns=ns, nh=nh, nc=nc),
        out_shape=[jax.ShapeDtypeStruct((BLOCK, cols), F32)] * nh,
        in_specs=[SMEM] + [VMEM] * (len(slices) + 1),
        out_specs=[VMEM] * nh,
        compiler_params=params(8),
        name="layer_out",
    )(scalars, *slices, out_weight)


def weight_kernel(scalars, *refs, ns, nh, nc):
    slices, cots = refs[: ns * nc], refs[ns * nc : ns * nc + nh * nc]
    out_ref, mark_ref, left, buf, sems = refs[ns * nc + nh * nc :]
    mine = scalars[1]
    places = QUARTERS + nh * nc
    cols = cots[0].shape[2]
    mark_ref[...] = jnp.zeros_like(mark_ref)
    copies = []
    for n in range(ns * nc):
        span = slice(n * LANES, (n + 1) * LANES)
        for k in range(ns):
            at = pl.multiple_of(jnp.bitwise_xor(mine, k) * BLOCK, BLOCK)
            left[span, k * BLOCK : (k + 1) * BLOCK] = slices[n][:, pl.ds(at, BLOCK)]
        for q in range(nh * nc):
            at = pl.multiple_of(scalars[QUARTERS + q] * cols, LANES)
            right = cots[q][...].reshape(ns * BLOCK, cols)
            buf[span, pl.ds(at, cols)] = mm(left[span, :], right, NN)
        to = pl.multiple_of(scalars[places + n] * LANES, LANES)
        copy = pltpu.make_async_copy(
            buf.at[pl.ds(n * LANES, LANES), :], out_ref.at[pl.ds(to, LANES), :], sems.at[n]
        )
        copy.start()
        copies.append(copy)
    for copy in copies:
        copy.wait()


def call_weight(scalars, slices, cots, width, ns, nh, nc):
    length = slices[0].shape[1]
    rows = ns * nc * LANES
    return pl.pallas_call(
        functools.partial(weight_kernel, ns=ns, nh=nh, nc=nc),
        out_shape=[
            jax.ShapeDtypeStruct((rows, width), F32),
            jax.ShapeDtypeStruct((SYM, LANES), F32),
        ],
        in_specs=[SMEM] + [VMEM] * (len(slices) + len(cots)),
        out_specs=[HBM, VMEM],
        scratch_shapes=[
            pltpu.VMEM((rows, length), BF16),
            pltpu.VMEM((rows, width), F32),
            pltpu.SemaphoreType.DMA((ns * nc,)),
        ],
        compiler_params=params(12),
        cost_estimate=pl.CostEstimate(
            flops=2 * rows * width * length, transcendentals=0, bytes_accessed=6 * rows * width
        ),
        name="weight_grad",
    )(scalars, *slices, *cots)


def final_kernel(scalars, *refs, ns, nh, vocab, places):
    packs, parts = refs[:ns], refs[ns : ns + nh]
    out_ref, xz_ref, bc_ref, dt_ref = refs[ns + nh + 1 :]
    total = parts[0][...]
    for a in parts[1:]:
        total = total + a[...]
    out_ref[...] = total.astype(BF16)
    d_bc = packs[0][:, 768:1024]
    for a in packs[1:]:
        d_bc = d_bc + a[:, 768:1024]
    for i in range(2):
        for k in range(vocab):
            bc_ref[k, i : i + 1, :] = d_bc[k : k + 1, i * 128 : i * 128 + 128]
    lane = lax.broadcasted_iota(jnp.int32, (SYM, dt_ref.shape[1]), 1)
    d_dt = jnp.zeros((SYM, dt_ref.shape[1]), F32)
    for n in range(2 * ns):
        j = scalars[places + n]
        piece = packs[n % ns][:, n // ns * 384 : n // ns * 384 + 384]
        for i in range(2):
            for k in range(vocab):
                xz_ref[k, i : i + 1, pl.ds(pl.multiple_of(j * LANES, LANES), LANES)] = piece[
                    k : k + 1, i * 128 : i * 128 + 128
                ]
            row = jnp.sum(piece[:, 256 + 64 * i : 320 + 64 * i], 1, keepdims=True)
            d_dt = jnp.where(lane == 2 * j + i, row, d_dt)
    dt_ref[...] = d_dt[:vocab]


def call_final(scalars, packs, parts, mark, raw, places):
    shapes = [raw[1].shape, raw[2].shape, raw[5].shape]
    arrays = list(packs) + list(parts)
    return pl.pallas_call(
        functools.partial(
            final_kernel, ns=len(packs), nh=len(parts), vocab=raw[1].shape[0], places=places
        ),
        out_shape=[jax.ShapeDtypeStruct(parts[0].shape, BF16)]
        + [jax.ShapeDtypeStruct(a, F32) for a in shapes],
        in_specs=[SMEM] + [VMEM] * (len(arrays) + 1),
        out_specs=[VMEM] * (len(shapes) + 1),
        compiler_params=params(8),
        name="place_grads",
    )(scalars, *arrays, mark)


def around(x, axis):
    n = lax.axis_size(axis)
    return [x] + [lax.ppermute(x, axis, [(i, i ^ k) for i in range(n)]) for k in range(1, n)]


def across(x, hops, nh, nc):
    pairs = [
        (a * nc + b, (a + hops[0]) % nh * nc + (b + hops[1]) % nc)
        for a in range(nh)
        for b in range(nc)
    ]
    return lax.ppermute(x, ("head", "sub"), pairs)


def by_channel(
    token_ids, basemap, xz_table, bc_table, dt_table, conv_x, conv_bc, a_log, skip_gain, out_weight, cotangent
):
    ns, nc, nh = lax.axis_size("seq"), lax.axis_size("sub"), lax.axis_size("head")
    s, c, h = lax.axis_index("seq"), lax.axis_index("sub"), lax.axis_index("head")
    width = out_weight.shape[1]
    cols = width // (nh * nc)
    raw = (basemap, xz_table, bc_table, conv_x, conv_bc, dt_table, a_log, skip_gain)
    symbols = jnp.pad(token_ids.astype(BF16).reshape(1, BLOCK), ((0, 15), (0, cols - BLOCK)))
    pays = around(jnp.concatenate([cotangent, symbols], 0), "seq")
    slot = jnp.arange(nh * nc, dtype=jnp.int32)
    quarters = (h - slot // nc) % nh * nc + (c - slot % nc) % nc
    slot = jnp.arange(ns * nc, dtype=jnp.int32)
    places = (c - slot // ns) % nc * ns + jnp.bitwise_xor(s, slot % ns)
    scalars = jnp.concatenate([jnp.stack([c * ns + s, s, c]), quarters, places]).astype(jnp.int32)
    stacked = jnp.stack([a[:BLOCK] for a in pays], 0)
    heads = [stacked] + [across(stacked, (k, 0), nh, nc) for k in range(1, nh)]
    conv, vocab = conv_x.shape[0], xz_table.shape[0]
    *tables, w, w2, rate = call_tables(scalars, raw)
    gated, *kept = call_forward(scalars, pays, w, w2, rate, tables[0], conv)
    heads, _ = lax.optimization_barrier((heads, gated))
    cots = [heads[0], across(heads[0], (0, 1), nh, nc)]
    for a in heads[1:]:
        cots += [a, across(a, (0, 1), nh, nc)]
    hop = lambda x, k: lax.ppermute(x, "seq", [(i, i ^ k) for i in range(ns)])
    direct = {k: hop(gated, k) for k in (1 << n for n in range(ns.bit_length() - 1))}
    grads = call_backward(scalars, tables, cots, out_weight, kept, conv, vocab)
    direct, _ = lax.optimization_barrier((direct, grads))
    held = {0: gated, **direct}
    for k in range(3, ns):
        if k not in held:
            held[k] = hop(held[k & (k - 1)], k & -k)
    slices = [held[k] for k in range(ns)]
    slices = slices + [across(a, (0, 1), nh, nc) for a in slices]
    shared = grads[:, 384:]
    beside = across(grads, (0, 1), nh, nc)
    for a in range(1, nh):
        for b in range(nc):
            shared = shared + across(grads[:, 384:], (a, b), nh, nc)
    packed = jnp.concatenate([grads[:, :384], beside[:, :384], shared + beside[:, 384:]], 1)
    packs = around(packed, "seq")
    parts = call_out(scalars, slices, out_weight, ns, nh, nc)
    parts = [parts[0]] + [across(parts[k], (nh - k, 0), nh, nc) for k in range(1, nh)]
    d_out_weight, mark = call_weight(scalars, slices, cots, width, ns, nh, nc)
    layer_out, d_xz, d_bc, d_dt = call_final(
        scalars, packs, parts, mark, raw, QUARTERS + nh * nc
    )
    return (layer_out, d_out_weight, d_xz, d_bc, d_dt)


PRECISE = lax.Precision.HIGHEST


def carried_in(part, axis, combine, identity):
    place = lax.axis_index(axis)
    gathered = jax.tree.map(lambda a: lax.all_gather(a, axis), part)
    state = jax.tree.map(lambda a, e: jnp.zeros_like(a) + jnp.asarray(e, a.dtype), part, identity)

    def one(hop, state):
        return combine(
            state, jax.tree.map(lambda a: lax.dynamic_index_in_dim(a, hop, 0, False), gathered)
        )

    return lax.fori_loop(0, place, one, state)


def carried_in_2(array, axis, combine, identity):
    length, mine = (lax.axis_size(axis), lax.axis_index(axis))
    everything = jax.tree.map(
        lambda part, kind: lax.all_gather(part.astype(kind), axis),
        array,
        jax.tree.map(lambda a: jnp.bfloat16 if a.dtype == jnp.float32 else a.dtype, array),
    )
    start = jax.tree.map(
        lambda part, zero: jnp.broadcast_to(jnp.asarray(zero, part.dtype), part.shape),
        array,
        identity,
    )

    def hop(k, before):
        at = length - 1 - k
        reached = at > mine
        new = combine(
            before, jax.tree.map(lambda part, own: part[at].astype(own.dtype), everything, array)
        )
        return jax.tree.map(lambda a, b: jnp.where(reached, a, b), new, before)

    return lax.fori_loop(0, length, hop, start)


def with_halo(block, sides, width):
    for axis, dim in sides:
        count = lax.axis_size(axis)
        forward = [(i, i + 1) for i in range(count - 1)]
        backward = [(target, source) for source, target in forward]
        low = lax.ppermute(
            lax.slice_in_dim(block, block.shape[dim] - width, None, axis=dim), axis, forward
        )
        high = lax.ppermute(lax.slice_in_dim(block, 0, width, axis=dim), axis, backward)
        block = jnp.concatenate([low, block, high], axis=dim)
    return block


def block_step(carry_state, pieces):
    scaled_x, logdec, b_mat, c_mat = pieces
    block_len = scaled_x.shape[0]
    running = jnp.cumsum(logdec, axis=0)
    by_head = running.T
    causal_mask = (jnp.arange(block_len)[:, None] >= jnp.arange(block_len)[None, :])[None, :, :]
    gap_matrix = by_head[:, :, None] - by_head[:, None, :]
    decay_mat = jnp.where(causal_mask, jnp.exp(jnp.where(causal_mask, gap_matrix, 0.0)), 0.0)
    scores = jnp.einsum("tn,sn->ts", c_mat, b_mat, precision=PRECISE)
    within = jnp.einsum("hts,shp->thp", scores[None, :, :] * decay_mat, scaled_x, precision=PRECISE)
    carried = jnp.exp(running)[:, :, None] * jnp.einsum(
        "tn,hpn->thp", c_mat, carry_state, precision=PRECISE
    )
    to_end = jnp.exp(running[-1][None, :] - running)
    gained = jnp.einsum("shp,sn->hpn", to_end[:, :, None] * scaled_x, b_mat, precision=PRECISE)
    return (jnp.exp(running[-1])[:, None, None] * carry_state + gained, within + carried)


def state_pass(inputs, start_state, block_len):
    scaled_x, logdec, b_mat, c_mat = inputs
    block_count = scaled_x.shape[0] // block_len
    pieces = (
        scaled_x.reshape((block_count, block_len) + scaled_x.shape[1:]),
        logdec.reshape(block_count, block_len, -1),
        b_mat.reshape(block_count, block_len, -1),
        c_mat.reshape(block_count, block_len, -1),
    )
    end_state, outputs = lax.scan(jax.checkpoint(block_step), start_state, pieces)
    return (outputs.reshape(scaled_x.shape), end_state)


def final_state(inputs):
    scaled_x, logdec, b_mat, c_mat = inputs
    running = jnp.cumsum(logdec, axis=0)
    to_end = jnp.exp(running[-1][None, :] - running)
    gained = jnp.einsum("shp,sn->hpn", to_end[:, :, None] * scaled_x, b_mat, precision=PRECISE)
    return (jnp.exp(running[-1]), gained)


def lookup(symbols, table):
    vocab_size = table.shape[0]
    onehot = (symbols[:, None] == jnp.arange(vocab_size, dtype=jnp.int32)[None, :]).astype(
        jnp.float32
    )
    return jnp.dot(onehot, table, precision=PRECISE)


def conv_rows(extended, weight, row_count, forward):
    conv_width = weight.shape[0]
    rim_width = conv_width - 1
    summed = jnp.zeros((row_count, extended.shape[1]), jnp.float32)
    for offset in range(conv_width):
        if forward:
            first_row = rim_width - offset
        else:
            first_row = rim_width + offset
        summed = summed + weight[offset][None, :] * extended[first_row : first_row + row_count]
    return summed


def open_inputs(ext_sym, inside_mask, tables, frozen):
    xz_tab, bc_tab, dt_tab = tables
    conv_inner, conv_shared, log_rates, skip_vals = frozen
    rim_width = conv_inner.shape[0] - 1
    row_count = ext_sym.shape[0] - 2 * rim_width
    vocab_size = xz_tab.shape[0]
    inner_dim = xz_tab.shape[2]
    head_count = dt_tab.shape[1]
    state_dim = bc_tab.shape[2]
    looked = lookup(ext_sym, xz_tab.reshape(vocab_size, 2 * inner_dim)) * inside_mask[:, None]
    pre_x = looked[:, :inner_dim]
    gate_act = jax.nn.silu(looked[rim_width : rim_width + row_count, inner_dim:])
    pre_bc = lookup(ext_sym, bc_tab.reshape(vocab_size, 2 * state_dim)) * inside_mask[:, None]
    dt_step = jax.nn.softplus(lookup(ext_sym[rim_width : rim_width + row_count], dt_tab))
    logdec = -jnp.exp(log_rates)[None, :] * dt_step
    flat_bc = conv_shared.reshape(conv_inner.shape[0], 2 * state_dim)

    def one_way(forward):
        x_conv = jax.nn.silu(conv_rows(pre_x, conv_inner, row_count, forward)).reshape(
            row_count, head_count, -1
        )
        bc_conv = jax.nn.silu(conv_rows(pre_bc, flat_bc, row_count, forward))
        return (x_conv, bc_conv[:, :state_dim], bc_conv[:, state_dim:])

    x_fwd, b_fwd, c_fwd = one_way(True)
    x_back, b_back, c_back = one_way(False)
    ahead_in = (x_fwd * dt_step[:, :, None], logdec, b_fwd, c_fwd)
    behind_in = (
        jnp.flip(x_back * dt_step[:, :, None], 0),
        jnp.flip(logdec, 0),
        jnp.flip(b_back, 0),
        jnp.flip(c_back, 0),
    )
    skip_term = skip_vals[None, :, None] * (x_fwd + x_back)
    return (ahead_in, behind_in, skip_term, gate_act)


def combine(earlier, later):
    decay_early, state_early = earlier
    decay_late, state_late = later
    return (decay_early * decay_late, decay_late[:, None, None] * state_early + state_late)


def carries(ahead_pair, behind_pair):
    ahead_out = carried_in(
        (ahead_pair[0], ahead_pair[1]),
        "seq",
        combine,
        (jnp.ones_like(ahead_pair[0]), jnp.zeros_like(ahead_pair[1])),
    )
    behind_out = carried_in_2(
        (behind_pair[0], behind_pair[1]),
        "seq",
        combine,
        (jnp.ones_like(behind_pair[0]), jnp.zeros_like(behind_pair[1])),
    )
    return (ahead_out[1], behind_out[1])


def decay_weights(adjoint, start_state):
    return jnp.sum(adjoint * start_state, axis=(1, 2))


def shards(
    token_ids,
    basemap,
    xz_table,
    bc_table,
    dt_table,
    conv_x,
    conv_bc,
    a_log,
    skip_gain,
    out_weight,
    cotangent,
):
    row_count = token_ids.shape[0]
    rim_width = conv_x.shape[0] - 1
    ext_ids = with_halo(token_ids, (("seq", 0),), rim_width)
    first_row = lax.axis_index("seq") * row_count - rim_width
    where_global = first_row + jnp.arange(row_count + 2 * rim_width, dtype=jnp.int32)
    inside_mask = jnp.logical_and(
        where_global >= 0, where_global < row_count * lax.axis_size("seq")
    ).astype(jnp.float32)
    vocab_size = basemap.shape[0]
    matches = ext_ids[:, None] == jnp.arange(vocab_size, dtype=jnp.int32)[None, :]
    mapped = jnp.sum(jnp.where(matches, basemap[None, :], 0), axis=1)
    ext_sym = jnp.where(lax.axis_index("sub") == 1, mapped, ext_ids)
    tables = (xz_table.astype(jnp.float32), bc_table.astype(jnp.float32), dt_table)
    frozen = (conv_x.astype(jnp.float32), conv_bc.astype(jnp.float32), a_log, skip_gain)

    def summary(tabs_in):
        ahead_in, behind_in, skip_term, gate_act = open_inputs(
            ext_sym, inside_mask, tabs_in, frozen
        )
        decay_fwd, end_fwd = final_state(ahead_in)
        decay_back, end_back = final_state(behind_in)
        return (decay_fwd, end_fwd, decay_back, end_back)

    (decay_fwd, end_fwd, decay_back, end_back), pull_summary = jax.vjp(summary, tables)
    start_fwd, start_back = carries((decay_fwd, end_fwd), (decay_back, end_back))

    def finished(tabs_in, begin_fwd, begin_back):
        ahead_in, behind_in, skip_term, gate_act = open_inputs(
            ext_sym, inside_mask, tabs_in, frozen
        )
        out_fwd, unused_fwd = state_pass(ahead_in, begin_fwd, BLOCK)
        out_back, unused_back = state_pass(behind_in, begin_back, BLOCK)
        return (out_fwd + jnp.flip(out_back, 0) + skip_term).reshape(row_count, -1) * gate_act

    gated, pull_finished = jax.vjp(finished, tables, start_fwd, start_back)
    gated_bf = gated.astype(jnp.bfloat16)
    products = jnp.dot(gated_bf, out_weight, preferred_element_type=jnp.float32)
    layer_out = lax.psum_scatter(products, ("head", "sub"), scatter_dimension=1, tiled=True).astype(
        jnp.bfloat16
    )
    full_cot = lax.all_gather(cotangent, ("head", "sub"), axis=1, tiled=True)
    d_gated = jnp.einsum(
        "tc,kc->tk", full_cot, out_weight, preferred_element_type=jnp.float32
    ).astype(jnp.bfloat16)
    weight_part = jnp.einsum("tk,tc->kc", gated_bf, full_cot, preferred_element_type=jnp.float32)
    d_gated_wide = lax.optimization_barrier(d_gated).astype(jnp.float32)
    grads_first, direct_fwd, direct_back = pull_finished(d_gated_wide)
    adjoint_back, adjoint_fwd = carries((decay_back, direct_back), (decay_fwd, direct_fwd))
    grads_second = pull_summary(
        (
            decay_weights(adjoint_fwd, start_fwd),
            adjoint_fwd,
            decay_weights(adjoint_back, start_back),
            adjoint_back,
        )
    )[0]
    d_tables = jax.tree.map(lambda former, latter: former + latter, grads_first, grads_second)
    d_xz, d_bc, d_dt = d_tables
    d_bc = lax.psum(d_bc, ("seq", "head", "sub"))
    d_out_weight, d_xz, d_dt = lax.psum((weight_part, d_xz, d_dt), ("seq", "sub"))
    return (layer_out, d_out_weight, d_xz, d_bc, d_dt)


def solution(mesh):
    in_specs = (
        P(("grp", "seq")),
        P(),
        P(None, None, "head"),
        P(),
        P(None, "head"),
        P(None, "head"),
        P(),
        P("head"),
        P("head"),
        P("head", None),
        P(("grp", "seq"), ("head", "sub")),
    )
    out_specs = (
        P(("grp", "seq"), ("head", "sub")),
        P(("grp", "head"), None),
        P("grp", None, "head"),
        P("grp", None, None),
        P("grp", "head"),
    )
    def run(*args):
        ns, nc = mesh.shape["seq"], mesh.shape["sub"]
        rows, inner, heads = args[0].shape[0], args[2].shape[2], args[4].shape[1]
        by_lanes = (
            rows == BLOCK
            and nc == 2
            and ns > 1
            and ns & (ns - 1) == 0
            and inner == ns * nc * LANES
            and inner == heads * (LANES // 2)
            and args[3].shape[2] == LANES
            and args[5].shape[0] == 4
            and args[9].shape[1] == args[10].shape[1] * nc * mesh.shape["head"]
        )
        return (by_channel if by_lanes else shards)(*args)

    return jax.shard_map(run, mesh=mesh, in_specs=in_specs, out_specs=out_specs, check_vma=False)
```
